32 devices in a mesh: fsdp: 4 (over y, core), ctx: 2 (over x), tp: 4 (over z).
Axes of the slice: x: 2, y: 2, z: 4, core: 2. Of those that a mesh axis runs over, the one named last changes fastest.
Arguments:
- tokens: bfloat16 [8192, 768], P(('fsdp', 'ctx')), may hold values from -6 to 6
- encoder: bfloat16 [16384, 768], P(('fsdp', 'ctx')), may hold values from -6 to 6
- cotangent: bfloat16 [8192, 768], P(('fsdp', 'ctx')), may hold values from -6 to 6
- parents: int32 [8, 8], P('fsdp'), may hold values from 0 to 6, as said below
- targets: int32 [8192], P(('fsdp', 'ctx')), may hold values from 0 to 32127
- w_query: bfloat16 [768, 768], P(('fsdp', 'ctx'), 'tp'), may hold values from -0.0546875 to 0.0546875
- w_key: bfloat16 [768, 768], P(('fsdp', 'ctx'), 'tp'), may hold values from -0.21875 to 0.21875
- w_value: bfloat16 [768, 768], P(('fsdp', 'ctx'), 'tp'), may hold values from -0.21875 to 0.21875
- w_out: bfloat16 [768, 768], P('tp', ('fsdp', 'ctx')), may hold values from -0.875 to 0.875
- c_query: bfloat16 [768, 768], P(('fsdp', 'ctx'), 'tp'), may hold values from -0.0546875 to 0.0546875
- c_key: bfloat16 [768, 768], P(('fsdp', 'ctx'), 'tp'), may hold values from -0.21875 to 0.21875
- c_value: bfloat16 [768, 768], P(('fsdp', 'ctx'), 'tp'), may hold values from -0.21875 to 0.21875
- c_out: bfloat16 [768, 768], P('tp', ('fsdp', 'ctx')), may hold values from -0.875 to 0.875
- w_gate: bfloat16 [768, 2048], P(('fsdp', 'ctx'), 'tp'), may hold values from -0.21875 to 0.21875
- w_up: bfloat16 [768, 2048], P(('fsdp', 'ctx'), 'tp'), may hold values from -0.21875 to 0.21875
- w_down: bfloat16 [2048, 768], P('tp', ('fsdp', 'ctx')), may hold values from -0.125 to 0.125
- embedding: bfloat16 [32128, 768], P('tp', ('fsdp', 'ctx')), may hold values from -12 to 12
- norm_self: bfloat16 [768], P(('fsdp', 'ctx')), may hold values from 0.5 to 1.5
- norm_cross: bfloat16 [768], P(('fsdp', 'ctx')), may hold values from 0.5 to 1.5
- norm_ff: bfloat16 [768], P(('fsdp', 'ctx')), may hold values from 0.5 to 1.5
- norm_exit: bfloat16 [768], P(('fsdp', 'ctx')), may hold values from 0.5 to 1.5
Outputs:
- mixed: bfloat16 [8192, 768], P(('fsdp', 'ctx'))
- exit_loss: float32 [8192], P(('fsdp', 'ctx'))
- exit_score: float32 [8192], P(('fsdp', 'ctx'))
- grad_tokens: float32 [8192, 768], P(('fsdp', 'ctx'))
- grad_encoder: float32 [16384, 768], P(('fsdp', 'ctx'))
- grad_w_query: float32 [768, 768], P(('fsdp', 'ctx'), 'tp')
- grad_w_key: float32 [768, 768], P(('fsdp', 'ctx'), 'tp')
- grad_w_value: float32 [768, 768], P(('fsdp', 'ctx'), 'tp')
- grad_w_out: float32 [768, 768], P('tp', ('fsdp', 'ctx'))
- grad_c_query: float32 [768, 768], P(('fsdp', 'ctx'), 'tp')
- grad_c_key: float32 [768, 768], P(('fsdp', 'ctx'), 'tp')
- grad_c_value: float32 [768, 768], P(('fsdp', 'ctx'), 'tp')
- grad_c_out: float32 [768, 768], P('tp', ('fsdp', 'ctx'))
- grad_w_gate: float32 [768, 2048], P(('fsdp', 'ctx'), 'tp')
- grad_w_up: float32 [768, 2048], P(('fsdp', 'ctx'), 'tp')
- grad_w_down: float32 [2048, 768], P('tp', ('fsdp', 'ctx'))
- grad_embedding: float32 [32128, 768], P('tp', ('fsdp', 'ctx'))
- grad_norm_self: float32 [768], P(('fsdp', 'ctx'))
- grad_norm_cross: float32 [768], P(('fsdp', 'ctx'))
- grad_norm_ff: float32 [768], P(('fsdp', 'ctx'))
- grad_norm_exit: float32 [768], P(('fsdp', 'ctx'))
The draws below stay inside these ranges and needn't reach their ends.
Inputs may be any that keep to these rules, and one draw needn't show every extreme that they name: parents[t, 0] = 0; blocks 1 to 3 each name the block before them; every later block names a block at index 3 or later that comes before it; the last block names the one before it.
All inputs are finite; a program needn't handle non-finite values.
Results may differ from the reference program's by a relative error of at most 0.03.
The reference program's roundings to bfloat16 on the way count: a program that leaves them out, or rounds other values in their place, can miss the bound.
Values may be sent and summed in bfloat16 or wider, within the bound.
A program may use at most 256 MiB of HBM per device.

```python
import math
import jax
import jax.numpy as jnp
from jax import lax

D = 768
H = 12
HD = 64
FF = 2048
VOCAB = 32128
BLK = 128
TREE_BLK = 8
MB = 2
INNER = 768
GROUP_TOK = 1024
TOK_MB = 512
ENC_DEV = 1024
TREES = 8
TOKENS = 8192
ENC_ALL = 16384
N_FSDP = 4
N_CTX = 2


def draw_parents(key, part):
    blocks = jnp.arange(TREE_BLK, dtype=jnp.int32)
    middle = TREE_BLK // 2
    lowest = jnp.where(blocks < middle, blocks - 1, middle - 1)
    spread = jnp.maximum(blocks - lowest, 1)
    raw_draws = jax.random.randint(key, (TREES, TREE_BLK), 0, 1 << 20, dtype=jnp.int32)
    parent = lowest[None, :] + raw_draws % spread[None, :]
    parent = jnp.where(blocks[None, :] == 0, 0, parent)
    parent = jnp.where(blocks[None, :] == TREE_BLK - 1, TREE_BLK - 2, parent)
    return parent.astype(jnp.int32)


def place_ends(result, stream_key, least, top_value):
    spot = [jax.random.randint(jax.random.fold_in(stream_key, axis), (), 0, length) for axis, length in enumerate(result.shape)]
    longest = result.shape.index(max(result.shape))
    next_to = spot[:longest] + [(spot[longest] + 1) % result.shape[longest]] + spot[longest + 1:]
    return result.at[tuple(spot)].set(least).at[tuple(next_to)].set(top_value)


def steps_of(key, dims, pieces, low, top_value):
    def one(position, parts):
        draws = jax.random.uniform(jax.random.fold_in(jax.random.fold_in(key, 6), position), (parts,), jnp.float32, low / len(pieces), top_value / len(pieces))
        return jnp.repeat(jnp.exp(draws), dims[position] // parts).reshape((-1,) + (1,) * (len(dims) - position - 1))

    level = one(*pieces[0])
    for cut in pieces[1:]:
        level = level * one(*cut)
    return level


def bell_draw(rng, shape, deviation, reach, pieces=(), kind=jnp.bfloat16):
    result = jax.random.normal(rng, shape, jnp.float32) * deviation
    if len(pieces) > 0:
        result = steps_of(rng, shape, pieces, -0.22, 0.18) * result
    return jnp.clip(result, min=-reach, max=reach).astype(kind)


def setup_inputs(seed: int = 0) -> dict:
    key_list = jax.random.split(jax.random.key(seed), 22)
    return {
        "tokens": bell_draw(key_list[0], (TOKENS, D), 1.0, 6.0, ((0, 8),)),
        "encoder": bell_draw(key_list[1], (ENC_ALL, D), 1.0, 6.0, ((0, 8),)),
        "cotangent": bell_draw(key_list[2], (TOKENS, D), 1.0, 6.0, ((0, 8),)),
        "parents": draw_parents(jax.random.fold_in(key_list[21], 71), 0),
        "targets": place_ends(jax.random.randint(key_list[4], (TOKENS,), 0, VOCAB), jax.random.fold_in(key_list[4], 1), 0, VOCAB - 1).astype(jnp.int32),
        "w_query": bell_draw(key_list[5], (D, INNER), (D * HD // 4) ** -0.5, 0.0546875, ((0, 8), (1, 4))),
        "w_key": bell_draw(key_list[6], (D, INNER), D ** -0.5, 0.21875, ((0, 8), (1, 4))),
        "w_value": bell_draw(key_list[7], (D, INNER), D ** -0.5, 0.21875, ((0, 8), (1, 4))),
        "w_out": bell_draw(key_list[8], (INNER, D), (INNER // 16) ** -0.5, 0.875, ((0, 4), (1, 8))),
        "c_query": bell_draw(key_list[9], (D, INNER), (D * HD // 4) ** -0.5, 0.0546875, ((0, 8), (1, 4))),
        "c_key": bell_draw(key_list[10], (D, INNER), D ** -0.5, 0.21875, ((0, 8), (1, 4))),
        "c_value": bell_draw(key_list[11], (D, INNER), D ** -0.5, 0.21875, ((0, 8), (1, 4))),
        "c_out": bell_draw(key_list[12], (INNER, D), (INNER // 16) ** -0.5, 0.875, ((0, 4), (1, 8))),
        "w_gate": bell_draw(key_list[13], (D, FF), D ** -0.5, 0.21875, ((0, 8), (1, 4))),
        "w_up": bell_draw(key_list[14], (D, FF), D ** -0.5, 0.21875, ((0, 8), (1, 4))),
        "w_down": bell_draw(key_list[15], (FF, D), FF ** -0.5, 0.125, ((0, 4), (1, 8))),
        "embedding": bell_draw(key_list[16], (VOCAB, D), 2.0, 12.0, ((0, 4), (1, 8))),
        "norm_self": jnp.clip(1.0 + 0.1 * jax.random.normal(key_list[17], (D,), jnp.float32), 0.5, 1.5).astype(jnp.bfloat16),
        "norm_cross": jnp.clip(1.0 + 0.1 * jax.random.normal(key_list[18], (D,), jnp.float32), 0.5, 1.5).astype(jnp.bfloat16),
        "norm_ff": jnp.clip(1.0 + 0.1 * jax.random.normal(key_list[19], (D,), jnp.float32), 0.5, 1.5).astype(jnp.bfloat16),
        "norm_exit": jnp.clip(1.0 + 0.1 * jax.random.normal(key_list[20], (D,), jnp.float32), 0.5, 1.5).astype(jnp.bfloat16),
    }


@jax.custom_vjp
def low(v):
    return lax.optimization_barrier(v.astype(jnp.bfloat16)).astype(jnp.float32)

@jax.custom_vjp
def low_back(v):
    return v

def low_keep(v):
    return (low(v), None)

def low_pass(kept, grad):
    return (grad,)

def back_keep(v):
    return (v, None)

def back_low(kept, grad):
    return (low(grad),)
low.defvjp(low_keep, low_pass)
low_back.defvjp(back_keep, back_low)
EPSILON = 1e-06
MASKED = -1000000000.0
HIGH = lax.Precision.HIGHEST

def product(left, right):
    return jnp.dot(left, right, precision=HIGH, preferred_element_type=jnp.float32)

def rms_scale(values):
    return lax.rsqrt(lax.optimization_barrier(jnp.mean(values * values, axis=-1, keepdims=True)) + EPSILON)

def ancestry(parent_row):
    block_count = parent_row.shape[0]
    blocks = jnp.arange(block_count, dtype=jnp.int32)
    current = blocks
    reachable = blocks[:, None] == blocks[None, :]
    for walking in range(block_count):
        current = parent_row[current].astype(jnp.int32)
        reachable = reachable | (current[:, None] == blocks[None, :])
    return reachable

def path_mask(parent_row):
    reachable = ancestry(parent_row)
    positions = jnp.arange(GROUP_TOK, dtype=jnp.int32)
    block_of = positions // BLK
    linked = reachable[block_of[:, None], block_of[None, :]]
    causal = (block_of[:, None] != block_of[None, :]) | (positions[None, :] <= positions[:, None])
    return linked & causal

def split_heads(values):
    return values.reshape(values.shape[0], H, HD)

def attend_block(query_block, keys_heads, values_heads, allowed_block):
    scores = low_back(jnp.einsum('qhd,khd->hqk', query_block, keys_heads, precision=HIGH))
    if allowed_block is not None:
        scores = jnp.where(allowed_block[None], scores, MASKED)
    weights = jax.nn.softmax(scores, axis=-1)
    return jnp.einsum('hqk,khd->qhd', low(weights), values_heads, precision=HIGH)

def attention(queries, keys_all, values_all, allowed):
    row_count = queries.shape[0]
    block_count = row_count // BLK
    query_blocks = split_heads(queries).reshape(block_count, BLK, H, HD)
    keys_heads = split_heads(keys_all)
    values_heads = split_heads(values_all)
    if allowed is None:
        block_step = jax.checkpoint(lambda query_block, keys_in, values_in: attend_block(query_block, keys_in, values_in, None))
        outcome = lax.map(lambda element: block_step(element, keys_heads, values_heads), query_blocks)
    else:
        block_step = jax.checkpoint(attend_block)
        mask_blocks = allowed.reshape(block_count, BLK, allowed.shape[1])
        outcome = lax.map(lambda element: block_step(element[0], keys_heads, values_heads, element[1]), (query_blocks, mask_blocks))
    return outcome.reshape(row_count, H * HD)

def exit_block(normed_block, target_block, embedding):
    logits = low_back(product(normed_block, embedding.T))
    log_total = jax.nn.logsumexp(logits, axis=-1)
    columns = jnp.arange(logits.shape[1], dtype=jnp.int32)
    picked = lax.optimization_barrier(jnp.sum(jnp.where(columns[None, :] == target_block[:, None], logits, 0.0), axis=-1))
    return (log_total - picked, lax.optimization_barrier(jnp.max(logits, axis=-1)) - log_total)

def layer_tree(tokens, encoder, weights, cotangent, allowed, targets):
    w_query, w_key, w_value, w_out, c_query, c_key, c_value, c_out, w_gate, w_up, w_down, embedding, norm_self, norm_cross, norm_ff, norm_exit = weights
    hidden_self = low(tokens * rms_scale(tokens) * norm_self)
    queries = low_back(low(product(hidden_self, w_query)))
    keys_self = low_back(low(product(hidden_self, w_key)))
    values_self = low_back(low(product(hidden_self, w_value)))
    attended = attention(queries, keys_self, values_self, allowed)
    after_self = tokens + low_back(product(low_back(low(attended)), w_out))
    hidden_cross = low(after_self * rms_scale(after_self) * norm_cross)
    cross_queries = low_back(low(product(hidden_cross, c_query)))
    cross_keys = low_back(low(product(encoder, c_key)))
    cross_values = low_back(low(product(encoder, c_value)))
    crossed = attention(cross_queries, cross_keys, cross_values, None)
    after_cross = after_self + low_back(product(low_back(low(crossed)), c_out))
    hidden_ff = low(after_cross * rms_scale(after_cross) * norm_ff)
    gate_pre = low_back(product(hidden_ff, w_gate))
    up_pre = low_back(product(hidden_ff, w_up))
    activated = low(jax.nn.gelu(gate_pre, approximate=True) * up_pre)
    mixed_float = after_cross + low_back(product(activated, w_down))
    exit_in = low(mixed_float * rms_scale(mixed_float) * norm_exit * (1.0 / math.sqrt(D)))
    block_count = exit_in.shape[0] // BLK
    block_step = jax.checkpoint(exit_block)
    losses, scores = lax.map(lambda element: block_step(element[0], element[1], embedding), (exit_in.reshape(block_count, BLK, D), targets.reshape(block_count, BLK)))
    losses = losses.reshape(-1)
    scores = scores.reshape(-1)
    objective = jnp.sum(losses) + jnp.sum(mixed_float * cotangent)
    return (objective, (mixed_float, losses, scores))

def to_trees(array, per_device):
    trailing = array.shape[1:]
    grouped = array.reshape((N_FSDP, N_CTX, MB, per_device) + trailing)
    grouped = jnp.swapaxes(grouped, 1, 2)
    return grouped.reshape((N_FSDP * MB, N_CTX * per_device) + trailing)

def from_trees(array, per_device):
    trailing = array.shape[2:]
    grouped = array.reshape((N_FSDP, MB, N_CTX, per_device) + trailing)
    grouped = jnp.swapaxes(grouped, 1, 2)
    return grouped.reshape((N_FSDP * N_CTX * MB * per_device,) + trailing)

def reference(tokens, encoder, cotangent, parents, targets, w_query, w_key, w_value, w_out, c_query, c_key, c_value, c_out, w_gate, w_up, w_down, embedding, norm_self, norm_cross, norm_ff, norm_exit):
    weights = tuple((element.astype(jnp.float32) for element in (w_query, w_key, w_value, w_out, c_query, c_key, c_value, c_out, w_gate, w_up, w_down, embedding, norm_self, norm_cross, norm_ff, norm_exit)))
    tree_tokens = to_trees(tokens.astype(jnp.float32), TOK_MB)
    tree_encoder = to_trees(encoder.astype(jnp.float32), ENC_DEV)
    tree_cotangent = to_trees(cotangent.astype(jnp.float32), TOK_MB)
    tree_targets = to_trees(targets, TOK_MB)

    def per_tree(running, element):
        tokens_tree, encoder_tree, cotangent_tree, parent_row, targets_tree = element
        allowed = path_mask(parent_row)

        def forward(tokens_in, encoder_in, weights_in):
            return layer_tree(tokens_in, encoder_in, weights_in, cotangent_tree, allowed, targets_tree)
        objective, pull_back, extras = jax.vjp(forward, tokens_tree, encoder_tree, weights, has_aux=True)
        grad_tokens, grad_encoder, grad_weights = pull_back(jnp.ones_like(objective))
        running = jax.tree.map(jnp.add, running, grad_weights)
        return (running, (extras[0], extras[1], extras[2], grad_tokens, grad_encoder))
    zero_grads = jax.tree.map(jnp.zeros_like, weights)
    weight_grads, stacked = lax.scan(per_tree, zero_grads, (tree_tokens, tree_encoder, tree_cotangent, parents, tree_targets))
    mixed = from_trees(stacked[0], TOK_MB).astype(jnp.bfloat16)
    exit_loss = from_trees(stacked[1], TOK_MB)
    exit_score = from_trees(stacked[2], TOK_MB)
    grad_tokens = from_trees(stacked[3], TOK_MB)
    grad_encoder = from_trees(stacked[4], ENC_DEV)
    return (mixed, exit_loss, exit_score, grad_tokens, grad_encoder, weight_grads[0], weight_grads[1], weight_grads[2], weight_grads[3], weight_grads[4], weight_grads[5], weight_grads[6], weight_grads[7], weight_grads[8], weight_grads[9], weight_grads[10], weight_grads[11], weight_grads[12], weight_grads[13], weight_grads[14], weight_grads[15])
```

```python
import functools
import math

import jax
import jax.numpy as jnp
from jax import lax
from jax.experimental import pallas as pl
from jax.experimental.pallas import tpu as pltpu
from jax.sharding import PartitionSpec as P

HD = 64
BLK = 128
MB = 2
EPSILON = 1e-06
MASKED = -1000000000.0
F32 = jnp.float32
BF16 = jnp.bfloat16
PLANE = ("fsdp", "ctx")
VMEM_LIMIT = 48 * 1024 * 1024


def mat(left, right):
    return jnp.dot(left, right, preferred_element_type=F32)


def mat_nt(left, right):
    return lax.dot_general(left, right, (((1,), (1,)), ((), ())), preferred_element_type=F32)


def mat_tn(left, right):
    return lax.dot_general(left, right, (((0,), (0,)), ((), ())), preferred_element_type=F32)


def swap(value, axis, bit):
    count = lax.axis_size(axis)
    return lax.ppermute(value, axis, [(i, i ^ bit) for i in range(count)])


def core_swap(value):
    return swap(value, "fsdp", 1)


def small_plane():
    return lax.axis_size("fsdp") == 4 and lax.axis_size("ctx") == 2


def coords():
    f = lax.axis_index("fsdp")
    return f // 2, f % 2, lax.axis_index("ctx")


def ordered(pieces, y, core, x):
    rows, columns = pieces[0][0][0].shape
    out = jnp.zeros((8 * rows, columns), pieces[0][0][0].dtype)
    for dy in range(2):
        for dc in range(2):
            for dx in range(2):
                index = ((y ^ dy) * 2 + (core ^ dc)) * 2 + (x ^ dx)
                out = lax.dynamic_update_slice(out, pieces[dy][dc][dx], (index * rows, 0))
    return out


def chips_gather(first, second):
    first_x = swap(first, "ctx", 1)
    second_y = swap(second, "fsdp", 2)
    first_pair = jnp.stack([first, first_x])
    second_pair = jnp.stack([second, second_y])
    first_far = swap(first_pair, "fsdp", 2)
    second_far = swap(second_pair, "ctx", 1)
    firsts = [[first, first_x], [first_far[0], first_far[1]]]
    seconds = [[second, second_far[0]], [second_y, second_far[1]]]
    return firsts, seconds


def plane_gather(shard):
    if not small_plane():
        return lax.all_gather(shard, PLANE, axis=0, tiled=True)
    y, core, x = coords()
    half = shard.shape[1] // 2
    firsts, seconds = chips_gather(shard[:, :half], shard[:, half:])
    mine = [
        [jnp.concatenate([firsts[dy][dx], seconds[dy][dx]], axis=1) for dx in range(2)]
        for dy in range(2)
    ]
    other = core_swap(jnp.stack([mine[0][0], mine[0][1], mine[1][0], mine[1][1]]))
    pieces = [[mine[dy], [other[dy * 2], other[dy * 2 + 1]]] for dy in range(2)]
    return ordered(pieces, y, core, x)


def embed_gather(shard):
    half = shard.shape[1] // 2
    y, core, x = coords()
    if not small_plane():
        whole = lax.all_gather(shard, PLANE, axis=0, tiled=True)
        return lax.dynamic_slice_in_dim(whole, core * half, half, 1)
    firsts, seconds = chips_gather(shard[:, :half], shard[:, half:])
    flat_first = jnp.stack([firsts[0][0], firsts[0][1], firsts[1][0], firsts[1][1]])
    flat_second = jnp.stack([seconds[0][0], seconds[0][1], seconds[1][0], seconds[1][1]])
    is_first = core == 0
    keep = jnp.where(is_first, flat_first, flat_second)
    give = jnp.where(is_first, flat_second, flat_first)
    other = core_swap(give)
    pieces = [
        [[keep[dy * 2], keep[dy * 2 + 1]], [other[dy * 2], other[dy * 2 + 1]]] for dy in range(2)
    ]
    return ordered(pieces, y, core, x)


def pick(value, index):
    return lax.dynamic_index_in_dim(value, index, 0, False)


def low_sum(left, right):
    return (left.astype(F32) + right.astype(F32)).astype(BF16)


def chips_scatter(first, second, y, x):
    first_mid = low_sum(pick(first, y), swap(pick(first, 1 - y), "fsdp", 2))
    moved = jnp.moveaxis(second, 1, 0)
    second_mid = low_sum(pick(moved, x), swap(pick(moved, 1 - x), "ctx", 1))
    first_out = pick(first_mid, x).astype(F32) + swap(pick(first_mid, 1 - x), "ctx", 1).astype(F32)
    second_out = pick(second_mid, y).astype(F32) + swap(pick(second_mid, 1 - y), "fsdp", 2).astype(
        F32
    )
    return first_out, second_out


def plane_scatter(total):
    if not small_plane():
        return lax.psum_scatter(total.astype(F32), PLANE, scatter_dimension=0, tiled=True)
    y, core, x = coords()
    rows, columns = total.shape[0] // 8, total.shape[1]
    blocks = total.reshape(2, 2, 2, rows, columns)
    keep = lax.dynamic_index_in_dim(blocks, core, 1, False)
    give = lax.dynamic_index_in_dim(blocks, 1 - core, 1, False)
    chip = low_sum(keep, core_swap(give))
    half = columns // 2
    first, second = chips_scatter(chip[..., :half], chip[..., half:], y, x)
    return jnp.concatenate([first, second], axis=1)


def embed_scatter(total):
    y, core, x = coords()
    rows, half = total.shape[0] // 8, total.shape[1]
    if not small_plane():
        n_plane = lax.axis_size("fsdp") * lax.axis_size("ctx")
        whole = jnp.zeros((total.shape[0], 2 * half), F32)
        whole = lax.dynamic_update_slice(whole, total.astype(F32), (0, core * half))
        return lax.psum_scatter(whole, PLANE, scatter_dimension=0, tiled=True)
    blocks = jnp.moveaxis(total.reshape(2, 2, 2, rows, half), 1, 2)
    first, second = chips_scatter(blocks[:, :, 0], blocks[:, :, 1], y, x)
    is_first = core == 0
    keep = jnp.where(is_first, first, second)
    give = jnp.where(is_first, second, first)
    other = core_swap(give.astype(BF16)).astype(F32)
    return jnp.concatenate(
        [jnp.where(is_first, keep, other), jnp.where(is_first, other, keep)], axis=1
    )


def tp_list(value):
    count = lax.axis_size("tp")
    return [value] + [
        lax.ppermute(value, "tp", [(i, (i + k) % count) for i in range(count)])
        for k in range(1, count)
    ]


def tp_sum(partial):
    count = lax.axis_size("tp")
    t = lax.axis_index("tp")
    rows = partial.shape[0] // count
    low = partial.astype(BF16)

    def block(k):
        return lax.dynamic_slice_in_dim(low, ((t + k) % count) * rows, rows, 0)

    total = lax.dynamic_slice_in_dim(partial, t * rows, rows, 0)
    for k in range(1, count):
        got = lax.ppermute(block(k), "tp", [(i, (i + k) % count) for i in range(count)])
        total = total + got.astype(F32)
    shares = tp_list(total.astype(BF16))
    ring = jnp.concatenate(shares[::-1] * 2, axis=0)
    return lax.dynamic_slice_in_dim(ring, ((count - 1 - t) % count) * rows, count * rows, 0).astype(
        F32
    )


def ctx_gather(value):
    if lax.axis_size("ctx") == 2:
        return jnp.concatenate([value, swap(value, "ctx", 1)], axis=0)
    return lax.all_gather(value, "ctx", axis=0, tiled=True)


def ctx_positions(rows):
    c, count = lax.axis_index("ctx"), lax.axis_size("ctx")
    if count == 2:
        return jnp.concatenate(
            [c * rows + jnp.arange(rows), (1 - c) * rows + jnp.arange(rows)]
        ).astype(jnp.int32)
    return jnp.arange(rows * count, dtype=jnp.int32)


def ctx_scatter(value):
    if lax.axis_size("ctx") == 2:
        rows = value.shape[0] // 2
        return low_sum(value[:rows], swap(value[rows:], "ctx", 1))
    return lax.psum_scatter(value.astype(F32), "ctx", scatter_dimension=0, tiled=True).astype(BF16)


def forward_kernel(heads, q_ref, kv_ref, bias_ref, out_ref, total_ref):
    width = heads * HD
    for h in range(heads):
        cols = slice(h * HD, (h + 1) * HD)
        keys = kv_ref[:, cols]
        values = kv_ref[:, width + h * HD : width + (h + 1) * HD]
        scores = mat_nt(keys, q_ref[:, cols])
        if bias_ref is not None:
            scores = scores + bias_ref[...]
        highest = jnp.max(scores, axis=0, keepdims=True)
        exponent = jnp.exp(scores - highest)
        denominator = jnp.sum(exponent, axis=0, keepdims=True)
        outcome = mat_tn(values, exponent.astype(BF16)) / denominator
        out_ref[:, cols] = outcome.T.astype(BF16)
        total_ref[h : h + 1, :] = highest + jnp.log(denominator)


def backward_kernel(
    heads, q_ref, kv_ref, bias_ref, total_ref, go_ref, dq_ref, dkv_ref, acc_ref
):
    width = heads * HD
    step = pl.program_id(0)

    @pl.when(step == 0)
    def _():
        acc_ref[...] = jnp.zeros_like(acc_ref)

    for h in range(heads):
        cols = slice(h * HD, (h + 1) * HD)
        vcols = slice(width + h * HD, width + (h + 1) * HD)
        keys, values = kv_ref[:, cols], kv_ref[:, vcols]
        queries, go = q_ref[:, cols], go_ref[:, cols]
        scores = mat_nt(keys, queries)
        if bias_ref is not None:
            scores = scores + bias_ref[...]
        probs = jnp.exp(scores - total_ref[h : h + 1, :])
        grad_probs = mat_nt(values, go)
        inner = jnp.sum(probs * grad_probs, axis=0, keepdims=True)
        grad_scores = (probs * (grad_probs - inner)).astype(BF16)
        acc_ref[:, vcols] += mat(probs.astype(BF16), go)
        acc_ref[:, cols] += mat(grad_scores, queries)
        dq_ref[:, cols] = mat_tn(keys, grad_scores).T.astype(BF16)

    @pl.when(step == pl.num_programs(0) - 1)
    def _():
        dkv_ref[...] = acc_ref[...].astype(BF16)


def attention_specs(rows, width, keys, tile, masked):
    specs = [
        pl.BlockSpec((tile, width), lambda i: (i, 0)),
        pl.BlockSpec((keys, 2 * width), lambda i: (0, 0)),
    ]
    if masked:
        specs.append(pl.BlockSpec((keys, tile), lambda i: (0, i)))
    return specs


def attend(queries, kv, bias):
    rows, width = queries.shape
    keys, heads = kv.shape[0], width // HD
    tile = min(rows, 256)
    masked = bias is not None
    body = functools.partial(forward_kernel, heads)
    if not masked:
        plain = body
        body = lambda q, k, o, t: plain(q, k, None, o, t)
    return pl.pallas_call(
        body,
        grid=(rows // tile,),
        in_specs=attention_specs(rows, width, keys, tile, masked),
        out_specs=[
            pl.BlockSpec((tile, width), lambda i: (i, 0)),
            pl.BlockSpec((heads, tile), lambda i: (0, i)),
        ],
        out_shape=[
            jax.ShapeDtypeStruct((rows, width), BF16),
            jax.ShapeDtypeStruct((heads, rows), F32),
        ],
        compiler_params=pltpu.CompilerParams(vmem_limit_bytes=VMEM_LIMIT),
        cost_estimate=pl.CostEstimate(
            flops=16 * rows * keys * width,
            bytes_accessed=4 * keys * width + 8 * rows * width,
            transcendentals=rows * keys * heads,
        ),
        name="attend_masked" if masked else "attend",
    )(*([queries, kv, bias] if masked else [queries, kv]))


def attend_back(queries, kv, bias, totals, go):
    rows, width = queries.shape
    keys, heads = kv.shape[0], width // HD
    tile = min(rows, 256)
    masked = bias is not None
    body = functools.partial(backward_kernel, heads)
    if not masked:
        plain = body
        body = lambda q, k, *rest: plain(q, k, None, *rest)
    specs = attention_specs(rows, width, keys, tile, masked) + [
        pl.BlockSpec((heads, tile), lambda i: (0, i)),
        pl.BlockSpec((tile, width), lambda i: (i, 0)),
    ]
    operands = ([queries, kv, bias] if masked else [queries, kv]) + [totals, go]
    return pl.pallas_call(
        body,
        grid=(rows // tile,),
        in_specs=specs,
        out_specs=[
            pl.BlockSpec((tile, width), lambda i: (i, 0)),
            pl.BlockSpec((keys, 2 * width), lambda i: (0, 0)),
        ],
        out_shape=[
            jax.ShapeDtypeStruct((rows, width), BF16),
            jax.ShapeDtypeStruct((keys, 2 * width), BF16),
        ],
        scratch_shapes=[pltpu.VMEM((keys, 2 * width), F32)],
        compiler_params=pltpu.CompilerParams(vmem_limit_bytes=VMEM_LIMIT),
        cost_estimate=pl.CostEstimate(
            flops=40 * rows * keys * width,
            bytes_accessed=8 * keys * width + 10 * rows * width,
            transcendentals=rows * keys * heads,
        ),
        name="attend_back_masked" if masked else "attend_back",
    )(*operands)


def rms_scale(values):
    return lax.rsqrt(jnp.mean(values * values, axis=-1, keepdims=True) + EPSILON)


def rms_back(grad_normed, normed, scale):
    return scale * (grad_normed - normed * jnp.mean(grad_normed * normed, axis=-1, keepdims=True))


def mask_bias(parent_row, row_count):
    block_count = parent_row.shape[0]
    blocks = jnp.arange(block_count, dtype=jnp.int32)
    current = blocks
    reachable = blocks[:, None] == blocks[None, :]
    for _ in range(block_count - 1):
        current = jnp.sum(
            jnp.where(current[:, None] == blocks[None, :], parent_row[None, :], 0), axis=1
        )
        reachable = reachable | (current[:, None] == blocks[None, :])
    query_pos = lax.axis_index("ctx") * row_count + jnp.arange(row_count, dtype=jnp.int32)
    key_pos = ctx_positions(row_count)
    query_onehot = (query_pos[:, None] // BLK == blocks[None, :]).astype(F32)
    key_onehot = (key_pos[:, None] // BLK == blocks[None, :]).astype(F32)
    linked = mat_nt(key_onehot, mat(query_onehot, reachable.astype(F32))) > 0.5
    causal = (query_pos[None, :] // BLK != key_pos[:, None] // BLK) | (
        key_pos[:, None] <= query_pos[None, :]
    )
    return jnp.where(linked & causal, 0.0, MASKED)


def gelu_parts(gate):
    root = math.sqrt(2.0 / math.pi)
    inner = jnp.tanh(root * (gate + 0.044715 * gate * gate * gate))
    value = 0.5 * gate * (1.0 + inner)
    slope = 0.5 * (1.0 + inner) + 0.5 * gate * (1.0 - inner * inner) * root * (
        1.0 + 3.0 * 0.044715 * gate * gate
    )
    return value, slope


def head_stats(stats):
    tp_count, f_count = lax.axis_size("tp"), lax.axis_size("fsdp")
    rows = stats.shape[1] // 2
    parts = []
    for dc in range(2):
        for k in range(tp_count):
            if dc == 0 and k == 0:
                parts.append(stats)
                continue
            perm = [
                (f * tp_count + t, (f ^ dc) * tp_count + (t + k) % tp_count)
                for f in range(f_count)
                for t in range(tp_count)
            ]
            got = lax.ppermute(stats, ("fsdp", "tp"), perm)
            if dc == 1:
                got = jnp.concatenate([got[:, rows:], got[:, :rows]], axis=1)
            parts.append(got)
    highest = functools.reduce(jnp.maximum, [part[0] for part in parts])
    total = sum(part[1] * jnp.exp(part[0] - highest) for part in parts)
    picked = sum(part[2] for part in parts)
    return highest, highest + jnp.log(total), picked


def local(
    tokens,
    encoder,
    cotangent,
    parents,
    targets,
    w_query,
    w_key,
    w_value,
    w_out,
    c_query,
    c_key,
    c_value,
    c_out,
    w_gate,
    w_up,
    w_down,
    embedding,
    norm_self,
    norm_cross,
    norm_ff,
    norm_exit,
):
    t = lax.axis_index("tp")
    core = lax.axis_index("fsdp") % 2
    rows = tokens.shape[0] // MB
    enc_rows = encoder.shape[0] // MB
    features = tokens.shape[1]
    width = w_query.shape[1]
    hidden_units = w_gate.shape[1]
    tp_count = lax.axis_size("tp")
    trees = range(MB)

    def tree_rows(value, i):
        count = value.shape[0] // MB
        return value[i * count : (i + 1) * count]

    w_heads = plane_gather(
        jnp.concatenate([w_query, w_key, w_value, c_key, c_value, c_query], axis=1)
    )
    w_qkv = w_heads[:, : 3 * width]
    c_kv = w_heads[:, 3 * width : 5 * width]
    c_q = w_heads[:, 5 * width :]
    gains = plane_gather(
        jnp.pad(
            jnp.stack([norm_self, norm_cross, norm_ff, norm_exit], axis=1), ((0, 0), (0, 252))
        )
    )[:, :4].astype(F32)
    gain_self, gain_cross, gain_ff, gain_exit = (gains[:, j][None, :] for j in range(4))
    pieces = tp_list(
        jnp.concatenate([w_out.T, c_out.T, c_query, w_gate, w_up, w_down.T], axis=1)
    )
    spans = [0, width, 2 * width, 3 * width]
    spans += [spans[-1] + hidden_units * j for j in (1, 2, 3)]
    ordered_pieces = [
        jnp.concatenate([piece[:, spans[j] : spans[j + 1]] for piece in pieces], axis=1)
        for j in range(6)
    ]
    whole = plane_gather(jnp.concatenate(ordered_pieces, axis=1))
    cuts = [tp_count * s for s in spans]
    w_out_t, c_out_t, c_query_all, gate_all, up_all, down_t = (
        whole[:, cuts[j] : cuts[j + 1]] for j in range(6)
    )
    embed_t = embed_gather(embedding.T)
    vocab_half = embed_t.shape[1]

    tok = tokens.astype(F32)
    scale_one = rms_scale(tok)
    normed_one = tok * scale_one
    hidden_one = (normed_one * gain_self).astype(BF16)
    qkv = mat(hidden_one, w_qkv).astype(BF16)
    enc_kv = mat(encoder, c_kv).astype(BF16)
    queries = [tree_rows(qkv, i)[:, :width] for i in trees]
    kv_self = [ctx_gather(tree_rows(qkv, i)[:, width:]) for i in trees]
    kv_cross = [ctx_gather(tree_rows(enc_kv, i)) for i in trees]
    biases = [mask_bias(parents[i], rows) for i in trees]
    targets_all = [
        jnp.concatenate([tree_rows(targets, i), core_swap(tree_rows(targets, i))]) for i in trees
    ]
    shrink = 1.0 / math.sqrt(features)

    saved = []
    for i in trees:
        attended, totals_self = attend(queries[i], kv_self[i], biases[i])
        attended_all = jnp.concatenate(tp_list(attended), axis=1)
        after_self = tree_rows(tok, i) + mat_nt(attended_all, w_out_t)
        scale_two = rms_scale(after_self)
        normed_two = after_self * scale_two
        hidden_two = (normed_two * gain_cross).astype(BF16)
        cross_q = mat(hidden_two, c_q).astype(BF16)
        crossed, totals_cross = attend(cross_q, kv_cross[i], None)
        crossed_all = jnp.concatenate(tp_list(crossed), axis=1)
        after_cross = after_self + mat_nt(crossed_all, c_out_t)
        scale_three = rms_scale(after_cross)
        normed_three = after_cross * scale_three
        hidden_three = (normed_three * gain_ff).astype(BF16)
        gate_pre = mat(hidden_three, gate_all)
        up_pre = mat(hidden_three, up_all)
        activated = (gelu_parts(gate_pre)[0] * up_pre).astype(BF16)
        mixed = after_cross + mat_nt(activated, down_t)
        scale_four = rms_scale(mixed)
        normed_four = mixed * scale_four
        exit_own = (normed_four * gain_exit * shrink).astype(BF16)
        exit_in = jnp.concatenate([exit_own, core_swap(exit_own)], axis=0)
        saved.append(
            dict(
                attended=attended,
                totals_self=totals_self,
                scale_two=scale_two,
                normed_two=normed_two,
                hidden_two=hidden_two,
                cross_q=cross_q,
                crossed=crossed,
                totals_cross=totals_cross,
                scale_three=scale_three,
                normed_three=normed_three,
                hidden_three=hidden_three,
                gate_pre=gate_pre,
                up_pre=up_pre,
                activated=activated,
                mixed=mixed,
                scale_four=scale_four,
                normed_four=normed_four,
                exit_in=exit_in,
            )
        )

    columns = (t * 2 + core) * vocab_half + jnp.arange(vocab_half, dtype=jnp.int32)
    losses, scores, grad_embed = [], [], None
    for i in trees:
        s = saved[i]
        logits = mat(s["exit_in"], embed_t)
        hits = columns[None, :] == targets_all[i][:, None]
        highest = jnp.max(logits, axis=-1)
        summed = jnp.sum(jnp.exp(logits - highest[:, None]), axis=-1)
        picked = jnp.sum(jnp.where(hits, logits, 0.0), axis=-1)
        top, log_total, picked = head_stats(jnp.stack([highest, summed, picked]))
        losses.append((log_total - picked)[:rows])
        scores.append((top - log_total)[:rows])
        grad_logits = (jnp.exp(logits - log_total[:, None]) - hits.astype(F32)).astype(BF16)
        grad_exit_part = mat_nt(grad_logits, embed_t)
        s["grad_exit_part"] = grad_exit_part[:rows] + core_swap(
            grad_exit_part[rows:].astype(BF16)
        ).astype(F32)
        s["grad_exit"] = tp_sum(s["grad_exit_part"]) * shrink
        term = mat_tn(s["exit_in"], grad_logits)
        grad_embed = term if grad_embed is None else grad_embed + term
    grad_embed_own = embed_scatter(grad_embed.astype(BF16))

    norm_terms = [0.0, 0.0, 0.0, 0.0]
    grads = [None] * 7

    def add(j, term):
        grads[j] = term if grads[j] is None else grads[j] + term

    def norm_add(j, grad, normed):
        norm_terms[j] = norm_terms[j] + jnp.sum(grad * normed, axis=0)

    grad_tokens, grad_encoder = [], []
    for i in trees:
        s = saved[i]
        grad_exit = s["grad_exit"]
        norm_add(3, grad_exit, s["normed_four"])
        grad_mixed = tree_rows(cotangent, i).astype(F32) + rms_back(
            grad_exit * gain_exit, s["normed_four"], s["scale_four"]
        )
        grad_mixed_low = grad_mixed.astype(BF16)
        add(6, mat_tn(grad_mixed_low, s["activated"][:, :hidden_units]))
        grad_act = mat(grad_mixed_low, down_t)
        value, slope = gelu_parts(s["gate_pre"])
        grad_gate = (grad_act * slope * s["up_pre"]).astype(BF16)
        grad_up = (grad_act * value).astype(BF16)
        add(4, mat_tn(s["hidden_three"], grad_gate[:, :hidden_units]))
        add(5, mat_tn(s["hidden_three"], grad_up[:, :hidden_units]))
        grad_three = mat_nt(grad_gate, gate_all) + mat_nt(grad_up, up_all)
        norm_add(2, grad_three, s["normed_three"])
        grad_after_cross = grad_mixed + rms_back(
            grad_three * gain_ff, s["normed_three"], s["scale_three"]
        )
        grad_cross_low = grad_after_cross.astype(BF16)
        add(3, mat_tn(grad_cross_low, s["crossed"]))
        grad_crossed = mat(grad_cross_low, c_out_t[:, :width]).astype(BF16)
        grad_cq, grad_kv = attend_back(
            s["cross_q"], kv_cross[i], None, s["totals_cross"], grad_crossed
        )
        grad_kv = ctx_scatter(grad_kv)
        s["grad_kv_cross"] = grad_kv
        grad_encoder.append(tp_sum(mat_nt(grad_kv, c_kv)))
        s["grad_cq"] = grad_cq
        grad_cq_all = jnp.concatenate(tp_list(grad_cq), axis=1)
        grad_two = mat_nt(grad_cq_all, c_query_all)
        norm_add(1, grad_two, s["normed_two"])
        grad_after_self = grad_after_cross + rms_back(
            grad_two * gain_cross, s["normed_two"], s["scale_two"]
        )
        grad_self_low = grad_after_self.astype(BF16)
        add(2, mat_tn(grad_self_low, s["attended"]))
        grad_attended = mat(grad_self_low, w_out_t[:, :width]).astype(BF16)
        grad_q, grad_kv = attend_back(
            queries[i], kv_self[i], biases[i], s["totals_self"], grad_attended
        )
        grad_qkv = jnp.concatenate([grad_q, ctx_scatter(grad_kv)], axis=1)
        add(0, mat_tn(tree_rows(hidden_one, i), grad_qkv))
        grad_one = tp_sum(mat_nt(grad_qkv, w_qkv))
        norm_add(0, grad_one, tree_rows(normed_one, i))
        grad_tokens.append(
            grad_after_self
            + rms_back(grad_one * gain_self, tree_rows(normed_one, i), tree_rows(scale_one, i))
        )
        add(
            1,
            jnp.concatenate(
                [
                    mat_tn(tree_rows(encoder, i), grad_kv_part)
                    for grad_kv_part in (s["grad_kv_cross"],)
                ]
                + [mat_tn(s["hidden_two"], grad_cq)],
                axis=1,
            ),
        )

    ff_own = plane_scatter(
        jnp.concatenate([grads[3], grads[4], grads[5], grads[6]], axis=1).astype(BF16)
    )
    norm_block = jnp.pad(jnp.stack(norm_terms, axis=1), ((0, 0), (0, 60)))
    own = plane_scatter(
        jnp.concatenate([grads[0], grads[1], grads[2], norm_block], axis=1).astype(BF16)
    )

    def part(value, start, size):
        return value[:, start : start + size]

    base = 7 * width
    return (
        jnp.concatenate([s["mixed"].astype(BF16) for s in saved], axis=0),
        jnp.concatenate(losses),
        jnp.concatenate(scores),
        jnp.concatenate(grad_tokens, axis=0),
        jnp.concatenate(grad_encoder, axis=0),
        part(own, 0, width),
        part(own, width, width),
        part(own, 2 * width, width),
        part(own, 6 * width, width).T,
        part(own, 5 * width, width),
        part(own, 3 * width, width),
        part(own, 4 * width, width),
        part(ff_own, 0, width).T,
        part(ff_own, width, hidden_units),
        part(ff_own, width + hidden_units, hidden_units),
        part(ff_own, width + 2 * hidden_units, hidden_units).T,
        grad_embed_own.T,
        own[:, base],
        own[:, base + 1],
        own[:, base + 2],
        own[:, base + 3],
    )


def solution(mesh):
    rows_cols = P(PLANE, "tp")
    cols_rows = P("tp", PLANE)
    data = P(PLANE, None)
    flat = P(PLANE)
    weights = (rows_cols,) * 3 + (cols_rows,) + (rows_cols,) * 3 + (cols_rows,)
    weights += (rows_cols,) * 2 + (cols_rows,) * 2 + (flat,) * 4
    return jax.shard_map(
        local,
        mesh=mesh,
        in_specs=(data, data, data, P("fsdp", None), flat) + weights,
        out_specs=(data, flat, flat, data, data) + weights,
        check_vma=False,
    )
```

```python
import functools
import math

import jax
import jax.numpy as jnp
from jax import lax
from jax.experimental import pallas as pl
from jax.experimental.pallas import tpu as pltpu
from jax.sharding import PartitionSpec as P

HD = 64
BLK = 128
MB = 2
EPSILON = 1e-06
MASKED = -1000000000.0
F32 = jnp.float32
BF16 = jnp.bfloat16
PLANE = ("fsdp", "ctx")
VMEM_LIMIT = 48 * 1024 * 1024
MESH = pl.DeviceIdType.MESH
TILE = 1024
LOWEST = -3.0e38


def mat(left, right):
    return jnp.dot(left, right, preferred_element_type=F32)


def mat_nt(left, right):
    return lax.dot_general(left, right, (((1,), (1,)), ((), ())), preferred_element_type=F32)


def mat_tn(left, right):
    return lax.dot_general(left, right, (((0,), (0,)), ((), ())), preferred_element_type=F32)


def small_plane():
    return lax.axis_size("fsdp") == 4 and lax.axis_size("ctx") == 2


def swap(value, axis, bit):
    count = lax.axis_size(axis)
    return lax.ppermute(value, axis, [(i, i ^ bit) for i in range(count)])


def low_sum(left, right):
    return (left.astype(F32) + right.astype(F32)).astype(BF16)


def here():
    return lax.axis_index("fsdp"), lax.axis_index("ctx"), lax.axis_index("tp")


def greet(peers):
    barrier = pltpu.get_barrier_semaphore()
    for peer in peers:
        pl.semaphore_signal(barrier, inc=1, device_id=peer, device_id_type=MESH)
    pl.semaphore_wait(barrier, len(peers))


def greet_line(t, count, left, right):
    barrier = pltpu.get_barrier_semaphore()

    @pl.when(t > 0)
    def _():
        pl.semaphore_signal(barrier, inc=1, device_id=left, device_id_type=MESH)

    @pl.when(t < count - 1)
    def _():
        pl.semaphore_signal(barrier, inc=1, device_id=right, device_id_type=MESH)

    at_end = (t == 0) | (t == count - 1)
    pl.semaphore_wait(barrier, jnp.where(at_end, 1, 2).astype(jnp.int32))


def remote(src, dst, send, recv, peer):
    return pltpu.make_async_remote_copy(
        src_ref=src, dst_ref=dst, send_sem=send, recv_sem=recv, device_id=peer, device_id_type=MESH
    )


def plane_gather_kernel(x_ref, out_ref, send, recv, core_send, core_recv):
    f, c, t = here()
    core = f % 2
    chips = [(0, 1), (2, 0), (2, 1)]
    peers = [(f ^ df, c ^ dc, t) for df, dc in chips]
    partner = (f ^ 1, c, t)
    greet(peers + [partner])

    def slot(df, dc):
        return (f ^ df) * 2 + (c ^ dc)

    own = slot(0, 0)
    copies = []
    for j, peer in enumerate(peers):
        copy = remote(x_ref, out_ref.at[own], send.at[j], recv.at[j], peer)
        copy.start()
        copies.append(copy)
    passes = [remote(x_ref, out_ref.at[own], core_send.at[3], core_recv.at[3], partner)]
    passes[0].start()
    out_ref[own] = x_ref[...]
    for j, (df, dc) in enumerate(chips):
        copies[j].wait_recv()
        there = slot(df, dc)
        copy = remote(
            out_ref.at[there], out_ref.at[there], core_send.at[j], core_recv.at[j], partner
        )
        copy.start()
        passes.append(copy)
    for copy in copies:
        copy.wait_send()
    for copy in passes:
        copy.wait()


def plane_gather(shard, collective_id):
    if not small_plane():
        return lax.all_gather(shard, PLANE, axis=0, tiled=True)
    rows, columns = shard.shape
    out = pl.pallas_call(
        plane_gather_kernel,
        in_specs=[pl.BlockSpec(memory_space=pltpu.VMEM)],
        out_specs=pl.BlockSpec(memory_space=pltpu.VMEM),
        out_shape=jax.ShapeDtypeStruct((8, rows, columns), shard.dtype),
        scratch_shapes=[
            pltpu.SemaphoreType.DMA((3,)),
            pltpu.SemaphoreType.DMA((3,)),
            pltpu.SemaphoreType.DMA((4,)),
            pltpu.SemaphoreType.DMA((4,)),
        ],
        compiler_params=pltpu.CompilerParams(
            collective_id=collective_id, has_side_effects=True, vmem_limit_bytes=VMEM_LIMIT
        ),
        name="plane_gather",
    )(shard)
    return out.reshape(8 * rows, columns)


def plane_scatter_kernel(
    x_ref, out_ref, chip, core_in, chip_in, send, recv, core_send, core_recv
):
    f, c, t = here()
    core = f % 2
    chips = [(2, 1), (0, 1), (2, 0)]
    peers = [(f ^ df, c ^ dc, t) for df, dc in chips]
    partner = (f ^ 1, c, t)
    greet(peers + [partner])
    order = chips + [(0, 0)]
    swaps = []
    for j, (df, dc) in enumerate(order):
        block = (f ^ df ^ 1) * 2 + (c ^ dc)
        copy = remote(x_ref.at[block], core_in.at[j], core_send.at[j], core_recv.at[j], partner)
        copy.start()
        swaps.append(copy)
    copies = []
    for j, (df, dc) in enumerate(order):
        swaps[j].wait_recv()
        block = (f ^ df) * 2 + (c ^ dc)
        total = x_ref[block].astype(F32) + core_in[j].astype(F32)
        if j < 3:
            chip[j] = total.astype(BF16)
            copy = remote(chip.at[j], chip_in.at[j], send.at[j], recv.at[j], peers[j])
            copy.start()
            copies.append(copy)
        else:
            out_ref[...] = total
    for copy in swaps:
        copy.wait_send()
    for j in range(3):
        copies[j].wait()
        out_ref[...] += chip_in[j].astype(F32)


def plane_scatter(total, collective_id):
    if not small_plane():
        return lax.psum_scatter(total.astype(F32), PLANE, scatter_dimension=0, tiled=True)
    rows, columns = total.shape[0] // 8, total.shape[1]
    return pl.pallas_call(
        plane_scatter_kernel,
        in_specs=[pl.BlockSpec(memory_space=pltpu.VMEM)],
        out_specs=pl.BlockSpec(memory_space=pltpu.VMEM),
        out_shape=jax.ShapeDtypeStruct((rows, columns), F32),
        scratch_shapes=[
            pltpu.VMEM((3, rows, columns), BF16),
            pltpu.VMEM((4, rows, columns), BF16),
            pltpu.VMEM((3, rows, columns), BF16),
            pltpu.SemaphoreType.DMA((3,)),
            pltpu.SemaphoreType.DMA((3,)),
            pltpu.SemaphoreType.DMA((4,)),
            pltpu.SemaphoreType.DMA((4,)),
        ],
        compiler_params=pltpu.CompilerParams(
            collective_id=collective_id, has_side_effects=True, vmem_limit_bytes=VMEM_LIMIT
        ),
        name="plane_scatter",
    )(total.reshape(8, rows, columns))


def line_project_kernel(
    count, chunks, x_ref, w_ref, base_ref, out_ref, held, send_right, send_left, recv
):
    f, c, t = here()
    right, left = (f, c, t + 1), (f, c, t - 1)
    greet_line(t, count, left, right)
    rows = x_ref.shape[0] // chunks

    def part(j):
        return pl.ds(j * rows, rows)

    def go(j, d, peer, origin, sems):
        src = x_ref.at[part(j)] if d == 0 else held.at[origin, part(j)]
        return remote(src, held.at[origin, part(j)], sems.at[d, j], recv.at[origin, j], peer)

    def go_right(j, d):
        return go(j, d, right, t - d, send_right)

    def go_left(j, d):
        return go(j, d, left, t + d, send_left)

    def arrived(j, origin):
        return remote(x_ref.at[part(j)], held.at[origin, part(j)], send_right.at[0, j], recv.at[origin, j], right)

    @pl.when(t < count - 1)
    def _():
        for j in range(chunks):
            go_right(j, 0).start()

    @pl.when(t > 0)
    def _():
        for j in range(chunks):
            go_left(j, 0).start()

    held[t] = x_ref[...]
    for d in range(1, count):
        for j in range(chunks):

            @pl.when(t - d >= 0)
            def _():
                arrived(j, t - d).wait_recv()
                if d < count - 1:

                    @pl.when(t < count - 1)
                    def _():
                        go_right(j, d).start()

            @pl.when(t + d < count)
            def _():
                arrived(j, t + d).wait_recv()
                if d < count - 1:

                    @pl.when(t > 0)
                    def _():
                        go_left(j, d).start()

            if d == count - 1:
                total = base_ref[part(j)]
                for origin in range(count):
                    total = total + mat_nt(held[origin, part(j)], w_ref[origin])
                out_ref[part(j)] = total

    for d in range(count - 1):
        for j in range(chunks):

            @pl.when((t - d >= 0) & (t < count - 1))
            def _():
                go_right(j, d).wait_send()

            @pl.when((t + d < count) & (t > 0))
            def _():
                go_left(j, d).wait_send()


def line_project(value, weights, base, collective_id):
    rows, width = value.shape
    count, features = weights.shape[0], weights.shape[1]
    chunks = 4
    return pl.pallas_call(
        functools.partial(line_project_kernel, count, chunks),
        in_specs=[pl.BlockSpec(memory_space=pltpu.VMEM)] * 3,
        out_specs=pl.BlockSpec(memory_space=pltpu.VMEM),
        out_shape=jax.ShapeDtypeStruct((rows, features), F32),
        scratch_shapes=[
            pltpu.VMEM((count, rows, width), BF16),
            pltpu.SemaphoreType.DMA((count, chunks)),
            pltpu.SemaphoreType.DMA((count, chunks)),
            pltpu.SemaphoreType.DMA((count, chunks)),
        ],
        compiler_params=pltpu.CompilerParams(
            collective_id=collective_id, has_side_effects=True, vmem_limit_bytes=VMEM_LIMIT
        ),
        name="line_project",
    )(value, weights, base)


def line_sum_kernel(
    count,
    chunks,
    window,
    lag,
    x_ref,
    out_ref,
    from_right,
    from_left,
    to_left,
    to_right,
    up_send,
    up_recv,
    down_send,
    down_recv,
    low_send,
    low_recv,
    high_send,
    high_recv,
):
    f, c, t = here()
    right, left = (f, c, t + 1), (f, c, t - 1)
    last = count - 1
    greet_line(t, count, left, right)
    half = x_ref.shape[0] // 2
    rows = half // chunks

    def low(j):
        return pl.ds(j * rows, rows)

    def high(j):
        return pl.ds(half + j * rows, rows)

    def down(j, own):
        src = x_ref.at[low(j)] if own else to_left.at[low(j)]
        return remote(src, from_right.at[low(j)], down_send.at[j], down_recv.at[j], left)

    def up(j, own):
        src = x_ref.at[high(j)] if own else to_right.at[low(j)]
        return remote(src, from_left.at[low(j)], up_send.at[j], up_recv.at[j], right)

    def low_back(j):
        return remote(out_ref.at[low(j)], out_ref.at[low(j)], low_send.at[j], low_recv.at[j], right)

    def high_back(j):
        return remote(
            out_ref.at[high(j)], out_ref.at[high(j)], high_send.at[j], high_recv.at[j], left
        )

    def pace(j, copy):
        if j == 0:
            for k in range(min(window, chunks)):
                copy(k, True).start()
        copy(j, True).wait_send()
        if j + window < chunks:
            copy(j + window, True).start()

    def low_step(j):
        @pl.when(t == last)
        def _():
            pace(j, down)

        @pl.when(t < last)
        def _():
            down(j, False).wait_recv()
            total = from_right[low(j)].astype(F32) + x_ref[low(j)].astype(F32)

            @pl.when(t > 0)
            def _():
                to_left[low(j)] = total.astype(BF16)
                down(j, False).start()

            @pl.when(t == 0)
            def _():
                out_ref[low(j)] = total.astype(BF16)
                low_back(j).start()

    def high_step(j):
        @pl.when(t == 0)
        def _():
            pace(j, up)

        @pl.when(t > 0)
        def _():
            up(j, False).wait_recv()
            total = from_left[low(j)].astype(F32) + x_ref[high(j)].astype(F32)

            @pl.when(t < last)
            def _():
                to_right[low(j)] = total.astype(BF16)
                up(j, False).start()

            @pl.when(t == last)
            def _():
                out_ref[high(j)] = total.astype(BF16)
                high_back(j).start()

    def low_forward(j):
        @pl.when(t > 0)
        def _():
            low_back(j).wait_recv()

            @pl.when(t < last)
            def _():
                low_back(j).start()

    def high_forward(j):
        @pl.when(t < last)
        def _():
            high_back(j).wait_recv()

            @pl.when(t > 0)
            def _():
                high_back(j).start()

    for j in range(chunks + lag):

        @pl.when(t < count // 2)
        def _():
            if j < chunks:
                high_step(j)
            if 0 <= j - 1 < chunks:
                low_step(j - 1)

        @pl.when(t >= count // 2)
        def _():
            if j < chunks:
                low_step(j)
            if 0 <= j - 1 < chunks:
                high_step(j - 1)

        if j >= lag:

            @pl.when(t < count // 2)
            def _():
                low_forward(j - lag)
                high_forward(j - lag)

            @pl.when(t >= count // 2)
            def _():
                high_forward(j - lag)
                low_forward(j - lag)

    for j in range(chunks):

        @pl.when(t > 0)
        def _():
            high_back(j).wait_send()

            @pl.when(t < last)
            def _():
                down(j, False).wait_send()

        @pl.when(t < last)
        def _():
            low_back(j).wait_send()

            @pl.when(t > 0)
            def _():
                up(j, False).wait_send()


def line_sum(partial, collective_id, chunks=4, window=2, lag=4):
    count = lax.axis_size("tp")
    rows, columns = partial.shape
    while (rows // 2) % (chunks * 16):
        chunks -= 1
    half = rows // 2
    return pl.pallas_call(
        functools.partial(line_sum_kernel, count, chunks, window, lag),
        in_specs=[pl.BlockSpec(memory_space=pltpu.VMEM)],
        out_specs=pl.BlockSpec(memory_space=pltpu.VMEM),
        out_shape=jax.ShapeDtypeStruct((rows, columns), BF16),
        scratch_shapes=[pltpu.VMEM((half, columns), BF16)] * 4
        + [pltpu.SemaphoreType.DMA((chunks,))] * 8,
        compiler_params=pltpu.CompilerParams(
            collective_id=collective_id, has_side_effects=True, vmem_limit_bytes=VMEM_LIMIT
        ),
        name="line_sum",
    )(partial)


def share_stats_kernel(count, x_ref, top_ref, log_ref, picked_ref, held, send, recv):
    f, c, t = here()
    peers = [(f, c, lax.rem(t + k, count)) for k in range(1, count)]
    greet(peers)
    copies = []
    for k in range(1, count):
        copy = remote(x_ref, held.at[t], send.at[k], recv.at[k], peers[k - 1])
        copy.start()
        copies.append(copy)
    held[t] = x_ref[...]
    for copy in copies:
        copy.wait()
    highest = functools.reduce(jnp.maximum, [held[k, 0] for k in range(count)])
    total = sum(held[k, 1] * jnp.exp(held[k, 0] - highest) for k in range(count))
    top_ref[...] = highest
    log_ref[...] = highest + jnp.log(total)
    picked_ref[...] = sum(held[k, 2] for k in range(count))


def share_stats(stats, collective_id):
    count = lax.axis_size("tp")
    shape = jax.ShapeDtypeStruct(stats.shape[1:], F32)
    return pl.pallas_call(
        functools.partial(share_stats_kernel, count),
        in_specs=[pl.BlockSpec(memory_space=pltpu.VMEM)],
        out_specs=[pl.BlockSpec(memory_space=pltpu.VMEM)] * 3,
        out_shape=[shape] * 3,
        scratch_shapes=[
            pltpu.VMEM((count,) + stats.shape, F32),
            pltpu.SemaphoreType.DMA((count,)),
            pltpu.SemaphoreType.DMA((count,)),
        ],
        compiler_params=pltpu.CompilerParams(collective_id=collective_id, has_side_effects=True),
        name="share_stats",
    )(stats)


def after(value, earlier):
    return lax.optimization_barrier((value, earlier))[0]


def tp_list(value):
    count = lax.axis_size("tp")
    return [value] + [
        lax.ppermute(value, "tp", [(i, (i + k) % count) for i in range(count)])
        for k in range(1, count)
    ]


def ctx_gather(value):
    if lax.axis_size("ctx") == 2:
        return jnp.concatenate([value, swap(value, "ctx", 1)], axis=0)
    return lax.all_gather(value, "ctx", axis=0, tiled=True)


def ctx_pair(value):
    if lax.axis_size("ctx") == 2:
        return [value, swap(value, "ctx", 1)]
    return [lax.all_gather(value, "ctx", axis=0, tiled=True)]


def ctx_join(parts):
    return jnp.concatenate(parts, axis=0)


def ctx_positions(rows):
    c, count = lax.axis_index("ctx"), lax.axis_size("ctx")
    if count == 2:
        return jnp.concatenate(
            [c * rows + jnp.arange(rows), (1 - c) * rows + jnp.arange(rows)]
        ).astype(jnp.int32)
    return jnp.arange(rows * count, dtype=jnp.int32)


def ctx_scatter(value):
    if lax.axis_size("ctx") == 2:
        rows = value.shape[0] // 2
        return low_sum(value[:rows], swap(value[rows:], "ctx", 1))
    return lax.psum_scatter(value.astype(F32), "ctx", scatter_dimension=0, tiled=True).astype(BF16)


def exit_forward_kernel(
    valid, x_ref, e_ref, target_ref, logits_ref, top_ref, sum_ref, picked_ref, m_acc, l_acc, p_acc
):
    step = pl.program_id(0)
    rows, tile = logits_ref.shape

    @pl.when(step == 0)
    def _():
        m_acc[...] = jnp.full_like(m_acc, LOWEST)
        l_acc[...] = jnp.zeros_like(l_acc)
        p_acc[...] = jnp.zeros_like(p_acc)

    lanes = lax.broadcasted_iota(jnp.int32, (rows, 128), 1)
    logits_ref[...] = mat(x_ref[...], e_ref[...])
    relative = target_ref[...] - step * tile
    limit = valid - step * tile
    groups = tile // 128
    highest = m_acc[...]
    for g in range(groups):
        cols = slice(g * 128, (g + 1) * 128)
        part = jnp.where(lanes < limit - g * 128, logits_ref[:, cols], LOWEST)
        highest = jnp.maximum(highest, part)
    total = l_acc[...] * jnp.exp(m_acc[...] - highest)
    picked = p_acc[...]
    for g in range(groups):
        cols = slice(g * 128, (g + 1) * 128)
        part = jnp.where(lanes < limit - g * 128, logits_ref[:, cols], LOWEST)
        total += jnp.exp(part - highest)
        picked += jnp.where(lanes == relative - g * 128, part, 0.0)
    m_acc[...] = highest
    l_acc[...] = total
    p_acc[...] = picked

    @pl.when(step == pl.num_programs(0) - 1)
    def _():
        top = jnp.max(m_acc[...], axis=1, keepdims=True)
        top_ref[...] = top
        sum_ref[...] = jnp.sum(l_acc[...] * jnp.exp(m_acc[...] - top), axis=1, keepdims=True)
        picked_ref[...] = jnp.sum(p_acc[...], axis=1, keepdims=True)


def exit_forward(exit_in, embed_t, targets_local, valid):
    rows, features = exit_in.shape
    padded = embed_t.shape[1]
    column = pl.BlockSpec((rows, 1), lambda i: (0, 0))
    stat = jax.ShapeDtypeStruct((rows, 1), F32)
    return pl.pallas_call(
        functools.partial(exit_forward_kernel, valid),
        grid=(padded // TILE,),
        in_specs=[
            pl.BlockSpec((rows, features), lambda i: (0, 0)),
            pl.BlockSpec((features, TILE), lambda i: (0, i)),
            column,
        ],
        out_specs=[pl.BlockSpec((rows, TILE), lambda i: (0, i)), column, column, column],
        out_shape=[jax.ShapeDtypeStruct((rows, padded), F32), stat, stat, stat],
        scratch_shapes=[pltpu.VMEM((rows, 128), F32)] * 3,
        compiler_params=pltpu.CompilerParams(vmem_limit_bytes=VMEM_LIMIT),
        cost_estimate=pl.CostEstimate(
            flops=2 * rows * features * padded,
            bytes_accessed=4 * rows * padded + 2 * features * padded,
            transcendentals=rows * padded,
        ),
        name="exit_forward",
    )(exit_in, embed_t, targets_local)


def exit_backward_kernel(
    valid, logits_ref, e_ref, x_t_ref, target_ref, log_ref, embed_ref, exit_ref, acc
):
    step = pl.program_id(0)
    rows, tile = logits_ref.shape

    @pl.when(step == 0)
    def _():
        acc[...] = jnp.zeros_like(acc)

    lanes = lax.broadcasted_iota(jnp.int32, (rows, tile), 1)
    relative = target_ref[...] - step * tile
    probs = jnp.exp(logits_ref[...] - log_ref[...])
    probs = jnp.where(lanes < valid - step * tile, probs, 0.0)
    grad = (probs - jnp.where(lanes == relative, 1.0, 0.0)).astype(BF16)
    acc[...] += mat_nt(grad, e_ref[...])
    embed_ref[...] = mat(x_t_ref[...], grad).astype(BF16)

    @pl.when(step == pl.num_programs(0) - 1)
    def _():
        exit_ref[...] = acc[...].astype(BF16)


def exit_backward(logits, embed_t, exit_in_t, targets_local, log_total, valid):
    rows, padded = logits.shape
    features = embed_t.shape[0]
    column = pl.BlockSpec((rows, 1), lambda i: (0, 0))
    return pl.pallas_call(
        functools.partial(exit_backward_kernel, valid),
        grid=(padded // TILE,),
        in_specs=[
            pl.BlockSpec((rows, TILE), lambda i: (0, i)),
            pl.BlockSpec((features, TILE), lambda i: (0, i)),
            pl.BlockSpec((features, rows), lambda i: (0, 0)),
            column,
            column,
        ],
        out_specs=[
            pl.BlockSpec((features, TILE), lambda i: (0, i)),
            pl.BlockSpec((rows, features), lambda i: (0, 0)),
        ],
        out_shape=[
            jax.ShapeDtypeStruct((features, padded), BF16),
            jax.ShapeDtypeStruct((rows, features), BF16),
        ],
        scratch_shapes=[pltpu.VMEM((rows, features), F32)],
        compiler_params=pltpu.CompilerParams(vmem_limit_bytes=VMEM_LIMIT),
        cost_estimate=pl.CostEstimate(
            flops=4 * rows * features * padded,
            bytes_accessed=4 * rows * padded + 4 * features * padded,
            transcendentals=rows * padded,
        ),
        name="exit_backward",
    )(logits, embed_t, exit_in_t, targets_local, log_total)


def forward_kernel(heads, q_ref, kv_ref, bias_ref, out_ref, total_ref):
    width = heads * HD
    for h in range(heads):
        cols = slice(h * HD, (h + 1) * HD)
        keys = kv_ref[:, cols]
        values = kv_ref[:, width + h * HD : width + (h + 1) * HD]
        scores = mat_nt(keys, q_ref[:, cols])
        if bias_ref is not None:
            scores = scores + bias_ref[...]
        highest = jnp.max(scores, axis=0, keepdims=True)
        exponent = jnp.exp(scores - highest)
        denominator = jnp.sum(exponent, axis=0, keepdims=True)
        outcome = mat_tn(values, exponent.astype(BF16)) / denominator
        out_ref[:, cols] = outcome.T.astype(BF16)
        total_ref[h : h + 1, :] = highest + jnp.log(denominator)


def backward_kernel(
    heads, q_ref, kv_ref, bias_ref, total_ref, go_ref, dq_ref, dkv_ref, acc_ref
):
    width = heads * HD
    step = pl.program_id(0)

    @pl.when(step == 0)
    def _():
        acc_ref[...] = jnp.zeros_like(acc_ref)

    for h in range(heads):
        cols = slice(h * HD, (h + 1) * HD)
        vcols = slice(width + h * HD, width + (h + 1) * HD)
        keys, values = kv_ref[:, cols], kv_ref[:, vcols]
        queries, go = q_ref[:, cols], go_ref[:, cols]
        scores = mat_nt(keys, queries)
        if bias_ref is not None:
            scores = scores + bias_ref[...]
        probs = jnp.exp(scores - total_ref[h : h + 1, :])
        grad_probs = mat_nt(values, go)
        inner = jnp.sum(probs * grad_probs, axis=0, keepdims=True)
        grad_scores = (probs * (grad_probs - inner)).astype(BF16)
        acc_ref[:, vcols] += mat(probs.astype(BF16), go)
        acc_ref[:, cols] += mat(grad_scores, queries)
        dq_ref[:, cols] = mat_tn(keys, grad_scores).T.astype(BF16)

    @pl.when(step == pl.num_programs(0) - 1)
    def _():
        dkv_ref[...] = acc_ref[...].astype(BF16)


def attention_specs(rows, width, keys, tile, masked):
    specs = [
        pl.BlockSpec((tile, width), lambda i: (i, 0)),
        pl.BlockSpec((keys, 2 * width), lambda i: (0, 0)),
    ]
    if masked:
        specs.append(pl.BlockSpec((keys, tile), lambda i: (0, i)))
    return specs


def attend(queries, kv, bias):
    rows, width = queries.shape
    keys, heads = kv.shape[0], width // HD
    tile = min(rows, 256)
    masked = bias is not None
    body = functools.partial(forward_kernel, heads)
    if not masked:
        plain = body
        body = lambda q, k, o, t: plain(q, k, None, o, t)
    return pl.pallas_call(
        body,
        grid=(rows // tile,),
        in_specs=attention_specs(rows, width, keys, tile, masked),
        out_specs=[
            pl.BlockSpec((tile, width), lambda i: (i, 0)),
            pl.BlockSpec((heads, tile), lambda i: (0, i)),
        ],
        out_shape=[
            jax.ShapeDtypeStruct((rows, width), BF16),
            jax.ShapeDtypeStruct((heads, rows), F32),
        ],
        compiler_params=pltpu.CompilerParams(vmem_limit_bytes=VMEM_LIMIT),
        cost_estimate=pl.CostEstimate(
            flops=16 * rows * keys * width,
            bytes_accessed=4 * keys * width + 8 * rows * width,
            transcendentals=rows * keys * heads,
        ),
        name="attend_masked" if masked else "attend",
    )(*([queries, kv, bias] if masked else [queries, kv]))


def attend_back(queries, kv, bias, totals, go):
    rows, width = queries.shape
    keys, heads = kv.shape[0], width // HD
    tile = min(rows, 256)
    masked = bias is not None
    body = functools.partial(backward_kernel, heads)
    if not masked:
        plain = body
        body = lambda q, k, *rest: plain(q, k, None, *rest)
    specs = attention_specs(rows, width, keys, tile, masked) + [
        pl.BlockSpec((heads, tile), lambda i: (0, i)),
        pl.BlockSpec((tile, width), lambda i: (i, 0)),
    ]
    operands = ([queries, kv, bias] if masked else [queries, kv]) + [totals, go]
    return pl.pallas_call(
        body,
        grid=(rows // tile,),
        in_specs=specs,
        out_specs=[
            pl.BlockSpec((tile, width), lambda i: (i, 0)),
            pl.BlockSpec((keys, 2 * width), lambda i: (0, 0)),
        ],
        out_shape=[
            jax.ShapeDtypeStruct((rows, width), BF16),
            jax.ShapeDtypeStruct((keys, 2 * width), BF16),
        ],
        scratch_shapes=[pltpu.VMEM((keys, 2 * width), F32)],
        compiler_params=pltpu.CompilerParams(vmem_limit_bytes=VMEM_LIMIT),
        cost_estimate=pl.CostEstimate(
            flops=40 * rows * keys * width,
            bytes_accessed=8 * keys * width + 10 * rows * width,
            transcendentals=rows * keys * heads,
        ),
        name="attend_back_masked" if masked else "attend_back",
    )(*operands)


def rms_scale(values):
    return lax.rsqrt(jnp.mean(values * values, axis=-1, keepdims=True) + EPSILON)


def rms_back(grad_normed, normed, scale):
    return scale * (grad_normed - normed * jnp.mean(grad_normed * normed, axis=-1, keepdims=True))


def mask_bias(parent_row, row_count):
    block_count = parent_row.shape[0]
    blocks = jnp.arange(block_count, dtype=jnp.int32)
    current = blocks
    reachable = blocks[:, None] == blocks[None, :]
    for _ in range(block_count - 1):
        current = jnp.sum(
            jnp.where(current[:, None] == blocks[None, :], parent_row[None, :], 0), axis=1
        )
        reachable = reachable | (current[:, None] == blocks[None, :])
    query_pos = lax.axis_index("ctx") * row_count + jnp.arange(row_count, dtype=jnp.int32)
    key_pos = ctx_positions(row_count)
    query_onehot = (query_pos[:, None] // BLK == blocks[None, :]).astype(F32)
    key_onehot = (key_pos[:, None] // BLK == blocks[None, :]).astype(F32)
    linked = mat_nt(key_onehot, mat(query_onehot, reachable.astype(F32))) > 0.5
    causal = (query_pos[None, :] // BLK != key_pos[:, None] // BLK) | (
        key_pos[:, None] <= query_pos[None, :]
    )
    return jnp.where(linked & causal, 0.0, MASKED)


def gelu_parts(gate):
    root = math.sqrt(2.0 / math.pi)
    inner = jnp.tanh(root * (gate + 0.044715 * gate * gate * gate))
    value = 0.5 * gate * (1.0 + inner)
    slope = 0.5 * (1.0 + inner) + 0.5 * gate * (1.0 - inner * inner) * root * (
        1.0 + 3.0 * 0.044715 * gate * gate
    )
    return value, slope


def local(
    tokens,
    encoder,
    cotangent,
    parents,
    targets,
    w_query,
    w_key,
    w_value,
    w_out,
    c_query,
    c_key,
    c_value,
    c_out,
    w_gate,
    w_up,
    w_down,
    embedding,
    norm_self,
    norm_cross,
    norm_ff,
    norm_exit,
):
    t = lax.axis_index("tp")
    rows = tokens.shape[0] // MB
    features = tokens.shape[1]
    width = w_query.shape[1]
    hidden_units = w_gate.shape[1]
    vocab = embedding.shape[0]
    tp_count = lax.axis_size("tp")
    trees = range(MB)

    def tree_rows(value, i):
        count = value.shape[0] // MB
        return value[i * count : (i + 1) * count]

    gains_in = jnp.pad(
        jnp.stack([norm_self, norm_cross, norm_ff, norm_exit], axis=1), ((0, 0), (0, 124))
    )
    w_heads = plane_gather(
        jnp.concatenate([w_query, w_key, w_value, c_key, c_value, c_query, gains_in], axis=1), 1
    )
    w_qkv = w_heads[:, : 3 * width]
    c_kv = w_heads[:, 3 * width : 5 * width]
    c_q = w_heads[:, 5 * width : 6 * width]
    gains = w_heads[:, 6 * width : 6 * width + 4].astype(F32).T
    gain_self, gain_cross, gain_ff, gain_exit = (gains[j][None, :] for j in range(4))

    pieces = tp_list(
        jnp.concatenate([w_out.T, c_out.T, c_query, w_gate, w_up, w_down.T], axis=1)
    )
    pieces = after(pieces, w_heads)
    pieces = lax.dynamic_slice_in_dim(jnp.stack(pieces[::-1] * 2), tp_count - 1 - t, tp_count, 0)
    spans = [0, width, 2 * width, 3 * width]
    spans += [spans[-1] + hidden_units * j for j in (1, 2, 3)]
    packed = jnp.concatenate(
        [
            jnp.concatenate([pieces[k, :, spans[j] : spans[j + 1]] for k in range(tp_count)], axis=1)
            for j in range(6)
        ],
        axis=1,
    )
    whole = lax.all_gather(packed, PLANE, axis=0, tiled=True)
    cuts = [tp_count * s for s in spans]
    gate_all, up_all, down_t = (whole[:, cuts[j] : cuts[j + 1]] for j in range(3, 6))

    def own_units(value):
        return lax.dynamic_slice_in_dim(value, t * hidden_units, hidden_units, 1)

    def own_heads(value):
        return lax.dynamic_index_in_dim(value, t, 0, False)

    def stacked(j):
        return jnp.stack(
            [whole[:, cuts[j] + k * width : cuts[j] + (k + 1) * width] for k in range(tp_count)]
        )

    w_out_4, c_out_4, c_query_4 = stacked(0), stacked(1), stacked(2)
    padded = -(-vocab // TILE) * TILE
    embed_t = lax.all_gather(
        jnp.pad(after(embedding, packed).T, ((0, 0), (0, padded - vocab))),
        PLANE,
        axis=0,
        tiled=True,
    )

    tok = tokens.astype(F32)
    scale_one = rms_scale(tok)
    normed_one = tok * scale_one
    hidden_one = (normed_one * gain_self).astype(BF16)
    qkv = mat(hidden_one, w_qkv).astype(BF16)
    enc_kv = mat(encoder, c_kv).astype(BF16)
    queries = [tree_rows(qkv, i)[:, :width] for i in trees]
    kv_self = [ctx_gather(tree_rows(qkv, i)[:, width:]) for i in trees]
    kv_cross = [ctx_pair(tree_rows(enc_kv, i)) for i in trees]
    biases = [mask_bias(parents[i], rows) for i in trees]
    shrink = 1.0 / math.sqrt(features)

    outcome = [attend(queries[i], kv_self[i], biases[i]) for i in trees]
    attended = jnp.concatenate([o[0] for o in outcome], axis=0)
    totals_self = [o[1] for o in outcome]
    after_self = line_project(attended, w_out_4, tok, 2)
    scale_two = rms_scale(after_self)
    normed_two = after_self * scale_two
    hidden_two = (normed_two * gain_cross).astype(BF16)
    cross_q = mat(hidden_two, c_q).astype(BF16)
    kv_cross = [ctx_join(after(kv_cross[i], after_self)) for i in trees]
    outcome = [attend(tree_rows(cross_q, i), kv_cross[i], None) for i in trees]
    crossed = jnp.concatenate([o[0] for o in outcome], axis=0)
    totals_cross = [o[1] for o in outcome]
    after_cross = line_project(crossed, c_out_4, after_self, 3)
    scale_three = rms_scale(after_cross)
    normed_three = after_cross * scale_three
    hidden_three = (normed_three * gain_ff).astype(BF16)
    gate_pre = mat(hidden_three, gate_all)
    up_pre = mat(hidden_three, up_all)
    activated = (gelu_parts(gate_pre)[0] * up_pre).astype(BF16)
    mixed = after_cross + mat_nt(activated, down_t)
    scale_four = rms_scale(mixed)
    normed_four = mixed * scale_four
    exit_in = (normed_four * gain_exit * shrink).astype(BF16)

    targets_local = targets - t * vocab
    inside = (targets_local >= 0) & (targets_local < vocab)
    targets_local = jnp.where(inside, targets_local, -1)[:, None]
    logits, top, summed, picked = exit_forward(exit_in, embed_t, targets_local, vocab)
    stats = jnp.stack([top, summed, picked]).reshape(3, MB * rows // 128, 128)
    top, log_total, picked = share_stats(stats, 4)
    losses = (log_total - picked).reshape(-1)
    scores = (top - log_total).reshape(-1)
    grad_embed, grad_exit_part = exit_backward(
        logits, embed_t, exit_in.T, targets_local, log_total.reshape(-1, 1), vocab
    )
    grad_embed_own = lax.optimization_barrier(
        lax.psum_scatter(grad_embed, PLANE, scatter_dimension=0, tiled=True)
    )
    grad_exit = line_sum(grad_exit_part, 5).astype(F32) * shrink

    def norm_grad(grad, normed):
        return jnp.sum(grad * normed, axis=0)

    norm_exit_grad = norm_grad(grad_exit, normed_four)
    grad_mixed = cotangent.astype(F32) + rms_back(grad_exit * gain_exit, normed_four, scale_four)
    grad_mixed_low = grad_mixed.astype(BF16)
    grad_down = mat_tn(grad_mixed_low, own_units(activated))
    grad_act = mat(grad_mixed_low, down_t)
    value, slope = gelu_parts(gate_pre)
    grad_gate = (grad_act * slope * up_pre).astype(BF16)
    grad_up = (grad_act * value).astype(BF16)
    grad_gate_w = mat_tn(hidden_three, own_units(grad_gate))
    grad_up_w = mat_tn(hidden_three, own_units(grad_up))
    grad_three = mat_nt(grad_gate, gate_all) + mat_nt(grad_up, up_all)
    norm_ff_grad = norm_grad(grad_three, normed_three)
    grad_after_cross = grad_mixed + rms_back(grad_three * gain_ff, normed_three, scale_three)
    grad_cross_low = grad_after_cross.astype(BF16)
    grad_c_out = mat_tn(grad_cross_low, crossed)
    ff_grads = jnp.concatenate([grad_c_out, grad_gate_w, grad_up_w, grad_down], axis=1).astype(BF16)
    grad_crossed = mat(grad_cross_low, own_heads(c_out_4)).astype(BF16)
    outcome = [
        attend_back(
            tree_rows(cross_q, i), kv_cross[i], None, totals_cross[i], tree_rows(grad_crossed, i)
        )
        for i in trees
    ]
    grad_cq = jnp.concatenate([o[0] for o in outcome], axis=0)
    grad_kv_cross = jnp.concatenate([ctx_scatter(o[1]) for o in outcome], axis=0)
    grad_c_kv = mat_tn(encoder, grad_kv_cross)
    grad_c_query = mat_tn(hidden_two, grad_cq)
    encoder_part = mat_nt(grad_kv_cross, c_kv).astype(BF16)
    grad_two = line_project(grad_cq, c_query_4, jnp.zeros_like(tok), 6)
    ff_own = lax.psum_scatter(after(ff_grads, grad_two), PLANE, scatter_dimension=0, tiled=True)
    norm_cross_grad = norm_grad(grad_two, normed_two)
    grad_after_self = grad_after_cross + rms_back(grad_two * gain_cross, normed_two, scale_two)
    grad_self_low = grad_after_self.astype(BF16)
    grad_w_out = mat_tn(grad_self_low, attended)
    grad_attended = mat(grad_self_low, own_heads(w_out_4)).astype(BF16)
    outcome = [
        attend_back(
            queries[i], kv_self[i], biases[i], totals_self[i], tree_rows(grad_attended, i)
        )
        for i in trees
    ]
    grad_qkv = jnp.concatenate(
        [
            jnp.concatenate([o[0] for o in outcome], axis=0),
            jnp.concatenate([ctx_scatter(o[1]) for o in outcome], axis=0),
        ],
        axis=1,
    )
    both = jnp.concatenate([mat_nt(grad_qkv, w_qkv).astype(BF16), encoder_part], axis=0)
    both = line_sum(both, 7, 12)
    grad_encoder = both[MB * rows :].astype(F32)
    grad_w_qkv = mat_tn(hidden_one, grad_qkv)
    grad_one = both[: MB * rows].astype(F32)
    norm_self_grad = norm_grad(grad_one, normed_one)
    grad_tokens = grad_after_self + rms_back(grad_one * gain_self, normed_one, scale_one)
    norm_block = jnp.pad(
        jnp.stack([norm_self_grad, norm_cross_grad, norm_ff_grad, norm_exit_grad], axis=1),
        ((0, 0), (0, 60)),
    )
    own = plane_scatter(
        jnp.concatenate(
            [grad_w_qkv, grad_c_kv, grad_c_query, grad_w_out, norm_block], axis=1
        ).astype(BF16),
        9,
    )

    def part(value, start, size):
        return value[:, start : start + size].astype(F32)

    base = 7 * width
    return (
        mixed.astype(BF16),
        losses,
        scores,
        grad_tokens,
        grad_encoder,
        part(own, 0, width),
        part(own, width, width),
        part(own, 2 * width, width),
        part(own, 6 * width, width).T,
        part(own, 5 * width, width),
        part(own, 3 * width, width),
        part(own, 4 * width, width),
        part(ff_own, 0, width).T,
        part(ff_own, width, hidden_units),
        part(ff_own, width + hidden_units, hidden_units),
        part(ff_own, width + 2 * hidden_units, hidden_units).T,
        grad_embed_own[:, :vocab].astype(F32).T,
        own[:, base],
        own[:, base + 1],
        own[:, base + 2],
        own[:, base + 3],
    )


def solution(mesh):
    rows_cols = P(PLANE, "tp")
    cols_rows = P("tp", PLANE)
    data = P(PLANE, None)
    flat = P(PLANE)
    weights = (rows_cols,) * 3 + (cols_rows,) + (rows_cols,) * 3 + (cols_rows,)
    weights += (rows_cols,) * 2 + (cols_rows,) * 2 + (flat,) * 4
    return jax.shard_map(
        local,
        mesh=mesh,
        in_specs=(data, data, data, P("fsdp", None), flat) + weights,
        out_specs=(data, flat, flat, data, data) + weights,
        check_vma=False,
    )
```

```python
import functools
import math

import jax
import jax.numpy as jnp
from jax import lax
from jax.experimental import pallas as pl
from jax.experimental.pallas import tpu as pltpu
from jax.sharding import PartitionSpec as P

HD = 64
BLK = 128
MB = 2
EPSILON = 1e-06
MASKED = -1000000000.0
F32 = jnp.float32
BF16 = jnp.bfloat16
PLANE = ("fsdp", "ctx")
VMEM_LIMIT = 48 * 1024 * 1024
MESH = pl.DeviceIdType.MESH
TILE = 1024
LOWEST = -3.0e38
VMEM_MOST = 58 * 1024 * 1024
Q2 = 1024


def mat(left, right):
    return jnp.dot(left, right, preferred_element_type=F32)


def mat_nt(left, right):
    return lax.dot_general(left, right, (((1,), (1,)), ((), ())), preferred_element_type=F32)


def mat_tn(left, right):
    return lax.dot_general(left, right, (((0,), (0,)), ((), ())), preferred_element_type=F32)


def small_plane():
    return lax.axis_size("fsdp") == 4 and lax.axis_size("ctx") == 2


def swap(value, axis, bit):
    count = lax.axis_size(axis)
    return lax.ppermute(value, axis, [(i, i ^ bit) for i in range(count)])


def low_sum(left, right):
    return (left.astype(F32) + right.astype(F32)).astype(BF16)


def here():
    return lax.axis_index("fsdp"), lax.axis_index("ctx"), lax.axis_index("tp")


def greet(peers):
    barrier = pltpu.get_barrier_semaphore()
    for peer in peers:
        pl.semaphore_signal(barrier, inc=1, device_id=peer, device_id_type=MESH)
    pl.semaphore_wait(barrier, len(peers))


def greet_line(t, count, left, right):
    barrier = pltpu.get_barrier_semaphore()

    @pl.when(t > 0)
    def _():
        pl.semaphore_signal(barrier, inc=1, device_id=left, device_id_type=MESH)

    @pl.when(t < count - 1)
    def _():
        pl.semaphore_signal(barrier, inc=1, device_id=right, device_id_type=MESH)

    at_end = (t == 0) | (t == count - 1)
    pl.semaphore_wait(barrier, jnp.where(at_end, 1, 2).astype(jnp.int32))


def remote(src, dst, send, recv, peer):
    return pltpu.make_async_remote_copy(
        src_ref=src, dst_ref=dst, send_sem=send, recv_sem=recv, device_id=peer, device_id_type=MESH
    )


def plane_gather_kernel(x_ref, out_ref, send, recv, core_send, core_recv):
    f, c, t = here()
    core = f % 2
    chips = [(0, 1), (2, 0), (2, 1)]
    peers = [(f ^ df, c ^ dc, t) for df, dc in chips]
    partner = (f ^ 1, c, t)
    greet(peers + [partner])

    def slot(df, dc):
        return (f ^ df) * 2 + (c ^ dc)

    own = slot(0, 0)
    copies = []
    for j, peer in enumerate(peers):
        copy = remote(x_ref, out_ref.at[own], send.at[j], recv.at[j], peer)
        copy.start()
        copies.append(copy)
    passes = [remote(x_ref, out_ref.at[own], core_send.at[3], core_recv.at[3], partner)]
    passes[0].start()
    out_ref[own] = x_ref[...]
    for j, (df, dc) in enumerate(chips):
        copies[j].wait_recv()
        there = slot(df, dc)
        copy = remote(
            out_ref.at[there], out_ref.at[there], core_send.at[j], core_recv.at[j], partner
        )
        copy.start()
        passes.append(copy)
    for copy in copies:
        copy.wait_send()
    for copy in passes:
        copy.wait()


def plane_gather(shard, collective_id):
    if not small_plane():
        return lax.all_gather(shard, PLANE, axis=0, tiled=True)
    rows, columns = shard.shape
    out = pl.pallas_call(
        plane_gather_kernel,
        in_specs=[pl.BlockSpec(memory_space=pltpu.VMEM)],
        out_specs=pl.BlockSpec(memory_space=pltpu.VMEM),
        out_shape=jax.ShapeDtypeStruct((8, rows, columns), shard.dtype),
        scratch_shapes=[
            pltpu.SemaphoreType.DMA((3,)),
            pltpu.SemaphoreType.DMA((3,)),
            pltpu.SemaphoreType.DMA((4,)),
            pltpu.SemaphoreType.DMA((4,)),
        ],
        compiler_params=pltpu.CompilerParams(
            collective_id=collective_id, has_side_effects=True, vmem_limit_bytes=VMEM_LIMIT
        ),
        name="plane_gather",
    )(shard)
    return out.reshape(8 * rows, columns)


def plane_scatter_kernel(
    x_ref, out_ref, chip, core_in, chip_in, send, recv, core_send, core_recv
):
    f, c, t = here()
    core = f % 2
    chips = [(2, 1), (0, 1), (2, 0)]
    peers = [(f ^ df, c ^ dc, t) for df, dc in chips]
    partner = (f ^ 1, c, t)
    greet(peers + [partner])
    order = chips + [(0, 0)]
    swaps = []
    for j, (df, dc) in enumerate(order):
        block = (f ^ df ^ 1) * 2 + (c ^ dc)
        copy = remote(x_ref.at[block], core_in.at[j], core_send.at[j], core_recv.at[j], partner)
        copy.start()
        swaps.append(copy)
    copies = []
    for j, (df, dc) in enumerate(order):
        swaps[j].wait_recv()
        block = (f ^ df) * 2 + (c ^ dc)
        total = x_ref[block].astype(F32) + core_in[j].astype(F32)
        if j < 3:
            chip[j] = total.astype(BF16)
            copy = remote(chip.at[j], chip_in.at[j], send.at[j], recv.at[j], peers[j])
            copy.start()
            copies.append(copy)
        else:
            out_ref[...] = total
    for copy in swaps:
        copy.wait_send()
    for j in range(3):
        copies[j].wait()
        out_ref[...] += chip_in[j].astype(F32)


def plane_scatter(total, collective_id):
    if not small_plane():
        return lax.psum_scatter(total.astype(F32), PLANE, scatter_dimension=0, tiled=True)
    rows, columns = total.shape[0] // 8, total.shape[1]
    return pl.pallas_call(
        plane_scatter_kernel,
        in_specs=[pl.BlockSpec(memory_space=pltpu.VMEM)],
        out_specs=pl.BlockSpec(memory_space=pltpu.VMEM),
        out_shape=jax.ShapeDtypeStruct((rows, columns), F32),
        scratch_shapes=[
            pltpu.VMEM((3, rows, columns), BF16),
            pltpu.VMEM((4, rows, columns), BF16),
            pltpu.VMEM((3, rows, columns), BF16),
            pltpu.SemaphoreType.DMA((3,)),
            pltpu.SemaphoreType.DMA((3,)),
            pltpu.SemaphoreType.DMA((4,)),
            pltpu.SemaphoreType.DMA((4,)),
        ],
        compiler_params=pltpu.CompilerParams(
            collective_id=collective_id, has_side_effects=True, vmem_limit_bytes=VMEM_LIMIT
        ),
        name="plane_scatter",
    )(total.reshape(8, rows, columns))


def line_project_kernel(
    count, chunks, x_ref, w_ref, base_ref, out_ref, held, send_right, send_left, recv
):
    f, c, t = here()
    right, left = (f, c, t + 1), (f, c, t - 1)
    greet_line(t, count, left, right)
    rows = x_ref.shape[0] // chunks

    def part(j):
        return pl.ds(j * rows, rows)

    def go(j, d, peer, origin, sems):
        src = x_ref.at[part(j)] if d == 0 else held.at[origin, part(j)]
        return remote(src, held.at[origin, part(j)], sems.at[d, j], recv.at[origin, j], peer)

    def go_right(j, d):
        return go(j, d, right, t - d, send_right)

    def go_left(j, d):
        return go(j, d, left, t + d, send_left)

    def arrived(j, origin):
        return remote(x_ref.at[part(j)], held.at[origin, part(j)], send_right.at[0, j], recv.at[origin, j], right)

    @pl.when(t < count - 1)
    def _():
        for j in range(chunks):
            go_right(j, 0).start()

    @pl.when(t > 0)
    def _():
        for j in range(chunks):
            go_left(j, 0).start()

    held[t] = x_ref[...]
    for d in range(1, count):
        for j in range(chunks):

            @pl.when(t - d >= 0)
            def _():
                arrived(j, t - d).wait_recv()
                if d < count - 1:

                    @pl.when(t < count - 1)
                    def _():
                        go_right(j, d).start()

            @pl.when(t + d < count)
            def _():
                arrived(j, t + d).wait_recv()
                if d < count - 1:

                    @pl.when(t > 0)
                    def _():
                        go_left(j, d).start()

            if d == count - 1:
                total = base_ref[part(j)]
                for origin in range(count):
                    total = total + mat_nt(held[origin, part(j)], w_ref[origin])
                out_ref[part(j)] = total

    for d in range(count - 1):
        for j in range(chunks):

            @pl.when((t - d >= 0) & (t < count - 1))
            def _():
                go_right(j, d).wait_send()

            @pl.when((t + d < count) & (t > 0))
            def _():
                go_left(j, d).wait_send()


def line_project(value, weights, base, collective_id):
    rows, width = value.shape
    count, features = weights.shape[0], weights.shape[1]
    chunks = 4
    return pl.pallas_call(
        functools.partial(line_project_kernel, count, chunks),
        in_specs=[pl.BlockSpec(memory_space=pltpu.VMEM)] * 3,
        out_specs=pl.BlockSpec(memory_space=pltpu.VMEM),
        out_shape=jax.ShapeDtypeStruct((rows, features), F32),
        scratch_shapes=[
            pltpu.VMEM((count, rows, width), BF16),
            pltpu.SemaphoreType.DMA((count, chunks)),
            pltpu.SemaphoreType.DMA((count, chunks)),
            pltpu.SemaphoreType.DMA((count, chunks)),
        ],
        compiler_params=pltpu.CompilerParams(
            collective_id=collective_id, has_side_effects=True, vmem_limit_bytes=VMEM_LIMIT
        ),
        name="line_project",
    )(value, weights, base)


def line_sum_kernel(
    count,
    chunks,
    window,
    lag,
    x_ref,
    out_ref,
    from_right,
    from_left,
    to_left,
    to_right,
    up_send,
    up_recv,
    down_send,
    down_recv,
    low_send,
    low_recv,
    high_send,
    high_recv,
):
    f, c, t = here()
    right, left = (f, c, t + 1), (f, c, t - 1)
    last = count - 1
    greet_line(t, count, left, right)
    half = x_ref.shape[0] // 2
    rows = half // chunks

    def low(j):
        return pl.ds(j * rows, rows)

    def high(j):
        return pl.ds(half + j * rows, rows)

    def down(j, own):
        src = x_ref.at[low(j)] if own else to_left.at[low(j)]
        return remote(src, from_right.at[low(j)], down_send.at[j], down_recv.at[j], left)

    def up(j, own):
        src = x_ref.at[high(j)] if own else to_right.at[low(j)]
        return remote(src, from_left.at[low(j)], up_send.at[j], up_recv.at[j], right)

    def low_back(j):
        return remote(out_ref.at[low(j)], out_ref.at[low(j)], low_send.at[j], low_recv.at[j], right)

    def high_back(j):
        return remote(
            out_ref.at[high(j)], out_ref.at[high(j)], high_send.at[j], high_recv.at[j], left
        )

    def pace(j, copy):
        if j == 0:
            for k in range(min(window, chunks)):
                copy(k, True).start()
        copy(j, True).wait_send()
        if j + window < chunks:
            copy(j + window, True).start()

    def low_step(j):
        @pl.when(t == last)
        def _():
            pace(j, down)

        @pl.when(t < last)
        def _():
            down(j, False).wait_recv()
            total = from_right[low(j)].astype(F32) + x_ref[low(j)].astype(F32)

            @pl.when(t > 0)
            def _():
                to_left[low(j)] = total.astype(BF16)
                down(j, False).start()

            @pl.when(t == 0)
            def _():
                out_ref[low(j)] = total.astype(BF16)
                low_back(j).start()

    def high_step(j):
        @pl.when(t == 0)
        def _():
            pace(j, up)

        @pl.when(t > 0)
        def _():
            up(j, False).wait_recv()
            total = from_left[low(j)].astype(F32) + x_ref[high(j)].astype(F32)

            @pl.when(t < last)
            def _():
                to_right[low(j)] = total.astype(BF16)
                up(j, False).start()

            @pl.when(t == last)
            def _():
                out_ref[high(j)] = total.astype(BF16)
                high_back(j).start()

    def low_forward(j):
        @pl.when(t > 0)
        def _():
            low_back(j).wait_recv()

            @pl.when(t < last)
            def _():
                low_back(j).start()

    def high_forward(j):
        @pl.when(t < last)
        def _():
            high_back(j).wait_recv()

            @pl.when(t > 0)
            def _():
                high_back(j).start()

    for j in range(chunks + lag):

        @pl.when(t < count // 2)
        def _():
            if j < chunks:
                high_step(j)
            if 0 <= j - 1 < chunks:
                low_step(j - 1)

        @pl.when(t >= count // 2)
        def _():
            if j < chunks:
                low_step(j)
            if 0 <= j - 1 < chunks:
                high_step(j - 1)

        if j >= lag:

            @pl.when(t < count // 2)
            def _():
                low_forward(j - lag)
                high_forward(j - lag)

            @pl.when(t >= count // 2)
            def _():
                high_forward(j - lag)
                low_forward(j - lag)

    for j in range(chunks):

        @pl.when(t > 0)
        def _():
            high_back(j).wait_send()

            @pl.when(t < last)
            def _():
                down(j, False).wait_send()

        @pl.when(t < last)
        def _():
            low_back(j).wait_send()

            @pl.when(t > 0)
            def _():
                up(j, False).wait_send()


def line_sum(partial, collective_id, chunks=4, window=2, lag=4):
    count = lax.axis_size("tp")
    rows, columns = partial.shape
    while (rows // 2) % (chunks * 16):
        chunks -= 1
    half = rows // 2
    return pl.pallas_call(
        functools.partial(line_sum_kernel, count, chunks, window, lag),
        in_specs=[pl.BlockSpec(memory_space=pltpu.VMEM)],
        out_specs=pl.BlockSpec(memory_space=pltpu.VMEM),
        out_shape=jax.ShapeDtypeStruct((rows, columns), BF16),
        scratch_shapes=[pltpu.VMEM((half, columns), BF16)] * 4
        + [pltpu.SemaphoreType.DMA((chunks,))] * 8,
        compiler_params=pltpu.CompilerParams(
            collective_id=collective_id, has_side_effects=True, vmem_limit_bytes=VMEM_LIMIT
        ),
        name="line_sum",
    )(partial)


def share_stats_kernel(count, x_ref, top_ref, log_ref, picked_ref, held, send, recv):
    f, c, t = here()
    peers = [(f, c, lax.rem(t + k, count)) for k in range(1, count)]
    greet(peers)
    copies = []
    for k in range(1, count):
        copy = remote(x_ref, held.at[t], send.at[k], recv.at[k], peers[k - 1])
        copy.start()
        copies.append(copy)
    held[t] = x_ref[...]
    for copy in copies:
        copy.wait()
    highest = functools.reduce(jnp.maximum, [held[k, 0] for k in range(count)])
    total = sum(held[k, 1] * jnp.exp(held[k, 0] - highest) for k in range(count))
    top_ref[...] = highest
    log_ref[...] = highest + jnp.log(total)
    picked_ref[...] = sum(held[k, 2] for k in range(count))


def share_stats(stats, collective_id):
    count = lax.axis_size("tp")
    shape = jax.ShapeDtypeStruct(stats.shape[1:], F32)
    return pl.pallas_call(
        functools.partial(share_stats_kernel, count),
        in_specs=[pl.BlockSpec(memory_space=pltpu.VMEM)],
        out_specs=[pl.BlockSpec(memory_space=pltpu.VMEM)] * 3,
        out_shape=[shape] * 3,
        scratch_shapes=[
            pltpu.VMEM((count,) + stats.shape, F32),
            pltpu.SemaphoreType.DMA((count,)),
            pltpu.SemaphoreType.DMA((count,)),
        ],
        compiler_params=pltpu.CompilerParams(collective_id=collective_id, has_side_effects=True),
        name="share_stats",
    )(stats)


def after(value, earlier):
    return lax.optimization_barrier((value, earlier))[0]


def tp_list(value):
    count = lax.axis_size("tp")
    return [value] + [
        lax.ppermute(value, "tp", [(i, (i + k) % count) for i in range(count)])
        for k in range(1, count)
    ]


def ctx_gather(value):
    if lax.axis_size("ctx") == 2:
        return jnp.concatenate([value, swap(value, "ctx", 1)], axis=0)
    return lax.all_gather(value, "ctx", axis=0, tiled=True)


def ctx_pair(value):
    if lax.axis_size("ctx") == 2:
        return [value, swap(value, "ctx", 1)]
    return [lax.all_gather(value, "ctx", axis=0, tiled=True)]


def ctx_join(parts):
    return jnp.concatenate(parts, axis=0)


def ctx_positions(rows):
    c, count = lax.axis_index("ctx"), lax.axis_size("ctx")
    if count == 2:
        return jnp.concatenate(
            [c * rows + jnp.arange(rows), (1 - c) * rows + jnp.arange(rows)]
        ).astype(jnp.int32)
    return jnp.arange(rows * count, dtype=jnp.int32)


def ctx_scatter(value):
    if lax.axis_size("ctx") == 2:
        rows = value.shape[0] // 2
        return low_sum(value[:rows], swap(value[rows:], "ctx", 1))
    return lax.psum_scatter(value.astype(F32), "ctx", scatter_dimension=0, tiled=True).astype(BF16)


def exit_forward_kernel(
    valid, x_ref, e_ref, target_ref, logits_ref, top_ref, sum_ref, picked_ref, m_acc, l_acc, p_acc
):
    step = pl.program_id(0)
    rows, tile = logits_ref.shape

    @pl.when(step == 0)
    def _():
        m_acc[...] = jnp.full_like(m_acc, LOWEST)
        l_acc[...] = jnp.zeros_like(l_acc)
        p_acc[...] = jnp.zeros_like(p_acc)

    lanes = lax.broadcasted_iota(jnp.int32, (rows, 128), 1)
    logits_ref[...] = mat(x_ref[...], e_ref[...])
    relative = target_ref[...] - step * tile
    limit = valid - step * tile
    groups = tile // 128
    highest = m_acc[...]
    for g in range(groups):
        cols = slice(g * 128, (g + 1) * 128)
        part = jnp.where(lanes < limit - g * 128, logits_ref[:, cols], LOWEST)
        highest = jnp.maximum(highest, part)
    total = l_acc[...] * jnp.exp(m_acc[...] - highest)
    picked = p_acc[...]
    for g in range(groups):
        cols = slice(g * 128, (g + 1) * 128)
        part = jnp.where(lanes < limit - g * 128, logits_ref[:, cols], LOWEST)
        total += jnp.exp(part - highest)
        picked += jnp.where(lanes == relative - g * 128, part, 0.0)
    m_acc[...] = highest
    l_acc[...] = total
    p_acc[...] = picked

    @pl.when(step == pl.num_programs(0) - 1)
    def _():
        top = jnp.max(m_acc[...], axis=1, keepdims=True)
        top_ref[...] = top
        sum_ref[...] = jnp.sum(l_acc[...] * jnp.exp(m_acc[...] - top), axis=1, keepdims=True)
        picked_ref[...] = jnp.sum(p_acc[...], axis=1, keepdims=True)


def exit_forward(exit_in, embed_t, targets_local, valid):
    rows, features = exit_in.shape
    padded = embed_t.shape[1]
    column = pl.BlockSpec((rows, 1), lambda i: (0, 0))
    stat = jax.ShapeDtypeStruct((rows, 1), F32)
    return pl.pallas_call(
        functools.partial(exit_forward_kernel, valid),
        grid=(padded // TILE,),
        in_specs=[
            pl.BlockSpec((rows, features), lambda i: (0, 0)),
            pl.BlockSpec((features, TILE), lambda i: (0, i)),
            column,
        ],
        out_specs=[pl.BlockSpec((rows, TILE), lambda i: (0, i)), column, column, column],
        out_shape=[jax.ShapeDtypeStruct((rows, padded), F32), stat, stat, stat],
        scratch_shapes=[pltpu.VMEM((rows, 128), F32)] * 3,
        compiler_params=pltpu.CompilerParams(vmem_limit_bytes=VMEM_LIMIT),
        cost_estimate=pl.CostEstimate(
            flops=2 * rows * features * padded,
            bytes_accessed=4 * rows * padded + 2 * features * padded,
            transcendentals=rows * padded,
        ),
        name="exit_forward",
    )(exit_in, embed_t, targets_local)


def exit_backward_kernel(
    valid, logits_ref, e_ref, x_t_ref, target_ref, log_ref, embed_ref, exit_ref, acc
):
    step = pl.program_id(0)
    rows, tile = logits_ref.shape

    @pl.when(step == 0)
    def _():
        acc[...] = jnp.zeros_like(acc)

    lanes = lax.broadcasted_iota(jnp.int32, (rows, tile), 1)
    relative = target_ref[...] - step * tile
    probs = jnp.exp(logits_ref[...] - log_ref[...])
    probs = jnp.where(lanes < valid - step * tile, probs, 0.0)
    grad = (probs - jnp.where(lanes == relative, 1.0, 0.0)).astype(BF16)
    acc[...] += mat_nt(grad, e_ref[...])
    embed_ref[...] = mat(x_t_ref[...], grad).astype(BF16)

    @pl.when(step == pl.num_programs(0) - 1)
    def _():
        exit_ref[...] = acc[...].astype(BF16)


def exit_backward(logits, embed_t, exit_in_t, targets_local, log_total, valid):
    rows, padded = logits.shape
    features = embed_t.shape[0]
    column = pl.BlockSpec((rows, 1), lambda i: (0, 0))
    return pl.pallas_call(
        functools.partial(exit_backward_kernel, valid),
        grid=(padded // TILE,),
        in_specs=[
            pl.BlockSpec((rows, TILE), lambda i: (0, i)),
            pl.BlockSpec((features, TILE), lambda i: (0, i)),
            pl.BlockSpec((features, rows), lambda i: (0, 0)),
            column,
            column,
        ],
        out_specs=[
            pl.BlockSpec((features, TILE), lambda i: (0, i)),
            pl.BlockSpec((rows, features), lambda i: (0, 0)),
        ],
        out_shape=[
            jax.ShapeDtypeStruct((features, padded), BF16),
            jax.ShapeDtypeStruct((rows, features), BF16),
        ],
        scratch_shapes=[pltpu.VMEM((rows, features), F32)],
        compiler_params=pltpu.CompilerParams(vmem_limit_bytes=VMEM_LIMIT),
        cost_estimate=pl.CostEstimate(
            flops=4 * rows * features * padded,
            bytes_accessed=4 * rows * padded + 4 * features * padded,
            transcendentals=rows * padded,
        ),
        name="exit_backward",
    )(logits, embed_t, exit_in_t, targets_local, log_total)


def forward_kernel(heads, q_ref, kv_ref, bias_ref, out_ref, total_ref):
    width = heads * HD
    for h in range(heads):
        cols = slice(h * HD, (h + 1) * HD)
        keys = kv_ref[:, cols]
        values = kv_ref[:, width + h * HD : width + (h + 1) * HD]
        scores = mat_nt(keys, q_ref[:, cols])
        if bias_ref is not None:
            scores = scores + bias_ref[...]
        highest = jnp.max(scores, axis=0, keepdims=True)
        exponent = jnp.exp(scores - highest)
        denominator = jnp.sum(exponent, axis=0, keepdims=True)
        outcome = mat_tn(values, exponent.astype(BF16)) / denominator
        out_ref[:, cols] = outcome.T.astype(BF16)
        total_ref[h : h + 1, :] = highest + jnp.log(denominator)


def backward_kernel(
    heads, q_ref, kv_ref, bias_ref, total_ref, go_ref, dq_ref, dkv_ref, acc_ref
):
    width = heads * HD
    step = pl.program_id(0)

    @pl.when(step == 0)
    def _():
        acc_ref[...] = jnp.zeros_like(acc_ref)

    for h in range(heads):
        cols = slice(h * HD, (h + 1) * HD)
        vcols = slice(width + h * HD, width + (h + 1) * HD)
        keys, values = kv_ref[:, cols], kv_ref[:, vcols]
        queries, go = q_ref[:, cols], go_ref[:, cols]
        scores = mat_nt(keys, queries)
        if bias_ref is not None:
            scores = scores + bias_ref[...]
        probs = jnp.exp(scores - total_ref[h : h + 1, :])
        grad_probs = mat_nt(values, go)
        inner = jnp.sum(probs * grad_probs, axis=0, keepdims=True)
        grad_scores = (probs * (grad_probs - inner)).astype(BF16)
        acc_ref[:, vcols] += mat(probs.astype(BF16), go)
        acc_ref[:, cols] += mat(grad_scores, queries)
        dq_ref[:, cols] = mat_tn(keys, grad_scores).T.astype(BF16)

    @pl.when(step == pl.num_programs(0) - 1)
    def _():
        dkv_ref[...] = acc_ref[...].astype(BF16)


def attention_specs(rows, width, keys, tile, masked):
    specs = [
        pl.BlockSpec((tile, width), lambda i: (i, 0)),
        pl.BlockSpec((keys, 2 * width), lambda i: (0, 0)),
    ]
    if masked:
        specs.append(pl.BlockSpec((keys, tile), lambda i: (0, i)))
    return specs


def attend(queries, kv, bias):
    rows, width = queries.shape
    keys, heads = kv.shape[0], width // HD
    tile = min(rows, 256)
    masked = bias is not None
    body = functools.partial(forward_kernel, heads)
    if not masked:
        plain = body
        body = lambda q, k, o, t: plain(q, k, None, o, t)
    return pl.pallas_call(
        body,
        grid=(rows // tile,),
        in_specs=attention_specs(rows, width, keys, tile, masked),
        out_specs=[
            pl.BlockSpec((tile, width), lambda i: (i, 0)),
            pl.BlockSpec((heads, tile), lambda i: (0, i)),
        ],
        out_shape=[
            jax.ShapeDtypeStruct((rows, width), BF16),
            jax.ShapeDtypeStruct((heads, rows), F32),
        ],
        compiler_params=pltpu.CompilerParams(vmem_limit_bytes=VMEM_LIMIT),
        cost_estimate=pl.CostEstimate(
            flops=16 * rows * keys * width,
            bytes_accessed=4 * keys * width + 8 * rows * width,
            transcendentals=rows * keys * heads,
        ),
        name="attend_masked" if masked else "attend",
    )(*([queries, kv, bias] if masked else [queries, kv]))


def attend_back(queries, kv, bias, totals, go):
    rows, width = queries.shape
    keys, heads = kv.shape[0], width // HD
    tile = min(rows, 256)
    masked = bias is not None
    body = functools.partial(backward_kernel, heads)
    if not masked:
        plain = body
        body = lambda q, k, *rest: plain(q, k, None, *rest)
    specs = attention_specs(rows, width, keys, tile, masked) + [
        pl.BlockSpec((heads, tile), lambda i: (0, i)),
        pl.BlockSpec((tile, width), lambda i: (i, 0)),
    ]
    operands = ([queries, kv, bias] if masked else [queries, kv]) + [totals, go]
    return pl.pallas_call(
        body,
        grid=(rows // tile,),
        in_specs=specs,
        out_specs=[
            pl.BlockSpec((tile, width), lambda i: (i, 0)),
            pl.BlockSpec((keys, 2 * width), lambda i: (0, 0)),
        ],
        out_shape=[
            jax.ShapeDtypeStruct((rows, width), BF16),
            jax.ShapeDtypeStruct((keys, 2 * width), BF16),
        ],
        scratch_shapes=[pltpu.VMEM((keys, 2 * width), F32)],
        compiler_params=pltpu.CompilerParams(vmem_limit_bytes=VMEM_LIMIT),
        cost_estimate=pl.CostEstimate(
            flops=40 * rows * keys * width,
            bytes_accessed=8 * keys * width + 10 * rows * width,
            transcendentals=rows * keys * heads,
        ),
        name="attend_back_masked" if masked else "attend_back",
    )(*operands)


def rms_scale(values):
    return lax.rsqrt(jnp.mean(values * values, axis=-1, keepdims=True) + EPSILON)


def rms_back(grad_normed, normed, scale):
    return scale * (grad_normed - normed * jnp.mean(grad_normed * normed, axis=-1, keepdims=True))


def mask_bias(parent_row, row_count):
    block_count = parent_row.shape[0]
    blocks = jnp.arange(block_count, dtype=jnp.int32)
    current = blocks
    reachable = blocks[:, None] == blocks[None, :]
    for _ in range(block_count - 1):
        current = jnp.sum(
            jnp.where(current[:, None] == blocks[None, :], parent_row[None, :], 0), axis=1
        )
        reachable = reachable | (current[:, None] == blocks[None, :])
    query_pos = lax.axis_index("ctx") * row_count + jnp.arange(row_count, dtype=jnp.int32)
    key_pos = ctx_positions(row_count)
    query_onehot = (query_pos[:, None] // BLK == blocks[None, :]).astype(F32)
    key_onehot = (key_pos[:, None] // BLK == blocks[None, :]).astype(F32)
    linked = mat_nt(key_onehot, mat(query_onehot, reachable.astype(F32))) > 0.5
    causal = (query_pos[None, :] // BLK != key_pos[:, None] // BLK) | (
        key_pos[:, None] <= query_pos[None, :]
    )
    return jnp.where(linked & causal, 0.0, MASKED)


def gelu_parts(gate):
    root = math.sqrt(2.0 / math.pi)
    inner = jnp.tanh(root * (gate + 0.044715 * gate * gate * gate))
    value = 0.5 * gate * (1.0 + inner)
    slope = 0.5 * (1.0 + inner) + 0.5 * gate * (1.0 - inner * inner) * root * (
        1.0 + 3.0 * 0.044715 * gate * gate
    )
    return value, slope


class Line:
    def __init__(self, t, count, left, right, own, place, sems):
        self.t, self.count, self.left, self.right = t, count, left, right
        self.own, self.place = own, place
        self.to_right, self.to_left, self.recv = sems

    def copy(self, d, way):
        origin = self.t - d if way == 0 else self.t + d
        sems, peer = (self.to_right, self.right) if way == 0 else (self.to_left, self.left)
        src = self.own if d == 0 else self.place(origin)
        return remote(src, self.place(origin), sems.at[d], self.recv.at[origin], peer)

    def landed(self, origin):
        return remote(
            self.place(origin),
            self.place(origin),
            self.to_right.at[0],
            self.recv.at[origin],
            self.right,
        )

    def start(self):
        @pl.when(self.t < self.count - 1)
        def _():
            self.copy(0, 0).start()

        @pl.when(self.t > 0)
        def _():
            self.copy(0, 1).start()

    def hop(self, d):
        t, last = self.t, self.count - 1

        @pl.when(t - d >= 0)
        def _():
            self.landed(t - d).wait_recv()
            if d < last:

                @pl.when(t < last)
                def _():
                    self.copy(d, 0).start()

        @pl.when(t + d <= last)
        def _():
            self.landed(t + d).wait_recv()
            if d < last:

                @pl.when(t > 0)
                def _():
                    self.copy(d, 1).start()

    def finish(self):
        t, last = self.t, self.count - 1
        for d in range(last):

            @pl.when((t - d >= 0) & (t < last))
            def _():
                self.copy(d, 0).wait_send()

            @pl.when((t + d <= last) & (t > 0))
            def _():
                self.copy(d, 1).wait_send()


class Spread:
    def __init__(self, x_peer, y_peer, core_peer, own, place, send, recv):
        self.send, self.recv = send, recv
        home, across, aside, diagonal = place(0, 0), place(0, 1), place(2, 0), place(2, 1)
        moves = [
            (own, home, x_peer),
            (own, home, y_peer),
            (across, across, y_peer),
            (own, home, core_peer),
            (across, across, core_peer),
            (aside, aside, core_peer),
            (diagonal, diagonal, core_peer),
        ]
        self.copies = [
            remote(src, dst, send.at[j], recv.at[j], peer)
            for j, (src, dst, peer) in enumerate(moves)
        ]

    def step(self, k):
        copies = self.copies
        if k == 0:
            for j in (0, 1, 3):
                copies[j].start()
        elif k == 1:
            copies[0].wait_recv()
            copies[2].start()
            copies[4].start()
        elif k == 2:
            copies[1].wait_recv()
            copies[5].start()
        elif k == 3:
            copies[2].wait_recv()
            copies[6].start()
        elif k == 4:
            for j in (3, 4, 5, 6):
                copies[j].wait_recv()
        else:
            for copy in copies:
                copy.wait_send()


def attend_head(h, i, tile, q_ref, kv_ref, bias_ref, out_ref, total_ref):
    rows, width = q_ref.shape[0] // MB, q_ref.shape[1]
    cols = slice(h * HD, (h + 1) * HD)
    vcols = slice(width + h * HD, width + (h + 1) * HD)

    @pl.loop(0, rows // tile)
    def _(n):
        at = pl.ds(pl.multiple_of(i * rows + n * tile, tile), tile)
        here_at = pl.ds(pl.multiple_of(n * tile, tile), tile)
        scores = mat_nt(kv_ref[i, :, cols], q_ref[at, cols])
        if bias_ref is not None:
            scores = scores + bias_ref[i, :, here_at]
        highest = jnp.max(scores, axis=0, keepdims=True)
        exponent = jnp.exp(scores - highest)
        denominator = jnp.sum(exponent, axis=0, keepdims=True)
        outcome = mat_tn(kv_ref[i, :, vcols], exponent.astype(BF16)) / denominator
        out_ref[at, cols] = outcome.T.astype(BF16)
        total_ref[i, h : h + 1, here_at] = highest + jnp.log(denominator)


def build_bias(parents_ref, bias_ref, c):
    trees, keys, rows = bias_ref.shape
    mine = rows // BLK
    block_count = keys // BLK
    key_iota = lax.broadcasted_iota(jnp.int32, (BLK, BLK), 0)
    query_iota = lax.broadcasted_iota(jnp.int32, (BLK, BLK), 1)
    causal = jnp.where(key_iota <= query_iota, 0.0, MASKED)
    for i in range(trees):
        lines = [jnp.int32(1)]
        for b in range(1, block_count):
            parent = parents_ref[i, b]
            line = jnp.int32(1 << b)
            for j in range(b):
                line = line + jnp.where(parent == j, lines[j], 0)
            lines.append(line)
        for q in range(mine):
            line = jnp.int32(0)
            for b in range(block_count):
                line = line + jnp.where(c * mine + q == b, lines[b], 0)
            for k in range(block_count):
                at = (slice(k * BLK, (k + 1) * BLK), slice(q * BLK, (q + 1) * BLK))
                if k == q:
                    bias_ref[(i,) + at] = causal
                    continue
                block = c * mine + k if k < mine else (1 - c) * mine + k - mine
                seen = lax.shift_right_logical(line, block) & 1
                value = jnp.where(seen == 1, 0.0, MASKED)
                bias_ref[(i,) + at] = jnp.full((BLK, BLK), value, F32)


def layer_forward_kernel(
    count,
    parents_ref,
    tok_ref,
    enc_ref,
    heads_in,
    op_in,
    ff_in,
    heads_all,
    op_all,
    ff_all,
    gains_out,
    bias,
    q_out,
    kvs,
    kvc,
    att,
    tots,
    cq,
    crs,
    totc,
    as_out,
    ac_out,
    zop,
    zff,
    held_s,
    held_c,
    spread_send,
    spread_recv,
    line_right,
    line_left,
    line_recv,
    ctx_send,
    ctx_recv,
    local_sem,
):
    f, c, t = here()
    right, left = (f, c, t + 1), (f, c, t - 1)
    x_peer, y_peer, core_peer = (f, 1 - c, t), (f ^ 2, c, t), (f ^ 1, c, t)
    rows, enc_rows = tok_ref.shape[0] // MB, enc_ref.shape[0] // MB
    width = q_out.shape[1]
    shard, ff_cols = ff_in.shape
    tile = 256

    barrier = pltpu.get_barrier_semaphore()
    for peer in (x_peer, y_peer, core_peer):
        pl.semaphore_signal(barrier, inc=1, device_id=peer, device_id_type=MESH)

    @pl.when(t > 0)
    def _():
        pl.semaphore_signal(barrier, inc=1, device_id=left, device_id_type=MESH)

    @pl.when(t < count - 1)
    def _():
        pl.semaphore_signal(barrier, inc=1, device_id=right, device_id_type=MESH)

    at_end = (t == 0) | (t == count - 1)
    pl.semaphore_wait(barrier, jnp.where(at_end, 4, 5).astype(jnp.int32))

    def block(df, dc):
        slot = (f ^ df) * 2 + (c ^ dc)
        return pl.ds(pl.multiple_of(slot * shard, shard), shard)

    def spread(j, own, place):
        return Spread(
            x_peer, y_peer, core_peer, own, place, spread_send.at[j], spread_recv.at[j]
        )

    def line(j, own, place):
        sems = (line_right.at[j], line_left.at[j], line_recv.at[j])
        return Line(t, count, left, right, own, place, sems)

    def part(i):
        return pl.ds(i * rows, rows)

    heads = spread(0, heads_in, lambda df, dc: heads_all.at[block(df, dc)])
    op_line = line(0, op_in, lambda origin: zop.at[:, origin])
    op = spread(1, zop, lambda df, dc: op_all.at[:, :, block(df, dc)])

    def ff_place(origin):
        return zff.at[:, pl.ds(pl.multiple_of(origin * ff_cols, 128), ff_cols)]

    ff_line = line(1, ff_in, ff_place)
    ff = spread(2, zff, lambda df, dc: ff_all.at[block(df, dc)])
    ff_own = pltpu.make_async_copy(zff, ff_all.at[block(0, 0)], local_sem)
    self_lines = [
        line(2 + i, att.at[part(i)], lambda origin, i=i: held_s.at[origin, part(i)])
        for i in range(MB)
    ]
    cross_lines = [
        line(4 + i, crs.at[part(i)], lambda origin, i=i: held_c.at[origin, part(i)])
        for i in range(MB)
    ]

    def ctx_copy(j, ref, i, size):
        return remote(
            ref.at[i, pl.ds(0, size)],
            ref.at[i, pl.ds(size, size)],
            ctx_send.at[j],
            ctx_recv.at[j],
            x_peer,
        )

    ctx_self = [ctx_copy(i, kvs, i, rows) for i in range(MB)]
    ctx_cross = [ctx_copy(2 + i, kvc, i, enc_rows) for i in range(MB)]

    def project_tokens(i):
        @pl.loop(0, rows // tile)
        def _(n):
            at = pl.ds(pl.multiple_of(i * rows + n * tile, tile), tile)
            value = tok_ref[at].astype(F32)
            hidden = (value * rms_scale(value) * gains_out[0:1]).astype(BF16)
            q_out[at] = mat(hidden, heads_all[:, 4 * width : 5 * width]).astype(BF16)
            inner = pl.ds(pl.multiple_of(n * tile, tile), tile)
            kvs[i, inner] = mat(hidden, heads_all[:, : 2 * width]).astype(BF16)

    def project_encoder(i):
        @pl.loop(0, enc_rows // tile)
        def _(n):
            at = pl.ds(pl.multiple_of(i * enc_rows + n * tile, tile), tile)
            inner = pl.ds(pl.multiple_of(n * tile, tile), tile)
            kvc[i, inner] = mat(enc_ref[at], heads_all[:, 2 * width : 4 * width]).astype(BF16)

    def self_head(i, h):
        attend_head(h, i, tile, q_out, kvs, bias, att, tots)

    def cross_head(i, h):
        attend_head(h, i, tile, cq, kvc, None, crs, totc)

    def out_self(i):
        @pl.loop(0, rows // tile)
        def _(n):
            at = pl.ds(pl.multiple_of(i * rows + n * tile, tile), tile)
            total = tok_ref[at].astype(F32)
            for origin in range(count):
                total = total + mat_nt(held_s[origin, at], op_all[0, origin])
            as_out[at] = total
            hidden = (total * rms_scale(total) * gains_out[1:2]).astype(BF16)
            cq[at] = mat(hidden, heads_all[:, Q2 : Q2 + width]).astype(BF16)

    def out_cross(i):
        @pl.loop(0, rows // tile)
        def _(n):
            at = pl.ds(pl.multiple_of(i * rows + n * tile, tile), tile)
            total = as_out[at]
            for origin in range(count):
                total = total + mat_nt(held_c[origin, at], op_all[1, origin])
            ac_out[at] = total

    heads.step(0)
    op_line.start()
    heads_all[block(0, 0)] = heads_in[...]
    zop[:, t] = op_in[...]
    zff[:, pl.ds(pl.multiple_of(t * ff_cols, 128), ff_cols)] = ff_in[...]
    build_bias(parents_ref, bias, c)
    op_line.hop(1)
    heads.step(1)
    op_line.hop(2)
    ff_line.start()
    heads.step(2)
    op_line.hop(3)
    op.step(0)
    op_all[:, :, block(0, 0)] = zop[...]
    heads.step(3)
    heads.step(4)
    gains_out[...] = heads_all[:, Q2 - 128 : Q2].astype(F32).T[64:72]
    project_tokens(0)
    ctx_self[0].start()
    project_tokens(1)
    ctx_self[1].start()
    op.step(1)
    ff_line.hop(1)
    project_encoder(0)
    ctx_cross[0].start()
    project_encoder(1)
    ctx_cross[1].start()
    op.step(2)
    ctx_self[0].wait_recv()
    self_head(0, 0)
    ff_line.hop(2)
    self_head(0, 1)
    op.step(3)
    self_head(0, 2)
    held_s[t, part(0)] = att[part(0)]
    self_lines[0].start()
    ff_line.hop(3)
    ff_own.start()
    ctx_self[1].wait_recv()
    self_head(1, 0)
    self_lines[0].hop(1)
    self_head(1, 1)
    op.step(4)
    self_head(1, 2)
    held_s[t, part(1)] = att[part(1)]
    self_lines[1].start()
    self_lines[0].hop(2)
    ff.step(0)
    self_lines[0].hop(3)
    out_self(0)
    self_lines[1].hop(1)
    ctx_cross[0].wait_recv()
    cross_head(0, 0)
    self_lines[1].hop(2)
    ff.step(1)
    cross_head(0, 1)
    self_lines[1].hop(3)
    cross_head(0, 2)
    held_c[t, part(0)] = crs[part(0)]
    cross_lines[0].start()
    out_self(1)
    ctx_cross[1].wait_recv()
    ff.step(2)
    cross_head(1, 0)
    cross_lines[0].hop(1)
    cross_head(1, 1)
    cross_lines[0].hop(2)
    cross_head(1, 2)
    held_c[t, part(1)] = crs[part(1)]
    cross_lines[1].start()
    cross_lines[0].hop(3)
    out_cross(0)
    cross_lines[1].hop(1)
    ff.step(3)
    cross_lines[1].hop(2)
    cross_lines[1].hop(3)
    out_cross(1)
    ff.step(4)
    heads.step(5)
    op.step(5)
    ff.step(5)
    for one in [op_line, ff_line] + self_lines + cross_lines:
        one.finish()
    for copy in ctx_self + ctx_cross:
        copy.wait_send()
    ff_own.wait()


def layer_forward(parents, tokens, encoder, heads_in, op_in, ff_in, collective_id):
    count = lax.axis_size("tp")
    tok_rows, features = tokens.shape
    enc_rows = encoder.shape[0]
    shard, ff_cols = ff_in.shape
    width = op_in.shape[2]
    nh = width // HD
    rows = tok_rows // MB
    vmem = pl.BlockSpec(memory_space=pltpu.VMEM)

    def low(*shape):
        return jax.ShapeDtypeStruct(shape, BF16)

    def full(*shape):
        return jax.ShapeDtypeStruct(shape, F32)

    return pl.pallas_call(
        functools.partial(layer_forward_kernel, count),
        in_specs=[pl.BlockSpec(memory_space=pltpu.SMEM)] + [vmem] * 5,
        out_specs=[vmem, vmem, pl.BlockSpec(memory_space=pl.ANY)] + [vmem] * 12,
        out_shape=[
            low(features, heads_in.shape[1]),
            low(3, count, features, width),
            low(features, count * ff_cols),
            full(8, features),
            full(MB, 2 * rows, rows),
            low(tok_rows, width),
            low(MB, 2 * rows, 2 * width),
            low(MB, enc_rows, 2 * width),
            low(tok_rows, width),
            full(MB, nh, rows),
            low(tok_rows, width),
            low(tok_rows, width),
            full(MB, nh, rows),
            full(tok_rows, features),
            full(tok_rows, features),
        ],
        scratch_shapes=[
            pltpu.VMEM((3, count, shard, width), BF16),
            pltpu.VMEM((shard, count * ff_cols), BF16),
            pltpu.VMEM((count, tok_rows, width), BF16),
            pltpu.VMEM((count, tok_rows, width), BF16),
            pltpu.SemaphoreType.DMA((3, 7)),
            pltpu.SemaphoreType.DMA((3, 7)),
            pltpu.SemaphoreType.DMA((6, count)),
            pltpu.SemaphoreType.DMA((6, count)),
            pltpu.SemaphoreType.DMA((6, count)),
            pltpu.SemaphoreType.DMA((4,)),
            pltpu.SemaphoreType.DMA((4,)),
            pltpu.SemaphoreType.DMA,
        ],
        compiler_params=pltpu.CompilerParams(
            collective_id=collective_id, has_side_effects=True, vmem_limit_bytes=VMEM_MOST
        ),
        name="layer_forward",
    )(parents, tokens, encoder, heads_in, op_in, ff_in)


def ff_forward_kernel(
    shrink, ac_ref, gains_ref, w_ref, gate_ref, up_ref, mixed_ref, low_ref, exit_ref, exit_t_ref, h_acc
):
    step = pl.program_id(0)
    rows = ac_ref.shape[0]
    units = gate_ref.shape[1]
    tile = min(rows, 256)

    @pl.loop(0, rows // tile)
    def _(n):
        at = pl.ds(pl.multiple_of(n * tile, tile), tile)

        @pl.when(step == 0)
        def _():
            value = ac_ref[at]
            h_acc[at] = (value * rms_scale(value) * gains_ref[2:3]).astype(BF16)
            mixed_ref[at] = value

        hidden = h_acc[at]
        gate = mat(hidden, w_ref[:, :units])
        up = mat(hidden, w_ref[:, units : 2 * units])
        gate_ref[at] = gate
        up_ref[at] = up
        activated = (gelu_parts(gate)[0] * up).astype(BF16)
        mixed_ref[at] += mat_nt(activated, w_ref[:, 2 * units :])

        @pl.when(step == pl.num_programs(0) - 1)
        def _():
            value = mixed_ref[at]
            low_ref[at] = value.astype(BF16)
            exit_in = value * rms_scale(value) * gains_ref[3:4] * shrink
            exit_ref[at] = exit_in.astype(BF16)

    @pl.when(step == pl.num_programs(0) - 1)
    def _():
        exit_t_ref[...] = exit_ref[...].T


def ff_forward(after_cross, gains, ff_all, count, shrink):
    rows, features = after_cross.shape
    cols = ff_all.shape[1] // count
    units = cols // 3

    def fixed(*shape):
        return pl.BlockSpec(shape, lambda i: (0,) * len(shape))

    moving = pl.BlockSpec((rows, units), lambda i: (0, i))
    return pl.pallas_call(
        functools.partial(ff_forward_kernel, shrink),
        grid=(count,),
        in_specs=[
            fixed(rows, features),
            fixed(8, features),
            pl.BlockSpec((features, cols), lambda i: (0, i)),
        ],
        out_specs=[moving, moving] + [fixed(rows, features)] * 3 + [fixed(features, rows)],
        out_shape=[
            jax.ShapeDtypeStruct((rows, count * units), F32),
            jax.ShapeDtypeStruct((rows, count * units), F32),
            jax.ShapeDtypeStruct((rows, features), F32),
            jax.ShapeDtypeStruct((rows, features), BF16),
            jax.ShapeDtypeStruct((rows, features), BF16),
            jax.ShapeDtypeStruct((features, rows), BF16),
        ],
        scratch_shapes=[pltpu.VMEM((rows, features), BF16)],
        compiler_params=pltpu.CompilerParams(vmem_limit_bytes=VMEM_MOST),
        cost_estimate=pl.CostEstimate(
            flops=2 * rows * features * count * cols,
            bytes_accessed=2 * features * count * cols + 8 * rows * count * units,
            transcendentals=rows * count * units,
        ),
        name="ff_forward",
    )(after_cross, gains, ff_all)


def ff_backward_kernel(
    shrink,
    ge_ref,
    mixed_ref,
    cot_ref,
    ac_ref,
    gains_ref,
    co_ref,
    w_ref,
    gate_ref,
    up_ref,
    gac_ref,
    low_ref,
    gcl_ref,
    gcr_ref,
    hid_ref,
    act_ref,
    gg_ref,
    gu_ref,
    norms_ref,
    acc,
):
    step = pl.program_id(0)
    t = lax.axis_index("tp")
    last = pl.num_programs(0) - 1
    rows = ac_ref.shape[0]
    units = gate_ref.shape[1]
    tile = min(rows, 256)

    @pl.when(step == 0)
    def _():
        norms_ref[...] = jnp.zeros_like(norms_ref)

    @pl.loop(0, rows // tile)
    def _(n):
        at = pl.ds(pl.multiple_of(n * tile, tile), tile)

        @pl.when(step == 0)
        def _():
            grad_exit = ge_ref[at].astype(F32) * shrink
            mixed = mixed_ref[at]
            scale = rms_scale(mixed)
            normed = mixed * scale
            norms_ref[0:1] += jnp.sum(grad_exit * normed, axis=0, keepdims=True)
            grad_mixed = cot_ref[at].astype(F32) + rms_back(
                grad_exit * gains_ref[3:4], normed, scale
            )
            gac_ref[at] = grad_mixed
            low_ref[at] = grad_mixed.astype(BF16)
            value = ac_ref[at]
            hid_ref[at] = (value * rms_scale(value) * gains_ref[2:3]).astype(BF16)
            acc[at] = jnp.zeros_like(acc[at])

        gate = gate_ref[at]
        up = up_ref[at]
        grad_act = mat(low_ref[at], w_ref[:, 2 * units :])
        value, slope = gelu_parts(gate)
        grad_gate = (grad_act * slope * up).astype(BF16)
        grad_up = (grad_act * value).astype(BF16)
        acc[at] += mat_nt(grad_gate, w_ref[:, :units]) + mat_nt(
            grad_up, w_ref[:, units : 2 * units]
        )

        @pl.when(step == t)
        def _():
            act_ref[at] = (value * up).astype(BF16)
            gg_ref[at] = grad_gate
            gu_ref[at] = grad_up

        @pl.when(step == last)
        def _():
            value = ac_ref[at]
            scale = rms_scale(value)
            normed = value * scale
            grad = acc[at]
            norms_ref[1:2] += jnp.sum(grad * normed, axis=0, keepdims=True)
            total = gac_ref[at] + rms_back(grad * gains_ref[2:3], normed, scale)
            gac_ref[at] = total
            gcl_ref[at] = total.astype(BF16)
            gcr_ref[at] = mat(total.astype(BF16), co_ref[...]).astype(BF16)


def ff_backward(
    grad_exit, mixed, cotangent, after_cross, gains, c_out_own, ff_all, gate, up, count, shrink
):
    rows, features = after_cross.shape
    cols = ff_all.shape[1] // count
    units = cols // 3
    width = c_out_own.shape[1]

    def fixed(*shape):
        return pl.BlockSpec(shape, lambda i: (0,) * len(shape))

    def low(*shape):
        return jax.ShapeDtypeStruct(shape, BF16)

    moving = pl.BlockSpec((rows, units), lambda i: (0, i))
    return pl.pallas_call(
        functools.partial(ff_backward_kernel, shrink),
        grid=(count,),
        in_specs=[fixed(rows, features)] * 4
        + [
            fixed(8, features),
            fixed(features, width),
            pl.BlockSpec((features, cols), lambda i: (0, i)),
            moving,
            moving,
        ],
        out_specs=[fixed(rows, features)] * 3
        + [fixed(rows, width), fixed(rows, features)]
        + [fixed(rows, units)] * 3
        + [fixed(8, features)],
        out_shape=[
            jax.ShapeDtypeStruct((rows, features), F32),
            low(rows, features),
            low(rows, features),
            low(rows, width),
            low(rows, features),
            low(rows, units),
            low(rows, units),
            low(rows, units),
            jax.ShapeDtypeStruct((8, features), F32),
        ],
        scratch_shapes=[pltpu.VMEM((rows, features), F32)],
        compiler_params=pltpu.CompilerParams(vmem_limit_bytes=VMEM_MOST),
        cost_estimate=pl.CostEstimate(
            flops=2 * rows * features * count * cols,
            bytes_accessed=2 * features * count * cols + 8 * rows * count * units,
            transcendentals=rows * count * units,
        ),
        name="ff_backward",
    )(grad_exit, mixed, cotangent, after_cross, gains, c_out_own, ff_all, gate, up)


def layer_forward_plain(parents, tokens, encoder, heads_in, op_in, ff_in, collective_id):
    rows = tokens.shape[0] // MB
    enc_rows = encoder.shape[0] // MB
    width = op_in.shape[2]
    heads_all = lax.all_gather(heads_in, PLANE, axis=0, tiled=True)
    op_all = lax.all_gather(
        lax.all_gather(op_in, "tp", axis=1, tiled=False), PLANE, axis=2, tiled=True
    )
    ff_all = lax.all_gather(
        lax.all_gather(ff_in, "tp", axis=1, tiled=True), PLANE, axis=0, tiled=True
    )
    gains = heads_all[:, Q2 - 64 : Q2 - 56].astype(F32).T
    tok = tokens.astype(F32)
    hidden_one = (tok * rms_scale(tok) * gains[0:1]).astype(BF16)
    queries = mat(hidden_one, heads_all[:, 4 * width : 5 * width]).astype(BF16)
    kv = mat(hidden_one, heads_all[:, : 2 * width]).astype(BF16)
    enc_kv = mat(encoder, heads_all[:, 2 * width : 4 * width]).astype(BF16)

    def both_sides(value, i, count):
        return ctx_gather(value[i * count : (i + 1) * count])

    kv_self = jnp.stack([both_sides(kv, i, rows) for i in range(MB)])
    kv_cross = jnp.stack([both_sides(enc_kv, i, enc_rows) for i in range(MB)])
    bias = jnp.stack([mask_bias(parents[i], rows) for i in range(MB)])

    def attention(values, keys_values, masks):
        outcome = [
            attend(
                values[i * rows : (i + 1) * rows],
                keys_values[i],
                None if masks is None else masks[i],
            )
            for i in range(MB)
        ]
        return jnp.concatenate([o[0] for o in outcome]), jnp.stack([o[1] for o in outcome])

    attended, totals_self = attention(queries, kv_self, bias)
    after_self = line_project(attended, op_all[0], tok, 2)
    hidden_two = (after_self * rms_scale(after_self) * gains[1:2]).astype(BF16)
    cross_q = mat(hidden_two, heads_all[:, Q2 : Q2 + width]).astype(BF16)
    crossed, totals_cross = attention(cross_q, kv_cross, None)
    after_cross = line_project(crossed, op_all[1], after_self, 3)
    return (
        heads_all,
        op_all,
        ff_all,
        gains,
        bias,
        queries,
        kv_self,
        kv_cross,
        attended,
        totals_self,
        cross_q,
        crossed,
        totals_cross,
        after_self,
        after_cross,
    )


def local(
    tokens,
    encoder,
    cotangent,
    parents,
    targets,
    w_query,
    w_key,
    w_value,
    w_out,
    c_query,
    c_key,
    c_value,
    c_out,
    w_gate,
    w_up,
    w_down,
    embedding,
    norm_self,
    norm_cross,
    norm_ff,
    norm_exit,
):
    t = lax.axis_index("tp")
    tp_count = lax.axis_size("tp")
    rows = tokens.shape[0] // MB
    features = tokens.shape[1]
    width = w_query.shape[1]
    hidden_units = w_gate.shape[1]
    vocab = embedding.shape[0]
    trees = range(MB)
    shrink = 1.0 / math.sqrt(features)

    def tree_rows(value, i):
        count = value.shape[0] // MB
        return value[i * count : (i + 1) * count]

    gains_in = jnp.stack([norm_self, norm_cross, norm_ff, norm_exit], axis=1)
    heads_in = jnp.concatenate(
        [w_key, w_value, c_key, c_value, w_query]
        + [jnp.pad(gains_in, ((0, 0), (0, 60))), c_query, jnp.zeros_like(c_query[:, :64])],
        axis=1,
    )
    op_in = jnp.stack([w_out.T, c_out.T, c_query])
    ff_in = jnp.concatenate([w_gate, w_up, w_down.T], axis=1)
    padded = -(-vocab // TILE) * TILE
    embed_in = jnp.pad(embedding.T, ((0, 0), (0, padded - vocab)))
    embed_t = lax.all_gather(embed_in, PLANE, axis=0, tiled=True)
    forward = layer_forward if small_plane() else layer_forward_plain
    (
        heads_all,
        op_all,
        ff_all,
        gains,
        bias,
        queries,
        kv_self,
        kv_cross,
        attended,
        totals_self,
        cross_q,
        crossed,
        totals_cross,
        after_self,
        after_cross,
    ) = forward(parents, after(tokens, embed_in), encoder, heads_in, op_in, ff_in, 1)
    gain_self, gain_cross = gains[0:1], gains[1:2]
    w_kv, w_q = heads_all[:, : 2 * width], heads_all[:, 4 * width : 5 * width]
    c_kv = heads_all[:, 2 * width : 4 * width]
    own_out = lax.dynamic_index_in_dim(op_all[:2], t, 1, False)
    w_out_own, c_out_own = own_out[0], own_out[1]
    gate_pre, up_pre, mixed, mixed_low, exit_in, exit_in_t = ff_forward(
        after_cross, gains, ff_all, tp_count, shrink
    )

    targets_local = targets - t * vocab
    inside = (targets_local >= 0) & (targets_local < vocab)
    targets_local = jnp.where(inside, targets_local, -1)[:, None]
    logits, top, summed, picked = exit_forward(exit_in, embed_t, targets_local, vocab)
    stats = jnp.stack([top, summed, picked]).reshape(3, MB * rows // 128, 128)
    top, log_total, picked = share_stats(stats, 4)
    losses = (log_total - picked).reshape(-1)
    scores = (top - log_total).reshape(-1)
    grad_embed, grad_exit_part = exit_backward(
        logits, embed_t, exit_in_t, targets_local, log_total.reshape(-1, 1), vocab
    )
    grad_embed_own = lax.optimization_barrier(
        lax.psum_scatter(grad_embed, PLANE, scatter_dimension=0, tiled=True)
    )
    grad_exit = line_sum(grad_exit_part, 5)

    (
        grad_after_cross,
        grad_mixed_low,
        grad_cross_low,
        grad_crossed,
        hidden_three,
        activated_own,
        grad_gate_own,
        grad_up_own,
        norms,
    ) = ff_backward(
        grad_exit,
        mixed,
        cotangent,
        after_cross,
        gains,
        c_out_own,
        ff_all,
        gate_pre,
        up_pre,
        tp_count,
        shrink,
    )
    outcome = [
        attend_back(
            tree_rows(cross_q, i), kv_cross[i], None, totals_cross[i], tree_rows(grad_crossed, i)
        )
        for i in trees
    ]
    grad_cq = jnp.concatenate([o[0] for o in outcome], axis=0)
    grad_kv_cross = jnp.concatenate([ctx_scatter(o[1]) for o in outcome], axis=0)
    encoder_part = mat_nt(grad_kv_cross, c_kv).astype(BF16)
    grad_two = line_project(grad_cq, op_all[2], jnp.zeros_like(after_self), 6)
    scale_two = rms_scale(after_self)
    normed_two = after_self * scale_two
    hidden_two = (normed_two * gain_cross).astype(BF16)
    norm_cross_grad = jnp.sum(grad_two * normed_two, axis=0)
    grad_after_self = grad_after_cross + rms_back(grad_two * gain_cross, normed_two, scale_two)
    grad_self_low = grad_after_self.astype(BF16)
    grad_attended = mat(grad_self_low, w_out_own).astype(BF16)
    outcome = [
        attend_back(
            tree_rows(queries, i), kv_self[i], bias[i], totals_self[i], tree_rows(grad_attended, i)
        )
        for i in trees
    ]
    grad_q = jnp.concatenate([o[0] for o in outcome], axis=0)
    grad_kv_self = jnp.concatenate([ctx_scatter(o[1]) for o in outcome], axis=0)
    one_part = (mat_nt(grad_q, w_q) + mat_nt(grad_kv_self, w_kv)).astype(BF16)
    both = line_sum(jnp.concatenate([one_part, encoder_part], axis=0), 7, 12)
    grad_one = both[: MB * rows].astype(F32)
    grad_encoder = both[MB * rows :].astype(F32)
    tok = tokens.astype(F32)
    scale_one = rms_scale(tok)
    normed_one = tok * scale_one
    hidden_one = (normed_one * gain_self).astype(BF16)
    norm_self_grad = jnp.sum(grad_one * normed_one, axis=0)
    grad_tokens = grad_after_self + rms_back(grad_one * gain_self, normed_one, scale_one)

    ff_grads = jnp.concatenate(
        [
            mat_tn(hidden_three, grad_gate_own),
            mat_tn(hidden_three, grad_up_own),
            mat_tn(grad_mixed_low, activated_own),
            mat_tn(grad_cross_low, crossed),
        ],
        axis=1,
    ).astype(BF16)
    ff_own = lax.psum_scatter(after(ff_grads, grad_two), PLANE, scatter_dimension=0, tiled=True)
    norm_block = jnp.pad(
        jnp.stack([norm_self_grad, norm_cross_grad, norms[1], norms[0]], axis=1),
        ((0, 0), (0, 60)),
    )
    own = plane_scatter(
        jnp.concatenate(
            [
                mat_tn(hidden_one, grad_kv_self),
                mat_tn(encoder, grad_kv_cross),
                mat_tn(hidden_one, grad_q),
                norm_block,
                mat_tn(hidden_two, grad_cq),
                mat_tn(grad_self_low, attended),
            ],
            axis=1,
        ).astype(BF16),
        9,
    )

    def part(value, start, size):
        return value[:, start : start + size].astype(F32)

    base = Q2 - 64
    return (
        mixed_low,
        losses,
        scores,
        grad_tokens,
        grad_encoder,
        part(own, 4 * width, width),
        part(own, 0, width),
        part(own, width, width),
        part(own, Q2 + width, width).T,
        part(own, Q2, width),
        part(own, 2 * width, width),
        part(own, 3 * width, width),
        part(ff_own, 3 * hidden_units, width).T,
        part(ff_own, 0, hidden_units),
        part(ff_own, hidden_units, hidden_units),
        part(ff_own, 2 * hidden_units, hidden_units).T,
        grad_embed_own[:, :vocab].astype(F32).T,
        own[:, base],
        own[:, base + 1],
        own[:, base + 2],
        own[:, base + 3],
    )


def solution(mesh):
    rows_cols = P(PLANE, "tp")
    cols_rows = P("tp", PLANE)
    data = P(PLANE, None)
    flat = P(PLANE)
    weights = (rows_cols,) * 3 + (cols_rows,) + (rows_cols,) * 3 + (cols_rows,)
    weights += (rows_cols,) * 2 + (cols_rows,) * 2 + (flat,) * 4
    return jax.shard_map(
        local,
        mesh=mesh,
        in_specs=(data, data, data, P("fsdp", None), flat) + weights,
        out_specs=(data, flat, flat, data, data) + weights,
        check_vma=False,
    )
```

```python
import functools
import math

import jax
import jax.numpy as jnp
from jax import lax
from jax.experimental import pallas as pl
from jax.experimental.pallas import tpu as pltpu
from jax.sharding import PartitionSpec as P

HD = 64
BLK = 128
MB = 2
EPSILON = 1e-06
MASKED = -1000000000.0
F32 = jnp.float32
BF16 = jnp.bfloat16
PLANE = ("fsdp", "ctx")
VMEM_LIMIT = 48 * 1024 * 1024
MESH = pl.DeviceIdType.MESH
TILE = 1024
LOWEST = -3.0e38
VMEM_MOST = 58 * 1024 * 1024
Q2 = 1024


def mat(left, right):
    return jnp.dot(left, right, preferred_element_type=F32)


def mat_nt(left, right):
    return lax.dot_general(left, right, (((1,), (1,)), ((), ())), preferred_element_type=F32)


def mat_tn(left, right):
    return lax.dot_general(left, right, (((0,), (0,)), ((), ())), preferred_element_type=F32)


def small_plane():
    return lax.axis_size("fsdp") == 4 and lax.axis_size("ctx") == 2


def swap(value, axis, bit):
    count = lax.axis_size(axis)
    return lax.ppermute(value, axis, [(i, i ^ bit) for i in range(count)])


def low_sum(left, right):
    return (left.astype(F32) + right.astype(F32)).astype(BF16)


def here():
    return lax.axis_index("fsdp"), lax.axis_index("ctx"), lax.axis_index("tp")


def greet(peers):
    barrier = pltpu.get_barrier_semaphore()
    for peer in peers:
        pl.semaphore_signal(barrier, inc=1, device_id=peer, device_id_type=MESH)
    pl.semaphore_wait(barrier, len(peers))


def greet_line(t, count, left, right):
    barrier = pltpu.get_barrier_semaphore()

    @pl.when(t > 0)
    def _():
        pl.semaphore_signal(barrier, inc=1, device_id=left, device_id_type=MESH)

    @pl.when(t < count - 1)
    def _():
        pl.semaphore_signal(barrier, inc=1, device_id=right, device_id_type=MESH)

    at_end = (t == 0) | (t == count - 1)
    pl.semaphore_wait(barrier, jnp.where(at_end, 1, 2).astype(jnp.int32))


def remote(src, dst, send, recv, peer):
    return pltpu.make_async_remote_copy(
        src_ref=src, dst_ref=dst, send_sem=send, recv_sem=recv, device_id=peer, device_id_type=MESH
    )


def plane_gather_kernel(x_ref, out_ref, send, recv, core_send, core_recv):
    f, c, t = here()
    core = f % 2
    chips = [(0, 1), (2, 0), (2, 1)]
    peers = [(f ^ df, c ^ dc, t) for df, dc in chips]
    partner = (f ^ 1, c, t)
    greet(peers + [partner])

    def slot(df, dc):
        return (f ^ df) * 2 + (c ^ dc)

    own = slot(0, 0)
    copies = []
    for j, peer in enumerate(peers):
        copy = remote(x_ref, out_ref.at[own], send.at[j], recv.at[j], peer)
        copy.start()
        copies.append(copy)
    passes = [remote(x_ref, out_ref.at[own], core_send.at[3], core_recv.at[3], partner)]
    passes[0].start()
    out_ref[own] = x_ref[...]
    for j, (df, dc) in enumerate(chips):
        copies[j].wait_recv()
        there = slot(df, dc)
        copy = remote(
            out_ref.at[there], out_ref.at[there], core_send.at[j], core_recv.at[j], partner
        )
        copy.start()
        passes.append(copy)
    for copy in copies:
        copy.wait_send()
    for copy in passes:
        copy.wait()


def plane_gather(shard, collective_id):
    if not small_plane():
        return lax.all_gather(shard, PLANE, axis=0, tiled=True)
    rows, columns = shard.shape
    out = pl.pallas_call(
        plane_gather_kernel,
        in_specs=[pl.BlockSpec(memory_space=pltpu.VMEM)],
        out_specs=pl.BlockSpec(memory_space=pltpu.VMEM),
        out_shape=jax.ShapeDtypeStruct((8, rows, columns), shard.dtype),
        scratch_shapes=[
            pltpu.SemaphoreType.DMA((3,)),
            pltpu.SemaphoreType.DMA((3,)),
            pltpu.SemaphoreType.DMA((4,)),
            pltpu.SemaphoreType.DMA((4,)),
        ],
        compiler_params=pltpu.CompilerParams(
            collective_id=collective_id, has_side_effects=True, vmem_limit_bytes=VMEM_LIMIT
        ),
        name="plane_gather",
    )(shard)
    return out.reshape(8 * rows, columns)


def plane_scatter_kernel(
    x_ref, out_ref, chip, core_in, chip_in, send, recv, core_send, core_recv
):
    f, c, t = here()
    core = f % 2
    chips = [(2, 1), (0, 1), (2, 0)]
    peers = [(f ^ df, c ^ dc, t) for df, dc in chips]
    partner = (f ^ 1, c, t)
    greet(peers + [partner])
    order = chips + [(0, 0)]
    swaps = []
    for j, (df, dc) in enumerate(order):
        block = (f ^ df ^ 1) * 2 + (c ^ dc)
        copy = remote(x_ref.at[block], core_in.at[j], core_send.at[j], core_recv.at[j], partner)
        copy.start()
        swaps.append(copy)
    copies = []
    for j, (df, dc) in enumerate(order):
        swaps[j].wait_recv()
        block = (f ^ df) * 2 + (c ^ dc)
        total = x_ref[block].astype(F32) + core_in[j].astype(F32)
        if j < 3:
            chip[j] = total.astype(BF16)
            copy = remote(chip.at[j], chip_in.at[j], send.at[j], recv.at[j], peers[j])
            copy.start()
            copies.append(copy)
        else:
            out_ref[...] = total
    for copy in swaps:
        copy.wait_send()
    for j in range(3):
        copies[j].wait()
        out_ref[...] += chip_in[j].astype(F32)


def plane_scatter(total, collective_id):
    if not small_plane():
        return lax.psum_scatter(total.astype(F32), PLANE, scatter_dimension=0, tiled=True)
    rows, columns = total.shape[0] // 8, total.shape[1]
    return pl.pallas_call(
        plane_scatter_kernel,
        in_specs=[pl.BlockSpec(memory_space=pltpu.VMEM)],
        out_specs=pl.BlockSpec(memory_space=pltpu.VMEM),
        out_shape=jax.ShapeDtypeStruct((rows, columns), F32),
        scratch_shapes=[
            pltpu.VMEM((3, rows, columns), BF16),
            pltpu.VMEM((4, rows, columns), BF16),
            pltpu.VMEM((3, rows, columns), BF16),
            pltpu.SemaphoreType.DMA((3,)),
            pltpu.SemaphoreType.DMA((3,)),
            pltpu.SemaphoreType.DMA((4,)),
            pltpu.SemaphoreType.DMA((4,)),
        ],
        compiler_params=pltpu.CompilerParams(
            collective_id=collective_id, has_side_effects=True, vmem_limit_bytes=VMEM_LIMIT
        ),
        name="plane_scatter",
    )(total.reshape(8, rows, columns))


def line_project_kernel(
    count, chunks, x_ref, w_ref, base_ref, out_ref, held, send_right, send_left, recv
):
    f, c, t = here()
    right, left = (f, c, t + 1), (f, c, t - 1)
    greet_line(t, count, left, right)
    rows = x_ref.shape[0] // chunks

    def part(j):
        return pl.ds(j * rows, rows)

    def go(j, d, peer, origin, sems):
        src = x_ref.at[part(j)] if d == 0 else held.at[origin, part(j)]
        return remote(src, held.at[origin, part(j)], sems.at[d, j], recv.at[origin, j], peer)

    def go_right(j, d):
        return go(j, d, right, t - d, send_right)

    def go_left(j, d):
        return go(j, d, left, t + d, send_left)

    def arrived(j, origin):
        return remote(x_ref.at[part(j)], held.at[origin, part(j)], send_right.at[0, j], recv.at[origin, j], right)

    @pl.when(t < count - 1)
    def _():
        for j in range(chunks):
            go_right(j, 0).start()

    @pl.when(t > 0)
    def _():
        for j in range(chunks):
            go_left(j, 0).start()

    held[t] = x_ref[...]
    for d in range(1, count):
        for j in range(chunks):

            @pl.when(t - d >= 0)
            def _():
                arrived(j, t - d).wait_recv()
                if d < count - 1:

                    @pl.when(t < count - 1)
                    def _():
                        go_right(j, d).start()

            @pl.when(t + d < count)
            def _():
                arrived(j, t + d).wait_recv()
                if d < count - 1:

                    @pl.when(t > 0)
                    def _():
                        go_left(j, d).start()

            if d == count - 1:
                total = base_ref[part(j)]
                for origin in range(count):
                    total = total + mat_nt(held[origin, part(j)], w_ref[origin])
                out_ref[part(j)] = total

    for d in range(count - 1):
        for j in range(chunks):

            @pl.when((t - d >= 0) & (t < count - 1))
            def _():
                go_right(j, d).wait_send()

            @pl.when((t + d < count) & (t > 0))
            def _():
                go_left(j, d).wait_send()


def line_project(value, weights, base, collective_id):
    rows, width = value.shape
    count, features = weights.shape[0], weights.shape[1]
    chunks = 4
    return pl.pallas_call(
        functools.partial(line_project_kernel, count, chunks),
        in_specs=[pl.BlockSpec(memory_space=pltpu.VMEM)] * 3,
        out_specs=pl.BlockSpec(memory_space=pltpu.VMEM),
        out_shape=jax.ShapeDtypeStruct((rows, features), F32),
        scratch_shapes=[
            pltpu.VMEM((count, rows, width), BF16),
            pltpu.SemaphoreType.DMA((count, chunks)),
            pltpu.SemaphoreType.DMA((count, chunks)),
            pltpu.SemaphoreType.DMA((count, chunks)),
        ],
        compiler_params=pltpu.CompilerParams(
            collective_id=collective_id, has_side_effects=True, vmem_limit_bytes=VMEM_LIMIT
        ),
        name="line_project",
    )(value, weights, base)


def line_sum_kernel(
    count,
    chunks,
    window,
    lag,
    x_ref,
    out_ref,
    from_right,
    from_left,
    to_left,
    to_right,
    up_send,
    up_recv,
    down_send,
    down_recv,
    low_send,
    low_recv,
    high_send,
    high_recv,
):
    f, c, t = here()
    right, left = (f, c, t + 1), (f, c, t - 1)
    last = count - 1
    greet_line(t, count, left, right)
    half = x_ref.shape[0] // 2
    rows = half // chunks

    def low(j):
        return pl.ds(j * rows, rows)

    def high(j):
        return pl.ds(half + j * rows, rows)

    def down(j, own):
        src = x_ref.at[low(j)] if own else to_left.at[low(j)]
        return remote(src, from_right.at[low(j)], down_send.at[j], down_recv.at[j], left)

    def up(j, own):
        src = x_ref.at[high(j)] if own else to_right.at[low(j)]
        return remote(src, from_left.at[low(j)], up_send.at[j], up_recv.at[j], right)

    def low_back(j):
        return remote(out_ref.at[low(j)], out_ref.at[low(j)], low_send.at[j], low_recv.at[j], right)

    def high_back(j):
        return remote(
            out_ref.at[high(j)], out_ref.at[high(j)], high_send.at[j], high_recv.at[j], left
        )

    def pace(j, copy):
        if j == 0:
            for k in range(min(window, chunks)):
                copy(k, True).start()
        copy(j, True).wait_send()
        if j + window < chunks:
            copy(j + window, True).start()

    def low_step(j):
        @pl.when(t == last)
        def _():
            pace(j, down)

        @pl.when(t < last)
        def _():
            down(j, False).wait_recv()
            total = from_right[low(j)].astype(F32) + x_ref[low(j)].astype(F32)

            @pl.when(t > 0)
            def _():
                to_left[low(j)] = total.astype(BF16)
                down(j, False).start()

            @pl.when(t == 0)
            def _():
                out_ref[low(j)] = total.astype(BF16)
                low_back(j).start()

    def high_step(j):
        @pl.when(t == 0)
        def _():
            pace(j, up)

        @pl.when(t > 0)
        def _():
            up(j, False).wait_recv()
            total = from_left[low(j)].astype(F32) + x_ref[high(j)].astype(F32)

            @pl.when(t < last)
            def _():
                to_right[low(j)] = total.astype(BF16)
                up(j, False).start()

            @pl.when(t == last)
            def _():
                out_ref[high(j)] = total.astype(BF16)
                high_back(j).start()

    def low_forward(j):
        @pl.when(t > 0)
        def _():
            low_back(j).wait_recv()

            @pl.when(t < last)
            def _():
                low_back(j).start()

    def high_forward(j):
        @pl.when(t < last)
        def _():
            high_back(j).wait_recv()

            @pl.when(t > 0)
            def _():
                high_back(j).start()

    for j in range(chunks + lag):

        @pl.when(t < count // 2)
        def _():
            if j < chunks:
                high_step(j)
            if 0 <= j - 1 < chunks:
                low_step(j - 1)

        @pl.when(t >= count // 2)
        def _():
            if j < chunks:
                low_step(j)
            if 0 <= j - 1 < chunks:
                high_step(j - 1)

        if j >= lag:

            @pl.when(t < count // 2)
            def _():
                low_forward(j - lag)
                high_forward(j - lag)

            @pl.when(t >= count // 2)
            def _():
                high_forward(j - lag)
                low_forward(j - lag)

    for j in range(chunks):

        @pl.when(t > 0)
        def _():
            high_back(j).wait_send()

            @pl.when(t < last)
            def _():
                down(j, False).wait_send()

        @pl.when(t < last)
        def _():
            low_back(j).wait_send()

            @pl.when(t > 0)
            def _():
                up(j, False).wait_send()


def line_sum(partial, collective_id, chunks=4, window=2, lag=4):
    count = lax.axis_size("tp")
    rows, columns = partial.shape
    while (rows // 2) % (chunks * 16):
        chunks -= 1
    half = rows // 2
    return pl.pallas_call(
        functools.partial(line_sum_kernel, count, chunks, window, lag),
        in_specs=[pl.BlockSpec(memory_space=pltpu.VMEM)],
        out_specs=pl.BlockSpec(memory_space=pltpu.VMEM),
        out_shape=jax.ShapeDtypeStruct((rows, columns), BF16),
        scratch_shapes=[pltpu.VMEM((half, columns), BF16)] * 4
        + [pltpu.SemaphoreType.DMA((chunks,))] * 8,
        compiler_params=pltpu.CompilerParams(
            collective_id=collective_id, has_side_effects=True, vmem_limit_bytes=VMEM_LIMIT
        ),
        name="line_sum",
    )(partial)


def share_stats_kernel(count, x_ref, top_ref, log_ref, picked_ref, held, send, recv):
    f, c, t = here()
    peers = [(f, c, lax.rem(t + k, count)) for k in range(1, count)]
    greet(peers)
    copies = []
    for k in range(1, count):
        copy = remote(x_ref, held.at[t], send.at[k], recv.at[k], peers[k - 1])
        copy.start()
        copies.append(copy)
    held[t] = x_ref[...]
    for copy in copies:
        copy.wait()
    highest = functools.reduce(jnp.maximum, [held[k, 0] for k in range(count)])
    total = sum(held[k, 1] * jnp.exp(held[k, 0] - highest) for k in range(count))
    top_ref[...] = highest
    log_ref[...] = highest + jnp.log(total)
    picked_ref[...] = sum(held[k, 2] for k in range(count))


def share_stats(stats, collective_id):
    count = lax.axis_size("tp")
    shape = jax.ShapeDtypeStruct(stats.shape[1:], F32)
    return pl.pallas_call(
        functools.partial(share_stats_kernel, count),
        in_specs=[pl.BlockSpec(memory_space=pltpu.VMEM)],
        out_specs=[pl.BlockSpec(memory_space=pltpu.VMEM)] * 3,
        out_shape=[shape] * 3,
        scratch_shapes=[
            pltpu.VMEM((count,) + stats.shape, F32),
            pltpu.SemaphoreType.DMA((count,)),
            pltpu.SemaphoreType.DMA((count,)),
        ],
        compiler_params=pltpu.CompilerParams(collective_id=collective_id, has_side_effects=True),
        name="share_stats",
    )(stats)


def after(value, earlier):
    return lax.optimization_barrier((value, earlier))[0]


def tp_list(value):
    count = lax.axis_size("tp")
    return [value] + [
        lax.ppermute(value, "tp", [(i, (i + k) % count) for i in range(count)])
        for k in range(1, count)
    ]


def ctx_gather(value):
    if lax.axis_size("ctx") == 2:
        return jnp.concatenate([value, swap(value, "ctx", 1)], axis=0)
    return lax.all_gather(value, "ctx", axis=0, tiled=True)


def ctx_pair(value):
    if lax.axis_size("ctx") == 2:
        return [value, swap(value, "ctx", 1)]
    return [lax.all_gather(value, "ctx", axis=0, tiled=True)]


def ctx_join(parts):
    return jnp.concatenate(parts, axis=0)


def ctx_positions(rows):
    c, count = lax.axis_index("ctx"), lax.axis_size("ctx")
    if count == 2:
        return jnp.concatenate(
            [c * rows + jnp.arange(rows), (1 - c) * rows + jnp.arange(rows)]
        ).astype(jnp.int32)
    return jnp.arange(rows * count, dtype=jnp.int32)


def ctx_scatter(value):
    if lax.axis_size("ctx") == 2:
        rows = value.shape[0] // 2
        return low_sum(value[:rows], swap(value[rows:], "ctx", 1))
    return lax.psum_scatter(value.astype(F32), "ctx", scatter_dimension=0, tiled=True).astype(BF16)


def exit_forward_kernel(
    valid, x_ref, e_ref, target_ref, logits_ref, top_ref, sum_ref, picked_ref, m_acc, l_acc, p_acc
):
    step = pl.program_id(0)
    rows, tile = logits_ref.shape

    @pl.when(step == 0)
    def _():
        m_acc[...] = jnp.full_like(m_acc, LOWEST)
        l_acc[...] = jnp.zeros_like(l_acc)
        p_acc[...] = jnp.zeros_like(p_acc)

    lanes = lax.broadcasted_iota(jnp.int32, (rows, 128), 1)
    logits_ref[...] = mat(x_ref[...], e_ref[...])
    relative = target_ref[...] - step * tile
    limit = valid - step * tile
    groups = tile // 128
    highest = m_acc[...]
    for g in range(groups):
        cols = slice(g * 128, (g + 1) * 128)
        part = jnp.where(lanes < limit - g * 128, logits_ref[:, cols], LOWEST)
        highest = jnp.maximum(highest, part)
    total = l_acc[...] * jnp.exp(m_acc[...] - highest)
    picked = p_acc[...]
    for g in range(groups):
        cols = slice(g * 128, (g + 1) * 128)
        part = jnp.where(lanes < limit - g * 128, logits_ref[:, cols], LOWEST)
        total += jnp.exp(part - highest)
        picked += jnp.where(lanes == relative - g * 128, part, 0.0)
    m_acc[...] = highest
    l_acc[...] = total
    p_acc[...] = picked

    @pl.when(step == pl.num_programs(0) - 1)
    def _():
        top = jnp.max(m_acc[...], axis=1, keepdims=True)
        top_ref[...] = top
        sum_ref[...] = jnp.sum(l_acc[...] * jnp.exp(m_acc[...] - top), axis=1, keepdims=True)
        picked_ref[...] = jnp.sum(p_acc[...], axis=1, keepdims=True)


def exit_forward(exit_in, embed_t, targets_local, valid):
    rows, features = exit_in.shape
    padded = embed_t.shape[1]
    column = pl.BlockSpec((rows, 1), lambda i: (0, 0))
    stat = jax.ShapeDtypeStruct((rows, 1), F32)
    return pl.pallas_call(
        functools.partial(exit_forward_kernel, valid),
        grid=(padded // TILE,),
        in_specs=[
            pl.BlockSpec((rows, features), lambda i: (0, 0)),
            pl.BlockSpec((features, TILE), lambda i: (0, i)),
            column,
        ],
        out_specs=[pl.BlockSpec((rows, TILE), lambda i: (0, i)), column, column, column],
        out_shape=[jax.ShapeDtypeStruct((rows, padded), F32), stat, stat, stat],
        scratch_shapes=[pltpu.VMEM((rows, 128), F32)] * 3,
        compiler_params=pltpu.CompilerParams(vmem_limit_bytes=VMEM_LIMIT),
        cost_estimate=pl.CostEstimate(
            flops=2 * rows * features * padded,
            bytes_accessed=4 * rows * padded + 2 * features * padded,
            transcendentals=rows * padded,
        ),
        name="exit_forward",
    )(exit_in, embed_t, targets_local)


def exit_backward_kernel(
    valid, logits_ref, e_ref, x_t_ref, target_ref, log_ref, embed_ref, exit_ref, acc
):
    step = pl.program_id(0)
    rows, tile = logits_ref.shape

    @pl.when(step == 0)
    def _():
        acc[...] = jnp.zeros_like(acc)

    lanes = lax.broadcasted_iota(jnp.int32, (rows, tile), 1)
    relative = target_ref[...] - step * tile
    probs = jnp.exp(logits_ref[...] - log_ref[...])
    probs = jnp.where(lanes < valid - step * tile, probs, 0.0)
    grad = (probs - jnp.where(lanes == relative, 1.0, 0.0)).astype(BF16)
    acc[...] += mat_nt(grad, e_ref[...])
    embed_ref[...] = mat(x_t_ref[...], grad).astype(BF16)

    @pl.when(step == pl.num_programs(0) - 1)
    def _():
        exit_ref[...] = acc[...].astype(BF16)


def exit_backward(logits, embed_t, exit_in_t, targets_local, log_total, valid):
    rows, padded = logits.shape
    features = embed_t.shape[0]
    column = pl.BlockSpec((rows, 1), lambda i: (0, 0))
    return pl.pallas_call(
        functools.partial(exit_backward_kernel, valid),
        grid=(padded // TILE,),
        in_specs=[
            pl.BlockSpec((rows, TILE), lambda i: (0, i)),
            pl.BlockSpec((features, TILE), lambda i: (0, i)),
            pl.BlockSpec((features, rows), lambda i: (0, 0)),
            column,
            column,
        ],
        out_specs=[
            pl.BlockSpec((features, TILE), lambda i: (0, i)),
            pl.BlockSpec((rows, features), lambda i: (0, 0)),
        ],
        out_shape=[
            jax.ShapeDtypeStruct((features, padded), BF16),
            jax.ShapeDtypeStruct((rows, features), BF16),
        ],
        scratch_shapes=[pltpu.VMEM((rows, features), F32)],
        compiler_params=pltpu.CompilerParams(vmem_limit_bytes=VMEM_LIMIT),
        cost_estimate=pl.CostEstimate(
            flops=4 * rows * features * padded,
            bytes_accessed=4 * rows * padded + 4 * features * padded,
            transcendentals=rows * padded,
        ),
        name="exit_backward",
    )(logits, embed_t, exit_in_t, targets_local, log_total)


def forward_kernel(heads, q_ref, kv_ref, bias_ref, out_ref, total_ref):
    width = heads * HD
    for h in range(heads):
        cols = slice(h * HD, (h + 1) * HD)
        keys = kv_ref[:, cols]
        values = kv_ref[:, width + h * HD : width + (h + 1) * HD]
        scores = mat_nt(keys, q_ref[:, cols])
        if bias_ref is not None:
            scores = scores + bias_ref[...]
        highest = jnp.max(scores, axis=0, keepdims=True)
        exponent = jnp.exp(scores - highest)
        denominator = jnp.sum(exponent, axis=0, keepdims=True)
        outcome = mat_tn(values, exponent.astype(BF16)) / denominator
        out_ref[:, cols] = outcome.T.astype(BF16)
        total_ref[h : h + 1, :] = highest + jnp.log(denominator)


def backward_kernel(
    heads, q_ref, kv_ref, bias_ref, total_ref, go_ref, dq_ref, dkv_ref, acc_ref
):
    width = heads * HD
    step = pl.program_id(0)

    @pl.when(step == 0)
    def _():
        acc_ref[...] = jnp.zeros_like(acc_ref)

    for h in range(heads):
        cols = slice(h * HD, (h + 1) * HD)
        vcols = slice(width + h * HD, width + (h + 1) * HD)
        keys, values = kv_ref[:, cols], kv_ref[:, vcols]
        queries, go = q_ref[:, cols], go_ref[:, cols]
        scores = mat_nt(keys, queries)
        if bias_ref is not None:
            scores = scores + bias_ref[...]
        probs = jnp.exp(scores - total_ref[h : h + 1, :])
        grad_probs = mat_nt(values, go)
        inner = jnp.sum(probs * grad_probs, axis=0, keepdims=True)
        grad_scores = (probs * (grad_probs - inner)).astype(BF16)
        acc_ref[:, vcols] += mat(probs.astype(BF16), go)
        acc_ref[:, cols] += mat(grad_scores, queries)
        dq_ref[:, cols] = mat_tn(keys, grad_scores).T.astype(BF16)

    @pl.when(step == pl.num_programs(0) - 1)
    def _():
        dkv_ref[...] = acc_ref[...].astype(BF16)


def attention_specs(rows, width, keys, tile, masked):
    specs = [
        pl.BlockSpec((tile, width), lambda i: (i, 0)),
        pl.BlockSpec((keys, 2 * width), lambda i: (0, 0)),
    ]
    if masked:
        specs.append(pl.BlockSpec((keys, tile), lambda i: (0, i)))
    return specs


def attend(queries, kv, bias):
    rows, width = queries.shape
    keys, heads = kv.shape[0], width // HD
    tile = min(rows, 256)
    masked = bias is not None
    body = functools.partial(forward_kernel, heads)
    if not masked:
        plain = body
        body = lambda q, k, o, t: plain(q, k, None, o, t)
    return pl.pallas_call(
        body,
        grid=(rows // tile,),
        in_specs=attention_specs(rows, width, keys, tile, masked),
        out_specs=[
            pl.BlockSpec((tile, width), lambda i: (i, 0)),
            pl.BlockSpec((heads, tile), lambda i: (0, i)),
        ],
        out_shape=[
            jax.ShapeDtypeStruct((rows, width), BF16),
            jax.ShapeDtypeStruct((heads, rows), F32),
        ],
        compiler_params=pltpu.CompilerParams(vmem_limit_bytes=VMEM_LIMIT),
        cost_estimate=pl.CostEstimate(
            flops=16 * rows * keys * width,
            bytes_accessed=4 * keys * width + 8 * rows * width,
            transcendentals=rows * keys * heads,
        ),
        name="attend_masked" if masked else "attend",
    )(*([queries, kv, bias] if masked else [queries, kv]))


def attend_back(queries, kv, bias, totals, go):
    rows, width = queries.shape
    keys, heads = kv.shape[0], width // HD
    tile = min(rows, 256)
    masked = bias is not None
    body = functools.partial(backward_kernel, heads)
    if not masked:
        plain = body
        body = lambda q, k, *rest: plain(q, k, None, *rest)
    specs = attention_specs(rows, width, keys, tile, masked) + [
        pl.BlockSpec((heads, tile), lambda i: (0, i)),
        pl.BlockSpec((tile, width), lambda i: (i, 0)),
    ]
    operands = ([queries, kv, bias] if masked else [queries, kv]) + [totals, go]
    return pl.pallas_call(
        body,
        grid=(rows // tile,),
        in_specs=specs,
        out_specs=[
            pl.BlockSpec((tile, width), lambda i: (i, 0)),
            pl.BlockSpec((keys, 2 * width), lambda i: (0, 0)),
        ],
        out_shape=[
            jax.ShapeDtypeStruct((rows, width), BF16),
            jax.ShapeDtypeStruct((keys, 2 * width), BF16),
        ],
        scratch_shapes=[pltpu.VMEM((keys, 2 * width), F32)],
        compiler_params=pltpu.CompilerParams(vmem_limit_bytes=VMEM_LIMIT),
        cost_estimate=pl.CostEstimate(
            flops=40 * rows * keys * width,
            bytes_accessed=8 * keys * width + 10 * rows * width,
            transcendentals=rows * keys * heads,
        ),
        name="attend_back_masked" if masked else "attend_back",
    )(*operands)


def rms_scale(values):
    return lax.rsqrt(jnp.mean(values * values, axis=-1, keepdims=True) + EPSILON)


def rms_back(grad_normed, normed, scale):
    return scale * (grad_normed - normed * jnp.mean(grad_normed * normed, axis=-1, keepdims=True))


def mask_bias(parent_row, row_count):
    block_count = parent_row.shape[0]
    blocks = jnp.arange(block_count, dtype=jnp.int32)
    current = blocks
    reachable = blocks[:, None] == blocks[None, :]
    for _ in range(block_count - 1):
        current = jnp.sum(
            jnp.where(current[:, None] == blocks[None, :], parent_row[None, :], 0), axis=1
        )
        reachable = reachable | (current[:, None] == blocks[None, :])
    query_pos = lax.axis_index("ctx") * row_count + jnp.arange(row_count, dtype=jnp.int32)
    key_pos = ctx_positions(row_count)
    query_onehot = (query_pos[:, None] // BLK == blocks[None, :]).astype(F32)
    key_onehot = (key_pos[:, None] // BLK == blocks[None, :]).astype(F32)
    linked = mat_nt(key_onehot, mat(query_onehot, reachable.astype(F32))) > 0.5
    causal = (query_pos[None, :] // BLK != key_pos[:, None] // BLK) | (
        key_pos[:, None] <= query_pos[None, :]
    )
    return jnp.where(linked & causal, 0.0, MASKED)


def gelu_parts(gate):
    root = math.sqrt(2.0 / math.pi)
    inner = jnp.tanh(root * (gate + 0.044715 * gate * gate * gate))
    value = 0.5 * gate * (1.0 + inner)
    slope = 0.5 * (1.0 + inner) + 0.5 * gate * (1.0 - inner * inner) * root * (
        1.0 + 3.0 * 0.044715 * gate * gate
    )
    return value, slope


class Line:
    def __init__(self, t, count, left, right, own, place, sems):
        self.t, self.count, self.left, self.right = t, count, left, right
        self.own, self.place = own, place
        self.to_right, self.to_left, self.recv = sems

    def copy(self, d, way):
        origin = self.t - d if way == 0 else self.t + d
        sems, peer = (self.to_right, self.right) if way == 0 else (self.to_left, self.left)
        src = self.own if d == 0 else self.place(origin)
        return remote(src, self.place(origin), sems.at[d], self.recv.at[origin], peer)

    def landed(self, origin):
        return remote(
            self.place(origin),
            self.place(origin),
            self.to_right.at[0],
            self.recv.at[origin],
            self.right,
        )

    def start(self):
        @pl.when(self.t < self.count - 1)
        def _():
            self.copy(0, 0).start()

        @pl.when(self.t > 0)
        def _():
            self.copy(0, 1).start()

    def hop(self, d):
        t, last = self.t, self.count - 1

        @pl.when(t - d >= 0)
        def _():
            self.landed(t - d).wait_recv()
            if d < last:

                @pl.when(t < last)
                def _():
                    self.copy(d, 0).start()

        @pl.when(t + d <= last)
        def _():
            self.landed(t + d).wait_recv()
            if d < last:

                @pl.when(t > 0)
                def _():
                    self.copy(d, 1).start()

    def finish(self):
        t, last = self.t, self.count - 1
        for d in range(last):

            @pl.when((t - d >= 0) & (t < last))
            def _():
                self.copy(d, 0).wait_send()

            @pl.when((t + d <= last) & (t > 0))
            def _():
                self.copy(d, 1).wait_send()


class Spread:
    def __init__(self, x_peer, y_peer, core_peer, own, place, send, recv):
        self.send, self.recv = send, recv
        home, across, aside, diagonal = place(0, 0), place(0, 1), place(2, 0), place(2, 1)
        moves = [
            (own, home, x_peer),
            (own, home, y_peer),
            (across, across, y_peer),
            (own, home, core_peer),
            (across, across, core_peer),
            (aside, aside, core_peer),
            (diagonal, diagonal, core_peer),
        ]
        self.copies = [
            remote(src, dst, send.at[j], recv.at[j], peer)
            for j, (src, dst, peer) in enumerate(moves)
        ]

    def step(self, k):
        copies = self.copies
        if k == 0:
            for j in (0, 1, 3):
                copies[j].start()
        elif k == 1:
            copies[0].wait_recv()
            copies[2].start()
            copies[4].start()
        elif k == 2:
            copies[1].wait_recv()
            copies[5].start()
        elif k == 3:
            copies[2].wait_recv()
            copies[6].start()
        elif k == 4:
            for j in (3, 4, 5, 6):
                copies[j].wait_recv()
        else:
            for copy in copies:
                copy.wait_send()


def attend_head(h, i, tile, q_ref, kv_ref, bias_ref, out_ref, total_ref):
    rows, width = q_ref.shape[0] // MB, q_ref.shape[1]
    cols = slice(h * HD, (h + 1) * HD)
    vcols = slice(width + h * HD, width + (h + 1) * HD)

    @pl.loop(0, rows // tile)
    def _(n):
        at = pl.ds(pl.multiple_of(i * rows + n * tile, tile), tile)
        here_at = pl.ds(pl.multiple_of(n * tile, tile), tile)
        scores = mat_nt(kv_ref[i, :, cols], q_ref[at, cols])
        if bias_ref is not None:
            scores = scores + bias_ref[i, :, here_at]
        highest = jnp.max(scores, axis=0, keepdims=True)
        exponent = jnp.exp(scores - highest)
        denominator = jnp.sum(exponent, axis=0, keepdims=True)
        outcome = mat_tn(kv_ref[i, :, vcols], exponent.astype(BF16)) / denominator
        out_ref[at, cols] = outcome.T.astype(BF16)
        total_ref[i, h : h + 1, here_at] = highest + jnp.log(denominator)


def build_bias(parents_ref, bias_ref, c):
    trees, keys, rows = bias_ref.shape
    mine = rows // BLK
    block_count = keys // BLK
    key_iota = lax.broadcasted_iota(jnp.int32, (BLK, BLK), 0)
    query_iota = lax.broadcasted_iota(jnp.int32, (BLK, BLK), 1)
    causal = jnp.where(key_iota <= query_iota, 0.0, MASKED)
    for i in range(trees):
        lines = [jnp.int32(1)]
        for b in range(1, block_count):
            parent = parents_ref[i, b]
            line = jnp.int32(1 << b)
            for j in range(b):
                line = line + jnp.where(parent == j, lines[j], 0)
            lines.append(line)
        for q in range(mine):
            line = jnp.int32(0)
            for b in range(block_count):
                line = line + jnp.where(c * mine + q == b, lines[b], 0)
            for k in range(block_count):
                at = (slice(k * BLK, (k + 1) * BLK), slice(q * BLK, (q + 1) * BLK))
                if k == q:
                    bias_ref[(i,) + at] = causal.astype(BF16)
                    continue
                block = c * mine + k if k < mine else (1 - c) * mine + k - mine
                seen = lax.shift_right_logical(line, block) & 1
                value = jnp.where(seen == 1, 0.0, MASKED)
                bias_ref[(i,) + at] = jnp.full((BLK, BLK), value, F32).astype(BF16)


def layer_forward_kernel(
    count,
    parents_ref,
    tok_ref,
    enc_ref,
    heads_in,
    op_in,
    ff_in,
    heads_all,
    op_all,
    ff_all,
    gains_out,
    bias,
    q_out,
    kvs,
    kvc,
    att,
    tots,
    cq,
    crs,
    totc,
    as_out,
    ac_out,
    zop,
    zff,
    held_s,
    held_c,
    spread_send,
    spread_recv,
    line_right,
    line_left,
    line_recv,
    ctx_send,
    ctx_recv,
    local_sem,
):
    f, c, t = here()
    right, left = (f, c, t + 1), (f, c, t - 1)
    x_peer, y_peer, core_peer = (f, 1 - c, t), (f ^ 2, c, t), (f ^ 1, c, t)
    rows, enc_rows = tok_ref.shape[0] // MB, enc_ref.shape[0] // MB
    width = q_out.shape[1]
    shard, ff_cols = ff_in.shape
    tile = 256

    barrier = pltpu.get_barrier_semaphore()
    for peer in (x_peer, y_peer, core_peer):
        pl.semaphore_signal(barrier, inc=1, device_id=peer, device_id_type=MESH)

    @pl.when(t > 0)
    def _():
        pl.semaphore_signal(barrier, inc=1, device_id=left, device_id_type=MESH)

    @pl.when(t < count - 1)
    def _():
        pl.semaphore_signal(barrier, inc=1, device_id=right, device_id_type=MESH)

    at_end = (t == 0) | (t == count - 1)
    pl.semaphore_wait(barrier, jnp.where(at_end, 4, 5).astype(jnp.int32))

    def block(df, dc):
        slot = (f ^ df) * 2 + (c ^ dc)
        return pl.ds(pl.multiple_of(slot * shard, shard), shard)

    def spread(j, own, place):
        return Spread(
            x_peer, y_peer, core_peer, own, place, spread_send.at[j], spread_recv.at[j]
        )

    def line(j, own, place):
        sems = (line_right.at[j], line_left.at[j], line_recv.at[j])
        return Line(t, count, left, right, own, place, sems)

    def part(i):
        return pl.ds(i * rows, rows)

    heads = spread(0, heads_in, lambda df, dc: heads_all.at[block(df, dc)])
    op_line = line(0, op_in, lambda origin: zop.at[:, origin])
    op = spread(1, zop, lambda df, dc: op_all.at[:, :, block(df, dc)])

    def ff_place(origin):
        return zff.at[:, pl.ds(pl.multiple_of(origin * ff_cols, 128), ff_cols)]

    ff_line = line(1, ff_in, ff_place)
    ff = spread(2, zff, lambda df, dc: ff_all.at[block(df, dc)])
    ff_own = pltpu.make_async_copy(zff, ff_all.at[block(0, 0)], local_sem)
    self_lines = [
        line(2 + i, att.at[part(i)], lambda origin, i=i: held_s.at[origin, part(i)])
        for i in range(MB)
    ]
    cross_lines = [
        line(4 + i, crs.at[part(i)], lambda origin, i=i: held_c.at[origin, part(i)])
        for i in range(MB)
    ]

    def ctx_copy(j, ref, i, size):
        return remote(
            ref.at[i, pl.ds(0, size)],
            ref.at[i, pl.ds(size, size)],
            ctx_send.at[j],
            ctx_recv.at[j],
            x_peer,
        )

    ctx_self = [ctx_copy(i, kvs, i, rows) for i in range(MB)]
    ctx_cross = [ctx_copy(2 + i, kvc, i, enc_rows) for i in range(MB)]

    def project_tokens(i):
        @pl.loop(0, rows // tile)
        def _(n):
            at = pl.ds(pl.multiple_of(i * rows + n * tile, tile), tile)
            value = tok_ref[at].astype(F32)
            hidden = (value * rms_scale(value) * gains_out[0:1]).astype(BF16)
            q_out[at] = mat(hidden, heads_all[:, 4 * width : 5 * width]).astype(BF16)
            inner = pl.ds(pl.multiple_of(n * tile, tile), tile)
            kvs[i, inner] = mat(hidden, heads_all[:, : 2 * width]).astype(BF16)

    def project_encoder(i):
        @pl.loop(0, enc_rows // tile)
        def _(n):
            at = pl.ds(pl.multiple_of(i * enc_rows + n * tile, tile), tile)
            inner = pl.ds(pl.multiple_of(n * tile, tile), tile)
            kvc[i, inner] = mat(enc_ref[at], heads_all[:, 2 * width : 4 * width]).astype(BF16)

    def self_head(i, h):
        attend_head(h, i, tile, q_out, kvs, bias, att, tots)

    def cross_head(i, h):
        attend_head(h, i, tile, cq, kvc, None, crs, totc)

    def out_self(i):
        @pl.loop(0, rows // tile)
        def _(n):
            at = pl.ds(pl.multiple_of(i * rows + n * tile, tile), tile)
            total = tok_ref[at].astype(F32)
            for origin in range(count):
                total = total + mat_nt(held_s[origin, at], op_all[0, origin])
            as_out[at] = total
            hidden = (total * rms_scale(total) * gains_out[1:2]).astype(BF16)
            cq[at] = mat(hidden, heads_all[:, Q2 : Q2 + width]).astype(BF16)

    def out_cross(i):
        @pl.loop(0, rows // tile)
        def _(n):
            at = pl.ds(pl.multiple_of(i * rows + n * tile, tile), tile)
            total = as_out[at]
            for origin in range(count):
                total = total + mat_nt(held_c[origin, at], op_all[1, origin])
            ac_out[at] = total

    heads.step(0)
    op_line.start()
    heads_all[block(0, 0)] = heads_in[...]
    zop[:, t] = op_in[...]
    zff[:, pl.ds(pl.multiple_of(t * ff_cols, 128), ff_cols)] = ff_in[...]
    build_bias(parents_ref, bias, c)
    op_line.hop(1)
    heads.step(1)
    op_line.hop(2)
    ff_line.start()
    heads.step(2)
    op_line.hop(3)
    op.step(0)
    op_all[:, :, block(0, 0)] = zop[...]
    heads.step(3)
    heads.step(4)
    gains_out[...] = heads_all[:, Q2 - 128 : Q2].astype(F32).T[64:72]
    project_tokens(0)
    ctx_self[0].start()
    project_tokens(1)
    ctx_self[1].start()
    op.step(1)
    ff_line.hop(1)
    project_encoder(0)
    ctx_cross[0].start()
    project_encoder(1)
    ctx_cross[1].start()
    op.step(2)
    ctx_self[0].wait_recv()
    self_head(0, 0)
    ff_line.hop(2)
    self_head(0, 1)
    op.step(3)
    self_head(0, 2)
    held_s[t, part(0)] = att[part(0)]
    self_lines[0].start()
    ff_line.hop(3)
    ff_own.start()
    ctx_self[1].wait_recv()
    self_head(1, 0)
    self_lines[0].hop(1)
    self_head(1, 1)
    op.step(4)
    self_head(1, 2)
    held_s[t, part(1)] = att[part(1)]
    self_lines[1].start()
    self_lines[0].hop(2)
    ff.step(0)
    self_lines[0].hop(3)
    out_self(0)
    self_lines[1].hop(1)
    ctx_cross[0].wait_recv()
    cross_head(0, 0)
    self_lines[1].hop(2)
    ff.step(1)
    cross_head(0, 1)
    self_lines[1].hop(3)
    cross_head(0, 2)
    held_c[t, part(0)] = crs[part(0)]
    cross_lines[0].start()
    out_self(1)
    ctx_cross[1].wait_recv()
    ff.step(2)
    cross_head(1, 0)
    cross_lines[0].hop(1)
    cross_head(1, 1)
    cross_lines[0].hop(2)
    cross_head(1, 2)
    held_c[t, part(1)] = crs[part(1)]
    cross_lines[1].start()
    cross_lines[0].hop(3)
    out_cross(0)
    cross_lines[1].hop(1)
    ff.step(3)
    cross_lines[1].hop(2)
    cross_lines[1].hop(3)
    out_cross(1)
    ff.step(4)
    heads.step(5)
    op.step(5)
    ff.step(5)
    for one in [op_line, ff_line] + self_lines + cross_lines:
        one.finish()
    for copy in ctx_self + ctx_cross:
        copy.wait_send()
    ff_own.wait()


def layer_forward(parents, tokens, encoder, heads_in, op_in, ff_in, collective_id):
    count = lax.axis_size("tp")
    tok_rows, features = tokens.shape
    enc_rows = encoder.shape[0]
    shard, ff_cols = ff_in.shape
    width = op_in.shape[2]
    nh = width // HD
    rows = tok_rows // MB
    vmem = pl.BlockSpec(memory_space=pltpu.VMEM)

    def low(*shape):
        return jax.ShapeDtypeStruct(shape, BF16)

    def full(*shape):
        return jax.ShapeDtypeStruct(shape, F32)

    return pl.pallas_call(
        functools.partial(layer_forward_kernel, count),
        in_specs=[pl.BlockSpec(memory_space=pltpu.SMEM)] + [vmem] * 5,
        out_specs=[vmem, vmem, pl.BlockSpec(memory_space=pl.ANY)] + [vmem] * 12,
        out_shape=[
            low(features, heads_in.shape[1]),
            low(3, count, features, width),
            low(features, count * ff_cols),
            full(8, features),
            low(MB, 2 * rows, rows),
            low(tok_rows, width),
            low(MB, 2 * rows, 2 * width),
            low(MB, enc_rows, 2 * width),
            low(tok_rows, width),
            full(MB, nh, rows),
            low(tok_rows, width),
            low(tok_rows, width),
            full(MB, nh, rows),
            full(tok_rows, features),
            full(tok_rows, features),
        ],
        scratch_shapes=[
            pltpu.VMEM((3, count, shard, width), BF16),
            pltpu.VMEM((shard, count * ff_cols), BF16),
            pltpu.VMEM((count, tok_rows, width), BF16),
            pltpu.VMEM((count, tok_rows, width), BF16),
            pltpu.SemaphoreType.DMA((3, 7)),
            pltpu.SemaphoreType.DMA((3, 7)),
            pltpu.SemaphoreType.DMA((6, count)),
            pltpu.SemaphoreType.DMA((6, count)),
            pltpu.SemaphoreType.DMA((6, count)),
            pltpu.SemaphoreType.DMA((4,)),
            pltpu.SemaphoreType.DMA((4,)),
            pltpu.SemaphoreType.DMA,
        ],
        compiler_params=pltpu.CompilerParams(
            collective_id=collective_id, has_side_effects=True, vmem_limit_bytes=VMEM_MOST
        ),
        name="layer_forward",
    )(parents, tokens, encoder, heads_in, op_in, ff_in)


def ff_forward_kernel(
    shrink, ac_ref, gains_ref, w_ref, gate_ref, up_ref, mixed_ref, low_ref, exit_ref, exit_t_ref, h_acc
):
    step = pl.program_id(0)
    rows = ac_ref.shape[0]
    units = gate_ref.shape[1]
    tile = min(rows, 256)

    @pl.loop(0, rows // tile)
    def _(n):
        at = pl.ds(pl.multiple_of(n * tile, tile), tile)

        @pl.when(step == 0)
        def _():
            value = ac_ref[at]
            h_acc[at] = (value * rms_scale(value) * gains_ref[2:3]).astype(BF16)
            mixed_ref[at] = value

        hidden = h_acc[at]
        gate = mat(hidden, w_ref[:, :units])
        up = mat(hidden, w_ref[:, units : 2 * units])
        gate_ref[at] = gate
        up_ref[at] = up
        activated = (gelu_parts(gate)[0] * up).astype(BF16)
        mixed_ref[at] += mat_nt(activated, w_ref[:, 2 * units :])

        @pl.when(step == pl.num_programs(0) - 1)
        def _():
            value = mixed_ref[at]
            low_ref[at] = value.astype(BF16)
            exit_in = value * rms_scale(value) * gains_ref[3:4] * shrink
            exit_ref[at] = exit_in.astype(BF16)

    @pl.when(step == pl.num_programs(0) - 1)
    def _():
        exit_t_ref[...] = exit_ref[...].T


def ff_forward(after_cross, gains, ff_all, count, shrink):
    rows, features = after_cross.shape
    cols = ff_all.shape[1] // count
    units = cols // 3

    def fixed(*shape):
        return pl.BlockSpec(shape, lambda i: (0,) * len(shape))

    moving = pl.BlockSpec((rows, units), lambda i: (0, i))
    return pl.pallas_call(
        functools.partial(ff_forward_kernel, shrink),
        grid=(count,),
        in_specs=[
            fixed(rows, features),
            fixed(8, features),
            pl.BlockSpec((features, cols), lambda i: (0, i)),
        ],
        out_specs=[moving, moving] + [fixed(rows, features)] * 3 + [fixed(features, rows)],
        out_shape=[
            jax.ShapeDtypeStruct((rows, count * units), F32),
            jax.ShapeDtypeStruct((rows, count * units), F32),
            jax.ShapeDtypeStruct((rows, features), F32),
            jax.ShapeDtypeStruct((rows, features), BF16),
            jax.ShapeDtypeStruct((rows, features), BF16),
            jax.ShapeDtypeStruct((features, rows), BF16),
        ],
        scratch_shapes=[pltpu.VMEM((rows, features), BF16)],
        compiler_params=pltpu.CompilerParams(vmem_limit_bytes=VMEM_MOST),
        cost_estimate=pl.CostEstimate(
            flops=2 * rows * features * count * cols,
            bytes_accessed=2 * features * count * cols + 8 * rows * count * units,
            transcendentals=rows * count * units,
        ),
        name="ff_forward",
    )(after_cross, gains, ff_all)


def ff_backward_kernel(
    shrink,
    ge_ref,
    mixed_ref,
    cot_ref,
    ac_ref,
    gains_ref,
    co_ref,
    w_ref,
    gate_ref,
    up_ref,
    gac_ref,
    low_ref,
    gcl_ref,
    gcr_ref,
    hid_ref,
    act_ref,
    gg_ref,
    gu_ref,
    norms_ref,
    acc,
):
    step = pl.program_id(0)
    t = lax.axis_index("tp")
    last = pl.num_programs(0) - 1
    rows = ac_ref.shape[0]
    units = gate_ref.shape[1]
    tile = min(rows, 256)

    @pl.when(step == 0)
    def _():
        norms_ref[...] = jnp.zeros_like(norms_ref)

    @pl.loop(0, rows // tile)
    def _(n):
        at = pl.ds(pl.multiple_of(n * tile, tile), tile)

        @pl.when(step == 0)
        def _():
            grad_exit = ge_ref[at].astype(F32) * shrink
            mixed = mixed_ref[at]
            scale = rms_scale(mixed)
            normed = mixed * scale
            norms_ref[0:1] += jnp.sum(grad_exit * normed, axis=0, keepdims=True)
            grad_mixed = cot_ref[at].astype(F32) + rms_back(
                grad_exit * gains_ref[3:4], normed, scale
            )
            gac_ref[at] = grad_mixed
            low_ref[at] = grad_mixed.astype(BF16)
            value = ac_ref[at]
            hid_ref[at] = (value * rms_scale(value) * gains_ref[2:3]).astype(BF16)
            acc[at] = jnp.zeros_like(acc[at])

        gate = gate_ref[at]
        up = up_ref[at]
        grad_act = mat(low_ref[at], w_ref[:, 2 * units :])
        value, slope = gelu_parts(gate)
        grad_gate = (grad_act * slope * up).astype(BF16)
        grad_up = (grad_act * value).astype(BF16)
        acc[at] += mat_nt(grad_gate, w_ref[:, :units]) + mat_nt(
            grad_up, w_ref[:, units : 2 * units]
        )

        @pl.when(step == t)
        def _():
            act_ref[at] = (value * up).astype(BF16)
            gg_ref[at] = grad_gate
            gu_ref[at] = grad_up

        @pl.when(step == last)
        def _():
            value = ac_ref[at]
            scale = rms_scale(value)
            normed = value * scale
            grad = acc[at]
            norms_ref[1:2] += jnp.sum(grad * normed, axis=0, keepdims=True)
            total = gac_ref[at] + rms_back(grad * gains_ref[2:3], normed, scale)
            gac_ref[at] = total
            gcl_ref[at] = total.astype(BF16)
            gcr_ref[at] = mat(total.astype(BF16), co_ref[...]).astype(BF16)


def ff_backward(
    grad_exit, mixed, cotangent, after_cross, gains, c_out_own, ff_all, gate, up, count, shrink
):
    rows, features = after_cross.shape
    cols = ff_all.shape[1] // count
    units = cols // 3
    width = c_out_own.shape[1]

    def fixed(*shape):
        return pl.BlockSpec(shape, lambda i: (0,) * len(shape))

    def low(*shape):
        return jax.ShapeDtypeStruct(shape, BF16)

    moving = pl.BlockSpec((rows, units), lambda i: (0, i))
    return pl.pallas_call(
        functools.partial(ff_backward_kernel, shrink),
        grid=(count,),
        in_specs=[fixed(rows, features)] * 4
        + [
            fixed(8, features),
            fixed(features, width),
            pl.BlockSpec((features, cols), lambda i: (0, i)),
            moving,
            moving,
        ],
        out_specs=[fixed(rows, features)] * 3
        + [fixed(rows, width), fixed(rows, features)]
        + [fixed(rows, units)] * 3
        + [fixed(8, features)],
        out_shape=[
            jax.ShapeDtypeStruct((rows, features), F32),
            low(rows, features),
            low(rows, features),
            low(rows, width),
            low(rows, features),
            low(rows, units),
            low(rows, units),
            low(rows, units),
            jax.ShapeDtypeStruct((8, features), F32),
        ],
        scratch_shapes=[pltpu.VMEM((rows, features), F32)],
        compiler_params=pltpu.CompilerParams(vmem_limit_bytes=VMEM_MOST),
        cost_estimate=pl.CostEstimate(
            flops=2 * rows * features * count * cols,
            bytes_accessed=2 * features * count * cols + 8 * rows * count * units,
            transcendentals=rows * count * units,
        ),
        name="ff_backward",
    )(grad_exit, mixed, cotangent, after_cross, gains, c_out_own, ff_all, gate, up)


def layer_forward_plain(parents, tokens, encoder, heads_in, op_in, ff_in, collective_id):
    rows = tokens.shape[0] // MB
    enc_rows = encoder.shape[0] // MB
    width = op_in.shape[2]
    heads_all = lax.all_gather(heads_in, PLANE, axis=0, tiled=True)
    op_all = lax.all_gather(
        lax.all_gather(op_in, "tp", axis=1, tiled=False), PLANE, axis=2, tiled=True
    )
    ff_all = lax.all_gather(
        lax.all_gather(ff_in, "tp", axis=1, tiled=True), PLANE, axis=0, tiled=True
    )
    gains = heads_all[:, Q2 - 64 : Q2 - 56].astype(F32).T
    tok = tokens.astype(F32)
    hidden_one = (tok * rms_scale(tok) * gains[0:1]).astype(BF16)
    queries = mat(hidden_one, heads_all[:, 4 * width : 5 * width]).astype(BF16)
    kv = mat(hidden_one, heads_all[:, : 2 * width]).astype(BF16)
    enc_kv = mat(encoder, heads_all[:, 2 * width : 4 * width]).astype(BF16)

    def both_sides(value, i, count):
        return ctx_gather(value[i * count : (i + 1) * count])

    kv_self = jnp.stack([both_sides(kv, i, rows) for i in range(MB)])
    kv_cross = jnp.stack([both_sides(enc_kv, i, enc_rows) for i in range(MB)])
    bias = jnp.stack([mask_bias(parents[i], rows) for i in range(MB)]).astype(BF16)

    def attention(values, keys_values, masks):
        outcome = [
            attend(
                values[i * rows : (i + 1) * rows],
                keys_values[i],
                None if masks is None else masks[i],
            )
            for i in range(MB)
        ]
        return jnp.concatenate([o[0] for o in outcome]), jnp.stack([o[1] for o in outcome])

    attended, totals_self = attention(queries, kv_self, bias)
    after_self = line_project(attended, op_all[0], tok, 2)
    hidden_two = (after_self * rms_scale(after_self) * gains[1:2]).astype(BF16)
    cross_q = mat(hidden_two, heads_all[:, Q2 : Q2 + width]).astype(BF16)
    crossed, totals_cross = attention(cross_q, kv_cross, None)
    after_cross = line_project(crossed, op_all[1], after_self, 3)
    return (
        heads_all,
        op_all,
        ff_all,
        gains,
        bias,
        queries,
        kv_self,
        kv_cross,
        attended,
        totals_self,
        cross_q,
        crossed,
        totals_cross,
        after_self,
        after_cross,
    )


class LineSum:
    def __init__(self, t, count, left, right, x, out, buffers, sems, chunks):
        self.t, self.count, self.left, self.right = t, count, left, right
        self.x, self.out, self.chunks = x, out, chunks
        self.low_in, self.high_in = buffers.at[0], buffers.at[1]
        self.sems = sems
        self.half = x.shape[0] // 2
        self.rows = self.half // chunks

    def low(self, j):
        return pl.ds(j * self.rows, self.rows)

    def high(self, j):
        return pl.ds(self.half + j * self.rows, self.rows)

    def down(self, j, own):
        src = self.x.at[self.low(j)] if own else self.low_in.at[self.low(j)]
        dst = self.low_in.at[self.low(j)]
        return remote(src, dst, self.sems.at[0, j], self.sems.at[1, j], self.left)

    def up(self, j, own):
        src = self.x.at[self.high(j)] if own else self.high_in.at[self.low(j)]
        dst = self.high_in.at[self.low(j)]
        return remote(src, dst, self.sems.at[2, j], self.sems.at[3, j], self.right)

    def low_back(self, j):
        ref = self.out.at[self.low(j)]
        return remote(ref, ref, self.sems.at[4, j], self.sems.at[5, j], self.right)

    def high_back(self, j):
        ref = self.out.at[self.high(j)]
        return remote(ref, ref, self.sems.at[6, j], self.sems.at[7, j], self.left)

    def start(self):
        @pl.when(self.t == self.count - 1)
        def _():
            for j in range(self.chunks):
                self.down(j, True).start()

        @pl.when(self.t == 0)
        def _():
            for j in range(self.chunks):
                self.up(j, True).start()

    def low_step(self, j):
        if not 0 <= j < self.chunks:
            return

        @pl.when(self.t < self.count - 1)
        def _():
            self.down(j, False).wait_recv()
            at = self.low(j)
            total = (self.low_in[at].astype(F32) + self.x[at].astype(F32)).astype(BF16)

            @pl.when(self.t > 0)
            def _():
                self.low_in[at] = total
                self.down(j, False).start()

            @pl.when(self.t == 0)
            def _():
                self.out[at] = total
                self.low_back(j).start()

    def high_step(self, j):
        if not 0 <= j < self.chunks:
            return

        @pl.when(self.t > 0)
        def _():
            self.up(j, False).wait_recv()
            at = self.high(j)
            total = (self.high_in[self.low(j)].astype(F32) + self.x[at].astype(F32)).astype(BF16)

            @pl.when(self.t < self.count - 1)
            def _():
                self.high_in[self.low(j)] = total
                self.up(j, False).start()

            @pl.when(self.t == self.count - 1)
            def _():
                self.out[at] = total
                self.high_back(j).start()

    def low_forward(self, j):
        @pl.when(self.t > 0)
        def _():
            self.low_back(j).wait_recv()

            @pl.when(self.t < self.count - 1)
            def _():
                self.low_back(j).start()

    def high_forward(self, j):
        @pl.when(self.t < self.count - 1)
        def _():
            self.high_back(j).wait_recv()

            @pl.when(self.t > 0)
            def _():
                self.high_back(j).start()

    def reduce(self, j):
        @pl.when(self.t < self.count // 2)
        def _():
            self.high_step(j)
            self.low_step(j - 1)

        @pl.when(self.t >= self.count // 2)
        def _():
            self.low_step(j)
            self.high_step(j - 1)

    def back(self, j):
        @pl.when(self.t < self.count // 2)
        def _():
            self.low_forward(j)
            self.high_forward(j)

        @pl.when(self.t >= self.count // 2)
        def _():
            self.high_forward(j)
            self.low_forward(j)

    def finish(self):
        last = self.count - 1
        for j in range(self.chunks):

            @pl.when(self.t > 0)
            def _():
                self.down(j, False).wait_send()
                self.high_back(j).wait_send()

            @pl.when(self.t < last)
            def _():
                self.up(j, False).wait_send()
                self.low_back(j).wait_send()


def attend_back_head(
    h, i, tile, q_ref, kv_ref, bias_ref, total_ref, go_ref, dq_ref, dkv_ref, acc_ref
):
    rows, width = q_ref.shape[0] // MB, q_ref.shape[1]
    keys_count = kv_ref.shape[1]
    cols = slice(h * HD, (h + 1) * HD)
    vcols = slice(width + h * HD, width + (h + 1) * HD)
    acc_ref[:keys_count] = jnp.zeros((keys_count, 2 * HD), F32)

    @pl.loop(0, rows // tile)
    def _(n):
        at = pl.ds(pl.multiple_of(i * rows + n * tile, tile), tile)
        here_at = pl.ds(pl.multiple_of(n * tile, tile), tile)
        keys, values = kv_ref[i, :, cols], kv_ref[i, :, vcols]
        queries, go = q_ref[at, cols], go_ref[at, cols]
        scores = mat_nt(keys, queries)
        if bias_ref is not None:
            scores = scores + bias_ref[i, :, here_at]
        probs = jnp.exp(scores - total_ref[i, h : h + 1, here_at])
        grad_probs = mat_nt(values, go)
        inner = jnp.sum(probs * grad_probs, axis=0, keepdims=True)
        grad_scores = (probs * (grad_probs - inner)).astype(BF16)
        acc_ref[:keys_count, :HD] += mat(grad_scores, queries)
        acc_ref[:keys_count, HD:] += mat(probs.astype(BF16), go)
        dq_ref[at, cols] = mat_tn(keys, grad_scores).T.astype(BF16)

    dkv_ref[i, :, cols] = acc_ref[:keys_count, :HD].astype(BF16)
    dkv_ref[i, :, vcols] = acc_ref[:keys_count, HD:].astype(BF16)


def layer_backward_kernel(
    count,
    gcr_ref,
    cq_ref,
    kvc_ref,
    totc_ref,
    q_ref,
    kvs_ref,
    bias_ref,
    tots_ref,
    gac_ref,
    as_ref,
    tok_ref,
    wo_ref,
    cq4_ref,
    heads_ref,
    gains_ref,
    gt_out,
    enc_sum,
    gcq,
    gkvc,
    gq,
    gkvs,
    gsl,
    norms,
    dkvc,
    dkvc_in,
    dkvs,
    dkvs_in,
    acc,
    held,
    gatt,
    enc_part,
    one_part,
    one_sum,
    enc_buffers,
    one_buffers,
    line_right,
    line_left,
    line_recv,
    ctx_send,
    ctx_recv,
    sum_sems,
):
    f, c, t = here()
    right, left = (f, c, t + 1), (f, c, t - 1)
    x_peer = (f, 1 - c, t)
    rows, enc_rows = tok_ref.shape[0] // MB, gkvc.shape[0] // MB
    width = q_ref.shape[1]
    tile = 256

    barrier = pltpu.get_barrier_semaphore()
    pl.semaphore_signal(barrier, inc=1, device_id=x_peer, device_id_type=MESH)

    @pl.when(t > 0)
    def _():
        pl.semaphore_signal(barrier, inc=1, device_id=left, device_id_type=MESH)

    @pl.when(t < count - 1)
    def _():
        pl.semaphore_signal(barrier, inc=1, device_id=right, device_id_type=MESH)

    at_end = (t == 0) | (t == count - 1)
    pl.semaphore_wait(barrier, jnp.where(at_end, 2, 3).astype(jnp.int32))

    def part(i):
        return pl.ds(i * rows, rows)

    def enc_at(i):
        return pl.ds(i * enc_rows, enc_rows)

    def line(j, own, place):
        sems = (line_right.at[j], line_left.at[j], line_recv.at[j])
        return Line(t, count, left, right, own, place, sems)

    query_lines = [
        line(i, gcq.at[part(i)], lambda origin, i=i: held.at[origin, part(i)]) for i in range(MB)
    ]

    def ctx_copy(j, ref, landing, i, size):
        return remote(
            ref.at[i, pl.ds(size, size)], landing.at[i], ctx_send.at[j], ctx_recv.at[j], x_peer
        )

    ctx_cross = [ctx_copy(i, dkvc, dkvc_in, i, enc_rows) for i in range(MB)]
    ctx_self = [ctx_copy(MB + i, dkvs, dkvs_in, i, rows) for i in range(MB)]

    def summed(j, x, out, buffers, chunks):
        return LineSum(t, count, left, right, x, out, buffers, sum_sems.at[j], chunks)

    enc_chunks = enc_rows // 256
    one_chunks = rows // 256
    enc_sums = [
        summed(i, enc_part.at[enc_at(i)], enc_sum.at[enc_at(i)], enc_buffers.at[i], enc_chunks)
        for i in range(MB)
    ]
    one_sums = [
        summed(MB + i, one_part.at[part(i)], one_sum.at[part(i)], one_buffers.at[i], one_chunks)
        for i in range(MB)
    ]

    def tiles(i, count_rows, body):
        @pl.loop(0, count_rows // tile)
        def _(n):
            at = pl.ds(pl.multiple_of(i * count_rows + n * tile, tile), tile)
            body(at, pl.ds(pl.multiple_of(n * tile, tile), tile))

    def cross_head(i, h):
        attend_back_head(h, i, tile, cq_ref, kvc_ref, None, totc_ref, gcr_ref, gcq, dkvc, acc)

    def self_head(i, h):
        attend_back_head(h, i, tile, q_ref, kvs_ref, bias_ref, tots_ref, gatt, gq, dkvs, acc)

    def send_queries(i):
        held[t, part(i)] = gcq[part(i)]
        query_lines[i].start()

    def encoder_part(i):
        ctx_cross[i].wait_recv()

        def body(at, inner):
            total = dkvc[i, inner].astype(F32) + dkvc_in[i, inner].astype(F32)
            gkvc[at] = total.astype(BF16)
            enc_part[at] = mat_nt(
                total.astype(BF16), heads_ref[:, 2 * width : 4 * width]
            ).astype(BF16)

        tiles(i, enc_rows, body)
        enc_sums[i].start()

    def after_queries(i):
        def body(at, inner):
            grad = mat_nt(held[0, at], cq4_ref[0])
            for origin in range(1, count):
                grad = grad + mat_nt(held[origin, at], cq4_ref[origin])
            value = as_ref[at]
            scale = rms_scale(value)
            normed = value * scale
            norms[1:2] += jnp.sum(grad * normed, axis=0, keepdims=True)
            total = gac_ref[at] + rms_back(grad * gains_ref[1:2], normed, scale)
            gt_out[at] = total
            gsl[at] = total.astype(BF16)
            gatt[at] = mat(total.astype(BF16), wo_ref[...]).astype(BF16)

        tiles(i, rows, body)

    def token_part(i):
        ctx_self[i].wait_recv()

        def body(at, inner):
            total = (dkvs[i, inner].astype(F32) + dkvs_in[i, inner].astype(F32)).astype(BF16)
            gkvs[at] = total
            product = mat_nt(total, heads_ref[:, : 2 * width])
            product = product + mat_nt(gq[at], heads_ref[:, 4 * width : 5 * width])
            one_part[at] = product.astype(BF16)

        tiles(i, rows, body)
        one_sums[i].start()

    def finish_tokens(i):
        def body(at, inner):
            grad = one_sum[at].astype(F32)
            value = tok_ref[at].astype(F32)
            scale = rms_scale(value)
            normed = value * scale
            norms[0:1] += jnp.sum(grad * normed, axis=0, keepdims=True)
            gt_out[at] = gt_out[at] + rms_back(grad * gains_ref[0:1], normed, scale)

        tiles(i, rows, body)

    norms[...] = jnp.zeros_like(norms)
    for h in range(width // HD):
        cross_head(0, h)
    send_queries(0)
    ctx_cross[0].start()
    cross_head(1, 0)
    query_lines[0].hop(1)
    cross_head(1, 1)
    query_lines[0].hop(2)
    cross_head(1, 2)
    send_queries(1)
    ctx_cross[1].start()
    query_lines[0].hop(3)
    after_queries(0)
    self_head(0, 0)
    query_lines[1].hop(1)
    self_head(0, 1)
    encoder_part(0)
    query_lines[1].hop(2)
    self_head(0, 2)
    ctx_self[0].start()
    enc_sums[0].reduce(0)
    query_lines[1].hop(3)
    after_queries(1)
    enc_sums[0].reduce(1)
    self_head(1, 0)
    enc_sums[0].reduce(2)
    self_head(1, 1)
    enc_sums[0].reduce(3)
    self_head(1, 2)
    ctx_self[1].start()
    token_part(0)
    encoder_part(1)
    enc_sums[0].reduce(4)
    one_sums[0].reduce(0)
    enc_sums[0].back(0)
    one_sums[0].reduce(1)
    enc_sums[1].reduce(0)
    token_part(1)
    one_sums[0].reduce(2)
    enc_sums[1].reduce(1)
    enc_sums[0].back(1)
    one_sums[1].reduce(0)
    enc_sums[1].reduce(2)
    one_sums[0].back(0)
    one_sums[1].reduce(1)
    enc_sums[0].back(2)
    enc_sums[1].reduce(3)
    one_sums[1].reduce(2)
    one_sums[0].back(1)
    enc_sums[1].reduce(4)
    enc_sums[0].back(3)
    finish_tokens(0)
    one_sums[1].back(0)
    enc_sums[1].back(0)
    one_sums[1].back(1)
    enc_sums[1].back(1)
    finish_tokens(1)
    enc_sums[1].back(2)
    enc_sums[1].back(3)
    for one in query_lines + enc_sums + one_sums:
        one.finish()
    for copy in ctx_self + ctx_cross:
        copy.wait_send()


def layer_backward(operands, tokens, enc_rows, collective_id):
    count = lax.axis_size("tp")
    tok_rows, features = tokens.shape
    rows = tok_rows // MB
    enc_tree = enc_rows // MB
    width = operands[0].shape[1]
    vmem = pl.BlockSpec(memory_space=pltpu.VMEM)
    outs = [
        ((tok_rows, features), F32),
        ((enc_rows, features), BF16),
        ((tok_rows, width), BF16),
        ((enc_rows, 2 * width), BF16),
        ((tok_rows, width), BF16),
        ((tok_rows, 2 * width), BF16),
        ((tok_rows, features), BF16),
        ((8, features), F32),
    ]
    scratch = [
        ((MB, 2 * enc_tree, 2 * width), BF16),
        ((MB, enc_tree, 2 * width), BF16),
        ((MB, 2 * rows, 2 * width), BF16),
        ((MB, rows, 2 * width), BF16),
        ((2 * enc_tree, 2 * HD), F32),
        ((count, tok_rows, width), BF16),
        ((tok_rows, width), BF16),
        ((enc_rows, features), BF16),
        ((tok_rows, features), BF16),
        ((tok_rows, features), BF16),
        ((MB, 2, enc_tree // 2, features), BF16),
        ((MB, 2, rows // 2, features), BF16),
    ]
    return pl.pallas_call(
        functools.partial(layer_backward_kernel, count),
        in_specs=[vmem] * 15,
        out_specs=[vmem] * len(outs),
        out_shape=[jax.ShapeDtypeStruct(shape, kind) for shape, kind in outs],
        scratch_shapes=[pltpu.VMEM(shape, kind) for shape, kind in scratch]
        + [
            pltpu.SemaphoreType.DMA((MB, count)),
            pltpu.SemaphoreType.DMA((MB, count)),
            pltpu.SemaphoreType.DMA((MB, count)),
            pltpu.SemaphoreType.DMA((2 * MB,)),
            pltpu.SemaphoreType.DMA((2 * MB,)),
            pltpu.SemaphoreType.DMA((2 * MB, 8, 4)),
        ],
        compiler_params=pltpu.CompilerParams(
            collective_id=collective_id, has_side_effects=True, vmem_limit_bytes=VMEM_MOST
        ),
        name="layer_backward",
    )(*operands)


def layer_backward_plain(operands, tokens, enc_rows, collective_id):
    (
        grad_crossed,
        cross_q,
        kv_cross,
        totals_cross,
        queries,
        kv_self,
        bias,
        totals_self,
        grad_after_cross,
        after_self,
        tokens,
        w_out_own,
        c_query_all,
        heads_all,
        gains,
    ) = operands
    rows, width = queries.shape[0] // MB, queries.shape[1]
    trees = range(MB)

    def tree_rows(value, i):
        return value[i * rows : (i + 1) * rows]

    outcome = [
        attend_back(
            tree_rows(cross_q, i), kv_cross[i], None, totals_cross[i], tree_rows(grad_crossed, i)
        )
        for i in trees
    ]
    grad_cq = jnp.concatenate([o[0] for o in outcome], axis=0)
    grad_kv_cross = jnp.concatenate([ctx_scatter(o[1]) for o in outcome], axis=0)
    encoder_part = mat_nt(grad_kv_cross, heads_all[:, 2 * width : 4 * width]).astype(BF16)
    grad_two = line_project(grad_cq, c_query_all, jnp.zeros_like(after_self), 6)
    scale_two = rms_scale(after_self)
    normed_two = after_self * scale_two
    norm_cross = jnp.sum(grad_two * normed_two, axis=0)
    grad_after_self = grad_after_cross + rms_back(grad_two * gains[1:2], normed_two, scale_two)
    grad_self_low = grad_after_self.astype(BF16)
    grad_attended = mat(grad_self_low, w_out_own).astype(BF16)
    outcome = [
        attend_back(
            tree_rows(queries, i), kv_self[i], bias[i], totals_self[i], tree_rows(grad_attended, i)
        )
        for i in trees
    ]
    grad_q = jnp.concatenate([o[0] for o in outcome], axis=0)
    grad_kv_self = jnp.concatenate([ctx_scatter(o[1]) for o in outcome], axis=0)
    part = mat_nt(grad_q, heads_all[:, 4 * width : 5 * width])
    part = (part + mat_nt(grad_kv_self, heads_all[:, : 2 * width])).astype(BF16)
    both = line_sum(jnp.concatenate([part, encoder_part], axis=0), 7, 12)
    grad_one = both[: MB * rows].astype(F32)
    tok = tokens.astype(F32)
    scale_one = rms_scale(tok)
    normed_one = tok * scale_one
    norm_self = jnp.sum(grad_one * normed_one, axis=0)
    grad_tokens = grad_after_self + rms_back(grad_one * gains[0:1], normed_one, scale_one)
    norms = jnp.stack([norm_self, norm_cross] + [jnp.zeros_like(norm_self)] * 6)
    return (
        grad_tokens,
        both[MB * rows :],
        grad_cq,
        grad_kv_cross,
        grad_q,
        grad_kv_self,
        grad_self_low,
        norms,
    )


def local(
    tokens,
    encoder,
    cotangent,
    parents,
    targets,
    w_query,
    w_key,
    w_value,
    w_out,
    c_query,
    c_key,
    c_value,
    c_out,
    w_gate,
    w_up,
    w_down,
    embedding,
    norm_self,
    norm_cross,
    norm_ff,
    norm_exit,
):
    t = lax.axis_index("tp")
    tp_count = lax.axis_size("tp")
    rows = tokens.shape[0] // MB
    features = tokens.shape[1]
    width = w_query.shape[1]
    hidden_units = w_gate.shape[1]
    vocab = embedding.shape[0]
    trees = range(MB)
    shrink = 1.0 / math.sqrt(features)

    def tree_rows(value, i):
        count = value.shape[0] // MB
        return value[i * count : (i + 1) * count]

    gains_in = jnp.stack([norm_self, norm_cross, norm_ff, norm_exit], axis=1)
    heads_in = jnp.concatenate(
        [w_key, w_value, c_key, c_value, w_query]
        + [jnp.pad(gains_in, ((0, 0), (0, 60))), c_query, jnp.zeros_like(c_query[:, :64])],
        axis=1,
    )
    op_in = jnp.stack([w_out.T, c_out.T, c_query])
    ff_in = jnp.concatenate([w_gate, w_up, w_down.T], axis=1)
    padded = -(-vocab // TILE) * TILE
    embed_in = jnp.pad(embedding.T, ((0, 0), (0, padded - vocab)))
    embed_t = lax.all_gather(embed_in, PLANE, axis=0, tiled=True)
    forward = layer_forward if small_plane() else layer_forward_plain
    (
        heads_all,
        op_all,
        ff_all,
        gains,
        bias,
        queries,
        kv_self,
        kv_cross,
        attended,
        totals_self,
        cross_q,
        crossed,
        totals_cross,
        after_self,
        after_cross,
    ) = forward(parents, after(tokens, embed_in), encoder, heads_in, op_in, ff_in, 1)
    gain_self, gain_cross = gains[0:1], gains[1:2]
    own_out = lax.dynamic_index_in_dim(op_all[:2], t, 1, False)
    w_out_own, c_out_own = own_out[0], own_out[1]
    gate_pre, up_pre, mixed, mixed_low, exit_in, exit_in_t = ff_forward(
        after_cross, gains, ff_all, tp_count, shrink
    )

    targets_local = targets - t * vocab
    inside = (targets_local >= 0) & (targets_local < vocab)
    targets_local = jnp.where(inside, targets_local, -1)[:, None]
    logits, top, summed, picked = exit_forward(exit_in, embed_t, targets_local, vocab)
    stats = jnp.stack([top, summed, picked]).reshape(3, MB * rows // 128, 128)
    top, log_total, picked = share_stats(stats, 4)
    losses = (log_total - picked).reshape(-1)
    scores = (top - log_total).reshape(-1)
    grad_embed, grad_exit_part = exit_backward(
        logits, embed_t, exit_in_t, targets_local, log_total.reshape(-1, 1), vocab
    )
    grad_embed_own = lax.optimization_barrier(
        lax.psum_scatter(grad_embed, PLANE, scatter_dimension=0, tiled=True)
    )
    grad_exit = line_sum(grad_exit_part, 5)

    (
        grad_after_cross,
        grad_mixed_low,
        grad_cross_low,
        grad_crossed,
        hidden_three,
        activated_own,
        grad_gate_own,
        grad_up_own,
        norms,
    ) = ff_backward(
        grad_exit,
        mixed,
        cotangent,
        after_cross,
        gains,
        c_out_own,
        ff_all,
        gate_pre,
        up_pre,
        tp_count,
        shrink,
    )
    backward = layer_backward if small_plane() else layer_backward_plain
    (
        grad_tokens,
        grad_encoder,
        grad_cq,
        grad_kv_cross,
        grad_q,
        grad_kv_self,
        grad_self_low,
        norms_low,
    ) = backward(
        (
            grad_crossed,
            cross_q,
            kv_cross,
            totals_cross,
            queries,
            kv_self,
            bias,
            totals_self,
            grad_after_cross,
            after_self,
            tokens,
            w_out_own,
            op_all[2],
            heads_all,
            gains,
        ),
        tokens,
        encoder.shape[0],
        6,
    )
    tok = tokens.astype(F32)
    hidden_one = (tok * rms_scale(tok) * gain_self).astype(BF16)
    hidden_two = (after_self * rms_scale(after_self) * gain_cross).astype(BF16)

    ff_grads = jnp.concatenate(
        [
            mat_tn(hidden_three, grad_gate_own),
            mat_tn(hidden_three, grad_up_own),
            mat_tn(grad_mixed_low, activated_own),
            mat_tn(grad_cross_low, crossed),
        ],
        axis=1,
    ).astype(BF16)
    ff_own = lax.psum_scatter(ff_grads, PLANE, scatter_dimension=0, tiled=True)
    norm_block = jnp.pad(
        jnp.stack([norms_low[0], norms_low[1], norms[1], norms[0]], axis=1),
        ((0, 0), (0, 60)),
    )
    own = plane_scatter(
        jnp.concatenate(
            [
                mat_tn(hidden_one, grad_kv_self),
                mat_tn(encoder, grad_kv_cross),
                mat_tn(hidden_one, grad_q),
                norm_block,
                mat_tn(hidden_two, grad_cq),
                mat_tn(grad_self_low, attended),
            ],
            axis=1,
        ).astype(BF16),
        9,
    )

    def part(value, start, size):
        return value[:, start : start + size].astype(F32)

    base = Q2 - 64
    return (
        mixed_low,
        losses,
        scores,
        grad_tokens,
        grad_encoder.astype(F32),
        part(own, 4 * width, width),
        part(own, 0, width),
        part(own, width, width),
        part(own, Q2 + width, width).T,
        part(own, Q2, width),
        part(own, 2 * width, width),
        part(own, 3 * width, width),
        part(ff_own, 3 * hidden_units, width).T,
        part(ff_own, 0, hidden_units),
        part(ff_own, hidden_units, hidden_units),
        part(ff_own, 2 * hidden_units, hidden_units).T,
        grad_embed_own[:, :vocab].astype(F32).T,
        own[:, base],
        own[:, base + 1],
        own[:, base + 2],
        own[:, base + 3],
    )


def solution(mesh):
    rows_cols = P(PLANE, "tp")
    cols_rows = P("tp", PLANE)
    data = P(PLANE, None)
    flat = P(PLANE)
    weights = (rows_cols,) * 3 + (cols_rows,) + (rows_cols,) * 3 + (cols_rows,)
    weights += (rows_cols,) * 2 + (cols_rows,) * 2 + (flat,) * 4
    return jax.shard_map(
        local,
        mesh=mesh,
        in_specs=(data, data, data, P("fsdp", None), flat) + weights,
        out_specs=(data, flat, flat, data, data) + weights,
        check_vma=False,
    )
```

```python
import functools
import math

import jax
import jax.numpy as jnp
from jax import lax
from jax.experimental import pallas as pl
from jax.experimental.pallas import tpu as pltpu
from jax.sharding import PartitionSpec as P

HD = 64
BLK = 128
MB = 2
EPSILON = 1e-06
MASKED = -1000000000.0
F32 = jnp.float32
BF16 = jnp.bfloat16
PLANE = ("fsdp", "ctx")
VMEM_LIMIT = 48 * 1024 * 1024
MESH = pl.DeviceIdType.MESH
TILE = 1024
LOWEST = -3.0e38
VMEM_MOST = 58 * 1024 * 1024
Q2 = 1024
EXIT_PIECES = 2
EXIT_CHUNKS = 4
EXIT_STEPS = 24


def mat(left, right):
    return jnp.dot(left, right, preferred_element_type=F32)


def mat_nt(left, right):
    return lax.dot_general(left, right, (((1,), (1,)), ((), ())), preferred_element_type=F32)


def mat_tn(left, right):
    return lax.dot_general(left, right, (((0,), (0,)), ((), ())), preferred_element_type=F32)


def small_plane():
    return lax.axis_size("fsdp") == 4 and lax.axis_size("ctx") == 2


def swap(value, axis, bit):
    count = lax.axis_size(axis)
    return lax.ppermute(value, axis, [(i, i ^ bit) for i in range(count)])


def low_sum(left, right):
    return (left.astype(F32) + right.astype(F32)).astype(BF16)


def here():
    return lax.axis_index("fsdp"), lax.axis_index("ctx"), lax.axis_index("tp")


def greet(peers):
    barrier = pltpu.get_barrier_semaphore()
    for peer in peers:
        pl.semaphore_signal(barrier, inc=1, device_id=peer, device_id_type=MESH)
    pl.semaphore_wait(barrier, len(peers))


def greet_line(t, count, left, right):
    barrier = pltpu.get_barrier_semaphore()

    @pl.when(t > 0)
    def _():
        pl.semaphore_signal(barrier, inc=1, device_id=left, device_id_type=MESH)

    @pl.when(t < count - 1)
    def _():
        pl.semaphore_signal(barrier, inc=1, device_id=right, device_id_type=MESH)

    at_end = (t == 0) | (t == count - 1)
    pl.semaphore_wait(barrier, jnp.where(at_end, 1, 2).astype(jnp.int32))


def remote(src, dst, send, recv, peer):
    return pltpu.make_async_remote_copy(
        src_ref=src, dst_ref=dst, send_sem=send, recv_sem=recv, device_id=peer, device_id_type=MESH
    )


def plane_gather_kernel(x_ref, out_ref, send, recv, core_send, core_recv):
    f, c, t = here()
    core = f % 2
    chips = [(0, 1), (2, 0), (2, 1)]
    peers = [(f ^ df, c ^ dc, t) for df, dc in chips]
    partner = (f ^ 1, c, t)
    greet(peers + [partner])

    def slot(df, dc):
        return (f ^ df) * 2 + (c ^ dc)

    own = slot(0, 0)
    copies = []
    for j, peer in enumerate(peers):
        copy = remote(x_ref, out_ref.at[own], send.at[j], recv.at[j], peer)
        copy.start()
        copies.append(copy)
    passes = [remote(x_ref, out_ref.at[own], core_send.at[3], core_recv.at[3], partner)]
    passes[0].start()
    out_ref[own] = x_ref[...]
    for j, (df, dc) in enumerate(chips):
        copies[j].wait_recv()
        there = slot(df, dc)
        copy = remote(
            out_ref.at[there], out_ref.at[there], core_send.at[j], core_recv.at[j], partner
        )
        copy.start()
        passes.append(copy)
    for copy in copies:
        copy.wait_send()
    for copy in passes:
        copy.wait()


def plane_gather(shard, collective_id):
    if not small_plane():
        return lax.all_gather(shard, PLANE, axis=0, tiled=True)
    rows, columns = shard.shape
    out = pl.pallas_call(
        plane_gather_kernel,
        in_specs=[pl.BlockSpec(memory_space=pltpu.VMEM)],
        out_specs=pl.BlockSpec(memory_space=pltpu.VMEM),
        out_shape=jax.ShapeDtypeStruct((8, rows, columns), shard.dtype),
        scratch_shapes=[
            pltpu.SemaphoreType.DMA((3,)),
            pltpu.SemaphoreType.DMA((3,)),
            pltpu.SemaphoreType.DMA((4,)),
            pltpu.SemaphoreType.DMA((4,)),
        ],
        compiler_params=pltpu.CompilerParams(
            collective_id=collective_id, has_side_effects=True, vmem_limit_bytes=VMEM_LIMIT
        ),
        name="plane_gather",
    )(shard)
    return out.reshape(8 * rows, columns)


def plane_scatter_kernel(
    x_ref, out_ref, chip, core_in, chip_in, send, recv, core_send, core_recv
):
    f, c, t = here()
    core = f % 2
    chips = [(2, 1), (0, 1), (2, 0)]
    peers = [(f ^ df, c ^ dc, t) for df, dc in chips]
    partner = (f ^ 1, c, t)
    greet(peers + [partner])
    order = chips + [(0, 0)]
    swaps = []
    for j, (df, dc) in enumerate(order):
        block = (f ^ df ^ 1) * 2 + (c ^ dc)
        copy = remote(x_ref.at[block], core_in.at[j], core_send.at[j], core_recv.at[j], partner)
        copy.start()
        swaps.append(copy)
    copies = []
    for j, (df, dc) in enumerate(order):
        swaps[j].wait_recv()
        block = (f ^ df) * 2 + (c ^ dc)
        total = x_ref[block].astype(F32) + core_in[j].astype(F32)
        if j < 3:
            chip[j] = total.astype(BF16)
            copy = remote(chip.at[j], chip_in.at[j], send.at[j], recv.at[j], peers[j])
            copy.start()
            copies.append(copy)
        else:
            out_ref[...] = total
    for copy in swaps:
        copy.wait_send()
    for j in range(3):
        copies[j].wait()
        out_ref[...] += chip_in[j].astype(F32)


def plane_scatter(total, collective_id):
    if not small_plane():
        return lax.psum_scatter(total.astype(F32), PLANE, scatter_dimension=0, tiled=True)
    rows, columns = total.shape[0] // 8, total.shape[1]
    return pl.pallas_call(
        plane_scatter_kernel,
        in_specs=[pl.BlockSpec(memory_space=pltpu.VMEM)],
        out_specs=pl.BlockSpec(memory_space=pltpu.VMEM),
        out_shape=jax.ShapeDtypeStruct((rows, columns), F32),
        scratch_shapes=[
            pltpu.VMEM((3, rows, columns), BF16),
            pltpu.VMEM((4, rows, columns), BF16),
            pltpu.VMEM((3, rows, columns), BF16),
            pltpu.SemaphoreType.DMA((3,)),
            pltpu.SemaphoreType.DMA((3,)),
            pltpu.SemaphoreType.DMA((4,)),
            pltpu.SemaphoreType.DMA((4,)),
        ],
        compiler_params=pltpu.CompilerParams(
            collective_id=collective_id, has_side_effects=True, vmem_limit_bytes=VMEM_LIMIT
        ),
        name="plane_scatter",
    )(total.reshape(8, rows, columns))


def line_project_kernel(
    count, chunks, x_ref, w_ref, base_ref, out_ref, held, send_right, send_left, recv
):
    f, c, t = here()
    right, left = (f, c, t + 1), (f, c, t - 1)
    greet_line(t, count, left, right)
    rows = x_ref.shape[0] // chunks

    def part(j):
        return pl.ds(j * rows, rows)

    def go(j, d, peer, origin, sems):
        src = x_ref.at[part(j)] if d == 0 else held.at[origin, part(j)]
        return remote(src, held.at[origin, part(j)], sems.at[d, j], recv.at[origin, j], peer)

    def go_right(j, d):
        return go(j, d, right, t - d, send_right)

    def go_left(j, d):
        return go(j, d, left, t + d, send_left)

    def arrived(j, origin):
        return remote(x_ref.at[part(j)], held.at[origin, part(j)], send_right.at[0, j], recv.at[origin, j], right)

    @pl.when(t < count - 1)
    def _():
        for j in range(chunks):
            go_right(j, 0).start()

    @pl.when(t > 0)
    def _():
        for j in range(chunks):
            go_left(j, 0).start()

    held[t] = x_ref[...]
    for d in range(1, count):
        for j in range(chunks):

            @pl.when(t - d >= 0)
            def _():
                arrived(j, t - d).wait_recv()
                if d < count - 1:

                    @pl.when(t < count - 1)
                    def _():
                        go_right(j, d).start()

            @pl.when(t + d < count)
            def _():
                arrived(j, t + d).wait_recv()
                if d < count - 1:

                    @pl.when(t > 0)
                    def _():
                        go_left(j, d).start()

            if d == count - 1:
                total = base_ref[part(j)]
                for origin in range(count):
                    total = total + mat_nt(held[origin, part(j)], w_ref[origin])
                out_ref[part(j)] = total

    for d in range(count - 1):
        for j in range(chunks):

            @pl.when((t - d >= 0) & (t < count - 1))
            def _():
                go_right(j, d).wait_send()

            @pl.when((t + d < count) & (t > 0))
            def _():
                go_left(j, d).wait_send()


def line_project(value, weights, base, collective_id):
    rows, width = value.shape
    count, features = weights.shape[0], weights.shape[1]
    chunks = 4
    return pl.pallas_call(
        functools.partial(line_project_kernel, count, chunks),
        in_specs=[pl.BlockSpec(memory_space=pltpu.VMEM)] * 3,
        out_specs=pl.BlockSpec(memory_space=pltpu.VMEM),
        out_shape=jax.ShapeDtypeStruct((rows, features), F32),
        scratch_shapes=[
            pltpu.VMEM((count, rows, width), BF16),
            pltpu.SemaphoreType.DMA((count, chunks)),
            pltpu.SemaphoreType.DMA((count, chunks)),
            pltpu.SemaphoreType.DMA((count, chunks)),
        ],
        compiler_params=pltpu.CompilerParams(
            collective_id=collective_id, has_side_effects=True, vmem_limit_bytes=VMEM_LIMIT
        ),
        name="line_project",
    )(value, weights, base)


def line_sum_kernel(
    count,
    chunks,
    window,
    lag,
    x_ref,
    out_ref,
    from_right,
    from_left,
    to_left,
    to_right,
    up_send,
    up_recv,
    down_send,
    down_recv,
    low_send,
    low_recv,
    high_send,
    high_recv,
):
    f, c, t = here()
    right, left = (f, c, t + 1), (f, c, t - 1)
    last = count - 1
    greet_line(t, count, left, right)
    half = x_ref.shape[0] // 2
    rows = half // chunks

    def low(j):
        return pl.ds(j * rows, rows)

    def high(j):
        return pl.ds(half + j * rows, rows)

    def down(j, own):
        src = x_ref.at[low(j)] if own else to_left.at[low(j)]
        return remote(src, from_right.at[low(j)], down_send.at[j], down_recv.at[j], left)

    def up(j, own):
        src = x_ref.at[high(j)] if own else to_right.at[low(j)]
        return remote(src, from_left.at[low(j)], up_send.at[j], up_recv.at[j], right)

    def low_back(j):
        return remote(out_ref.at[low(j)], out_ref.at[low(j)], low_send.at[j], low_recv.at[j], right)

    def high_back(j):
        return remote(
            out_ref.at[high(j)], out_ref.at[high(j)], high_send.at[j], high_recv.at[j], left
        )

    def pace(j, copy):
        if j == 0:
            for k in range(min(window, chunks)):
                copy(k, True).start()
        copy(j, True).wait_send()
        if j + window < chunks:
            copy(j + window, True).start()

    def low_step(j):
        @pl.when(t == last)
        def _():
            pace(j, down)

        @pl.when(t < last)
        def _():
            down(j, False).wait_recv()
            total = from_right[low(j)].astype(F32) + x_ref[low(j)].astype(F32)

            @pl.when(t > 0)
            def _():
                to_left[low(j)] = total.astype(BF16)
                down(j, False).start()

            @pl.when(t == 0)
            def _():
                out_ref[low(j)] = total.astype(BF16)
                low_back(j).start()

    def high_step(j):
        @pl.when(t == 0)
        def _():
            pace(j, up)

        @pl.when(t > 0)
        def _():
            up(j, False).wait_recv()
            total = from_left[low(j)].astype(F32) + x_ref[high(j)].astype(F32)

            @pl.when(t < last)
            def _():
                to_right[low(j)] = total.astype(BF16)
                up(j, False).start()

            @pl.when(t == last)
            def _():
                out_ref[high(j)] = total.astype(BF16)
                high_back(j).start()

    def low_forward(j):
        @pl.when(t > 0)
        def _():
            low_back(j).wait_recv()

            @pl.when(t < last)
            def _():
                low_back(j).start()

    def high_forward(j):
        @pl.when(t < last)
        def _():
            high_back(j).wait_recv()

            @pl.when(t > 0)
            def _():
                high_back(j).start()

    for j in range(chunks + lag):

        @pl.when(t < count // 2)
        def _():
            if j < chunks:
                high_step(j)
            if 0 <= j - 1 < chunks:
                low_step(j - 1)

        @pl.when(t >= count // 2)
        def _():
            if j < chunks:
                low_step(j)
            if 0 <= j - 1 < chunks:
                high_step(j - 1)

        if j >= lag:

            @pl.when(t < count // 2)
            def _():
                low_forward(j - lag)
                high_forward(j - lag)

            @pl.when(t >= count // 2)
            def _():
                high_forward(j - lag)
                low_forward(j - lag)

    for j in range(chunks):

        @pl.when(t > 0)
        def _():
            high_back(j).wait_send()

            @pl.when(t < last)
            def _():
                down(j, False).wait_send()

        @pl.when(t < last)
        def _():
            low_back(j).wait_send()

            @pl.when(t > 0)
            def _():
                up(j, False).wait_send()


def line_sum(partial, collective_id, chunks=4, window=2, lag=4):
    count = lax.axis_size("tp")
    rows, columns = partial.shape
    while (rows // 2) % (chunks * 16):
        chunks -= 1
    half = rows // 2
    return pl.pallas_call(
        functools.partial(line_sum_kernel, count, chunks, window, lag),
        in_specs=[pl.BlockSpec(memory_space=pltpu.VMEM)],
        out_specs=pl.BlockSpec(memory_space=pltpu.VMEM),
        out_shape=jax.ShapeDtypeStruct((rows, columns), BF16),
        scratch_shapes=[pltpu.VMEM((half, columns), BF16)] * 4
        + [pltpu.SemaphoreType.DMA((chunks,))] * 8,
        compiler_params=pltpu.CompilerParams(
            collective_id=collective_id, has_side_effects=True, vmem_limit_bytes=VMEM_LIMIT
        ),
        name="line_sum",
    )(partial)


def share_stats_kernel(count, x_ref, top_ref, log_ref, picked_ref, held, send, recv):
    f, c, t = here()
    peers = [(f, c, lax.rem(t + k, count)) for k in range(1, count)]
    greet(peers)
    copies = []
    for k in range(1, count):
        copy = remote(x_ref, held.at[t], send.at[k], recv.at[k], peers[k - 1])
        copy.start()
        copies.append(copy)
    held[t] = x_ref[...]
    for copy in copies:
        copy.wait()
    highest = functools.reduce(jnp.maximum, [held[k, 0] for k in range(count)])
    total = sum(held[k, 1] * jnp.exp(held[k, 0] - highest) for k in range(count))
    top_ref[...] = highest
    log_ref[...] = highest + jnp.log(total)
    picked_ref[...] = sum(held[k, 2] for k in range(count))


def share_stats(stats, collective_id):
    count = lax.axis_size("tp")
    shape = jax.ShapeDtypeStruct(stats.shape[1:], F32)
    return pl.pallas_call(
        functools.partial(share_stats_kernel, count),
        in_specs=[pl.BlockSpec(memory_space=pltpu.VMEM)],
        out_specs=[pl.BlockSpec(memory_space=pltpu.VMEM)] * 3,
        out_shape=[shape] * 3,
        scratch_shapes=[
            pltpu.VMEM((count,) + stats.shape, F32),
            pltpu.SemaphoreType.DMA((count,)),
            pltpu.SemaphoreType.DMA((count,)),
        ],
        compiler_params=pltpu.CompilerParams(collective_id=collective_id, has_side_effects=True),
        name="share_stats",
    )(stats)


def after(value, earlier):
    return lax.optimization_barrier((value, earlier))[0]


def tp_list(value):
    count = lax.axis_size("tp")
    return [value] + [
        lax.ppermute(value, "tp", [(i, (i + k) % count) for i in range(count)])
        for k in range(1, count)
    ]


def ctx_gather(value):
    if lax.axis_size("ctx") == 2:
        return jnp.concatenate([value, swap(value, "ctx", 1)], axis=0)
    return lax.all_gather(value, "ctx", axis=0, tiled=True)


def ctx_pair(value):
    if lax.axis_size("ctx") == 2:
        return [value, swap(value, "ctx", 1)]
    return [lax.all_gather(value, "ctx", axis=0, tiled=True)]


def ctx_join(parts):
    return jnp.concatenate(parts, axis=0)


def ctx_positions(rows):
    c, count = lax.axis_index("ctx"), lax.axis_size("ctx")
    if count == 2:
        return jnp.concatenate(
            [c * rows + jnp.arange(rows), (1 - c) * rows + jnp.arange(rows)]
        ).astype(jnp.int32)
    return jnp.arange(rows * count, dtype=jnp.int32)


def ctx_scatter(value):
    if lax.axis_size("ctx") == 2:
        rows = value.shape[0] // 2
        return low_sum(value[:rows], swap(value[rows:], "ctx", 1))
    return lax.psum_scatter(value.astype(F32), "ctx", scatter_dimension=0, tiled=True).astype(BF16)


def exit_forward_kernel(
    valid, x_ref, e_ref, target_ref, logits_ref, top_ref, sum_ref, picked_ref, m_acc, l_acc, p_acc
):
    step = pl.program_id(0)
    rows, tile = logits_ref.shape

    @pl.when(step == 0)
    def _():
        m_acc[...] = jnp.full_like(m_acc, LOWEST)
        l_acc[...] = jnp.zeros_like(l_acc)
        p_acc[...] = jnp.zeros_like(p_acc)

    lanes = lax.broadcasted_iota(jnp.int32, (rows, 128), 1)
    logits_ref[...] = mat(x_ref[...], e_ref[...])
    relative = target_ref[...] - step * tile
    limit = valid - step * tile
    groups = tile // 128
    highest = m_acc[...]
    for g in range(groups):
        cols = slice(g * 128, (g + 1) * 128)
        part = jnp.where(lanes < limit - g * 128, logits_ref[:, cols], LOWEST)
        highest = jnp.maximum(highest, part)
    total = l_acc[...] * jnp.exp(m_acc[...] - highest)
    picked = p_acc[...]
    for g in range(groups):
        cols = slice(g * 128, (g + 1) * 128)
        part = jnp.where(lanes < limit - g * 128, logits_ref[:, cols], LOWEST)
        total += jnp.exp(part - highest)
        picked += jnp.where(lanes == relative - g * 128, part, 0.0)
    m_acc[...] = highest
    l_acc[...] = total
    p_acc[...] = picked

    @pl.when(step == pl.num_programs(0) - 1)
    def _():
        top = jnp.max(m_acc[...], axis=1, keepdims=True)
        top_ref[...] = top
        sum_ref[...] = jnp.sum(l_acc[...] * jnp.exp(m_acc[...] - top), axis=1, keepdims=True)
        picked_ref[...] = jnp.sum(p_acc[...], axis=1, keepdims=True)


def exit_forward(exit_in, embed_t, targets_local, valid):
    rows, features = exit_in.shape
    padded = embed_t.shape[1]
    column = pl.BlockSpec((rows, 1), lambda i: (0, 0))
    stat = jax.ShapeDtypeStruct((rows, 1), F32)
    return pl.pallas_call(
        functools.partial(exit_forward_kernel, valid),
        grid=(padded // TILE,),
        in_specs=[
            pl.BlockSpec((rows, features), lambda i: (0, 0)),
            pl.BlockSpec((features, TILE), lambda i: (0, i)),
            column,
        ],
        out_specs=[pl.BlockSpec((rows, TILE), lambda i: (0, i)), column, column, column],
        out_shape=[jax.ShapeDtypeStruct((rows, padded), F32), stat, stat, stat],
        scratch_shapes=[pltpu.VMEM((rows, 128), F32)] * 3,
        compiler_params=pltpu.CompilerParams(vmem_limit_bytes=VMEM_LIMIT),
        cost_estimate=pl.CostEstimate(
            flops=2 * rows * features * padded,
            bytes_accessed=4 * rows * padded + 2 * features * padded,
            transcendentals=rows * padded,
        ),
        name="exit_forward",
    )(exit_in, embed_t, targets_local)


def forward_kernel(heads, q_ref, kv_ref, bias_ref, out_ref, total_ref):
    width = heads * HD
    for h in range(heads):
        cols = slice(h * HD, (h + 1) * HD)
        keys = kv_ref[:, cols]
        values = kv_ref[:, width + h * HD : width + (h + 1) * HD]
        scores = mat_nt(keys, q_ref[:, cols])
        if bias_ref is not None:
            scores = scores + bias_ref[...]
        highest = jnp.max(scores, axis=0, keepdims=True)
        exponent = jnp.exp(scores - highest)
        denominator = jnp.sum(exponent, axis=0, keepdims=True)
        outcome = mat_tn(values, exponent.astype(BF16)) / denominator
        out_ref[:, cols] = outcome.T.astype(BF16)
        total_ref[h : h + 1, :] = highest + jnp.log(denominator)


def backward_kernel(
    heads, q_ref, kv_ref, bias_ref, total_ref, go_ref, dq_ref, dkv_ref, acc_ref
):
    width = heads * HD
    step = pl.program_id(0)

    @pl.when(step == 0)
    def _():
        acc_ref[...] = jnp.zeros_like(acc_ref)

    for h in range(heads):
        cols = slice(h * HD, (h + 1) * HD)
        vcols = slice(width + h * HD, width + (h + 1) * HD)
        keys, values = kv_ref[:, cols], kv_ref[:, vcols]
        queries, go = q_ref[:, cols], go_ref[:, cols]
        scores = mat_nt(keys, queries)
        if bias_ref is not None:
            scores = scores + bias_ref[...]
        probs = jnp.exp(scores - total_ref[h : h + 1, :])
        grad_probs = mat_nt(values, go)
        inner = jnp.sum(probs * grad_probs, axis=0, keepdims=True)
        grad_scores = (probs * (grad_probs - inner)).astype(BF16)
        acc_ref[:, vcols] += mat(probs.astype(BF16), go)
        acc_ref[:, cols] += mat(grad_scores, queries)
        dq_ref[:, cols] = mat_tn(keys, grad_scores).T.astype(BF16)

    @pl.when(step == pl.num_programs(0) - 1)
    def _():
        dkv_ref[...] = acc_ref[...].astype(BF16)


def attention_specs(rows, width, keys, tile, masked):
    specs = [
        pl.BlockSpec((tile, width), lambda i: (i, 0)),
        pl.BlockSpec((keys, 2 * width), lambda i: (0, 0)),
    ]
    if masked:
        specs.append(pl.BlockSpec((keys, tile), lambda i: (0, i)))
    return specs


def attend(queries, kv, bias):
    rows, width = queries.shape
    keys, heads = kv.shape[0], width // HD
    tile = min(rows, 256)
    masked = bias is not None
    body = functools.partial(forward_kernel, heads)
    if not masked:
        plain = body
        body = lambda q, k, o, t: plain(q, k, None, o, t)
    return pl.pallas_call(
        body,
        grid=(rows // tile,),
        in_specs=attention_specs(rows, width, keys, tile, masked),
        out_specs=[
            pl.BlockSpec((tile, width), lambda i: (i, 0)),
            pl.BlockSpec((heads, tile), lambda i: (0, i)),
        ],
        out_shape=[
            jax.ShapeDtypeStruct((rows, width), BF16),
            jax.ShapeDtypeStruct((heads, rows), F32),
        ],
        compiler_params=pltpu.CompilerParams(vmem_limit_bytes=VMEM_LIMIT),
        cost_estimate=pl.CostEstimate(
            flops=16 * rows * keys * width,
            bytes_accessed=4 * keys * width + 8 * rows * width,
            transcendentals=rows * keys * heads,
        ),
        name="attend_masked" if masked else "attend",
    )(*([queries, kv, bias] if masked else [queries, kv]))


def attend_back(queries, kv, bias, totals, go):
    rows, width = queries.shape
    keys, heads = kv.shape[0], width // HD
    tile = min(rows, 256)
    masked = bias is not None
    body = functools.partial(backward_kernel, heads)
    if not masked:
        plain = body
        body = lambda q, k, *rest: plain(q, k, None, *rest)
    specs = attention_specs(rows, width, keys, tile, masked) + [
        pl.BlockSpec((heads, tile), lambda i: (0, i)),
        pl.BlockSpec((tile, width), lambda i: (i, 0)),
    ]
    operands = ([queries, kv, bias] if masked else [queries, kv]) + [totals, go]
    return pl.pallas_call(
        body,
        grid=(rows // tile,),
        in_specs=specs,
        out_specs=[
            pl.BlockSpec((tile, width), lambda i: (i, 0)),
            pl.BlockSpec((keys, 2 * width), lambda i: (0, 0)),
        ],
        out_shape=[
            jax.ShapeDtypeStruct((rows, width), BF16),
            jax.ShapeDtypeStruct((keys, 2 * width), BF16),
        ],
        scratch_shapes=[pltpu.VMEM((keys, 2 * width), F32)],
        compiler_params=pltpu.CompilerParams(vmem_limit_bytes=VMEM_LIMIT),
        cost_estimate=pl.CostEstimate(
            flops=40 * rows * keys * width,
            bytes_accessed=8 * keys * width + 10 * rows * width,
            transcendentals=rows * keys * heads,
        ),
        name="attend_back_masked" if masked else "attend_back",
    )(*operands)


def rms_scale(values):
    return lax.rsqrt(jnp.mean(values * values, axis=-1, keepdims=True) + EPSILON)


def rms_back(grad_normed, normed, scale):
    return scale * (grad_normed - normed * jnp.mean(grad_normed * normed, axis=-1, keepdims=True))


def mask_bias(parent_row, row_count):
    block_count = parent_row.shape[0]
    blocks = jnp.arange(block_count, dtype=jnp.int32)
    current = blocks
    reachable = blocks[:, None] == blocks[None, :]
    for _ in range(block_count - 1):
        current = jnp.sum(
            jnp.where(current[:, None] == blocks[None, :], parent_row[None, :], 0), axis=1
        )
        reachable = reachable | (current[:, None] == blocks[None, :])
    query_pos = lax.axis_index("ctx") * row_count + jnp.arange(row_count, dtype=jnp.int32)
    key_pos = ctx_positions(row_count)
    query_onehot = (query_pos[:, None] // BLK == blocks[None, :]).astype(F32)
    key_onehot = (key_pos[:, None] // BLK == blocks[None, :]).astype(F32)
    linked = mat_nt(key_onehot, mat(query_onehot, reachable.astype(F32))) > 0.5
    causal = (query_pos[None, :] // BLK != key_pos[:, None] // BLK) | (
        key_pos[:, None] <= query_pos[None, :]
    )
    return jnp.where(linked & causal, 0.0, MASKED)


def gelu_parts(gate):
    root = math.sqrt(2.0 / math.pi)
    inner = jnp.tanh(root * (gate + 0.044715 * gate * gate * gate))
    value = 0.5 * gate * (1.0 + inner)
    slope = 0.5 * (1.0 + inner) + 0.5 * gate * (1.0 - inner * inner) * root * (
        1.0 + 3.0 * 0.044715 * gate * gate
    )
    return value, slope


FORWARD_ORDER = (
    ("GX", "h"), ("CP",), ("FL", 0), ("GY", "h"), ("OL", 0), ("GX", "e0"), ("GA", "h"),
    ("GY", "e2"), ("GF", "h"), ("GX", "e2"), ("OL", 1), ("FL", 1), ("GD", "h"), ("GY", "e0"),
    ("GE", "h"), ("GF", "e0"), ("GF", "e2"), ("OL", 2), ("PT", 1), ("CS", 1), ("FL", 2),
    ("PT", 0), ("BI",), ("OL", 3), ("CS", 0), ("GX", "e1"), ("GA", "e2"), ("PE", 1), ("FL", 3),
    ("WS", 1), ("GY", "o"), ("PE", 0), ("GX", "o"), ("S", 1, 0), ("S", 1, 1), ("S", 1, 2),
    ("WS", 0), ("GY", "e1"), ("GA", "o"), ("S", 0, 0), ("AL", 1), ("CC", 0), ("AH", 1, 1),
    ("GA", "e0"), ("S", 0, 1), ("GF", "o"), ("S", 0, 2), ("AH", 1, 2), ("AL", 0), ("GD", "o"),
    ("CC", 1), ("GY", "f0"), ("GX", "f0"), ("AH", 0, 1), ("AH", 0, 2), ("AH", 0, 3), ("GE", "o"),
    ("GX", "f1"), ("OS", 0), ("WC", 0), ("AH", 1, 3), ("GD", "e0"), ("GA", "f0"), ("X", 0, 0),
    ("X", 0, 1), ("GF", "e1"), ("X", 0, 2), ("BL", 0), ("OS", 1), ("WC", 1), ("GY", "f1"),
    ("X", 1, 0), ("BH", 0, 1), ("GF", "f0"), ("GF", "f1"), ("GE", "e0"), ("GA", "e1"),
    ("X", 1, 1), ("GD", "e2"), ("X", 1, 2), ("BL", 1), ("GD", "e1"), ("BH", 0, 2), ("BH", 0, 3),
    ("GE", "e2"), ("OC", 0), ("BH", 1, 1), ("GD", "f0"), ("BH", 1, 2), ("GA", "f1"), ("GD", "f1"),
    ("BH", 1, 3), ("GE", "e1"), ("GE", "f0"), ("OC", 1), ("GE", "f1"),
)
EMBED_PIECES = ((2816, "xy"), (2816, "xy"), (2560, "yx"))


class Line:
    def __init__(self, t, count, left, right, own, place, sems):
        self.t, self.count, self.left, self.right = t, count, left, right
        self.own, self.place = own, place
        self.to_right, self.to_left, self.recv = sems

    def copy(self, d, way):
        origin = self.t - d if way == 0 else self.t + d
        sems, peer = (self.to_right, self.right) if way == 0 else (self.to_left, self.left)
        src = self.own if d == 0 else self.place(origin)
        return remote(src, self.place(origin), sems.at[d], self.recv.at[origin], peer)

    def landed(self, origin):
        return remote(
            self.place(origin),
            self.place(origin),
            self.to_right.at[0],
            self.recv.at[origin],
            self.right,
        )

    def start(self):
        @pl.when(self.t < self.count - 1)
        def _():
            self.copy(0, 0).start()

        @pl.when(self.t > 0)
        def _():
            self.copy(0, 1).start()

    def hop(self, d):
        t, last = self.t, self.count - 1

        @pl.when(t - d >= 0)
        def _():
            self.landed(t - d).wait_recv()
            if d < last:

                @pl.when(t < last)
                def _():
                    self.copy(d, 0).start()

        @pl.when(t + d <= last)
        def _():
            self.landed(t + d).wait_recv()
            if d < last:

                @pl.when(t > 0)
                def _():
                    self.copy(d, 1).start()

    def finish(self):
        t, last = self.t, self.count - 1
        for d in range(last):

            @pl.when((t - d >= 0) & (t < last))
            def _():
                self.copy(d, 0).wait_send()

            @pl.when((t + d <= last) & (t > 0))
            def _():
                self.copy(d, 1).wait_send()


class Spread:
    def __init__(self, peers, own, blocks, send, recv):
        first_peer, second_peer, core_peer = peers
        home, across, aside, diagonal = blocks
        moves = [
            (own, home, first_peer),
            (own, home, second_peer),
            (across, across, second_peer),
            (own, home, core_peer),
            (across, across, core_peer),
            (aside, aside, core_peer),
            (diagonal, diagonal, core_peer),
        ]
        self.copies = [
            remote(src, dst, send.at[j], recv.at[j], peer)
            for j, (src, dst, peer) in enumerate(moves)
        ]

    def start_first(self):
        self.copies[0].start()

    def start_second(self):
        self.copies[1].start()
        self.copies[3].start()

    def pass_across(self):
        self.copies[0].wait_recv()
        self.copies[2].start()
        self.copies[4].start()

    def pass_aside(self):
        self.copies[1].wait_recv()
        self.copies[5].start()

    def pass_diagonal(self):
        self.copies[2].wait_recv()
        self.copies[6].start()

    def arrive(self):
        for j in (3, 4, 5, 6):
            self.copies[j].wait_recv()

    def finish(self):
        for copy in self.copies:
            copy.wait_send()


def attend_head(h, i, tile, q_ref, kv_ref, bias_ref, out_ref, total_ref):
    rows, width = q_ref.shape[0] // MB, q_ref.shape[1]
    cols = slice(h * HD, (h + 1) * HD)
    vcols = slice(width + h * HD, width + (h + 1) * HD)

    @pl.loop(0, rows // tile)
    def _(n):
        at = pl.ds(pl.multiple_of(i * rows + n * tile, tile), tile)
        here_at = pl.ds(pl.multiple_of(n * tile, tile), tile)
        scores = mat_nt(kv_ref[i, :, cols], q_ref[at, cols])
        if bias_ref is not None:
            scores = scores + bias_ref[i, :, here_at]
        highest = jnp.max(scores, axis=0, keepdims=True)
        exponent = jnp.exp(scores - highest)
        denominator = jnp.sum(exponent, axis=0, keepdims=True)
        outcome = mat_tn(kv_ref[i, :, vcols], exponent.astype(BF16)) / denominator
        out_ref[at, cols] = outcome.T.astype(BF16)
        total_ref[i, h : h + 1, here_at] = highest + jnp.log(denominator)


def build_bias(parents_ref, bias_ref, c):
    trees, keys, rows = bias_ref.shape
    mine = rows // BLK
    block_count = keys // BLK
    key_iota = lax.broadcasted_iota(jnp.int32, (BLK, BLK), 0)
    query_iota = lax.broadcasted_iota(jnp.int32, (BLK, BLK), 1)
    causal = jnp.where(key_iota <= query_iota, 0.0, MASKED)
    for i in range(trees):
        lines = [jnp.int32(1)]
        for b in range(1, block_count):
            parent = parents_ref[i, b]
            line = jnp.int32(1 << b)
            for j in range(b):
                line = line + jnp.where(parent == j, lines[j], 0)
            lines.append(line)
        for q in range(mine):
            line = jnp.int32(0)
            for b in range(block_count):
                line = line + jnp.where(c * mine + q == b, lines[b], 0)
            for k in range(block_count):
                at = (slice(k * BLK, (k + 1) * BLK), slice(q * BLK, (q + 1) * BLK))
                if k == q:
                    bias_ref[(i,) + at] = causal.astype(BF16)
                    continue
                block = c * mine + k if k < mine else (1 - c) * mine + k - mine
                seen = lax.shift_right_logical(line, block) & 1
                value = jnp.where(seen == 1, 0.0, MASKED)
                bias_ref[(i,) + at] = jnp.full((BLK, BLK), value, F32).astype(BF16)


def layer_forward_kernel(
    count,
    parents_ref,
    tok_ref,
    enc_ref,
    heads_in,
    op_in,
    ff_in,
    embed_in,
    heads_all,
    op_all,
    ff_all,
    embed_all,
    gains_out,
    bias,
    q_out,
    kvs,
    kvc,
    att,
    tots,
    cq,
    crs,
    totc,
    as_out,
    ac_out,
    zop,
    zff,
    held_s,
    held_c,
    spread_send,
    spread_recv,
    line_right,
    line_left,
    line_recv,
    ctx_send,
    ctx_recv,
    local_sem,
):
    f, c, t = here()
    right, left = (f, c, t + 1), (f, c, t - 1)
    x_peer, y_peer, core_peer = (f, 1 - c, t), (f ^ 2, c, t), (f ^ 1, c, t)
    rows, enc_rows = tok_ref.shape[0] // MB, enc_ref.shape[0] // MB
    width = q_out.shape[1]
    shard, ff_cols = ff_in.shape
    tile = 256

    barrier = pltpu.get_barrier_semaphore()
    for peer in (x_peer, y_peer, core_peer):
        pl.semaphore_signal(barrier, inc=1, device_id=peer, device_id_type=MESH)

    @pl.when(t > 0)
    def _():
        pl.semaphore_signal(barrier, inc=1, device_id=left, device_id_type=MESH)

    @pl.when(t < count - 1)
    def _():
        pl.semaphore_signal(barrier, inc=1, device_id=right, device_id_type=MESH)

    at_end = (t == 0) | (t == count - 1)
    pl.semaphore_wait(barrier, jnp.where(at_end, 4, 5).astype(jnp.int32))

    def block(df, dc):
        slot = (f ^ df) * 2 + (c ^ dc)
        return pl.ds(pl.multiple_of(slot * shard, shard), shard)

    def spread(j, way, own, place):
        blocks = [place(block(df, dc)) for df, dc in ((0, 0), (0, 1), (2, 0), (2, 1))]
        peers = (x_peer, y_peer, core_peer)
        if way == "yx":
            blocks = [blocks[0], blocks[2], blocks[1], blocks[3]]
            peers = (y_peer, x_peer, core_peer)
        return Spread(peers, own, blocks, spread_send.at[j], spread_recv.at[j])

    def line(j, own, place):
        sems = (line_right.at[j], line_left.at[j], line_recv.at[j])
        return Line(t, count, left, right, own, place, sems)

    def part(i):
        return pl.ds(i * rows, rows)

    def ff_place(origin):
        return zff.at[:, pl.ds(pl.multiple_of(origin * ff_cols, 128), ff_cols)]

    op_line = line(0, op_in, lambda origin: zop.at[:, origin])
    ff_line = line(1, ff_in, ff_place)
    spreads = {
        "h": spread(0, "xy", heads_in, lambda at: heads_all.at[at]),
        "o": spread(1, "xy", zop, lambda at: op_all.at[:, :, at]),
    }
    ff_half = zff.shape[1] // 2
    pieces = [("f0", "xy", zff, ff_all, 0, ff_half), ("f1", "yx", zff, ff_all, ff_half, ff_half)]
    start = 0
    for j, (size, way) in enumerate(EMBED_PIECES):
        pieces.append(("e%d" % j, way, embed_in, embed_all, start, size))
        start += size
    for name, way, own, target, first, size in pieces:
        cols = pl.ds(first, size)
        spreads[name] = spread(
            len(spreads), way, own.at[:, cols], lambda at, ref=target, cols=cols: ref.at[at, cols]
        )
    ff_own = pltpu.make_async_copy(zff, ff_all.at[block(0, 0)], local_sem.at[0])
    embed_own = pltpu.make_async_copy(embed_in, embed_all.at[block(0, 0)], local_sem.at[1])
    self_lines = [
        line(2 + i, att.at[part(i)], lambda origin, i=i: held_s.at[origin, part(i)])
        for i in range(MB)
    ]
    cross_lines = [
        line(4 + i, crs.at[part(i)], lambda origin, i=i: held_c.at[origin, part(i)])
        for i in range(MB)
    ]

    def ctx_copy(j, ref, i, size):
        return remote(
            ref.at[i, pl.ds(0, size)],
            ref.at[i, pl.ds(size, size)],
            ctx_send.at[j],
            ctx_recv.at[j],
            x_peer,
        )

    ctx_self = [ctx_copy(i, kvs, i, rows) for i in range(MB)]
    ctx_cross = [ctx_copy(2 + i, kvc, i, enc_rows) for i in range(MB)]

    def project_tokens(i):
        @pl.loop(0, rows // tile)
        def _(n):
            at = pl.ds(pl.multiple_of(i * rows + n * tile, tile), tile)
            value = tok_ref[at].astype(F32)
            hidden = (value * rms_scale(value) * gains_out[0:1]).astype(BF16)
            q_out[at] = mat(hidden, heads_all[:, 4 * width : 5 * width]).astype(BF16)
            inner = pl.ds(pl.multiple_of(n * tile, tile), tile)
            kvs[i, inner] = mat(hidden, heads_all[:, : 2 * width]).astype(BF16)

    def project_encoder(i):
        @pl.loop(0, enc_rows // tile)
        def _(n):
            at = pl.ds(pl.multiple_of(i * enc_rows + n * tile, tile), tile)
            inner = pl.ds(pl.multiple_of(n * tile, tile), tile)
            kvc[i, inner] = mat(enc_ref[at], heads_all[:, 2 * width : 4 * width]).astype(BF16)

    def self_head(i, h):
        attend_head(h, i, tile, q_out, kvs, bias, att, tots)

    def cross_head(i, h):
        attend_head(h, i, tile, cq, kvc, None, crs, totc)

    def out_self(i):
        @pl.loop(0, rows // tile)
        def _(n):
            at = pl.ds(pl.multiple_of(i * rows + n * tile, tile), tile)
            total = tok_ref[at].astype(F32)
            for origin in range(count):
                total = total + mat_nt(held_s[origin, at], op_all[0, origin])
            as_out[at] = total
            hidden = (total * rms_scale(total) * gains_out[1:2]).astype(BF16)
            cq[at] = mat(hidden, heads_all[:, Q2 : Q2 + width]).astype(BF16)

    def out_cross(i):
        @pl.loop(0, rows // tile)
        def _(n):
            at = pl.ds(pl.multiple_of(i * rows + n * tile, tile), tile)
            total = as_out[at]
            for origin in range(count):
                total = total + mat_nt(held_c[origin, at], op_all[1, origin])
            ac_out[at] = total

    def own_parts():
        heads_all[block(0, 0)] = heads_in[...]
        zop[:, t] = op_in[...]
        zff[:, pl.ds(pl.multiple_of(t * ff_cols, 128), ff_cols)] = ff_in[...]
        embed_own.start()

    def gather_done(name):
        spreads[name].arrive()
        if name == "h":
            gains_out[...] = heads_all[:, Q2 - 128 : Q2].astype(F32).T[64:72]

    def gather_first(name):
        spreads[name].start_first()
        if name == "o":
            op_all[:, :, block(0, 0)] = zop[...]
        if name == "f0":
            ff_own.start()

    def along(one, d):
        if d == 0:
            one.start()
        else:
            one.hop(d)

    def send_self(i):
        held_s[t, part(i)] = att[part(i)]
        self_lines[i].start()

    def send_cross(i):
        held_c[t, part(i)] = crs[part(i)]
        cross_lines[i].start()

    steps = {
        "GX": gather_first,
        "GY": lambda name: spreads[name].start_second(),
        "GF": lambda name: spreads[name].pass_across(),
        "GA": lambda name: spreads[name].pass_aside(),
        "GD": lambda name: spreads[name].pass_diagonal(),
        "GE": gather_done,
        "OL": lambda d: along(op_line, d),
        "FL": lambda d: along(ff_line, d),
        "CP": own_parts,
        "BI": lambda: build_bias(parents_ref, bias, c),
        "PT": project_tokens,
        "PE": project_encoder,
        "CS": lambda i: ctx_self[i].start(),
        "CC": lambda i: ctx_cross[i].start(),
        "WS": lambda i: ctx_self[i].wait_recv(),
        "WC": lambda i: ctx_cross[i].wait_recv(),
        "S": self_head,
        "X": cross_head,
        "AL": send_self,
        "AH": lambda i, d: self_lines[i].hop(d),
        "BL": send_cross,
        "BH": lambda i, d: cross_lines[i].hop(d),
        "OS": out_self,
        "OC": out_cross,
    }
    for name, *rest in FORWARD_ORDER:
        steps[name](*rest)
    for one in list(spreads.values()) + [op_line, ff_line] + self_lines + cross_lines:
        one.finish()
    for copy in ctx_self + ctx_cross:
        copy.wait_send()
    ff_own.wait()
    embed_own.wait()


def layer_forward(parents, tokens, encoder, heads_in, op_in, ff_in, embed_in, collective_id):
    count = lax.axis_size("tp")
    tok_rows, features = tokens.shape
    enc_rows = encoder.shape[0]
    shard, ff_cols = ff_in.shape
    width = op_in.shape[2]
    nh = width // HD
    rows = tok_rows // MB
    vmem = pl.BlockSpec(memory_space=pltpu.VMEM)
    anywhere = pl.BlockSpec(memory_space=pl.ANY)

    def low(*shape):
        return jax.ShapeDtypeStruct(shape, BF16)

    def full(*shape):
        return jax.ShapeDtypeStruct(shape, F32)

    return pl.pallas_call(
        functools.partial(layer_forward_kernel, count),
        in_specs=[pl.BlockSpec(memory_space=pltpu.SMEM)] + [vmem] * 5 + [anywhere],
        out_specs=[vmem, vmem, anywhere, anywhere] + [vmem] * 12,
        out_shape=[
            low(features, heads_in.shape[1]),
            low(3, count, features, width),
            low(features, count * ff_cols),
            low(features, embed_in.shape[1]),
            full(8, features),
            low(MB, 2 * rows, rows),
            low(tok_rows, width),
            low(MB, 2 * rows, 2 * width),
            low(MB, enc_rows, 2 * width),
            low(tok_rows, width),
            full(MB, nh, rows),
            low(tok_rows, width),
            low(tok_rows, width),
            full(MB, nh, rows),
            full(tok_rows, features),
            full(tok_rows, features),
        ],
        scratch_shapes=[
            pltpu.VMEM((3, count, shard, width), BF16),
            pltpu.VMEM((shard, count * ff_cols), BF16),
            pltpu.VMEM((count, tok_rows, width), BF16),
            pltpu.VMEM((count, tok_rows, width), BF16),
            pltpu.SemaphoreType.DMA((4 + len(EMBED_PIECES), 7)),
            pltpu.SemaphoreType.DMA((4 + len(EMBED_PIECES), 7)),
            pltpu.SemaphoreType.DMA((6, count)),
            pltpu.SemaphoreType.DMA((6, count)),
            pltpu.SemaphoreType.DMA((6, count)),
            pltpu.SemaphoreType.DMA((4,)),
            pltpu.SemaphoreType.DMA((4,)),
            pltpu.SemaphoreType.DMA((2,)),
        ],
        compiler_params=pltpu.CompilerParams(
            collective_id=collective_id, has_side_effects=True, vmem_limit_bytes=VMEM_MOST
        ),
        name="layer_forward",
    )(parents, tokens, encoder, heads_in, op_in, ff_in, embed_in)


def ff_forward_kernel(
    shrink, ac_ref, gains_ref, w_ref, gate_ref, up_ref, mixed_ref, low_ref, exit_ref, exit_t_ref, h_acc
):
    step = pl.program_id(0)
    rows = ac_ref.shape[0]
    units = gate_ref.shape[1]
    tile = min(rows, 256)

    @pl.loop(0, rows // tile)
    def _(n):
        at = pl.ds(pl.multiple_of(n * tile, tile), tile)

        @pl.when(step == 0)
        def _():
            value = ac_ref[at]
            h_acc[at] = (value * rms_scale(value) * gains_ref[2:3]).astype(BF16)
            mixed_ref[at] = value

        hidden = h_acc[at]
        gate = mat(hidden, w_ref[:, :units])
        up = mat(hidden, w_ref[:, units : 2 * units])
        gate_ref[at] = gate
        up_ref[at] = up
        activated = (gelu_parts(gate)[0] * up).astype(BF16)
        mixed_ref[at] += mat_nt(activated, w_ref[:, 2 * units :])

        @pl.when(step == pl.num_programs(0) - 1)
        def _():
            value = mixed_ref[at]
            low_ref[at] = value.astype(BF16)
            exit_in = value * rms_scale(value) * gains_ref[3:4] * shrink
            exit_ref[at] = exit_in.astype(BF16)

    @pl.when(step == pl.num_programs(0) - 1)
    def _():
        exit_t_ref[...] = exit_ref[...].T


def ff_forward(after_cross, gains, ff_all, count, shrink):
    rows, features = after_cross.shape
    cols = ff_all.shape[1] // count
    units = cols // 3

    def fixed(*shape):
        return pl.BlockSpec(shape, lambda i: (0,) * len(shape))

    moving = pl.BlockSpec((rows, units), lambda i: (0, i))
    return pl.pallas_call(
        functools.partial(ff_forward_kernel, shrink),
        grid=(count,),
        in_specs=[
            fixed(rows, features),
            fixed(8, features),
            pl.BlockSpec((features, cols), lambda i: (0, i)),
        ],
        out_specs=[moving, moving] + [fixed(rows, features)] * 3 + [fixed(features, rows)],
        out_shape=[
            jax.ShapeDtypeStruct((rows, count * units), F32),
            jax.ShapeDtypeStruct((rows, count * units), F32),
            jax.ShapeDtypeStruct((rows, features), F32),
            jax.ShapeDtypeStruct((rows, features), BF16),
            jax.ShapeDtypeStruct((rows, features), BF16),
            jax.ShapeDtypeStruct((features, rows), BF16),
        ],
        scratch_shapes=[pltpu.VMEM((rows, features), BF16)],
        compiler_params=pltpu.CompilerParams(vmem_limit_bytes=VMEM_MOST),
        cost_estimate=pl.CostEstimate(
            flops=2 * rows * features * count * cols,
            bytes_accessed=2 * features * count * cols + 8 * rows * count * units,
            transcendentals=rows * count * units,
        ),
        name="ff_forward",
    )(after_cross, gains, ff_all)


def ff_backward_kernel(
    shrink,
    ge_ref,
    mixed_ref,
    cot_ref,
    ac_ref,
    gains_ref,
    co_ref,
    w_ref,
    gate_ref,
    up_ref,
    gac_ref,
    low_ref,
    gcl_ref,
    gcr_ref,
    hid_ref,
    act_ref,
    gg_ref,
    gu_ref,
    norms_ref,
    acc,
):
    step = pl.program_id(0)
    t = lax.axis_index("tp")
    last = pl.num_programs(0) - 1
    rows = ac_ref.shape[0]
    units = gate_ref.shape[1]
    tile = min(rows, 256)

    @pl.when(step == 0)
    def _():
        norms_ref[...] = jnp.zeros_like(norms_ref)

    @pl.loop(0, rows // tile)
    def _(n):
        at = pl.ds(pl.multiple_of(n * tile, tile), tile)

        @pl.when(step == 0)
        def _():
            grad_exit = ge_ref[at].astype(F32) * shrink
            mixed = mixed_ref[at]
            scale = rms_scale(mixed)
            normed = mixed * scale
            norms_ref[0:1] += jnp.sum(grad_exit * normed, axis=0, keepdims=True)
            grad_mixed = cot_ref[at].astype(F32) + rms_back(
                grad_exit * gains_ref[3:4], normed, scale
            )
            gac_ref[at] = grad_mixed
            low_ref[at] = grad_mixed.astype(BF16)
            value = ac_ref[at]
            hid_ref[at] = (value * rms_scale(value) * gains_ref[2:3]).astype(BF16)
            acc[at] = jnp.zeros_like(acc[at])

        gate = gate_ref[at]
        up = up_ref[at]
        grad_act = mat(low_ref[at], w_ref[:, 2 * units :])
        value, slope = gelu_parts(gate)
        grad_gate = (grad_act * slope * up).astype(BF16)
        grad_up = (grad_act * value).astype(BF16)
        acc[at] += mat_nt(grad_gate, w_ref[:, :units]) + mat_nt(
            grad_up, w_ref[:, units : 2 * units]
        )

        @pl.when(step == t)
        def _():
            act_ref[at] = (value * up).astype(BF16)
            gg_ref[at] = grad_gate
            gu_ref[at] = grad_up

        @pl.when(step == last)
        def _():
            value = ac_ref[at]
            scale = rms_scale(value)
            normed = value * scale
            grad = acc[at]
            norms_ref[1:2] += jnp.sum(grad * normed, axis=0, keepdims=True)
            total = gac_ref[at] + rms_back(grad * gains_ref[2:3], normed, scale)
            gac_ref[at] = total
            gcl_ref[at] = total.astype(BF16)
            gcr_ref[at] = mat(total.astype(BF16), co_ref[...]).astype(BF16)


def ff_backward(
    grad_exit, mixed, cotangent, after_cross, gains, c_out_own, ff_all, gate, up, count, shrink
):
    rows, features = after_cross.shape
    cols = ff_all.shape[1] // count
    units = cols // 3
    width = c_out_own.shape[1]

    def fixed(*shape):
        return pl.BlockSpec(shape, lambda i: (0,) * len(shape))

    def low(*shape):
        return jax.ShapeDtypeStruct(shape, BF16)

    moving = pl.BlockSpec((rows, units), lambda i: (0, i))
    return pl.pallas_call(
        functools.partial(ff_backward_kernel, shrink),
        grid=(count,),
        in_specs=[fixed(rows, features)] * 4
        + [
            fixed(8, features),
            fixed(features, width),
            pl.BlockSpec((features, cols), lambda i: (0, i)),
            moving,
            moving,
        ],
        out_specs=[fixed(rows, features)] * 3
        + [fixed(rows, width), fixed(rows, features)]
        + [fixed(rows, units)] * 3
        + [fixed(8, features)],
        out_shape=[
            jax.ShapeDtypeStruct((rows, features), F32),
            low(rows, features),
            low(rows, features),
            low(rows, width),
            low(rows, features),
            low(rows, units),
            low(rows, units),
            low(rows, units),
            jax.ShapeDtypeStruct((8, features), F32),
        ],
        scratch_shapes=[pltpu.VMEM((rows, features), F32)],
        compiler_params=pltpu.CompilerParams(vmem_limit_bytes=VMEM_MOST),
        cost_estimate=pl.CostEstimate(
            flops=2 * rows * features * count * cols,
            bytes_accessed=2 * features * count * cols + 8 * rows * count * units,
            transcendentals=rows * count * units,
        ),
        name="ff_backward",
    )(grad_exit, mixed, cotangent, after_cross, gains, c_out_own, ff_all, gate, up)


def layer_forward_plain(
    parents, tokens, encoder, heads_in, op_in, ff_in, embed_in, collective_id
):
    rows = tokens.shape[0] // MB
    enc_rows = encoder.shape[0] // MB
    width = op_in.shape[2]
    heads_all = lax.all_gather(heads_in, PLANE, axis=0, tiled=True)
    op_all = lax.all_gather(
        lax.all_gather(op_in, "tp", axis=1, tiled=False), PLANE, axis=2, tiled=True
    )
    ff_all = lax.all_gather(
        lax.all_gather(ff_in, "tp", axis=1, tiled=True), PLANE, axis=0, tiled=True
    )
    embed_all = lax.all_gather(embed_in, PLANE, axis=0, tiled=True)
    gains = heads_all[:, Q2 - 64 : Q2 - 56].astype(F32).T
    tok = tokens.astype(F32)
    hidden_one = (tok * rms_scale(tok) * gains[0:1]).astype(BF16)
    queries = mat(hidden_one, heads_all[:, 4 * width : 5 * width]).astype(BF16)
    kv = mat(hidden_one, heads_all[:, : 2 * width]).astype(BF16)
    enc_kv = mat(encoder, heads_all[:, 2 * width : 4 * width]).astype(BF16)

    def both_sides(value, i, count):
        return ctx_gather(value[i * count : (i + 1) * count])

    kv_self = jnp.stack([both_sides(kv, i, rows) for i in range(MB)])
    kv_cross = jnp.stack([both_sides(enc_kv, i, enc_rows) for i in range(MB)])
    bias = jnp.stack([mask_bias(parents[i], rows) for i in range(MB)]).astype(BF16)

    def attention(values, keys_values, masks):
        outcome = [
            attend(
                values[i * rows : (i + 1) * rows],
                keys_values[i],
                None if masks is None else masks[i],
            )
            for i in range(MB)
        ]
        return jnp.concatenate([o[0] for o in outcome]), jnp.stack([o[1] for o in outcome])

    attended, totals_self = attention(queries, kv_self, bias)
    after_self = line_project(attended, op_all[0], tok, 2)
    hidden_two = (after_self * rms_scale(after_self) * gains[1:2]).astype(BF16)
    cross_q = mat(hidden_two, heads_all[:, Q2 : Q2 + width]).astype(BF16)
    crossed, totals_cross = attention(cross_q, kv_cross, None)
    after_cross = line_project(crossed, op_all[1], after_self, 3)
    return (
        heads_all,
        op_all,
        ff_all,
        embed_all,
        gains,
        bias,
        queries,
        kv_self,
        kv_cross,
        attended,
        totals_self,
        cross_q,
        crossed,
        totals_cross,
        after_self,
        after_cross,
    )


BACKWARD_ORDER = (
    ("X", 0, 0), ("X", 0, 1), ("X", 0, 2), ("XC", 0), ("SQ", 0), ("X", 1, 0), ("X", 1, 1),
    ("X", 1, 2), ("XC", 1), ("QH", 0, 1), ("SQ", 1), ("EP", 0), ("QH", 0, 2), ("ERN", 0, 0),
    ("QH", 1, 1), ("QH", 0, 3), ("AQ", 0), ("ERN", 0, 1), ("S", 0, 0), ("EP", 1), ("QH", 1, 2),
    ("ERF", 0, 0), ("QH", 1, 3), ("ERN", 0, 2), ("AQ", 1), ("ERF", 0, 1), ("ERN", 1, 0),
    ("S", 0, 1), ("S", 0, 2), ("ERN", 1, 1), ("XS", 0), ("ERF", 1, 0), ("ERN", 0, 3),
    ("ERF", 1, 1), ("ERN", 1, 2), ("S", 1, 0), ("ERF", 0, 2), ("S", 1, 1), ("EBN", 0, 0),
    ("ERF", 0, 3), ("S", 1, 2), ("EBN", 0, 1), ("TP", 0), ("ERF", 1, 2), ("EBN", 1, 0),
    ("EBF", 0, 0), ("XS", 1), ("ERN", 1, 3), ("EBN", 1, 1), ("EBF", 0, 1), ("EBF", 1, 0),
    ("EBN", 0, 2), ("TP", 1), ("EBF", 1, 1), ("ERF", 1, 3), ("ORN", 0, 0), ("ORN", 0, 1),
    ("EBN", 1, 2), ("EBF", 0, 2), ("ORF", 0, 0), ("ORF", 0, 1), ("ORN", 1, 0), ("EBF", 1, 2),
    ("ORN", 1, 1), ("EBN", 0, 3), ("ORF", 1, 0), ("ORF", 1, 1), ("OBN", 0, 0), ("OBN", 0, 1),
    ("EBF", 0, 3), ("OBF", 0, 0), ("OBF", 0, 1), ("OBN", 1, 0), ("OBN", 1, 1), ("EBN", 1, 3),
    ("FT", 0), ("OBF", 1, 0), ("OBF", 1, 1), ("FT", 1), ("EBF", 1, 3),
)


class LineSum:
    def __init__(self, t, count, left, right, x, out, buffers, sems, chunks):
        self.t, self.count, self.left, self.right = t, count, left, right
        self.x, self.out, self.chunks = x, out, chunks
        self.low_in, self.high_in = buffers.at[0], buffers.at[1]
        self.sems = sems
        self.half = x.shape[0] // 2
        self.rows = self.half // chunks

    def low(self, j):
        return pl.ds(j * self.rows, self.rows)

    def high(self, j):
        return pl.ds(self.half + j * self.rows, self.rows)

    def down(self, j, own):
        src = self.x.at[self.low(j)] if own else self.low_in.at[self.low(j)]
        dst = self.low_in.at[self.low(j)]
        return remote(src, dst, self.sems.at[0, j], self.sems.at[1, j], self.left)

    def up(self, j, own):
        src = self.x.at[self.high(j)] if own else self.high_in.at[self.low(j)]
        dst = self.high_in.at[self.low(j)]
        return remote(src, dst, self.sems.at[2, j], self.sems.at[3, j], self.right)

    def low_back(self, j):
        ref = self.out.at[self.low(j)]
        return remote(ref, ref, self.sems.at[4, j], self.sems.at[5, j], self.right)

    def high_back(self, j):
        ref = self.out.at[self.high(j)]
        return remote(ref, ref, self.sems.at[6, j], self.sems.at[7, j], self.left)

    def start(self):
        @pl.when(self.t == self.count - 1)
        def _():
            for j in range(self.chunks):
                self.down(j, True).start()

        @pl.when(self.t == 0)
        def _():
            for j in range(self.chunks):
                self.up(j, True).start()

    def low_step(self, j):
        if not 0 <= j < self.chunks:
            return

        @pl.when(self.t < self.count - 1)
        def _():
            self.down(j, False).wait_recv()
            at = self.low(j)
            total = (self.low_in[at].astype(F32) + self.x[at].astype(F32)).astype(BF16)

            @pl.when(self.t > 0)
            def _():
                self.low_in[at] = total
                self.down(j, False).start()

            @pl.when(self.t == 0)
            def _():
                self.out[at] = total
                self.low_back(j).start()

    def high_step(self, j):
        if not 0 <= j < self.chunks:
            return

        @pl.when(self.t > 0)
        def _():
            self.up(j, False).wait_recv()
            at = self.high(j)
            total = (self.high_in[self.low(j)].astype(F32) + self.x[at].astype(F32)).astype(BF16)

            @pl.when(self.t < self.count - 1)
            def _():
                self.high_in[self.low(j)] = total
                self.up(j, False).start()

            @pl.when(self.t == self.count - 1)
            def _():
                self.out[at] = total
                self.high_back(j).start()

    def low_forward(self, j):
        @pl.when(self.t > 0)
        def _():
            self.low_back(j).wait_recv()

            @pl.when(self.t < self.count - 1)
            def _():
                self.low_back(j).start()

    def high_forward(self, j):
        @pl.when(self.t < self.count - 1)
        def _():
            self.high_back(j).wait_recv()

            @pl.when(self.t > 0)
            def _():
                self.high_back(j).start()

    def by_side(self, first, second, j):
        @pl.when(self.t < self.count // 2)
        def _():
            first(j)

        @pl.when(self.t >= self.count // 2)
        def _():
            second(j)

    def reduce_near(self, j):
        self.by_side(self.high_step, self.low_step, j)

    def reduce_far(self, j):
        self.by_side(self.low_step, self.high_step, j)

    def back_near(self, j):
        self.by_side(self.low_forward, self.high_forward, j)

    def back_far(self, j):
        self.by_side(self.high_forward, self.low_forward, j)

    def finish(self):
        last = self.count - 1
        for j in range(self.chunks):

            @pl.when(self.t > 0)
            def _():
                self.down(j, False).wait_send()
                self.high_back(j).wait_send()

            @pl.when(self.t < last)
            def _():
                self.up(j, False).wait_send()
                self.low_back(j).wait_send()


def attend_back_head(
    h, i, tile, q_ref, kv_ref, bias_ref, total_ref, go_ref, dq_ref, dkv_ref, acc_ref
):
    rows, width = q_ref.shape[0] // MB, q_ref.shape[1]
    keys_count = kv_ref.shape[1]
    cols = slice(h * HD, (h + 1) * HD)
    vcols = slice(width + h * HD, width + (h + 1) * HD)
    acc_ref[:keys_count] = jnp.zeros((keys_count, 2 * HD), F32)

    @pl.loop(0, rows // tile)
    def _(n):
        at = pl.ds(pl.multiple_of(i * rows + n * tile, tile), tile)
        here_at = pl.ds(pl.multiple_of(n * tile, tile), tile)
        keys, values = kv_ref[i, :, cols], kv_ref[i, :, vcols]
        queries, go = q_ref[at, cols], go_ref[at, cols]
        scores = mat_nt(keys, queries)
        if bias_ref is not None:
            scores = scores + bias_ref[i, :, here_at]
        probs = jnp.exp(scores - total_ref[i, h : h + 1, here_at])
        grad_probs = mat_nt(values, go)
        inner = jnp.sum(probs * grad_probs, axis=0, keepdims=True)
        grad_scores = (probs * (grad_probs - inner)).astype(BF16)
        acc_ref[:keys_count, :HD] += mat(grad_scores, queries)
        acc_ref[:keys_count, HD:] += mat(probs.astype(BF16), go)
        dq_ref[at, cols] = mat_tn(keys, grad_scores).T.astype(BF16)

    dkv_ref[i, :, cols] = acc_ref[:keys_count, :HD].astype(BF16)
    dkv_ref[i, :, vcols] = acc_ref[:keys_count, HD:].astype(BF16)


def layer_backward_kernel(
    count,
    gcr_ref,
    cq_ref,
    kvc_ref,
    totc_ref,
    q_ref,
    kvs_ref,
    bias_ref,
    tots_ref,
    gac_ref,
    as_ref,
    tok_ref,
    wo_ref,
    cq4_ref,
    heads_ref,
    gains_ref,
    gt_out,
    enc_sum,
    gcq,
    gkvc,
    gq,
    gkvs,
    gsl,
    norms,
    dkvc,
    dkvc_in,
    dkvs,
    dkvs_in,
    acc,
    held,
    gatt,
    enc_part,
    one_part,
    one_sum,
    enc_buffers,
    one_buffers,
    line_right,
    line_left,
    line_recv,
    ctx_send,
    ctx_recv,
    sum_sems,
):
    f, c, t = here()
    right, left = (f, c, t + 1), (f, c, t - 1)
    x_peer = (f, 1 - c, t)
    rows, enc_rows = tok_ref.shape[0] // MB, gkvc.shape[0] // MB
    width = q_ref.shape[1]
    tile = 256

    barrier = pltpu.get_barrier_semaphore()
    pl.semaphore_signal(barrier, inc=1, device_id=x_peer, device_id_type=MESH)

    @pl.when(t > 0)
    def _():
        pl.semaphore_signal(barrier, inc=1, device_id=left, device_id_type=MESH)

    @pl.when(t < count - 1)
    def _():
        pl.semaphore_signal(barrier, inc=1, device_id=right, device_id_type=MESH)

    at_end = (t == 0) | (t == count - 1)
    pl.semaphore_wait(barrier, jnp.where(at_end, 2, 3).astype(jnp.int32))

    def part(i):
        return pl.ds(i * rows, rows)

    def enc_at(i):
        return pl.ds(i * enc_rows, enc_rows)

    def line(j, own, place):
        sems = (line_right.at[j], line_left.at[j], line_recv.at[j])
        return Line(t, count, left, right, own, place, sems)

    query_lines = [
        line(i, gcq.at[part(i)], lambda origin, i=i: held.at[origin, part(i)]) for i in range(MB)
    ]

    def ctx_copy(j, ref, landing, i, size):
        return remote(
            ref.at[i, pl.ds(size, size)], landing.at[i], ctx_send.at[j], ctx_recv.at[j], x_peer
        )

    ctx_cross = [ctx_copy(i, dkvc, dkvc_in, i, enc_rows) for i in range(MB)]
    ctx_self = [ctx_copy(MB + i, dkvs, dkvs_in, i, rows) for i in range(MB)]

    def summed(j, x, out, buffers, chunks):
        return LineSum(t, count, left, right, x, out, buffers, sum_sems.at[j], chunks)

    enc_chunks = enc_rows // 256
    one_chunks = rows // 256
    enc_sums = [
        summed(i, enc_part.at[enc_at(i)], enc_sum.at[enc_at(i)], enc_buffers.at[i], enc_chunks)
        for i in range(MB)
    ]
    one_sums = [
        summed(MB + i, one_part.at[part(i)], one_sum.at[part(i)], one_buffers.at[i], one_chunks)
        for i in range(MB)
    ]

    def tiles(i, count_rows, body):
        @pl.loop(0, count_rows // tile)
        def _(n):
            at = pl.ds(pl.multiple_of(i * count_rows + n * tile, tile), tile)
            body(at, pl.ds(pl.multiple_of(n * tile, tile), tile))

    def cross_head(i, h):
        attend_back_head(h, i, tile, cq_ref, kvc_ref, None, totc_ref, gcr_ref, gcq, dkvc, acc)

    def self_head(i, h):
        attend_back_head(h, i, tile, q_ref, kvs_ref, bias_ref, tots_ref, gatt, gq, dkvs, acc)

    def send_queries(i):
        held[t, part(i)] = gcq[part(i)]
        query_lines[i].start()

    def encoder_part(i):
        ctx_cross[i].wait_recv()

        def body(at, inner):
            total = dkvc[i, inner].astype(F32) + dkvc_in[i, inner].astype(F32)
            gkvc[at] = total.astype(BF16)
            enc_part[at] = mat_nt(
                total.astype(BF16), heads_ref[:, 2 * width : 4 * width]
            ).astype(BF16)

        tiles(i, enc_rows, body)
        enc_sums[i].start()

    def after_queries(i):
        def body(at, inner):
            grad = mat_nt(held[0, at], cq4_ref[0])
            for origin in range(1, count):
                grad = grad + mat_nt(held[origin, at], cq4_ref[origin])
            value = as_ref[at]
            scale = rms_scale(value)
            normed = value * scale
            norms[1:2] += jnp.sum(grad * normed, axis=0, keepdims=True)
            total = gac_ref[at] + rms_back(grad * gains_ref[1:2], normed, scale)
            gt_out[at] = total
            gsl[at] = total.astype(BF16)
            gatt[at] = mat(total.astype(BF16), wo_ref[...]).astype(BF16)

        tiles(i, rows, body)

    def token_part(i):
        ctx_self[i].wait_recv()

        def body(at, inner):
            total = (dkvs[i, inner].astype(F32) + dkvs_in[i, inner].astype(F32)).astype(BF16)
            gkvs[at] = total
            product = mat_nt(total, heads_ref[:, : 2 * width])
            product = product + mat_nt(gq[at], heads_ref[:, 4 * width : 5 * width])
            one_part[at] = product.astype(BF16)

        tiles(i, rows, body)
        one_sums[i].start()

    def finish_tokens(i):
        def body(at, inner):
            grad = one_sum[at].astype(F32)
            value = tok_ref[at].astype(F32)
            scale = rms_scale(value)
            normed = value * scale
            norms[0:1] += jnp.sum(grad * normed, axis=0, keepdims=True)
            gt_out[at] = gt_out[at] + rms_back(grad * gains_ref[0:1], normed, scale)

        tiles(i, rows, body)

    norms[...] = jnp.zeros_like(norms)
    steps = {
        "X": cross_head,
        "SQ": send_queries,
        "XC": lambda i: ctx_cross[i].start(),
        "QH": lambda i, d: query_lines[i].hop(d),
        "AQ": after_queries,
        "S": self_head,
        "EP": encoder_part,
        "XS": lambda i: ctx_self[i].start(),
        "TP": token_part,
        "FT": finish_tokens,
        "ERN": lambda i, j: enc_sums[i].reduce_near(j),
        "ERF": lambda i, j: enc_sums[i].reduce_far(j),
        "EBN": lambda i, j: enc_sums[i].back_near(j),
        "EBF": lambda i, j: enc_sums[i].back_far(j),
        "ORN": lambda i, j: one_sums[i].reduce_near(j),
        "ORF": lambda i, j: one_sums[i].reduce_far(j),
        "OBN": lambda i, j: one_sums[i].back_near(j),
        "OBF": lambda i, j: one_sums[i].back_far(j),
    }
    for name, *rest in BACKWARD_ORDER:
        steps[name](*rest)
    for one in query_lines + enc_sums + one_sums:
        one.finish()
    for copy in ctx_self + ctx_cross:
        copy.wait_send()


def layer_backward(operands, tokens, enc_rows, collective_id):
    count = lax.axis_size("tp")
    tok_rows, features = tokens.shape
    rows = tok_rows // MB
    enc_tree = enc_rows // MB
    width = operands[0].shape[1]
    vmem = pl.BlockSpec(memory_space=pltpu.VMEM)
    outs = [
        ((tok_rows, features), F32),
        ((enc_rows, features), BF16),
        ((tok_rows, width), BF16),
        ((enc_rows, 2 * width), BF16),
        ((tok_rows, width), BF16),
        ((tok_rows, 2 * width), BF16),
        ((tok_rows, features), BF16),
        ((8, features), F32),
    ]
    scratch = [
        ((MB, 2 * enc_tree, 2 * width), BF16),
        ((MB, enc_tree, 2 * width), BF16),
        ((MB, 2 * rows, 2 * width), BF16),
        ((MB, rows, 2 * width), BF16),
        ((2 * enc_tree, 2 * HD), F32),
        ((count, tok_rows, width), BF16),
        ((tok_rows, width), BF16),
        ((enc_rows, features), BF16),
        ((tok_rows, features), BF16),
        ((tok_rows, features), BF16),
        ((MB, 2, enc_tree // 2, features), BF16),
        ((MB, 2, rows // 2, features), BF16),
    ]
    return pl.pallas_call(
        functools.partial(layer_backward_kernel, count),
        in_specs=[vmem] * 15,
        out_specs=[vmem] * len(outs),
        out_shape=[jax.ShapeDtypeStruct(shape, kind) for shape, kind in outs],
        scratch_shapes=[pltpu.VMEM(shape, kind) for shape, kind in scratch]
        + [
            pltpu.SemaphoreType.DMA((MB, count)),
            pltpu.SemaphoreType.DMA((MB, count)),
            pltpu.SemaphoreType.DMA((MB, count)),
            pltpu.SemaphoreType.DMA((2 * MB,)),
            pltpu.SemaphoreType.DMA((2 * MB,)),
            pltpu.SemaphoreType.DMA((2 * MB, 8, 4)),
        ],
        compiler_params=pltpu.CompilerParams(
            collective_id=collective_id, has_side_effects=True, vmem_limit_bytes=VMEM_MOST
        ),
        name="layer_backward",
    )(*operands)


EXIT_ORDER = (
    (8, "ST", 0), (11, "RN", 0, 0), (13, "RN", 0, 1), (14, "RN", 0, 2), (15, "ST", 1),
    (15, "RN", 0, 3), (15, "RF", 0, 0), (17, "RN", 1, 0), (17, "RF", 0, 1), (17, "RF", 0, 2),
    (17, "RN", 1, 1), (17, "RN", 1, 2), (17, "RF", 1, 0), (18, "RF", 1, 1), (18, "BN", 0, 0),
    (19, "RF", 0, 3), (19, "RN", 1, 3), (19, "BN", 0, 1), (19, "RF", 1, 2), (19, "BF", 0, 0),
    (19, "RF", 1, 3), (19, "BN", 1, 0), (20, "BN", 1, 1), (20, "BN", 0, 2), (20, "BF", 0, 1),
    (21, "BF", 1, 0), (21, "BN", 1, 2), (21, "BF", 1, 1), (22, "BN", 0, 3), (22, "BF", 0, 2),
    (23, "BN", 1, 3), (23, "BF", 1, 2), (23, "BF", 0, 3), (23, "BF", 1, 3),
)


def exit_backward_kernel(
    count,
    valid,
    logits_ref,
    e_ref,
    x_t_ref,
    target_ref,
    log_ref,
    embed_ref,
    sum_ref,
    grads,
    acc,
    partial,
    total,
    buffers,
    sems,
):
    f, c, t = here()
    right, left = (f, c, t + 1), (f, c, t - 1)
    step = pl.program_id(0)
    size, tile = logits_ref.shape
    tiles = grads.shape[1] // tile
    sums = [
        LineSum(
            t,
            count,
            left,
            right,
            partial.at[pl.ds(p * size, size)],
            total.at[pl.ds(p * size, size)],
            buffers.at[p],
            sems.at[p],
            EXIT_CHUNKS,
        )
        for p in range(EXIT_PIECES)
    ]

    @pl.when(step == 0)
    def _():
        greet_line(t, count, left, right)

    @pl.when(step < EXIT_PIECES * tiles)
    def _():
        piece, k = step // tiles, lax.rem(step, tiles)
        lanes = lax.broadcasted_iota(jnp.int32, (size, tile), 1)
        probs = jnp.exp(logits_ref[...] - log_ref[...])
        probs = jnp.where(lanes < valid - k * tile, probs, 0.0)
        hits = jnp.where(lanes == target_ref[...] - k * tile, 1.0, 0.0)
        grad = (probs - hits).astype(BF16)
        rows = pl.ds(pl.multiple_of(piece * size, size), size)
        grads[rows, pl.ds(pl.multiple_of(k * tile, tile), tile)] = grad
        product = mat_nt(grad, e_ref[...])

        @pl.when(k == 0)
        def _():
            acc[...] = product

        @pl.when(k > 0)
        def _():
            acc[...] += product

        @pl.when(k == tiles - 1)
        def _():
            partial[rows] = acc[...].astype(BF16)

    @pl.when(step >= EXIT_PIECES * tiles)
    def _():
        k = step - EXIT_PIECES * tiles
        columns = pl.ds(pl.multiple_of(k * tile, tile), tile)
        embed_ref[...] = mat(x_t_ref[...], grads[:, columns]).astype(BF16)

    steps = {
        "ST": lambda p: sums[p].start(),
        "RN": lambda p, j: sums[p].reduce_near(j),
        "RF": lambda p, j: sums[p].reduce_far(j),
        "BN": lambda p, j: sums[p].back_near(j),
        "BF": lambda p, j: sums[p].back_far(j),
    }
    for when in sorted({item[0] for item in EXIT_ORDER}):

        @pl.when(step == when)
        def _():
            for at, name, *rest in EXIT_ORDER:
                if at == when:
                    steps[name](*rest)

    @pl.when(step == pl.num_programs(0) - 1)
    def _():
        for one in sums:
            one.finish()
        sum_ref[...] = total[...]


def exit_backward(logits, embed_t, exit_in_t, targets_local, log_total, valid, collective_id):
    rows, padded = logits.shape
    features = embed_t.shape[0]
    count = lax.axis_size("tp")
    size = rows // EXIT_PIECES
    tiles = padded // TILE
    if tiles * (EXIT_PIECES + 1) != EXIT_STEPS:
        raise ValueError("steps")

    def piece_of(i):
        return jnp.minimum(i // tiles, EXIT_PIECES - 1)

    def tile_of(i):
        return jnp.where(i < EXIT_PIECES * tiles, lax.rem(i, tiles), tiles - 1)

    column = pl.BlockSpec((size, 1), lambda i: (piece_of(i), 0))
    return pl.pallas_call(
        functools.partial(exit_backward_kernel, count, valid),
        grid=(EXIT_STEPS,),
        in_specs=[
            pl.BlockSpec((size, TILE), lambda i: (piece_of(i), tile_of(i))),
            pl.BlockSpec((features, TILE), lambda i: (0, tile_of(i))),
            pl.BlockSpec((features, rows), lambda i: (0, 0)),
            column,
            column,
        ],
        out_specs=[
            pl.BlockSpec((features, TILE), lambda i: (0, jnp.maximum(i - EXIT_PIECES * tiles, 0))),
            pl.BlockSpec((rows, features), lambda i: (0, 0)),
        ],
        out_shape=[
            jax.ShapeDtypeStruct((features, padded), BF16),
            jax.ShapeDtypeStruct((rows, features), BF16),
        ],
        scratch_shapes=[
            pltpu.VMEM((rows, padded), BF16),
            pltpu.VMEM((size, features), F32),
            pltpu.VMEM((rows, features), BF16),
            pltpu.VMEM((rows, features), BF16),
            pltpu.VMEM((EXIT_PIECES, 2, size // 2, features), BF16),
            pltpu.SemaphoreType.DMA((EXIT_PIECES, 8, EXIT_CHUNKS)),
        ],
        compiler_params=pltpu.CompilerParams(
            collective_id=collective_id, has_side_effects=True, vmem_limit_bytes=VMEM_MOST
        ),
        cost_estimate=pl.CostEstimate(
            flops=4 * rows * features * padded,
            bytes_accessed=4 * rows * padded + 4 * features * padded,
            transcendentals=rows * padded,
        ),
        name="exit_backward",
    )(logits, embed_t, exit_in_t, targets_local, log_total)


def layer_backward_plain(operands, tokens, enc_rows, collective_id):
    (
        grad_crossed,
        cross_q,
        kv_cross,
        totals_cross,
        queries,
        kv_self,
        bias,
        totals_self,
        grad_after_cross,
        after_self,
        tokens,
        w_out_own,
        c_query_all,
        heads_all,
        gains,
    ) = operands
    rows, width = queries.shape[0] // MB, queries.shape[1]
    trees = range(MB)

    def tree_rows(value, i):
        return value[i * rows : (i + 1) * rows]

    outcome = [
        attend_back(
            tree_rows(cross_q, i), kv_cross[i], None, totals_cross[i], tree_rows(grad_crossed, i)
        )
        for i in trees
    ]
    grad_cq = jnp.concatenate([o[0] for o in outcome], axis=0)
    grad_kv_cross = jnp.concatenate([ctx_scatter(o[1]) for o in outcome], axis=0)
    encoder_part = mat_nt(grad_kv_cross, heads_all[:, 2 * width : 4 * width]).astype(BF16)
    grad_two = line_project(grad_cq, c_query_all, jnp.zeros_like(after_self), 6)
    scale_two = rms_scale(after_self)
    normed_two = after_self * scale_two
    norm_cross = jnp.sum(grad_two * normed_two, axis=0)
    grad_after_self = grad_after_cross + rms_back(grad_two * gains[1:2], normed_two, scale_two)
    grad_self_low = grad_after_self.astype(BF16)
    grad_attended = mat(grad_self_low, w_out_own).astype(BF16)
    outcome = [
        attend_back(
            tree_rows(queries, i), kv_self[i], bias[i], totals_self[i], tree_rows(grad_attended, i)
        )
        for i in trees
    ]
    grad_q = jnp.concatenate([o[0] for o in outcome], axis=0)
    grad_kv_self = jnp.concatenate([ctx_scatter(o[1]) for o in outcome], axis=0)
    part = mat_nt(grad_q, heads_all[:, 4 * width : 5 * width])
    part = (part + mat_nt(grad_kv_self, heads_all[:, : 2 * width])).astype(BF16)
    both = line_sum(jnp.concatenate([part, encoder_part], axis=0), 7, 12)
    grad_one = both[: MB * rows].astype(F32)
    tok = tokens.astype(F32)
    scale_one = rms_scale(tok)
    normed_one = tok * scale_one
    norm_self = jnp.sum(grad_one * normed_one, axis=0)
    grad_tokens = grad_after_self + rms_back(grad_one * gains[0:1], normed_one, scale_one)
    norms = jnp.stack([norm_self, norm_cross] + [jnp.zeros_like(norm_self)] * 6)
    return (
        grad_tokens,
        both[MB * rows :],
        grad_cq,
        grad_kv_cross,
        grad_q,
        grad_kv_self,
        grad_self_low,
        norms,
    )


def local(
    tokens,
    encoder,
    cotangent,
    parents,
    targets,
    w_query,
    w_key,
    w_value,
    w_out,
    c_query,
    c_key,
    c_value,
    c_out,
    w_gate,
    w_up,
    w_down,
    embedding,
    norm_self,
    norm_cross,
    norm_ff,
    norm_exit,
):
    t = lax.axis_index("tp")
    tp_count = lax.axis_size("tp")
    rows = tokens.shape[0] // MB
    features = tokens.shape[1]
    width = w_query.shape[1]
    hidden_units = w_gate.shape[1]
    vocab = embedding.shape[0]
    trees = range(MB)
    shrink = 1.0 / math.sqrt(features)

    def tree_rows(value, i):
        count = value.shape[0] // MB
        return value[i * count : (i + 1) * count]

    gains_in = jnp.stack([norm_self, norm_cross, norm_ff, norm_exit], axis=1)
    heads_in = jnp.concatenate(
        [w_key, w_value, c_key, c_value, w_query]
        + [jnp.pad(gains_in, ((0, 0), (0, 60))), c_query, jnp.zeros_like(c_query[:, :64])],
        axis=1,
    )
    op_in = jnp.stack([w_out.T, c_out.T, c_query])
    ff_in = jnp.concatenate([w_gate, w_up, w_down.T], axis=1)
    padded = -(-vocab // TILE) * TILE
    embed_in = jnp.pad(embedding.T, ((0, 0), (0, padded - vocab)))
    forward = layer_forward if small_plane() else layer_forward_plain
    (
        heads_all,
        op_all,
        ff_all,
        embed_t,
        gains,
        bias,
        queries,
        kv_self,
        kv_cross,
        attended,
        totals_self,
        cross_q,
        crossed,
        totals_cross,
        after_self,
        after_cross,
    ) = forward(parents, tokens, encoder, heads_in, op_in, ff_in, embed_in, 1)
    gain_self, gain_cross = gains[0:1], gains[1:2]
    own_out = lax.dynamic_index_in_dim(op_all[:2], t, 1, False)
    w_out_own, c_out_own = own_out[0], own_out[1]
    gate_pre, up_pre, mixed, mixed_low, exit_in, exit_in_t = ff_forward(
        after_cross, gains, ff_all, tp_count, shrink
    )

    targets_local = targets - t * vocab
    inside = (targets_local >= 0) & (targets_local < vocab)
    targets_local = jnp.where(inside, targets_local, -1)[:, None]
    logits, top, summed, picked = exit_forward(exit_in, embed_t, targets_local, vocab)
    stats = jnp.stack([top, summed, picked]).reshape(3, MB * rows // 128, 128)
    top, log_total, picked = share_stats(stats, 4)
    losses = (log_total - picked).reshape(-1)
    scores = (top - log_total).reshape(-1)
    grad_embed, grad_exit = exit_backward(
        logits, embed_t, exit_in_t, targets_local, log_total.reshape(-1, 1), vocab, 5
    )
    grad_embed_own = lax.optimization_barrier(
        lax.psum_scatter(grad_embed, PLANE, scatter_dimension=0, tiled=True)
    )

    (
        grad_after_cross,
        grad_mixed_low,
        grad_cross_low,
        grad_crossed,
        hidden_three,
        activated_own,
        grad_gate_own,
        grad_up_own,
        norms,
    ) = ff_backward(
        grad_exit,
        mixed,
        cotangent,
        after_cross,
        gains,
        c_out_own,
        ff_all,
        gate_pre,
        up_pre,
        tp_count,
        shrink,
    )
    backward = layer_backward if small_plane() else layer_backward_plain
    (
        grad_tokens,
        grad_encoder,
        grad_cq,
        grad_kv_cross,
        grad_q,
        grad_kv_self,
        grad_self_low,
        norms_low,
    ) = backward(
        (
            grad_crossed,
            cross_q,
            kv_cross,
            totals_cross,
            queries,
            kv_self,
            bias,
            totals_self,
            grad_after_cross,
            after_self,
            tokens,
            w_out_own,
            op_all[2],
            heads_all,
            gains,
        ),
        tokens,
        encoder.shape[0],
        6,
    )
    tok = tokens.astype(F32)
    hidden_one = (tok * rms_scale(tok) * gain_self).astype(BF16)
    hidden_two = (after_self * rms_scale(after_self) * gain_cross).astype(BF16)

    ff_grads = jnp.concatenate(
        [
            mat_tn(hidden_three, grad_gate_own),
            mat_tn(hidden_three, grad_up_own),
            mat_tn(grad_mixed_low, activated_own),
            mat_tn(grad_cross_low, crossed),
        ],
        axis=1,
    ).astype(BF16)
    ff_own = lax.psum_scatter(ff_grads, PLANE, scatter_dimension=0, tiled=True)
    norm_block = jnp.pad(
        jnp.stack([norms_low[0], norms_low[1], norms[1], norms[0]], axis=1),
        ((0, 0), (0, 60)),
    )
    own = plane_scatter(
        jnp.concatenate(
            [
                mat_tn(hidden_one, grad_kv_self),
                mat_tn(encoder, grad_kv_cross),
                mat_tn(hidden_one, grad_q),
                norm_block,
                mat_tn(hidden_two, grad_cq),
                mat_tn(grad_self_low, attended),
            ],
            axis=1,
        ).astype(BF16),
        9,
    )

    def part(value, start, size):
        return value[:, start : start + size].astype(F32)

    base = Q2 - 64
    return (
        mixed_low,
        losses,
        scores,
        grad_tokens,
        grad_encoder.astype(F32),
        part(own, 4 * width, width),
        part(own, 0, width),
        part(own, width, width),
        part(own, Q2 + width, width).T,
        part(own, Q2, width),
        part(own, 2 * width, width),
        part(own, 3 * width, width),
        part(ff_own, 3 * hidden_units, width).T,
        part(ff_own, 0, hidden_units),
        part(ff_own, hidden_units, hidden_units),
        part(ff_own, 2 * hidden_units, hidden_units).T,
        grad_embed_own[:, :vocab].astype(F32).T,
        own[:, base],
        own[:, base + 1],
        own[:, base + 2],
        own[:, base + 3],
    )


def solution(mesh):
    rows_cols = P(PLANE, "tp")
    cols_rows = P("tp", PLANE)
    data = P(PLANE, None)
    flat = P(PLANE)
    weights = (rows_cols,) * 3 + (cols_rows,) + (rows_cols,) * 3 + (cols_rows,)
    weights += (rows_cols,) * 2 + (cols_rows,) * 2 + (flat,) * 4
    return jax.shard_map(
        local,
        mesh=mesh,
        in_specs=(data, data, data, P("fsdp", None), flat) + weights,
        out_specs=(data, flat, flat, data, data) + weights,
        check_vma=False,
    )
```

```python
import functools
import math

import jax
import jax.numpy as jnp
from jax import lax
from jax.experimental import pallas as pl
from jax.experimental.pallas import tpu as pltpu
from jax.sharding import PartitionSpec as P

HD = 64
BLK = 128
MB = 2
EPSILON = 1e-06
MASKED = -1000000000.0
F32 = jnp.float32
BF16 = jnp.bfloat16
PLANE = ("fsdp", "ctx")
VMEM_LIMIT = 48 * 1024 * 1024
MESH = pl.DeviceIdType.MESH
TILE = 1024
LOWEST = -3.0e38
VMEM_MOST = 58 * 1024 * 1024
Q2 = 1024
EXIT_PIECES = 2
EXIT_CHUNKS = 4
EXIT_STEPS = 24


def mat(left, right):
    return jnp.dot(left, right, preferred_element_type=F32)


def mat_nt(left, right):
    return lax.dot_general(left, right, (((1,), (1,)), ((), ())), preferred_element_type=F32)


def mat_tn(left, right):
    return lax.dot_general(left, right, (((0,), (0,)), ((), ())), preferred_element_type=F32)


def small_plane():
    return lax.axis_size("fsdp") == 4 and lax.axis_size("ctx") == 2


def swap(value, axis, bit):
    count = lax.axis_size(axis)
    return lax.ppermute(value, axis, [(i, i ^ bit) for i in range(count)])


def low_sum(left, right):
    return (left.astype(F32) + right.astype(F32)).astype(BF16)


def here():
    return lax.axis_index("fsdp"), lax.axis_index("ctx"), lax.axis_index("tp")


def greet(peers):
    barrier = pltpu.get_barrier_semaphore()
    for peer in peers:
        pl.semaphore_signal(barrier, inc=1, device_id=peer, device_id_type=MESH)
    pl.semaphore_wait(barrier, len(peers))


def greet_line(t, count, left, right):
    barrier = pltpu.get_barrier_semaphore()

    @pl.when(t > 0)
    def _():
        pl.semaphore_signal(barrier, inc=1, device_id=left, device_id_type=MESH)

    @pl.when(t < count - 1)
    def _():
        pl.semaphore_signal(barrier, inc=1, device_id=right, device_id_type=MESH)

    at_end = (t == 0) | (t == count - 1)
    pl.semaphore_wait(barrier, jnp.where(at_end, 1, 2).astype(jnp.int32))


def remote(src, dst, send, recv, peer):
    return pltpu.make_async_remote_copy(
        src_ref=src, dst_ref=dst, send_sem=send, recv_sem=recv, device_id=peer, device_id_type=MESH
    )


def weight_scatter_kernel(
    enc_ref,
    gkvc_ref,
    tok_ref,
    gkvs_ref,
    gq_ref,
    as_ref,
    gcq_ref,
    gsl_ref,
    att_ref,
    gains_ref,
    norms_low_ref,
    norms_ref,
    out_ref,
    hidden_one,
    hidden_two,
    norm_rows,
    x_ref,
    chip,
    core_in,
    chip_in,
    send,
    recv,
    core_send,
    core_recv,
):
    f, c, t = here()
    chips = [(2, 1), (0, 1), (2, 0)]
    peers = [(f ^ df, c ^ dc, t) for df, dc in chips]
    partner = (f ^ 1, c, t)
    greet(peers + [partner])
    features = x_ref.shape[0]
    shard = features // 8
    rows = tok_ref.shape[0]
    kv, width = gkvs_ref.shape[1], gq_ref.shape[1]
    order = chips + [(0, 0)]
    spans = [(0, kv), (kv, kv), (Q2 - 256, 256), (Q2, 2 * width)]

    def block(df, dc):
        slot = (f ^ df) * 2 + (c ^ dc)
        return pl.ds(pl.multiple_of(slot * shard, shard), shard)

    def swap_copy(g, j):
        cols = pl.ds(*spans[g])
        df, dc = order[j]
        return remote(
            x_ref.at[block(df ^ 1, dc), cols],
            core_in.at[j, :, cols],
            core_send.at[g, j],
            core_recv.at[g, j],
            partner,
        )

    def chip_copy(g, j):
        cols = pl.ds(*spans[g])
        return remote(
            chip.at[j, :, cols], chip_in.at[j, :, cols], send.at[g, j], recv.at[g, j], peers[j]
        )

    def product(left, right, start, size):
        @pl.loop(0, features // 256)
        def _(n):
            at = pl.ds(pl.multiple_of(n * 256, 256), 256)
            x_ref[at, start : start + size] = mat_tn(left[:, at], right[...]).astype(BF16)

    def swap_group(g):
        for j in range(4):
            swap_copy(g, j).start()

    def chip_group(g):
        cols = slice(spans[g][0], spans[g][0] + spans[g][1])
        for j in range(4):
            swap_copy(g, j).wait_recv()
            total = x_ref[block(*order[j]), cols].astype(F32) + core_in[j, :, cols].astype(F32)
            if j < 3:
                chip[j, :, cols] = total.astype(BF16)
                chip_copy(g, j).start()
            else:
                out_ref[:, cols] = total

    def hidden(source, gain, target):
        @pl.loop(0, rows // 256)
        def _(n):
            at = pl.ds(pl.multiple_of(n * 256, 256), 256)
            value = source[at].astype(F32)
            target[at] = (value * rms_scale(value) * gains_ref[gain : gain + 1]).astype(BF16)

    product(enc_ref, gkvc_ref, 0, kv)
    swap_group(0)
    hidden(tok_ref, 0, hidden_one)
    product(hidden_one, gkvs_ref, kv, kv)
    swap_group(1)
    chip_group(0)
    product(hidden_one, gq_ref, 2 * kv, width)
    norm_rows[...] = jnp.zeros_like(norm_rows)
    norm_rows[0:2] = norms_low_ref[0:2]
    norm_rows[2:3] = norms_ref[1:2]
    norm_rows[3:4] = norms_ref[0:1]
    x_ref[:, Q2 - 64 : Q2] = norm_rows[...].T.astype(BF16)
    swap_group(2)
    chip_group(1)
    hidden(as_ref, 1, hidden_two)
    product(hidden_two, gcq_ref, Q2, width)
    product(gsl_ref, att_ref, Q2 + width, width)
    swap_group(3)
    chip_group(2)
    chip_group(3)
    for g in range(4):
        cols = slice(spans[g][0], spans[g][0] + spans[g][1])
        for j in range(3):
            chip_copy(g, j).wait_recv()
            out_ref[:, cols] += chip_in[j, :, cols].astype(F32)
    for g in range(4):
        for j in range(4):
            swap_copy(g, j).wait_send()
        for j in range(3):
            chip_copy(g, j).wait_send()


def weight_scatter(operands, collective_id):
    features = operands[0].shape[1]
    kv, width = operands[3].shape[1], operands[4].shape[1]
    rows, shard, columns = operands[2].shape[0], features // 8, Q2 + 2 * width
    return pl.pallas_call(
        weight_scatter_kernel,
        in_specs=[pl.BlockSpec(memory_space=pltpu.VMEM)] * len(operands),
        out_specs=pl.BlockSpec(memory_space=pltpu.VMEM),
        out_shape=jax.ShapeDtypeStruct((shard, columns), F32),
        scratch_shapes=[
            pltpu.VMEM((rows, features), BF16),
            pltpu.VMEM((rows, features), BF16),
            pltpu.VMEM((64, features), F32),
            pltpu.VMEM((features, columns), BF16),
            pltpu.VMEM((3, shard, columns), BF16),
            pltpu.VMEM((4, shard, columns), BF16),
            pltpu.VMEM((3, shard, columns), BF16),
            pltpu.SemaphoreType.DMA((4, 3)),
            pltpu.SemaphoreType.DMA((4, 3)),
            pltpu.SemaphoreType.DMA((4, 4)),
            pltpu.SemaphoreType.DMA((4, 4)),
        ],
        compiler_params=pltpu.CompilerParams(
            collective_id=collective_id, has_side_effects=True, vmem_limit_bytes=VMEM_MOST
        ),
        name="weight_scatter",
    )(*operands)


def weight_scatter_plain(operands, collective_id):
    enc, gkvc, tokens, gkvs, gq, after_self, gcq, gsl, attended, gains, norms_low, norms = operands
    tok = tokens.astype(F32)
    hidden_one = (tok * rms_scale(tok) * gains[0:1]).astype(BF16)
    hidden_two = (after_self * rms_scale(after_self) * gains[1:2]).astype(BF16)
    norm_block = jnp.pad(
        jnp.stack([norms_low[0], norms_low[1], norms[1], norms[0]], axis=1), ((0, 0), (0, 60))
    )
    parts = [
        mat_tn(enc, gkvc),
        mat_tn(hidden_one, gkvs),
        mat_tn(hidden_one, gq),
        norm_block,
        mat_tn(hidden_two, gcq),
        mat_tn(gsl, attended),
    ]
    return lax.psum_scatter(
        jnp.concatenate(parts, axis=1), PLANE, scatter_dimension=0, tiled=True
    )


def line_project_kernel(
    count, chunks, x_ref, w_ref, base_ref, out_ref, held, send_right, send_left, recv
):
    f, c, t = here()
    right, left = (f, c, t + 1), (f, c, t - 1)
    greet_line(t, count, left, right)
    rows = x_ref.shape[0] // chunks

    def part(j):
        return pl.ds(j * rows, rows)

    def go(j, d, peer, origin, sems):
        src = x_ref.at[part(j)] if d == 0 else held.at[origin, part(j)]
        return remote(src, held.at[origin, part(j)], sems.at[d, j], recv.at[origin, j], peer)

    def go_right(j, d):
        return go(j, d, right, t - d, send_right)

    def go_left(j, d):
        return go(j, d, left, t + d, send_left)

    def arrived(j, origin):
        return remote(x_ref.at[part(j)], held.at[origin, part(j)], send_right.at[0, j], recv.at[origin, j], right)

    @pl.when(t < count - 1)
    def _():
        for j in range(chunks):
            go_right(j, 0).start()

    @pl.when(t > 0)
    def _():
        for j in range(chunks):
            go_left(j, 0).start()

    held[t] = x_ref[...]
    for d in range(1, count):
        for j in range(chunks):

            @pl.when(t - d >= 0)
            def _():
                arrived(j, t - d).wait_recv()
                if d < count - 1:

                    @pl.when(t < count - 1)
                    def _():
                        go_right(j, d).start()

            @pl.when(t + d < count)
            def _():
                arrived(j, t + d).wait_recv()
                if d < count - 1:

                    @pl.when(t > 0)
                    def _():
                        go_left(j, d).start()

            if d == count - 1:
                total = base_ref[part(j)]
                for origin in range(count):
                    total = total + mat_nt(held[origin, part(j)], w_ref[origin])
                out_ref[part(j)] = total

    for d in range(count - 1):
        for j in range(chunks):

            @pl.when((t - d >= 0) & (t < count - 1))
            def _():
                go_right(j, d).wait_send()

            @pl.when((t + d < count) & (t > 0))
            def _():
                go_left(j, d).wait_send()


def line_project(value, weights, base, collective_id):
    rows, width = value.shape
    count, features = weights.shape[0], weights.shape[1]
    chunks = 4
    return pl.pallas_call(
        functools.partial(line_project_kernel, count, chunks),
        in_specs=[pl.BlockSpec(memory_space=pltpu.VMEM)] * 3,
        out_specs=pl.BlockSpec(memory_space=pltpu.VMEM),
        out_shape=jax.ShapeDtypeStruct((rows, features), F32),
        scratch_shapes=[
            pltpu.VMEM((count, rows, width), BF16),
            pltpu.SemaphoreType.DMA((count, chunks)),
            pltpu.SemaphoreType.DMA((count, chunks)),
            pltpu.SemaphoreType.DMA((count, chunks)),
        ],
        compiler_params=pltpu.CompilerParams(
            collective_id=collective_id, has_side_effects=True, vmem_limit_bytes=VMEM_LIMIT
        ),
        name="line_project",
    )(value, weights, base)


def line_sum_kernel(
    count,
    chunks,
    window,
    lag,
    x_ref,
    out_ref,
    from_right,
    from_left,
    to_left,
    to_right,
    up_send,
    up_recv,
    down_send,
    down_recv,
    low_send,
    low_recv,
    high_send,
    high_recv,
):
    f, c, t = here()
    right, left = (f, c, t + 1), (f, c, t - 1)
    last = count - 1
    greet_line(t, count, left, right)
    half = x_ref.shape[0] // 2
    rows = half // chunks

    def low(j):
        return pl.ds(j * rows, rows)

    def high(j):
        return pl.ds(half + j * rows, rows)

    def down(j, own):
        src = x_ref.at[low(j)] if own else to_left.at[low(j)]
        return remote(src, from_right.at[low(j)], down_send.at[j], down_recv.at[j], left)

    def up(j, own):
        src = x_ref.at[high(j)] if own else to_right.at[low(j)]
        return remote(src, from_left.at[low(j)], up_send.at[j], up_recv.at[j], right)

    def low_back(j):
        return remote(out_ref.at[low(j)], out_ref.at[low(j)], low_send.at[j], low_recv.at[j], right)

    def high_back(j):
        return remote(
            out_ref.at[high(j)], out_ref.at[high(j)], high_send.at[j], high_recv.at[j], left
        )

    def pace(j, copy):
        if j == 0:
            for k in range(min(window, chunks)):
                copy(k, True).start()
        copy(j, True).wait_send()
        if j + window < chunks:
            copy(j + window, True).start()

    def low_step(j):
        @pl.when(t == last)
        def _():
            pace(j, down)

        @pl.when(t < last)
        def _():
            down(j, False).wait_recv()
            total = from_right[low(j)].astype(F32) + x_ref[low(j)].astype(F32)

            @pl.when(t > 0)
            def _():
                to_left[low(j)] = total.astype(BF16)
                down(j, False).start()

            @pl.when(t == 0)
            def _():
                out_ref[low(j)] = total.astype(BF16)
                low_back(j).start()

    def high_step(j):
        @pl.when(t == 0)
        def _():
            pace(j, up)

        @pl.when(t > 0)
        def _():
            up(j, False).wait_recv()
            total = from_left[low(j)].astype(F32) + x_ref[high(j)].astype(F32)

            @pl.when(t < last)
            def _():
                to_right[low(j)] = total.astype(BF16)
                up(j, False).start()

            @pl.when(t == last)
            def _():
                out_ref[high(j)] = total.astype(BF16)
                high_back(j).start()

    def low_forward(j):
        @pl.when(t > 0)
        def _():
            low_back(j).wait_recv()

            @pl.when(t < last)
            def _():
                low_back(j).start()

    def high_forward(j):
        @pl.when(t < last)
        def _():
            high_back(j).wait_recv()

            @pl.when(t > 0)
            def _():
                high_back(j).start()

    for j in range(chunks + lag):

        @pl.when(t < count // 2)
        def _():
            if j < chunks:
                high_step(j)
            if 0 <= j - 1 < chunks:
                low_step(j - 1)

        @pl.when(t >= count // 2)
        def _():
            if j < chunks:
                low_step(j)
            if 0 <= j - 1 < chunks:
                high_step(j - 1)

        if j >= lag:

            @pl.when(t < count // 2)
            def _():
                low_forward(j - lag)
                high_forward(j - lag)

            @pl.when(t >= count // 2)
            def _():
                high_forward(j - lag)
                low_forward(j - lag)

    for j in range(chunks):

        @pl.when(t > 0)
        def _():
            high_back(j).wait_send()

            @pl.when(t < last)
            def _():
                down(j, False).wait_send()

        @pl.when(t < last)
        def _():
            low_back(j).wait_send()

            @pl.when(t > 0)
            def _():
                up(j, False).wait_send()


def line_sum(partial, collective_id, chunks=4, window=2, lag=4):
    count = lax.axis_size("tp")
    rows, columns = partial.shape
    while (rows // 2) % (chunks * 16):
        chunks -= 1
    half = rows // 2
    return pl.pallas_call(
        functools.partial(line_sum_kernel, count, chunks, window, lag),
        in_specs=[pl.BlockSpec(memory_space=pltpu.VMEM)],
        out_specs=pl.BlockSpec(memory_space=pltpu.VMEM),
        out_shape=jax.ShapeDtypeStruct((rows, columns), BF16),
        scratch_shapes=[pltpu.VMEM((half, columns), BF16)] * 4
        + [pltpu.SemaphoreType.DMA((chunks,))] * 8,
        compiler_params=pltpu.CompilerParams(
            collective_id=collective_id, has_side_effects=True, vmem_limit_bytes=VMEM_LIMIT
        ),
        name="line_sum",
    )(partial)


def share_stats_kernel(count, x_ref, top_ref, log_ref, picked_ref, held, send, recv):
    f, c, t = here()
    peers = [(f, c, lax.rem(t + k, count)) for k in range(1, count)]
    greet(peers)
    copies = []
    for k in range(1, count):
        copy = remote(x_ref, held.at[t], send.at[k], recv.at[k], peers[k - 1])
        copy.start()
        copies.append(copy)
    held[t] = x_ref[...]
    for copy in copies:
        copy.wait()
    highest = functools.reduce(jnp.maximum, [held[k, 0] for k in range(count)])
    total = sum(held[k, 1] * jnp.exp(held[k, 0] - highest) for k in range(count))
    top_ref[...] = highest
    log_ref[...] = highest + jnp.log(total)
    picked_ref[...] = sum(held[k, 2] for k in range(count))


def share_stats(stats, collective_id):
    count = lax.axis_size("tp")
    shape = jax.ShapeDtypeStruct(stats.shape[1:], F32)
    return pl.pallas_call(
        functools.partial(share_stats_kernel, count),
        in_specs=[pl.BlockSpec(memory_space=pltpu.VMEM)],
        out_specs=[pl.BlockSpec(memory_space=pltpu.VMEM)] * 3,
        out_shape=[shape] * 3,
        scratch_shapes=[
            pltpu.VMEM((count,) + stats.shape, F32),
            pltpu.SemaphoreType.DMA((count,)),
            pltpu.SemaphoreType.DMA((count,)),
        ],
        compiler_params=pltpu.CompilerParams(collective_id=collective_id, has_side_effects=True),
        name="share_stats",
    )(stats)


def after(value, earlier):
    return lax.optimization_barrier((value, earlier))[0]


def tp_list(value):
    count = lax.axis_size("tp")
    return [value] + [
        lax.ppermute(value, "tp", [(i, (i + k) % count) for i in range(count)])
        for k in range(1, count)
    ]


def ctx_gather(value):
    if lax.axis_size("ctx") == 2:
        return jnp.concatenate([value, swap(value, "ctx", 1)], axis=0)
    return lax.all_gather(value, "ctx", axis=0, tiled=True)


def ctx_pair(value):
    if lax.axis_size("ctx") == 2:
        return [value, swap(value, "ctx", 1)]
    return [lax.all_gather(value, "ctx", axis=0, tiled=True)]


def ctx_join(parts):
    return jnp.concatenate(parts, axis=0)


def ctx_positions(rows):
    c, count = lax.axis_index("ctx"), lax.axis_size("ctx")
    if count == 2:
        return jnp.concatenate(
            [c * rows + jnp.arange(rows), (1 - c) * rows + jnp.arange(rows)]
        ).astype(jnp.int32)
    return jnp.arange(rows * count, dtype=jnp.int32)


def ctx_scatter(value):
    if lax.axis_size("ctx") == 2:
        rows = value.shape[0] // 2
        return low_sum(value[:rows], swap(value[rows:], "ctx", 1))
    return lax.psum_scatter(value.astype(F32), "ctx", scatter_dimension=0, tiled=True).astype(BF16)


def exit_forward_kernel(
    valid, x_ref, e_ref, target_ref, logits_ref, top_ref, sum_ref, picked_ref, m_acc, l_acc, p_acc
):
    step = pl.program_id(0)
    rows, tile = logits_ref.shape

    @pl.when(step == 0)
    def _():
        m_acc[...] = jnp.full_like(m_acc, LOWEST)
        l_acc[...] = jnp.zeros_like(l_acc)
        p_acc[...] = jnp.zeros_like(p_acc)

    lanes = lax.broadcasted_iota(jnp.int32, (rows, 128), 1)
    logits_ref[...] = mat(x_ref[...], e_ref[...])
    relative = target_ref[...] - step * tile
    limit = valid - step * tile
    groups = tile // 128
    highest = m_acc[...]
    for g in range(groups):
        cols = slice(g * 128, (g + 1) * 128)
        part = jnp.where(lanes < limit - g * 128, logits_ref[:, cols], LOWEST)
        highest = jnp.maximum(highest, part)
    total = l_acc[...] * jnp.exp(m_acc[...] - highest)
    picked = p_acc[...]
    for g in range(groups):
        cols = slice(g * 128, (g + 1) * 128)
        part = jnp.where(lanes < limit - g * 128, logits_ref[:, cols], LOWEST)
        total += jnp.exp(part - highest)
        picked += jnp.where(lanes == relative - g * 128, part, 0.0)
    m_acc[...] = highest
    l_acc[...] = total
    p_acc[...] = picked

    @pl.when(step == pl.num_programs(0) - 1)
    def _():
        top = jnp.max(m_acc[...], axis=1, keepdims=True)
        top_ref[...] = top
        sum_ref[...] = jnp.sum(l_acc[...] * jnp.exp(m_acc[...] - top), axis=1, keepdims=True)
        picked_ref[...] = jnp.sum(p_acc[...], axis=1, keepdims=True)


def exit_forward(exit_in, embed_t, targets_local, valid):
    rows, features = exit_in.shape
    padded = embed_t.shape[1]
    column = pl.BlockSpec((rows, 1), lambda i: (0, 0))
    stat = jax.ShapeDtypeStruct((rows, 1), F32)
    return pl.pallas_call(
        functools.partial(exit_forward_kernel, valid),
        grid=(padded // TILE,),
        in_specs=[
            pl.BlockSpec((rows, features), lambda i: (0, 0)),
            pl.BlockSpec((features, TILE), lambda i: (0, i)),
            column,
        ],
        out_specs=[pl.BlockSpec((rows, TILE), lambda i: (0, i)), column, column, column],
        out_shape=[jax.ShapeDtypeStruct((rows, padded), F32), stat, stat, stat],
        scratch_shapes=[pltpu.VMEM((rows, 128), F32)] * 3,
        compiler_params=pltpu.CompilerParams(vmem_limit_bytes=VMEM_LIMIT),
        cost_estimate=pl.CostEstimate(
            flops=2 * rows * features * padded,
            bytes_accessed=4 * rows * padded + 2 * features * padded,
            transcendentals=rows * padded,
        ),
        name="exit_forward",
    )(exit_in, embed_t, targets_local)


def forward_kernel(heads, q_ref, kv_ref, bias_ref, out_ref, total_ref):
    width = heads * HD
    for h in range(heads):
        cols = slice(h * HD, (h + 1) * HD)
        keys = kv_ref[:, cols]
        values = kv_ref[:, width + h * HD : width + (h + 1) * HD]
        scores = mat_nt(keys, q_ref[:, cols])
        if bias_ref is not None:
            scores = scores + bias_ref[...]
        highest = jnp.max(scores, axis=0, keepdims=True)
        exponent = jnp.exp(scores - highest)
        denominator = jnp.sum(exponent, axis=0, keepdims=True)
        outcome = mat_tn(values, exponent.astype(BF16)) / denominator
        out_ref[:, cols] = outcome.T.astype(BF16)
        total_ref[h : h + 1, :] = highest + jnp.log(denominator)


def backward_kernel(
    heads, q_ref, kv_ref, bias_ref, total_ref, go_ref, dq_ref, dkv_ref, acc_ref
):
    width = heads * HD
    step = pl.program_id(0)

    @pl.when(step == 0)
    def _():
        acc_ref[...] = jnp.zeros_like(acc_ref)

    for h in range(heads):
        cols = slice(h * HD, (h + 1) * HD)
        vcols = slice(width + h * HD, width + (h + 1) * HD)
        keys, values = kv_ref[:, cols], kv_ref[:, vcols]
        queries, go = q_ref[:, cols], go_ref[:, cols]
        scores = mat_nt(keys, queries)
        if bias_ref is not None:
            scores = scores + bias_ref[...]
        probs = jnp.exp(scores - total_ref[h : h + 1, :])
        grad_probs = mat_nt(values, go)
        inner = jnp.sum(probs * grad_probs, axis=0, keepdims=True)
        grad_scores = (probs * (grad_probs - inner)).astype(BF16)
        acc_ref[:, vcols] += mat(probs.astype(BF16), go)
        acc_ref[:, cols] += mat(grad_scores, queries)
        dq_ref[:, cols] = mat_tn(keys, grad_scores).T.astype(BF16)

    @pl.when(step == pl.num_programs(0) - 1)
    def _():
        dkv_ref[...] = acc_ref[...].astype(BF16)


def attention_specs(rows, width, keys, tile, masked):
    specs = [
        pl.BlockSpec((tile, width), lambda i: (i, 0)),
        pl.BlockSpec((keys, 2 * width), lambda i: (0, 0)),
    ]
    if masked:
        specs.append(pl.BlockSpec((keys, tile), lambda i: (0, i)))
    return specs


def attend(queries, kv, bias):
    rows, width = queries.shape
    keys, heads = kv.shape[0], width // HD
    tile = min(rows, 256)
    masked = bias is not None
    body = functools.partial(forward_kernel, heads)
    if not masked:
        plain = body
        body = lambda q, k, o, t: plain(q, k, None, o, t)
    return pl.pallas_call(
        body,
        grid=(rows // tile,),
        in_specs=attention_specs(rows, width, keys, tile, masked),
        out_specs=[
            pl.BlockSpec((tile, width), lambda i: (i, 0)),
            pl.BlockSpec((heads, tile), lambda i: (0, i)),
        ],
        out_shape=[
            jax.ShapeDtypeStruct((rows, width), BF16),
            jax.ShapeDtypeStruct((heads, rows), F32),
        ],
        compiler_params=pltpu.CompilerParams(vmem_limit_bytes=VMEM_LIMIT),
        cost_estimate=pl.CostEstimate(
            flops=16 * rows * keys * width,
            bytes_accessed=4 * keys * width + 8 * rows * width,
            transcendentals=rows * keys * heads,
        ),
        name="attend_masked" if masked else "attend",
    )(*([queries, kv, bias] if masked else [queries, kv]))


def attend_back(queries, kv, bias, totals, go):
    rows, width = queries.shape
    keys, heads = kv.shape[0], width // HD
    tile = min(rows, 256)
    masked = bias is not None
    body = functools.partial(backward_kernel, heads)
    if not masked:
        plain = body
        body = lambda q, k, *rest: plain(q, k, None, *rest)
    specs = attention_specs(rows, width, keys, tile, masked) + [
        pl.BlockSpec((heads, tile), lambda i: (0, i)),
        pl.BlockSpec((tile, width), lambda i: (i, 0)),
    ]
    operands = ([queries, kv, bias] if masked else [queries, kv]) + [totals, go]
    return pl.pallas_call(
        body,
        grid=(rows // tile,),
        in_specs=specs,
        out_specs=[
            pl.BlockSpec((tile, width), lambda i: (i, 0)),
            pl.BlockSpec((keys, 2 * width), lambda i: (0, 0)),
        ],
        out_shape=[
            jax.ShapeDtypeStruct((rows, width), BF16),
            jax.ShapeDtypeStruct((keys, 2 * width), BF16),
        ],
        scratch_shapes=[pltpu.VMEM((keys, 2 * width), F32)],
        compiler_params=pltpu.CompilerParams(vmem_limit_bytes=VMEM_LIMIT),
        cost_estimate=pl.CostEstimate(
            flops=40 * rows * keys * width,
            bytes_accessed=8 * keys * width + 10 * rows * width,
            transcendentals=rows * keys * heads,
        ),
        name="attend_back_masked" if masked else "attend_back",
    )(*operands)


def rms_scale(values):
    return lax.rsqrt(jnp.mean(values * values, axis=-1, keepdims=True) + EPSILON)


def rms_back(grad_normed, normed, scale):
    return scale * (grad_normed - normed * jnp.mean(grad_normed * normed, axis=-1, keepdims=True))


def mask_bias(parent_row, row_count):
    block_count = parent_row.shape[0]
    blocks = jnp.arange(block_count, dtype=jnp.int32)
    current = blocks
    reachable = blocks[:, None] == blocks[None, :]
    for _ in range(block_count - 1):
        current = jnp.sum(
            jnp.where(current[:, None] == blocks[None, :], parent_row[None, :], 0), axis=1
        )
        reachable = reachable | (current[:, None] == blocks[None, :])
    query_pos = lax.axis_index("ctx") * row_count + jnp.arange(row_count, dtype=jnp.int32)
    key_pos = ctx_positions(row_count)
    query_onehot = (query_pos[:, None] // BLK == blocks[None, :]).astype(F32)
    key_onehot = (key_pos[:, None] // BLK == blocks[None, :]).astype(F32)
    linked = mat_nt(key_onehot, mat(query_onehot, reachable.astype(F32))) > 0.5
    causal = (query_pos[None, :] // BLK != key_pos[:, None] // BLK) | (
        key_pos[:, None] <= query_pos[None, :]
    )
    return jnp.where(linked & causal, 0.0, MASKED)


def gelu_parts(gate):
    root = math.sqrt(2.0 / math.pi)
    inner = jnp.tanh(root * (gate + 0.044715 * gate * gate * gate))
    value = 0.5 * gate * (1.0 + inner)
    slope = 0.5 * (1.0 + inner) + 0.5 * gate * (1.0 - inner * inner) * root * (
        1.0 + 3.0 * 0.044715 * gate * gate
    )
    return value, slope


FORWARD_ORDER = (
    ("GX", "h"), ("CP",), ("FL", 0), ("GY", "h"), ("OL", 0), ("GX", "e0"), ("GA", "h"),
    ("GY", "e2"), ("GF", "h"), ("GX", "e2"), ("OL", 1), ("FL", 1), ("GD", "h"), ("GY", "e0"),
    ("GE", "h"), ("GF", "e0"), ("GF", "e2"), ("OL", 2), ("PT", 1), ("CS", 1), ("FL", 2),
    ("PT", 0), ("BI",), ("OL", 3), ("CS", 0), ("GX", "e1"), ("GA", "e2"), ("PE", 1), ("FL", 3),
    ("WS", 1), ("GY", "o"), ("PE", 0), ("GX", "o"), ("S", 1, 0), ("S", 1, 1), ("S", 1, 2),
    ("WS", 0), ("GY", "e1"), ("GA", "o"), ("S", 0, 0), ("AL", 1), ("CC", 0), ("AH", 1, 1),
    ("GA", "e0"), ("S", 0, 1), ("GF", "o"), ("S", 0, 2), ("AH", 1, 2), ("AL", 0), ("GD", "o"),
    ("CC", 1), ("GY", "f0"), ("GX", "f0"), ("AH", 0, 1), ("AH", 0, 2), ("AH", 0, 3), ("GE", "o"),
    ("GX", "f1"), ("OS", 0), ("WC", 0), ("AH", 1, 3), ("GD", "e0"), ("GA", "f0"), ("X", 0, 0),
    ("X", 0, 1), ("GF", "e1"), ("X", 0, 2), ("BL", 0), ("OS", 1), ("WC", 1), ("GY", "f1"),
    ("X", 1, 0), ("BH", 0, 1), ("GF", "f0"), ("GF", "f1"), ("GE", "e0"), ("GA", "e1"),
    ("X", 1, 1), ("GD", "e2"), ("X", 1, 2), ("BL", 1), ("GD", "e1"), ("BH", 0, 2), ("BH", 0, 3),
    ("GE", "e2"), ("OC", 0), ("BH", 1, 1), ("GD", "f0"), ("BH", 1, 2), ("GA", "f1"), ("GD", "f1"),
    ("BH", 1, 3), ("GE", "e1"), ("GE", "f0"), ("OC", 1), ("GE", "f1"),
)
EMBED_PIECES = ((2816, "xy"), (2816, "xy"), (2560, "yx"))


class Line:
    def __init__(self, t, count, left, right, own, place, sems):
        self.t, self.count, self.left, self.right = t, count, left, right
        self.own, self.place = own, place
        self.to_right, self.to_left, self.recv = sems

    def copy(self, d, way):
        origin = self.t - d if way == 0 else self.t + d
        sems, peer = (self.to_right, self.right) if way == 0 else (self.to_left, self.left)
        src = self.own if d == 0 else self.place(origin)
        return remote(src, self.place(origin), sems.at[d], self.recv.at[origin], peer)

    def landed(self, origin):
        return remote(
            self.place(origin),
            self.place(origin),
            self.to_right.at[0],
            self.recv.at[origin],
            self.right,
        )

    def start(self):
        @pl.when(self.t < self.count - 1)
        def _():
            self.copy(0, 0).start()

        @pl.when(self.t > 0)
        def _():
            self.copy(0, 1).start()

    def hop(self, d):
        t, last = self.t, self.count - 1

        @pl.when(t - d >= 0)
        def _():
            self.landed(t - d).wait_recv()
            if d < last:

                @pl.when(t < last)
                def _():
                    self.copy(d, 0).start()

        @pl.when(t + d <= last)
        def _():
            self.landed(t + d).wait_recv()
            if d < last:

                @pl.when(t > 0)
                def _():
                    self.copy(d, 1).start()

    def finish(self):
        t, last = self.t, self.count - 1
        for d in range(last):

            @pl.when((t - d >= 0) & (t < last))
            def _():
                self.copy(d, 0).wait_send()

            @pl.when((t + d <= last) & (t > 0))
            def _():
                self.copy(d, 1).wait_send()


class Spread:
    def __init__(self, peers, own, blocks, send, recv):
        first_peer, second_peer, core_peer = peers
        home, across, aside, diagonal = blocks
        moves = [
            (own, home, first_peer),
            (own, home, second_peer),
            (across, across, second_peer),
            (own, home, core_peer),
            (across, across, core_peer),
            (aside, aside, core_peer),
            (diagonal, diagonal, core_peer),
        ]
        self.copies = [
            remote(src, dst, send.at[j], recv.at[j], peer)
            for j, (src, dst, peer) in enumerate(moves)
        ]

    def start_first(self):
        self.copies[0].start()

    def start_second(self):
        self.copies[1].start()
        self.copies[3].start()

    def pass_across(self):
        self.copies[0].wait_recv()
        self.copies[2].start()
        self.copies[4].start()

    def pass_aside(self):
        self.copies[1].wait_recv()
        self.copies[5].start()

    def pass_diagonal(self):
        self.copies[2].wait_recv()
        self.copies[6].start()

    def arrive(self):
        for j in (3, 4, 5, 6):
            self.copies[j].wait_recv()

    def finish(self):
        for copy in self.copies:
            copy.wait_send()


def attend_head(h, i, tile, q_ref, kv_ref, bias_ref, out_ref, total_ref):
    rows, width = q_ref.shape[0] // MB, q_ref.shape[1]
    cols = slice(h * HD, (h + 1) * HD)
    vcols = slice(width + h * HD, width + (h + 1) * HD)

    @pl.loop(0, rows // tile)
    def _(n):
        at = pl.ds(pl.multiple_of(i * rows + n * tile, tile), tile)
        here_at = pl.ds(pl.multiple_of(n * tile, tile), tile)
        scores = mat_nt(kv_ref[i, :, cols], q_ref[at, cols])
        if bias_ref is not None:
            scores = scores + bias_ref[i, :, here_at]
        highest = jnp.max(scores, axis=0, keepdims=True)
        exponent = jnp.exp(scores - highest)
        denominator = jnp.sum(exponent, axis=0, keepdims=True)
        outcome = mat_tn(kv_ref[i, :, vcols], exponent.astype(BF16)) / denominator
        out_ref[at, cols] = outcome.T.astype(BF16)
        total_ref[i, h : h + 1, here_at] = highest + jnp.log(denominator)


def build_bias(parents_ref, bias_ref, c):
    trees, keys, rows = bias_ref.shape
    mine = rows // BLK
    block_count = keys // BLK
    key_iota = lax.broadcasted_iota(jnp.int32, (BLK, BLK), 0)
    query_iota = lax.broadcasted_iota(jnp.int32, (BLK, BLK), 1)
    causal = jnp.where(key_iota <= query_iota, 0.0, MASKED)
    for i in range(trees):
        lines = [jnp.int32(1)]
        for b in range(1, block_count):
            parent = parents_ref[i, b]
            line = jnp.int32(1 << b)
            for j in range(b):
                line = line + jnp.where(parent == j, lines[j], 0)
            lines.append(line)
        for q in range(mine):
            line = jnp.int32(0)
            for b in range(block_count):
                line = line + jnp.where(c * mine + q == b, lines[b], 0)
            for k in range(block_count):
                at = (slice(k * BLK, (k + 1) * BLK), slice(q * BLK, (q + 1) * BLK))
                if k == q:
                    bias_ref[(i,) + at] = causal.astype(BF16)
                    continue
                block = c * mine + k if k < mine else (1 - c) * mine + k - mine
                seen = lax.shift_right_logical(line, block) & 1
                value = jnp.where(seen == 1, 0.0, MASKED)
                bias_ref[(i,) + at] = jnp.full((BLK, BLK), value, F32).astype(BF16)


def layer_forward_kernel(
    count, parents_ref, tok_ref, enc_ref, heads_in, op_in, ff_in, embed_in, *refs
):
    ff_all, embed_all = refs[:2]
    results, staged = refs[2:17], refs[17:32]
    (
        heads_all,
        own_out,
        query_all,
        gains_out,
        bias,
        q_out,
        kvs,
        kvc,
        att,
        tots,
        cq,
        as_out,
        crs,
        totc,
        ac_out,
    ) = staged
    (
        op_all,
        zop,
        zff,
        held_s,
        held_c,
        spread_send,
        spread_recv,
        line_right,
        line_left,
        line_recv,
        ctx_send,
        ctx_recv,
        local_sem,
    ) = refs[32:]
    f, c, t = here()
    right, left = (f, c, t + 1), (f, c, t - 1)
    x_peer, y_peer, core_peer = (f, 1 - c, t), (f ^ 2, c, t), (f ^ 1, c, t)
    rows, enc_rows = tok_ref.shape[0] // MB, enc_ref.shape[0] // MB
    width = q_out.shape[1]
    shard, ff_cols = ff_in.shape
    tile = 256

    barrier = pltpu.get_barrier_semaphore()
    for peer in (x_peer, y_peer, core_peer):
        pl.semaphore_signal(barrier, inc=1, device_id=peer, device_id_type=MESH)

    @pl.when(t > 0)
    def _():
        pl.semaphore_signal(barrier, inc=1, device_id=left, device_id_type=MESH)

    @pl.when(t < count - 1)
    def _():
        pl.semaphore_signal(barrier, inc=1, device_id=right, device_id_type=MESH)

    at_end = (t == 0) | (t == count - 1)
    pl.semaphore_wait(barrier, jnp.where(at_end, 4, 5).astype(jnp.int32))

    def block(df, dc):
        slot = (f ^ df) * 2 + (c ^ dc)
        return pl.ds(pl.multiple_of(slot * shard, shard), shard)

    def spread(j, way, own, place):
        blocks = [place(block(df, dc)) for df, dc in ((0, 0), (0, 1), (2, 0), (2, 1))]
        peers = (x_peer, y_peer, core_peer)
        if way == "yx":
            blocks = [blocks[0], blocks[2], blocks[1], blocks[3]]
            peers = (y_peer, x_peer, core_peer)
        return Spread(peers, own, blocks, spread_send.at[j], spread_recv.at[j])

    def line(j, own, place):
        sems = (line_right.at[j], line_left.at[j], line_recv.at[j])
        return Line(t, count, left, right, own, place, sems)

    def part(i):
        return pl.ds(i * rows, rows)

    def ff_place(origin):
        return zff.at[:, pl.ds(pl.multiple_of(origin * ff_cols, 128), ff_cols)]

    op_line = line(0, op_in, lambda origin: zop.at[:, origin])
    ff_line = line(1, ff_in, ff_place)
    spreads = {
        "h": spread(0, "xy", heads_in, lambda at: heads_all.at[at]),
        "o": spread(1, "xy", zop, lambda at: op_all.at[:, :, at]),
    }
    ff_half = zff.shape[1] // 2
    pieces = [("f0", "xy", zff, ff_all, 0, ff_half), ("f1", "yx", zff, ff_all, ff_half, ff_half)]
    start = 0
    for j, (size, way) in enumerate(EMBED_PIECES):
        pieces.append(("e%d" % j, way, embed_in, embed_all, start, size))
        start += size
    for name, way, own, target, first, size in pieces:
        cols = pl.ds(first, size)
        spreads[name] = spread(
            len(spreads), way, own.at[:, cols], lambda at, ref=target, cols=cols: ref.at[at, cols]
        )
    ff_own = pltpu.make_async_copy(zff, ff_all.at[block(0, 0)], local_sem.at[0])
    embed_own = pltpu.make_async_copy(embed_in, embed_all.at[block(0, 0)], local_sem.at[1])
    self_lines = [
        line(2 + i, att.at[part(i)], lambda origin, i=i: held_s.at[origin, part(i)])
        for i in range(MB)
    ]
    cross_lines = [
        line(4 + i, crs.at[part(i)], lambda origin, i=i: held_c.at[origin, part(i)])
        for i in range(MB)
    ]

    def ctx_copy(j, ref, i, size):
        return remote(
            ref.at[i, pl.ds(0, size)],
            ref.at[i, pl.ds(size, size)],
            ctx_send.at[j],
            ctx_recv.at[j],
            x_peer,
        )

    ctx_self = [ctx_copy(i, kvs, i, rows) for i in range(MB)]
    ctx_cross = [ctx_copy(2 + i, kvc, i, enc_rows) for i in range(MB)]

    def project_tokens(i):
        @pl.loop(0, rows // tile)
        def _(n):
            at = pl.ds(pl.multiple_of(i * rows + n * tile, tile), tile)
            value = tok_ref[at].astype(F32)
            hidden = (value * rms_scale(value) * gains_out[0:1]).astype(BF16)
            q_out[at] = mat(hidden, heads_all[:, 4 * width : 5 * width]).astype(BF16)
            inner = pl.ds(pl.multiple_of(n * tile, tile), tile)
            kvs[i, inner] = mat(hidden, heads_all[:, : 2 * width]).astype(BF16)

    def project_encoder(i):
        @pl.loop(0, enc_rows // tile)
        def _(n):
            at = pl.ds(pl.multiple_of(i * enc_rows + n * tile, tile), tile)
            inner = pl.ds(pl.multiple_of(n * tile, tile), tile)
            kvc[i, inner] = mat(enc_ref[at], heads_all[:, 2 * width : 4 * width]).astype(BF16)

    def self_head(i, h):
        attend_head(h, i, tile, q_out, kvs, bias, att, tots)

    def cross_head(i, h):
        attend_head(h, i, tile, cq, kvc, None, crs, totc)

    def out_self(i):
        @pl.loop(0, rows // tile)
        def _(n):
            at = pl.ds(pl.multiple_of(i * rows + n * tile, tile), tile)
            total = tok_ref[at].astype(F32)
            for origin in range(count):
                total = total + mat_nt(held_s[origin, at], op_all[0, origin])
            as_out[at] = total
            hidden = (total * rms_scale(total) * gains_out[1:2]).astype(BF16)
            cq[at] = mat(hidden, heads_all[:, Q2 : Q2 + width]).astype(BF16)

    def out_cross(i):
        @pl.loop(0, rows // tile)
        def _(n):
            at = pl.ds(pl.multiple_of(i * rows + n * tile, tile), tile)
            total = as_out[at]
            for origin in range(count):
                total = total + mat_nt(held_c[origin, at], op_all[1, origin])
            ac_out[at] = total

    def own_parts():
        heads_all[block(0, 0)] = heads_in[...]
        zop[:, t] = op_in[...]
        zff[:, pl.ds(pl.multiple_of(t * ff_cols, 128), ff_cols)] = ff_in[...]
        embed_own.start()

    def gather_done(name):
        spreads[name].arrive()
        if name == "h":
            gains_out[...] = heads_all[:, Q2 - 128 : Q2].astype(F32).T[64:72]

    def gather_first(name):
        spreads[name].start_first()
        if name == "o":
            op_all[:, :, block(0, 0)] = zop[...]
        if name == "f0":
            ff_own.start()

    def along(one, d):
        if d == 0:
            one.start()
        else:
            one.hop(d)

    def send_self(i):
        held_s[t, part(i)] = att[part(i)]
        self_lines[i].start()

    def send_cross(i):
        held_c[t, part(i)] = crs[part(i)]
        cross_lines[i].start()

    steps = {
        "GX": gather_first,
        "GY": lambda name: spreads[name].start_second(),
        "GF": lambda name: spreads[name].pass_across(),
        "GA": lambda name: spreads[name].pass_aside(),
        "GD": lambda name: spreads[name].pass_diagonal(),
        "GE": gather_done,
        "OL": lambda d: along(op_line, d),
        "FL": lambda d: along(ff_line, d),
        "CP": own_parts,
        "BI": lambda: build_bias(parents_ref, bias, c),
        "PT": project_tokens,
        "PE": project_encoder,
        "CS": lambda i: ctx_self[i].start(),
        "CC": lambda i: ctx_cross[i].start(),
        "WS": lambda i: ctx_self[i].wait_recv(),
        "WC": lambda i: ctx_cross[i].wait_recv(),
        "S": self_head,
        "X": cross_head,
        "AL": send_self,
        "AH": lambda i, d: self_lines[i].hop(d),
        "BL": send_cross,
        "BH": lambda i, d: cross_lines[i].hop(d),
        "OS": out_self,
        "OC": out_cross,
    }
    leaving = [
        pltpu.make_async_copy(src, dst, local_sem.at[2 + j])
        for j, (src, dst) in enumerate(zip(staged, results))
    ]
    ready = {("OS", 1), ("WC", 1), ("WC", 0), ("GE", "o")}
    for name, *rest in FORWARD_ORDER:
        steps[name](*rest)
        if (name, *rest) in ready:
            ready.remove((name, *rest))
            if not ready:
                own_out[...] = op_all[:2, t]
                query_all[...] = op_all[2]
                for copy in leaving[:12]:
                    copy.start()
    for copy in leaving[12:]:
        copy.start()
    for one in list(spreads.values()) + [op_line, ff_line] + self_lines + cross_lines:
        one.finish()
    for copy in ctx_self + ctx_cross:
        copy.wait_send()
    ff_own.wait()
    embed_own.wait()
    for copy in leaving:
        copy.wait()


def layer_forward(parents, tokens, encoder, heads_in, op_in, ff_in, embed_in, collective_id):
    count = lax.axis_size("tp")
    tok_rows, features = tokens.shape
    enc_rows = encoder.shape[0]
    shard, ff_cols = ff_in.shape
    width = op_in.shape[2]
    nh = width // HD
    rows = tok_rows // MB
    vmem = pl.BlockSpec(memory_space=pltpu.VMEM)
    anywhere = pl.BlockSpec(memory_space=pl.ANY)

    def low(*shape):
        return jax.ShapeDtypeStruct(shape, BF16)

    def full(*shape):
        return jax.ShapeDtypeStruct(shape, F32)

    results = [
        low(features, heads_in.shape[1]),
        low(2, features, width),
        low(count, features, width),
        full(8, features),
        low(MB, 2 * rows, rows),
        low(tok_rows, width),
        low(MB, 2 * rows, 2 * width),
        low(MB, enc_rows, 2 * width),
        low(tok_rows, width),
        full(MB, nh, rows),
        low(tok_rows, width),
        full(tok_rows, features),
        low(tok_rows, width),
        full(MB, nh, rows),
        full(tok_rows, features),
    ]
    outcome = pl.pallas_call(
        functools.partial(layer_forward_kernel, count),
        in_specs=[pl.BlockSpec(memory_space=pltpu.SMEM)] + [vmem] * 5 + [anywhere],
        out_specs=[anywhere] * 17,
        out_shape=[low(features, count * ff_cols), low(features, embed_in.shape[1])] + results,
        scratch_shapes=[pltpu.VMEM(r.shape, r.dtype) for r in results]
        + [
            pltpu.VMEM((3, count, features, width), BF16),
            pltpu.VMEM((3, count, shard, width), BF16),
            pltpu.VMEM((shard, count * ff_cols), BF16),
            pltpu.VMEM((count, tok_rows, width), BF16),
            pltpu.VMEM((count, tok_rows, width), BF16),
            pltpu.SemaphoreType.DMA((4 + len(EMBED_PIECES), 7)),
            pltpu.SemaphoreType.DMA((4 + len(EMBED_PIECES), 7)),
            pltpu.SemaphoreType.DMA((6, count)),
            pltpu.SemaphoreType.DMA((6, count)),
            pltpu.SemaphoreType.DMA((6, count)),
            pltpu.SemaphoreType.DMA((4,)),
            pltpu.SemaphoreType.DMA((4,)),
            pltpu.SemaphoreType.DMA((17,)),
        ],
        compiler_params=pltpu.CompilerParams(
            collective_id=collective_id, has_side_effects=True, vmem_limit_bytes=VMEM_MOST
        ),
        name="layer_forward",
    )(parents, tokens, encoder, heads_in, op_in, ff_in, embed_in)
    ff_all, embed_all, heads_all, own_out, query_all, gains, bias, q, kvs, kvc = outcome[:10]
    att, tots, cq, after_self, crs, totc, after_cross = outcome[10:]
    gathered = (heads_all, own_out, query_all, ff_all, embed_all, gains)
    return gathered + (bias, q, kvs, kvc, att, tots, cq, crs, totc, after_self, after_cross)


def ff_forward_kernel(
    shrink, ac_ref, gains_ref, w_ref, gate_ref, up_ref, mixed_ref, low_ref, exit_ref, exit_t_ref, h_acc
):
    step = pl.program_id(0)
    rows = ac_ref.shape[0]
    units = gate_ref.shape[1]
    tile = min(rows, 512)

    @pl.loop(0, rows // tile)
    def _(n):
        at = pl.ds(pl.multiple_of(n * tile, tile), tile)

        @pl.when(step == 0)
        def _():
            value = ac_ref[at]
            h_acc[at] = (value * rms_scale(value) * gains_ref[2:3]).astype(BF16)
            mixed_ref[at] = value

        hidden = h_acc[at]
        gate = mat(hidden, w_ref[:, :units])
        up = mat(hidden, w_ref[:, units : 2 * units])
        gate_ref[at] = gate
        up_ref[at] = up
        activated = (gelu_parts(gate)[0] * up).astype(BF16)
        mixed_ref[at] += mat_nt(activated, w_ref[:, 2 * units :])

        @pl.when(step == pl.num_programs(0) - 1)
        def _():
            value = mixed_ref[at]
            low_ref[at] = value.astype(BF16)
            exit_in = value * rms_scale(value) * gains_ref[3:4] * shrink
            exit_ref[at] = exit_in.astype(BF16)

    @pl.when(step == pl.num_programs(0) - 1)
    def _():
        exit_t_ref[...] = exit_ref[...].T


def ff_forward(after_cross, gains, ff_all, count, shrink):
    rows, features = after_cross.shape
    cols = ff_all.shape[1] // count
    units = cols // 3

    def fixed(*shape):
        return pl.BlockSpec(shape, lambda i: (0,) * len(shape))

    moving = pl.BlockSpec((rows, units), lambda i: (0, i))
    return pl.pallas_call(
        functools.partial(ff_forward_kernel, shrink),
        grid=(count,),
        in_specs=[
            fixed(rows, features),
            fixed(8, features),
            pl.BlockSpec((features, cols), lambda i: (0, i)),
        ],
        out_specs=[moving, moving] + [fixed(rows, features)] * 3 + [fixed(features, rows)],
        out_shape=[
            jax.ShapeDtypeStruct((rows, count * units), F32),
            jax.ShapeDtypeStruct((rows, count * units), F32),
            jax.ShapeDtypeStruct((rows, features), F32),
            jax.ShapeDtypeStruct((rows, features), BF16),
            jax.ShapeDtypeStruct((rows, features), BF16),
            jax.ShapeDtypeStruct((features, rows), BF16),
        ],
        scratch_shapes=[pltpu.VMEM((rows, features), BF16)],
        compiler_params=pltpu.CompilerParams(vmem_limit_bytes=VMEM_MOST),
        cost_estimate=pl.CostEstimate(
            flops=2 * rows * features * count * cols,
            bytes_accessed=2 * features * count * cols + 8 * rows * count * units,
            transcendentals=rows * count * units,
        ),
        name="ff_forward",
    )(after_cross, gains, ff_all)


def ff_backward_kernel(
    shrink,
    ge_ref,
    mixed_ref,
    cot_ref,
    ac_ref,
    gains_ref,
    co_ref,
    w_ref,
    gate_ref,
    up_ref,
    gac_ref,
    low_ref,
    gcl_ref,
    gcr_ref,
    hid_ref,
    act_ref,
    gg_ref,
    gu_ref,
    norms_ref,
    acc,
):
    step = pl.program_id(0)
    t = lax.axis_index("tp")
    last = pl.num_programs(0) - 1
    rows = ac_ref.shape[0]
    units = gate_ref.shape[1]
    tile = min(rows, 512)

    @pl.when(step == 0)
    def _():
        norms_ref[...] = jnp.zeros_like(norms_ref)

    @pl.loop(0, rows // tile)
    def _(n):
        at = pl.ds(pl.multiple_of(n * tile, tile), tile)

        @pl.when(step == 0)
        def _():
            grad_exit = ge_ref[at].astype(F32) * shrink
            mixed = mixed_ref[at]
            scale = rms_scale(mixed)
            normed = mixed * scale
            norms_ref[0:1] += jnp.sum(grad_exit * normed, axis=0, keepdims=True)
            grad_mixed = cot_ref[at].astype(F32) + rms_back(
                grad_exit * gains_ref[3:4], normed, scale
            )
            gac_ref[at] = grad_mixed
            low_ref[at] = grad_mixed.astype(BF16)
            value = ac_ref[at]
            hid_ref[at] = (value * rms_scale(value) * gains_ref[2:3]).astype(BF16)
            acc[at] = jnp.zeros_like(acc[at])

        gate = gate_ref[at]
        up = up_ref[at]
        grad_act = mat(low_ref[at], w_ref[:, 2 * units :])
        value, slope = gelu_parts(gate)
        grad_gate = (grad_act * slope * up).astype(BF16)
        grad_up = (grad_act * value).astype(BF16)
        acc[at] += mat_nt(grad_gate, w_ref[:, :units]) + mat_nt(
            grad_up, w_ref[:, units : 2 * units]
        )

        @pl.when(step == t)
        def _():
            act_ref[at] = (value * up).astype(BF16)
            gg_ref[at] = grad_gate
            gu_ref[at] = grad_up

        @pl.when(step == last)
        def _():
            value = ac_ref[at]
            scale = rms_scale(value)
            normed = value * scale
            grad = acc[at]
            norms_ref[1:2] += jnp.sum(grad * normed, axis=0, keepdims=True)
            total = gac_ref[at] + rms_back(grad * gains_ref[2:3], normed, scale)
            gac_ref[at] = total
            gcl_ref[at] = total.astype(BF16)
            gcr_ref[at] = mat(total.astype(BF16), co_ref[...]).astype(BF16)


def ff_backward(
    grad_exit, mixed, cotangent, after_cross, gains, c_out_own, ff_all, gate, up, count, shrink
):
    rows, features = after_cross.shape
    cols = ff_all.shape[1] // count
    units = cols // 3
    width = c_out_own.shape[1]

    def fixed(*shape):
        return pl.BlockSpec(shape, lambda i: (0,) * len(shape))

    def low(*shape):
        return jax.ShapeDtypeStruct(shape, BF16)

    moving = pl.BlockSpec((rows, units), lambda i: (0, i))
    return pl.pallas_call(
        functools.partial(ff_backward_kernel, shrink),
        grid=(count,),
        in_specs=[fixed(rows, features)] * 4
        + [
            fixed(8, features),
            fixed(features, width),
            pl.BlockSpec((features, cols), lambda i: (0, i)),
            moving,
            moving,
        ],
        out_specs=[fixed(rows, features)] * 3
        + [fixed(rows, width), fixed(rows, features)]
        + [fixed(rows, units)] * 3
        + [fixed(8, features)],
        out_shape=[
            jax.ShapeDtypeStruct((rows, features), F32),
            low(rows, features),
            low(rows, features),
            low(rows, width),
            low(rows, features),
            low(rows, units),
            low(rows, units),
            low(rows, units),
            jax.ShapeDtypeStruct((8, features), F32),
        ],
        scratch_shapes=[pltpu.VMEM((rows, features), F32)],
        compiler_params=pltpu.CompilerParams(vmem_limit_bytes=VMEM_MOST),
        cost_estimate=pl.CostEstimate(
            flops=2 * rows * features * count * cols,
            bytes_accessed=2 * features * count * cols + 8 * rows * count * units,
            transcendentals=rows * count * units,
        ),
        name="ff_backward",
    )(grad_exit, mixed, cotangent, after_cross, gains, c_out_own, ff_all, gate, up)


def layer_forward_plain(
    parents, tokens, encoder, heads_in, op_in, ff_in, embed_in, collective_id
):
    rows = tokens.shape[0] // MB
    enc_rows = encoder.shape[0] // MB
    width = op_in.shape[2]
    heads_all = lax.all_gather(heads_in, PLANE, axis=0, tiled=True)
    op_all = lax.all_gather(
        lax.all_gather(op_in, "tp", axis=1, tiled=False), PLANE, axis=2, tiled=True
    )
    ff_all = lax.all_gather(
        lax.all_gather(ff_in, "tp", axis=1, tiled=True), PLANE, axis=0, tiled=True
    )
    embed_all = lax.all_gather(embed_in, PLANE, axis=0, tiled=True)
    gains = heads_all[:, Q2 - 64 : Q2 - 56].astype(F32).T
    tok = tokens.astype(F32)
    hidden_one = (tok * rms_scale(tok) * gains[0:1]).astype(BF16)
    queries = mat(hidden_one, heads_all[:, 4 * width : 5 * width]).astype(BF16)
    kv = mat(hidden_one, heads_all[:, : 2 * width]).astype(BF16)
    enc_kv = mat(encoder, heads_all[:, 2 * width : 4 * width]).astype(BF16)

    def both_sides(value, i, count):
        return ctx_gather(value[i * count : (i + 1) * count])

    kv_self = jnp.stack([both_sides(kv, i, rows) for i in range(MB)])
    kv_cross = jnp.stack([both_sides(enc_kv, i, enc_rows) for i in range(MB)])
    bias = jnp.stack([mask_bias(parents[i], rows) for i in range(MB)]).astype(BF16)

    def attention(values, keys_values, masks):
        outcome = [
            attend(
                values[i * rows : (i + 1) * rows],
                keys_values[i],
                None if masks is None else masks[i],
            )
            for i in range(MB)
        ]
        return jnp.concatenate([o[0] for o in outcome]), jnp.stack([o[1] for o in outcome])

    attended, totals_self = attention(queries, kv_self, bias)
    after_self = line_project(attended, op_all[0], tok, 2)
    hidden_two = (after_self * rms_scale(after_self) * gains[1:2]).astype(BF16)
    cross_q = mat(hidden_two, heads_all[:, Q2 : Q2 + width]).astype(BF16)
    crossed, totals_cross = attention(cross_q, kv_cross, None)
    after_cross = line_project(crossed, op_all[1], after_self, 3)
    return (
        heads_all,
        lax.dynamic_index_in_dim(op_all[:2], lax.axis_index("tp"), 1, False),
        op_all[2],
        ff_all,
        embed_all,
        gains,
        bias,
        queries,
        kv_self,
        kv_cross,
        attended,
        totals_self,
        cross_q,
        crossed,
        totals_cross,
        after_self,
        after_cross,
    )


BACKWARD_ORDER = (
    ("X", 0, 0), ("X", 0, 1), ("X", 0, 2), ("XC", 0), ("SQ", 0), ("X", 1, 0), ("X", 1, 1),
    ("X", 1, 2), ("XC", 1), ("QH", 0, 1), ("SQ", 1), ("EP", 0), ("QH", 0, 2), ("ERN", 0, 0),
    ("QH", 1, 1), ("QH", 0, 3), ("AQ", 0), ("ERN", 0, 1), ("S", 0, 0), ("EP", 1), ("QH", 1, 2),
    ("ERF", 0, 0), ("QH", 1, 3), ("ERN", 0, 2), ("AQ", 1), ("ERF", 0, 1), ("ERN", 1, 0),
    ("S", 0, 1), ("S", 0, 2), ("ERN", 1, 1), ("XS", 0), ("ERF", 1, 0), ("ERN", 0, 3),
    ("ERF", 1, 1), ("ERN", 1, 2), ("S", 1, 0), ("ERF", 0, 2), ("S", 1, 1), ("EBN", 0, 0),
    ("ERF", 0, 3), ("S", 1, 2), ("EBN", 0, 1), ("TP", 0), ("ERF", 1, 2), ("EBN", 1, 0),
    ("EBF", 0, 0), ("XS", 1), ("ERN", 1, 3), ("EBN", 1, 1), ("EBF", 0, 1), ("EBF", 1, 0),
    ("EBN", 0, 2), ("TP", 1), ("EBF", 1, 1), ("ERF", 1, 3), ("ORN", 0, 0), ("ORN", 0, 1),
    ("EBN", 1, 2), ("EBF", 0, 2), ("ORF", 0, 0), ("ORF", 0, 1), ("ORN", 1, 0), ("EBF", 1, 2),
    ("ORN", 1, 1), ("EBN", 0, 3), ("ORF", 1, 0), ("ORF", 1, 1), ("OBN", 0, 0), ("OBN", 0, 1),
    ("EBF", 0, 3), ("OBF", 0, 0), ("OBF", 0, 1), ("OBN", 1, 0), ("OBN", 1, 1), ("EBN", 1, 3),
    ("FT", 0), ("OBF", 1, 0), ("OBF", 1, 1), ("FT", 1), ("EBF", 1, 3),
)


class LineSum:
    def __init__(self, t, count, left, right, x, out, buffers, sems, chunks):
        self.t, self.count, self.left, self.right = t, count, left, right
        self.x, self.out, self.chunks = x, out, chunks
        self.low_in, self.high_in = buffers.at[0], buffers.at[1]
        self.sems = sems
        self.half = x.shape[0] // 2
        self.rows = self.half // chunks

    def low(self, j):
        return pl.ds(j * self.rows, self.rows)

    def high(self, j):
        return pl.ds(self.half + j * self.rows, self.rows)

    def down(self, j, own):
        src = self.x.at[self.low(j)] if own else self.low_in.at[self.low(j)]
        dst = self.low_in.at[self.low(j)]
        return remote(src, dst, self.sems.at[0, j], self.sems.at[1, j], self.left)

    def up(self, j, own):
        src = self.x.at[self.high(j)] if own else self.high_in.at[self.low(j)]
        dst = self.high_in.at[self.low(j)]
        return remote(src, dst, self.sems.at[2, j], self.sems.at[3, j], self.right)

    def low_back(self, j):
        ref = self.out.at[self.low(j)]
        return remote(ref, ref, self.sems.at[4, j], self.sems.at[5, j], self.right)

    def high_back(self, j):
        ref = self.out.at[self.high(j)]
        return remote(ref, ref, self.sems.at[6, j], self.sems.at[7, j], self.left)

    def start(self):
        @pl.when(self.t == self.count - 1)
        def _():
            for j in range(self.chunks):
                self.down(j, True).start()

        @pl.when(self.t == 0)
        def _():
            for j in range(self.chunks):
                self.up(j, True).start()

    def low_step(self, j):
        if not 0 <= j < self.chunks:
            return

        @pl.when(self.t < self.count - 1)
        def _():
            self.down(j, False).wait_recv()
            at = self.low(j)
            total = (self.low_in[at].astype(F32) + self.x[at].astype(F32)).astype(BF16)

            @pl.when(self.t > 0)
            def _():
                self.low_in[at] = total
                self.down(j, False).start()

            @pl.when(self.t == 0)
            def _():
                self.out[at] = total
                self.low_back(j).start()

    def high_step(self, j):
        if not 0 <= j < self.chunks:
            return

        @pl.when(self.t > 0)
        def _():
            self.up(j, False).wait_recv()
            at = self.high(j)
            total = (self.high_in[self.low(j)].astype(F32) + self.x[at].astype(F32)).astype(BF16)

            @pl.when(self.t < self.count - 1)
            def _():
                self.high_in[self.low(j)] = total
                self.up(j, False).start()

            @pl.when(self.t == self.count - 1)
            def _():
                self.out[at] = total
                self.high_back(j).start()

    def low_forward(self, j):
        @pl.when(self.t > 0)
        def _():
            self.low_back(j).wait_recv()

            @pl.when(self.t < self.count - 1)
            def _():
                self.low_back(j).start()

    def high_forward(self, j):
        @pl.when(self.t < self.count - 1)
        def _():
            self.high_back(j).wait_recv()

            @pl.when(self.t > 0)
            def _():
                self.high_back(j).start()

    def by_side(self, first, second, j):
        @pl.when(self.t < self.count // 2)
        def _():
            first(j)

        @pl.when(self.t >= self.count // 2)
        def _():
            second(j)

    def reduce_near(self, j):
        self.by_side(self.high_step, self.low_step, j)

    def reduce_far(self, j):
        self.by_side(self.low_step, self.high_step, j)

    def back_near(self, j):
        self.by_side(self.low_forward, self.high_forward, j)

    def back_far(self, j):
        self.by_side(self.high_forward, self.low_forward, j)

    def finish(self):
        last = self.count - 1
        for j in range(self.chunks):

            @pl.when(self.t > 0)
            def _():
                self.down(j, False).wait_send()
                self.high_back(j).wait_send()

            @pl.when(self.t < last)
            def _():
                self.up(j, False).wait_send()
                self.low_back(j).wait_send()


def attend_back_head(
    h, i, tile, q_ref, kv_ref, bias_ref, total_ref, go_ref, dq_ref, dkv_ref, acc_ref
):
    rows, width = q_ref.shape[0] // MB, q_ref.shape[1]
    keys_count = kv_ref.shape[1]
    cols = slice(h * HD, (h + 1) * HD)
    vcols = slice(width + h * HD, width + (h + 1) * HD)
    acc_ref[:keys_count] = jnp.zeros((keys_count, 2 * HD), F32)

    @pl.loop(0, rows // tile)
    def _(n):
        at = pl.ds(pl.multiple_of(i * rows + n * tile, tile), tile)
        here_at = pl.ds(pl.multiple_of(n * tile, tile), tile)
        keys, values = kv_ref[i, :, cols], kv_ref[i, :, vcols]
        queries, go = q_ref[at, cols], go_ref[at, cols]
        scores = mat_nt(keys, queries)
        if bias_ref is not None:
            scores = scores + bias_ref[i, :, here_at]
        probs = jnp.exp(scores - total_ref[i, h : h + 1, here_at])
        grad_probs = mat_nt(values, go)
        inner = jnp.sum(probs * grad_probs, axis=0, keepdims=True)
        grad_scores = (probs * (grad_probs - inner)).astype(BF16)
        acc_ref[:keys_count, :HD] += mat(grad_scores, queries)
        acc_ref[:keys_count, HD:] += mat(probs.astype(BF16), go)
        dq_ref[at, cols] = mat_tn(keys, grad_scores).T.astype(BF16)

    dkv_ref[i, :, cols] = acc_ref[:keys_count, :HD].astype(BF16)
    dkv_ref[i, :, vcols] = acc_ref[:keys_count, HD:].astype(BF16)


def layer_backward_kernel(
    count, gcr_ref, cq_ref, kvc_ref, totc_ref, q_ref, tots_ref, wo_ref, gains_ref, *refs
):
    late, outs, scratch = refs[:7], refs[7:15], refs[15:]
    gt_out, enc_sum, gcq, gkvc, gq, gkvs, gsl, norms = outs
    dkvc, dkvc_in, dkvs, dkvs_in, acc, held, gatt, enc_part, one_part, one_sum = scratch[:10]
    enc_buffers, one_buffers = scratch[10:12]
    landed = scratch[12:19]
    line_right, line_left, line_recv, ctx_send, ctx_recv, sum_sems, load_sem = scratch[19:]
    heads_ref, query_ref, as_ref, gac_ref, kvs_ref, bias_ref, tok_ref = landed
    loads = [
        pltpu.make_async_copy(src, dst, load_sem.at[j])
        for j, (src, dst) in enumerate(zip(late, landed))
    ]
    for copy in loads:
        copy.start()
    waiting = list(range(len(loads)))

    def need(*numbers):
        for j in numbers:
            if j in waiting:
                waiting.remove(j)
                loads[j].wait()

    f, c, t = here()
    right, left = (f, c, t + 1), (f, c, t - 1)
    x_peer = (f, 1 - c, t)
    rows, enc_rows = tok_ref.shape[0] // MB, gkvc.shape[0] // MB
    width = q_ref.shape[1]
    tile = 256

    barrier = pltpu.get_barrier_semaphore()
    pl.semaphore_signal(barrier, inc=1, device_id=x_peer, device_id_type=MESH)

    @pl.when(t > 0)
    def _():
        pl.semaphore_signal(barrier, inc=1, device_id=left, device_id_type=MESH)

    @pl.when(t < count - 1)
    def _():
        pl.semaphore_signal(barrier, inc=1, device_id=right, device_id_type=MESH)

    at_end = (t == 0) | (t == count - 1)
    pl.semaphore_wait(barrier, jnp.where(at_end, 2, 3).astype(jnp.int32))

    def part(i):
        return pl.ds(i * rows, rows)

    def enc_at(i):
        return pl.ds(i * enc_rows, enc_rows)

    def line(j, own, place):
        sems = (line_right.at[j], line_left.at[j], line_recv.at[j])
        return Line(t, count, left, right, own, place, sems)

    query_lines = [
        line(i, gcq.at[part(i)], lambda origin, i=i: held.at[origin, part(i)]) for i in range(MB)
    ]

    def ctx_copy(j, ref, landing, i, size):
        return remote(
            ref.at[i, pl.ds(size, size)], landing.at[i], ctx_send.at[j], ctx_recv.at[j], x_peer
        )

    ctx_cross = [ctx_copy(i, dkvc, dkvc_in, i, enc_rows) for i in range(MB)]
    ctx_self = [ctx_copy(MB + i, dkvs, dkvs_in, i, rows) for i in range(MB)]

    def summed(j, x, out, buffers, chunks):
        return LineSum(t, count, left, right, x, out, buffers, sum_sems.at[j], chunks)

    enc_chunks = enc_rows // 256
    one_chunks = rows // 256
    enc_sums = [
        summed(i, enc_part.at[enc_at(i)], enc_sum.at[enc_at(i)], enc_buffers.at[i], enc_chunks)
        for i in range(MB)
    ]
    one_sums = [
        summed(MB + i, one_part.at[part(i)], one_sum.at[part(i)], one_buffers.at[i], one_chunks)
        for i in range(MB)
    ]

    def tiles(i, count_rows, body):
        @pl.loop(0, count_rows // tile)
        def _(n):
            at = pl.ds(pl.multiple_of(i * count_rows + n * tile, tile), tile)
            body(at, pl.ds(pl.multiple_of(n * tile, tile), tile))

    def cross_head(i, h):
        attend_back_head(h, i, tile, cq_ref, kvc_ref, None, totc_ref, gcr_ref, gcq, dkvc, acc)

    def self_head(i, h):
        attend_back_head(h, i, tile, q_ref, kvs_ref, bias_ref, tots_ref, gatt, gq, dkvs, acc)

    def send_queries(i):
        held[t, part(i)] = gcq[part(i)]
        query_lines[i].start()

    def encoder_part(i):
        ctx_cross[i].wait_recv()

        def body(at, inner):
            total = dkvc[i, inner].astype(F32) + dkvc_in[i, inner].astype(F32)
            gkvc[at] = total.astype(BF16)
            enc_part[at] = mat_nt(
                total.astype(BF16), heads_ref[:, 2 * width : 4 * width]
            ).astype(BF16)

        tiles(i, enc_rows, body)
        enc_sums[i].start()

    def after_queries(i):
        def body(at, inner):
            grad = mat_nt(held[0, at], query_ref[0])
            for origin in range(1, count):
                grad = grad + mat_nt(held[origin, at], query_ref[origin])
            value = as_ref[at]
            scale = rms_scale(value)
            normed = value * scale
            norms[1:2] += jnp.sum(grad * normed, axis=0, keepdims=True)
            total = gac_ref[at] + rms_back(grad * gains_ref[1:2], normed, scale)
            gt_out[at] = total
            gsl[at] = total.astype(BF16)
            gatt[at] = mat(total.astype(BF16), wo_ref[...]).astype(BF16)

        tiles(i, rows, body)

    def token_part(i):
        ctx_self[i].wait_recv()

        def body(at, inner):
            total = (dkvs[i, inner].astype(F32) + dkvs_in[i, inner].astype(F32)).astype(BF16)
            gkvs[at] = total
            product = mat_nt(total, heads_ref[:, : 2 * width])
            product = product + mat_nt(gq[at], heads_ref[:, 4 * width : 5 * width])
            one_part[at] = product.astype(BF16)

        tiles(i, rows, body)
        one_sums[i].start()

    def finish_tokens(i):
        def body(at, inner):
            grad = one_sum[at].astype(F32)
            value = tok_ref[at].astype(F32)
            scale = rms_scale(value)
            normed = value * scale
            norms[0:1] += jnp.sum(grad * normed, axis=0, keepdims=True)
            gt_out[at] = gt_out[at] + rms_back(grad * gains_ref[0:1], normed, scale)

        tiles(i, rows, body)

    norms[...] = jnp.zeros_like(norms)
    steps = {
        "X": cross_head,
        "SQ": send_queries,
        "XC": lambda i: ctx_cross[i].start(),
        "QH": lambda i, d: query_lines[i].hop(d),
        "AQ": after_queries,
        "S": self_head,
        "EP": encoder_part,
        "XS": lambda i: ctx_self[i].start(),
        "TP": token_part,
        "FT": finish_tokens,
        "ERN": lambda i, j: enc_sums[i].reduce_near(j),
        "ERF": lambda i, j: enc_sums[i].reduce_far(j),
        "EBN": lambda i, j: enc_sums[i].back_near(j),
        "EBF": lambda i, j: enc_sums[i].back_far(j),
        "ORN": lambda i, j: one_sums[i].reduce_near(j),
        "ORF": lambda i, j: one_sums[i].reduce_far(j),
        "OBN": lambda i, j: one_sums[i].back_near(j),
        "OBF": lambda i, j: one_sums[i].back_far(j),
    }
    needs = {"EP": (0,), "AQ": (1, 2, 3), "S": (4, 5), "TP": (0,), "FT": (6,)}
    for name, *rest in BACKWARD_ORDER:
        need(*needs.get(name, ()))
        steps[name](*rest)
    for one in query_lines + enc_sums + one_sums:
        one.finish()
    for copy in ctx_self + ctx_cross:
        copy.wait_send()


def layer_backward(operands, tokens, enc_rows, collective_id):
    count = lax.axis_size("tp")
    tok_rows, features = tokens.shape
    rows = tok_rows // MB
    enc_tree = enc_rows // MB
    width = operands[0].shape[1]
    vmem = pl.BlockSpec(memory_space=pltpu.VMEM)
    gcr, cq, kvc, totc, q, kvs, bias, tots, gac, after_self, tok, wo, query, heads, gains = operands
    late = (heads, query, after_self, gac, kvs, bias, tok)
    outs = [
        ((tok_rows, features), F32),
        ((enc_rows, features), BF16),
        ((tok_rows, width), BF16),
        ((enc_rows, 2 * width), BF16),
        ((tok_rows, width), BF16),
        ((tok_rows, 2 * width), BF16),
        ((tok_rows, features), BF16),
        ((8, features), F32),
    ]
    scratch = [
        ((MB, 2 * enc_tree, 2 * width), BF16),
        ((MB, enc_tree, 2 * width), BF16),
        ((MB, 2 * rows, 2 * width), BF16),
        ((MB, rows, 2 * width), BF16),
        ((2 * enc_tree, 2 * HD), F32),
        ((count, tok_rows, width), BF16),
        ((tok_rows, width), BF16),
        ((enc_rows, features), BF16),
        ((tok_rows, features), BF16),
        ((tok_rows, features), BF16),
        ((MB, 2, enc_tree // 2, features), BF16),
        ((MB, 2, rows // 2, features), BF16),
    ]
    return pl.pallas_call(
        functools.partial(layer_backward_kernel, count),
        in_specs=[vmem] * 8 + [pl.BlockSpec(memory_space=pl.ANY)] * len(late),
        out_specs=[vmem] * len(outs),
        out_shape=[jax.ShapeDtypeStruct(shape, kind) for shape, kind in outs],
        scratch_shapes=[pltpu.VMEM(shape, kind) for shape, kind in scratch]
        + [pltpu.VMEM(value.shape, value.dtype) for value in late]
        + [
            pltpu.SemaphoreType.DMA((MB, count)),
            pltpu.SemaphoreType.DMA((MB, count)),
            pltpu.SemaphoreType.DMA((MB, count)),
            pltpu.SemaphoreType.DMA((2 * MB,)),
            pltpu.SemaphoreType.DMA((2 * MB,)),
            pltpu.SemaphoreType.DMA((2 * MB, 8, 4)),
            pltpu.SemaphoreType.DMA((len(late),)),
        ],
        compiler_params=pltpu.CompilerParams(
            collective_id=collective_id, has_side_effects=True, vmem_limit_bytes=VMEM_MOST
        ),
        name="layer_backward",
    )(gcr, cq, kvc, totc, q, tots, wo, gains, *late)


EXIT_ORDER = (
    (8, "ST", 0), (11, "RN", 0, 0), (13, "RN", 0, 1), (14, "RN", 0, 2), (15, "ST", 1),
    (15, "RN", 0, 3), (15, "RF", 0, 0), (17, "RN", 1, 0), (17, "RF", 0, 1), (17, "RF", 0, 2),
    (17, "RN", 1, 1), (17, "RN", 1, 2), (17, "RF", 1, 0), (18, "RF", 1, 1), (18, "BN", 0, 0),
    (19, "RF", 0, 3), (19, "RN", 1, 3), (19, "BN", 0, 1), (19, "RF", 1, 2), (19, "BF", 0, 0),
    (19, "RF", 1, 3), (19, "BN", 1, 0), (20, "BN", 1, 1), (20, "BN", 0, 2), (20, "BF", 0, 1),
    (21, "BF", 1, 0), (21, "BN", 1, 2), (21, "BF", 1, 1), (22, "BN", 0, 3), (22, "BF", 0, 2),
    (23, "BN", 1, 3), (23, "BF", 1, 2), (23, "BF", 0, 3), (23, "BF", 1, 3),
)


def exit_backward_kernel(
    count,
    valid,
    logits_ref,
    e_ref,
    x_t_ref,
    target_ref,
    log_ref,
    embed_ref,
    sum_ref,
    grads,
    acc,
    partial,
    total,
    buffers,
    sems,
):
    f, c, t = here()
    right, left = (f, c, t + 1), (f, c, t - 1)
    step = pl.program_id(0)
    size, tile = logits_ref.shape
    tiles = grads.shape[1] // tile
    sums = [
        LineSum(
            t,
            count,
            left,
            right,
            partial.at[pl.ds(p * size, size)],
            total.at[pl.ds(p * size, size)],
            buffers.at[p],
            sems.at[p],
            EXIT_CHUNKS,
        )
        for p in range(EXIT_PIECES)
    ]

    @pl.when(step == 0)
    def _():
        greet_line(t, count, left, right)

    @pl.when(step < EXIT_PIECES * tiles)
    def _():
        piece, k = step // tiles, lax.rem(step, tiles)
        lanes = lax.broadcasted_iota(jnp.int32, (size, tile), 1)
        probs = jnp.exp(logits_ref[...] - log_ref[...])
        probs = jnp.where(lanes < valid - k * tile, probs, 0.0)
        hits = jnp.where(lanes == target_ref[...] - k * tile, 1.0, 0.0)
        grad = (probs - hits).astype(BF16)
        rows = pl.ds(pl.multiple_of(piece * size, size), size)
        grads[rows, pl.ds(pl.multiple_of(k * tile, tile), tile)] = grad
        product = mat_nt(grad, e_ref[...])

        @pl.when(k == 0)
        def _():
            acc[...] = product

        @pl.when(k > 0)
        def _():
            acc[...] += product

        @pl.when(k == tiles - 1)
        def _():
            partial[rows] = acc[...].astype(BF16)

    @pl.when(step >= EXIT_PIECES * tiles)
    def _():
        k = step - EXIT_PIECES * tiles
        columns = pl.ds(pl.multiple_of(k * tile, tile), tile)
        embed_ref[...] = mat(x_t_ref[...], grads[:, columns]).astype(BF16)

    steps = {
        "ST": lambda p: sums[p].start(),
        "RN": lambda p, j: sums[p].reduce_near(j),
        "RF": lambda p, j: sums[p].reduce_far(j),
        "BN": lambda p, j: sums[p].back_near(j),
        "BF": lambda p, j: sums[p].back_far(j),
    }
    for when in sorted({item[0] for item in EXIT_ORDER}):

        @pl.when(step == when)
        def _():
            for at, name, *rest in EXIT_ORDER:
                if at == when:
                    steps[name](*rest)

    @pl.when(step == pl.num_programs(0) - 1)
    def _():
        for one in sums:
            one.finish()
        sum_ref[...] = total[...]


def exit_backward(logits, embed_t, exit_in_t, targets_local, log_total, valid, collective_id):
    rows, padded = logits.shape
    features = embed_t.shape[0]
    count = lax.axis_size("tp")
    size = rows // EXIT_PIECES
    tiles = padded // TILE
    if tiles * (EXIT_PIECES + 1) != EXIT_STEPS:
        raise ValueError("steps")

    def piece_of(i):
        return jnp.minimum(i // tiles, EXIT_PIECES - 1)

    def tile_of(i):
        return jnp.where(i < EXIT_PIECES * tiles, lax.rem(i, tiles), tiles - 1)

    column = pl.BlockSpec((size, 1), lambda i: (piece_of(i), 0))
    return pl.pallas_call(
        functools.partial(exit_backward_kernel, count, valid),
        grid=(EXIT_STEPS,),
        in_specs=[
            pl.BlockSpec((size, TILE), lambda i: (piece_of(i), tile_of(i))),
            pl.BlockSpec((features, TILE), lambda i: (0, tile_of(i))),
            pl.BlockSpec((features, rows), lambda i: (0, 0)),
            column,
            column,
        ],
        out_specs=[
            pl.BlockSpec((features, TILE), lambda i: (0, jnp.maximum(i - EXIT_PIECES * tiles, 0))),
            pl.BlockSpec((rows, features), lambda i: (0, 0)),
        ],
        out_shape=[
            jax.ShapeDtypeStruct((features, padded), BF16),
            jax.ShapeDtypeStruct((rows, features), BF16),
        ],
        scratch_shapes=[
            pltpu.VMEM((rows, padded), BF16),
            pltpu.VMEM((size, features), F32),
            pltpu.VMEM((rows, features), BF16),
            pltpu.VMEM((rows, features), BF16),
            pltpu.VMEM((EXIT_PIECES, 2, size // 2, features), BF16),
            pltpu.SemaphoreType.DMA((EXIT_PIECES, 8, EXIT_CHUNKS)),
        ],
        compiler_params=pltpu.CompilerParams(
            collective_id=collective_id, has_side_effects=True, vmem_limit_bytes=VMEM_MOST
        ),
        cost_estimate=pl.CostEstimate(
            flops=4 * rows * features * padded,
            bytes_accessed=4 * rows * padded + 4 * features * padded,
            transcendentals=rows * padded,
        ),
        name="exit_backward",
    )(logits, embed_t, exit_in_t, targets_local, log_total)


def layer_backward_plain(operands, tokens, enc_rows, collective_id):
    (
        grad_crossed,
        cross_q,
        kv_cross,
        totals_cross,
        queries,
        kv_self,
        bias,
        totals_self,
        grad_after_cross,
        after_self,
        tokens,
        w_out_own,
        c_query_all,
        heads_all,
        gains,
    ) = operands
    rows, width = queries.shape[0] // MB, queries.shape[1]
    trees = range(MB)

    def tree_rows(value, i):
        return value[i * rows : (i + 1) * rows]

    outcome = [
        attend_back(
            tree_rows(cross_q, i), kv_cross[i], None, totals_cross[i], tree_rows(grad_crossed, i)
        )
        for i in trees
    ]
    grad_cq = jnp.concatenate([o[0] for o in outcome], axis=0)
    grad_kv_cross = jnp.concatenate([ctx_scatter(o[1]) for o in outcome], axis=0)
    encoder_part = mat_nt(grad_kv_cross, heads_all[:, 2 * width : 4 * width]).astype(BF16)
    grad_two = line_project(grad_cq, c_query_all, jnp.zeros_like(after_self), 6)
    scale_two = rms_scale(after_self)
    normed_two = after_self * scale_two
    norm_cross = jnp.sum(grad_two * normed_two, axis=0)
    grad_after_self = grad_after_cross + rms_back(grad_two * gains[1:2], normed_two, scale_two)
    grad_self_low = grad_after_self.astype(BF16)
    grad_attended = mat(grad_self_low, w_out_own).astype(BF16)
    outcome = [
        attend_back(
            tree_rows(queries, i), kv_self[i], bias[i], totals_self[i], tree_rows(grad_attended, i)
        )
        for i in trees
    ]
    grad_q = jnp.concatenate([o[0] for o in outcome], axis=0)
    grad_kv_self = jnp.concatenate([ctx_scatter(o[1]) for o in outcome], axis=0)
    part = mat_nt(grad_q, heads_all[:, 4 * width : 5 * width])
    part = (part + mat_nt(grad_kv_self, heads_all[:, : 2 * width])).astype(BF16)
    both = line_sum(jnp.concatenate([part, encoder_part], axis=0), 7, 12)
    grad_one = both[: MB * rows].astype(F32)
    tok = tokens.astype(F32)
    scale_one = rms_scale(tok)
    normed_one = tok * scale_one
    norm_self = jnp.sum(grad_one * normed_one, axis=0)
    grad_tokens = grad_after_self + rms_back(grad_one * gains[0:1], normed_one, scale_one)
    norms = jnp.stack([norm_self, norm_cross] + [jnp.zeros_like(norm_self)] * 6)
    return (
        grad_tokens,
        both[MB * rows :],
        grad_cq,
        grad_kv_cross,
        grad_q,
        grad_kv_self,
        grad_self_low,
        norms,
    )


def local(
    tokens,
    encoder,
    cotangent,
    parents,
    targets,
    w_query,
    w_key,
    w_value,
    w_out,
    c_query,
    c_key,
    c_value,
    c_out,
    w_gate,
    w_up,
    w_down,
    embedding,
    norm_self,
    norm_cross,
    norm_ff,
    norm_exit,
):
    t = lax.axis_index("tp")
    tp_count = lax.axis_size("tp")
    rows = tokens.shape[0] // MB
    features = tokens.shape[1]
    width = w_query.shape[1]
    hidden_units = w_gate.shape[1]
    vocab = embedding.shape[0]
    trees = range(MB)
    shrink = 1.0 / math.sqrt(features)

    def tree_rows(value, i):
        count = value.shape[0] // MB
        return value[i * count : (i + 1) * count]

    gains_in = jnp.stack([norm_self, norm_cross, norm_ff, norm_exit], axis=1)
    heads_in = jnp.concatenate(
        [w_key, w_value, c_key, c_value, w_query]
        + [jnp.pad(gains_in, ((0, 0), (0, 60))), c_query, jnp.zeros_like(c_query[:, :64])],
        axis=1,
    )
    op_in = jnp.stack([w_out.T, c_out.T, c_query])
    ff_in = jnp.concatenate([w_gate, w_up, w_down.T], axis=1)
    padded = -(-vocab // TILE) * TILE
    embed_in = jnp.pad(embedding.T, ((0, 0), (0, padded - vocab)))
    forward = layer_forward if small_plane() else layer_forward_plain
    (
        heads_all,
        own_out,
        query_all,
        ff_all,
        embed_t,
        gains,
        bias,
        queries,
        kv_self,
        kv_cross,
        attended,
        totals_self,
        cross_q,
        crossed,
        totals_cross,
        after_self,
        after_cross,
    ) = forward(parents, tokens, encoder, heads_in, op_in, ff_in, embed_in, 1)
    w_out_own, c_out_own = own_out[0], own_out[1]
    gate_pre, up_pre, mixed, mixed_low, exit_in, exit_in_t = ff_forward(
        after_cross, gains, ff_all, tp_count, shrink
    )

    targets_local = targets - t * vocab
    inside = (targets_local >= 0) & (targets_local < vocab)
    targets_local = jnp.where(inside, targets_local, -1)[:, None]
    logits, top, summed, picked = exit_forward(exit_in, embed_t, targets_local, vocab)
    stats = jnp.stack([top, summed, picked]).reshape(3, MB * rows // 128, 128)
    top, log_total, picked = share_stats(stats, 4)
    losses = (log_total - picked).reshape(-1)
    scores = (top - log_total).reshape(-1)
    grad_embed, grad_exit = exit_backward(
        logits, embed_t, exit_in_t, targets_local, log_total.reshape(-1, 1), vocab, 5
    )
    grad_embed_own = lax.optimization_barrier(
        lax.psum_scatter(grad_embed, PLANE, scatter_dimension=0, tiled=True)
    )

    (
        grad_after_cross,
        grad_mixed_low,
        grad_cross_low,
        grad_crossed,
        hidden_three,
        activated_own,
        grad_gate_own,
        grad_up_own,
        norms,
    ) = ff_backward(
        grad_exit,
        mixed,
        cotangent,
        after_cross,
        gains,
        c_out_own,
        ff_all,
        gate_pre,
        up_pre,
        tp_count,
        shrink,
    )
    backward = layer_backward if small_plane() else layer_backward_plain
    (
        grad_tokens,
        grad_encoder,
        grad_cq,
        grad_kv_cross,
        grad_q,
        grad_kv_self,
        grad_self_low,
        norms_low,
    ) = backward(
        (
            grad_crossed,
            cross_q,
            kv_cross,
            totals_cross,
            queries,
            kv_self,
            bias,
            totals_self,
            grad_after_cross,
            after_self,
            tokens,
            w_out_own,
            query_all,
            heads_all,
            gains,
        ),
        tokens,
        encoder.shape[0],
        6,
    )
    ff_grads = jnp.concatenate(
        [
            mat_tn(hidden_three, grad_gate_own),
            mat_tn(hidden_three, grad_up_own),
            mat_tn(grad_mixed_low, activated_own),
            mat_tn(grad_cross_low, crossed),
        ],
        axis=1,
    ).astype(BF16)
    ff_own = lax.psum_scatter(ff_grads, PLANE, scatter_dimension=0, tiled=True)
    scatter = weight_scatter if small_plane() else weight_scatter_plain
    own = scatter(
        (
            encoder,
            grad_kv_cross,
            tokens,
            grad_kv_self,
            grad_q,
            after_self,
            grad_cq,
            grad_self_low,
            attended,
            gains,
            norms_low,
            norms,
        ),
        9,
    )

    def part(value, start, size):
        return value[:, start : start + size].astype(F32)

    base = Q2 - 64
    return (
        mixed_low,
        losses,
        scores,
        grad_tokens,
        grad_encoder.astype(F32),
        part(own, 4 * width, width),
        part(own, 2 * width, width),
        part(own, 3 * width, width),
        part(own, Q2 + width, width).T,
        part(own, Q2, width),
        part(own, 0, width),
        part(own, width, width),
        part(ff_own, 3 * hidden_units, width).T,
        part(ff_own, 0, hidden_units),
        part(ff_own, hidden_units, hidden_units),
        part(ff_own, 2 * hidden_units, hidden_units).T,
        grad_embed_own[:, :vocab].astype(F32).T,
        own[:, base],
        own[:, base + 1],
        own[:, base + 2],
        own[:, base + 3],
    )


def solution(mesh):
    rows_cols = P(PLANE, "tp")
    cols_rows = P("tp", PLANE)
    data = P(PLANE, None)
    flat = P(PLANE)
    weights = (rows_cols,) * 3 + (cols_rows,) + (rows_cols,) * 3 + (cols_rows,)
    weights += (rows_cols,) * 2 + (cols_rows,) * 2 + (flat,) * 4
    return jax.shard_map(
        local,
        mesh=mesh,
        in_specs=(data, data, data, P("fsdp", None), flat) + weights,
        out_specs=(data, flat, flat, data, data) + weights,
        check_vma=False,
    )
```

```python
import functools
import math

import jax
import jax.numpy as jnp
from jax import lax
from jax.experimental import pallas as pl
from jax.experimental.pallas import tpu as pltpu
from jax.sharding import PartitionSpec as P

HD = 64
BLK = 128
MB = 2
EPSILON = 1e-06
MASKED = -1000000000.0
F32 = jnp.float32
BF16 = jnp.bfloat16
PLANE = ("fsdp", "ctx")
VMEM_LIMIT = 48 * 1024 * 1024
MESH = pl.DeviceIdType.MESH
TILE = 1024
LOWEST = -3.0e38
VMEM_MOST = 58 * 1024 * 1024
Q2 = 1024
EXIT_PIECES = 2
EXIT_CHUNKS = 4
EXIT_STEPS = 24
FF_TILE = 512


def mat(left, right):
    return jnp.dot(left, right, preferred_element_type=F32)


def mat_nt(left, right):
    return lax.dot_general(left, right, (((1,), (1,)), ((), ())), preferred_element_type=F32)


def mat_tn(left, right):
    return lax.dot_general(left, right, (((0,), (0,)), ((), ())), preferred_element_type=F32)


def small_plane():
    return lax.axis_size("fsdp") == 4 and lax.axis_size("ctx") == 2


def swap(value, axis, bit):
    count = lax.axis_size(axis)
    return lax.ppermute(value, axis, [(i, i ^ bit) for i in range(count)])


def low_sum(left, right):
    return (left.astype(F32) + right.astype(F32)).astype(BF16)


def here():
    return lax.axis_index("fsdp"), lax.axis_index("ctx"), lax.axis_index("tp")


def greet(peers):
    barrier = pltpu.get_barrier_semaphore()
    for peer in peers:
        pl.semaphore_signal(barrier, inc=1, device_id=peer, device_id_type=MESH)
    pl.semaphore_wait(barrier, len(peers))


def greet_line(t, count, left, right):
    barrier = pltpu.get_barrier_semaphore()

    @pl.when(t > 0)
    def _():
        pl.semaphore_signal(barrier, inc=1, device_id=left, device_id_type=MESH)

    @pl.when(t < count - 1)
    def _():
        pl.semaphore_signal(barrier, inc=1, device_id=right, device_id_type=MESH)

    at_end = (t == 0) | (t == count - 1)
    pl.semaphore_wait(barrier, jnp.where(at_end, 1, 2).astype(jnp.int32))


def remote(src, dst, send, recv, peer):
    return pltpu.make_async_remote_copy(
        src_ref=src, dst_ref=dst, send_sem=send, recv_sem=recv, device_id=peer, device_id_type=MESH
    )


def weight_scatter_kernel(
    enc_ref,
    gkvc_ref,
    tok_ref,
    gkvs_ref,
    gq_ref,
    as_ref,
    gcq_ref,
    gsl_ref,
    att_ref,
    gains_ref,
    norms_low_ref,
    norms_ref,
    out_ref,
    hidden_one,
    hidden_two,
    norm_rows,
    x_ref,
    chip,
    core_in,
    chip_in,
    send,
    recv,
    core_send,
    core_recv,
):
    f, c, t = here()
    chips = [(2, 1), (0, 1), (2, 0)]
    peers = [(f ^ df, c ^ dc, t) for df, dc in chips]
    partner = (f ^ 1, c, t)
    greet(peers + [partner])
    features = x_ref.shape[0]
    shard = features // 8
    rows = tok_ref.shape[0]
    kv, width = gkvs_ref.shape[1], gq_ref.shape[1]
    order = chips + [(0, 0)]
    spans = [(0, kv), (kv, kv), (Q2 - 256, 256), (Q2, 2 * width)]

    def block(df, dc):
        slot = (f ^ df) * 2 + (c ^ dc)
        return pl.ds(pl.multiple_of(slot * shard, shard), shard)

    def swap_copy(g, j):
        cols = pl.ds(*spans[g])
        df, dc = order[j]
        return remote(
            x_ref.at[block(df ^ 1, dc), cols],
            core_in.at[j, :, cols],
            core_send.at[g, j],
            core_recv.at[g, j],
            partner,
        )

    def chip_copy(g, j):
        cols = pl.ds(*spans[g])
        return remote(
            chip.at[j, :, cols], chip_in.at[j, :, cols], send.at[g, j], recv.at[g, j], peers[j]
        )

    def product(left, right, start, size):
        @pl.loop(0, features // 256)
        def _(n):
            at = pl.ds(pl.multiple_of(n * 256, 256), 256)
            x_ref[at, start : start + size] = mat_tn(left[:, at], right[...]).astype(BF16)

    def swap_group(g):
        for j in range(4):
            swap_copy(g, j).start()

    def chip_group(g):
        cols = slice(spans[g][0], spans[g][0] + spans[g][1])
        for j in range(4):
            swap_copy(g, j).wait_recv()
            total = x_ref[block(*order[j]), cols].astype(F32) + core_in[j, :, cols].astype(F32)
            if j < 3:
                chip[j, :, cols] = total.astype(BF16)
                chip_copy(g, j).start()
            else:
                out_ref[:, cols] = total

    def hidden(source, gain, target):
        @pl.loop(0, rows // 256)
        def _(n):
            at = pl.ds(pl.multiple_of(n * 256, 256), 256)
            value = source[at].astype(F32)
            target[at] = (value * rms_scale(value) * gains_ref[gain : gain + 1]).astype(BF16)

    product(enc_ref, gkvc_ref, 0, kv)
    swap_group(0)
    hidden(tok_ref, 0, hidden_one)
    product(hidden_one, gkvs_ref, kv, kv)
    swap_group(1)
    chip_group(0)
    product(hidden_one, gq_ref, 2 * kv, width)
    norm_rows[...] = jnp.zeros_like(norm_rows)
    norm_rows[0:2] = norms_low_ref[0:2]
    norm_rows[2:3] = norms_ref[1:2]
    norm_rows[3:4] = norms_ref[0:1]
    x_ref[:, Q2 - 64 : Q2] = norm_rows[...].T.astype(BF16)
    swap_group(2)
    chip_group(1)
    hidden(as_ref, 1, hidden_two)
    product(hidden_two, gcq_ref, Q2, width)
    product(gsl_ref, att_ref, Q2 + width, width)
    swap_group(3)
    chip_group(2)
    chip_group(3)
    for g in range(4):
        cols = slice(spans[g][0], spans[g][0] + spans[g][1])
        for j in range(3):
            chip_copy(g, j).wait_recv()
            out_ref[:, cols] += chip_in[j, :, cols].astype(F32)
    for g in range(4):
        for j in range(4):
            swap_copy(g, j).wait_send()
        for j in range(3):
            chip_copy(g, j).wait_send()


def weight_scatter(operands, collective_id):
    features = operands[0].shape[1]
    kv, width = operands[3].shape[1], operands[4].shape[1]
    rows, shard, columns = operands[2].shape[0], features // 8, Q2 + 2 * width
    return pl.pallas_call(
        weight_scatter_kernel,
        in_specs=[pl.BlockSpec(memory_space=pltpu.VMEM)] * len(operands),
        out_specs=pl.BlockSpec(memory_space=pltpu.VMEM),
        out_shape=jax.ShapeDtypeStruct((shard, columns), F32),
        scratch_shapes=[
            pltpu.VMEM((rows, features), BF16),
            pltpu.VMEM((rows, features), BF16),
            pltpu.VMEM((64, features), F32),
            pltpu.VMEM((features, columns), BF16),
            pltpu.VMEM((3, shard, columns), BF16),
            pltpu.VMEM((4, shard, columns), BF16),
            pltpu.VMEM((3, shard, columns), BF16),
            pltpu.SemaphoreType.DMA((4, 3)),
            pltpu.SemaphoreType.DMA((4, 3)),
            pltpu.SemaphoreType.DMA((4, 4)),
            pltpu.SemaphoreType.DMA((4, 4)),
        ],
        compiler_params=pltpu.CompilerParams(
            collective_id=collective_id, has_side_effects=True, vmem_limit_bytes=VMEM_MOST
        ),
        name="weight_scatter",
    )(*operands)


def weight_scatter_plain(operands, collective_id):
    enc, gkvc, tokens, gkvs, gq, after_self, gcq, gsl, attended, gains, norms_low, norms = operands
    tok = tokens.astype(F32)
    hidden_one = (tok * rms_scale(tok) * gains[0:1]).astype(BF16)
    hidden_two = (after_self * rms_scale(after_self) * gains[1:2]).astype(BF16)
    norm_block = jnp.pad(
        jnp.stack([norms_low[0], norms_low[1], norms[1], norms[0]], axis=1), ((0, 0), (0, 60))
    )
    parts = [
        mat_tn(enc, gkvc),
        mat_tn(hidden_one, gkvs),
        mat_tn(hidden_one, gq),
        norm_block,
        mat_tn(hidden_two, gcq),
        mat_tn(gsl, attended),
    ]
    return lax.psum_scatter(
        jnp.concatenate(parts, axis=1), PLANE, scatter_dimension=0, tiled=True
    )


def line_project_kernel(
    count, chunks, x_ref, w_ref, base_ref, out_ref, held, send_right, send_left, recv
):
    f, c, t = here()
    right, left = (f, c, t + 1), (f, c, t - 1)
    greet_line(t, count, left, right)
    rows = x_ref.shape[0] // chunks

    def part(j):
        return pl.ds(j * rows, rows)

    def go(j, d, peer, origin, sems):
        src = x_ref.at[part(j)] if d == 0 else held.at[origin, part(j)]
        return remote(src, held.at[origin, part(j)], sems.at[d, j], recv.at[origin, j], peer)

    def go_right(j, d):
        return go(j, d, right, t - d, send_right)

    def go_left(j, d):
        return go(j, d, left, t + d, send_left)

    def arrived(j, origin):
        return remote(x_ref.at[part(j)], held.at[origin, part(j)], send_right.at[0, j], recv.at[origin, j], right)

    @pl.when(t < count - 1)
    def _():
        for j in range(chunks):
            go_right(j, 0).start()

    @pl.when(t > 0)
    def _():
        for j in range(chunks):
            go_left(j, 0).start()

    held[t] = x_ref[...]
    for d in range(1, count):
        for j in range(chunks):

            @pl.when(t - d >= 0)
            def _():
                arrived(j, t - d).wait_recv()
                if d < count - 1:

                    @pl.when(t < count - 1)
                    def _():
                        go_right(j, d).start()

            @pl.when(t + d < count)
            def _():
                arrived(j, t + d).wait_recv()
                if d < count - 1:

                    @pl.when(t > 0)
                    def _():
                        go_left(j, d).start()

            if d == count - 1:
                total = base_ref[part(j)]
                for origin in range(count):
                    total = total + mat_nt(held[origin, part(j)], w_ref[origin])
                out_ref[part(j)] = total

    for d in range(count - 1):
        for j in range(chunks):

            @pl.when((t - d >= 0) & (t < count - 1))
            def _():
                go_right(j, d).wait_send()

            @pl.when((t + d < count) & (t > 0))
            def _():
                go_left(j, d).wait_send()


def line_project(value, weights, base, collective_id):
    rows, width = value.shape
    count, features = weights.shape[0], weights.shape[1]
    chunks = 4
    return pl.pallas_call(
        functools.partial(line_project_kernel, count, chunks),
        in_specs=[pl.BlockSpec(memory_space=pltpu.VMEM)] * 3,
        out_specs=pl.BlockSpec(memory_space=pltpu.VMEM),
        out_shape=jax.ShapeDtypeStruct((rows, features), F32),
        scratch_shapes=[
            pltpu.VMEM((count, rows, width), BF16),
            pltpu.SemaphoreType.DMA((count, chunks)),
            pltpu.SemaphoreType.DMA((count, chunks)),
            pltpu.SemaphoreType.DMA((count, chunks)),
        ],
        compiler_params=pltpu.CompilerParams(
            collective_id=collective_id, has_side_effects=True, vmem_limit_bytes=VMEM_LIMIT
        ),
        name="line_project",
    )(value, weights, base)


def line_sum_kernel(
    count,
    chunks,
    window,
    lag,
    x_ref,
    out_ref,
    from_right,
    from_left,
    to_left,
    to_right,
    up_send,
    up_recv,
    down_send,
    down_recv,
    low_send,
    low_recv,
    high_send,
    high_recv,
):
    f, c, t = here()
    right, left = (f, c, t + 1), (f, c, t - 1)
    last = count - 1
    greet_line(t, count, left, right)
    half = x_ref.shape[0] // 2
    rows = half // chunks

    def low(j):
        return pl.ds(j * rows, rows)

    def high(j):
        return pl.ds(half + j * rows, rows)

    def down(j, own):
        src = x_ref.at[low(j)] if own else to_left.at[low(j)]
        return remote(src, from_right.at[low(j)], down_send.at[j], down_recv.at[j], left)

    def up(j, own):
        src = x_ref.at[high(j)] if own else to_right.at[low(j)]
        return remote(src, from_left.at[low(j)], up_send.at[j], up_recv.at[j], right)

    def low_back(j):
        return remote(out_ref.at[low(j)], out_ref.at[low(j)], low_send.at[j], low_recv.at[j], right)

    def high_back(j):
        return remote(
            out_ref.at[high(j)], out_ref.at[high(j)], high_send.at[j], high_recv.at[j], left
        )

    def pace(j, copy):
        if j == 0:
            for k in range(min(window, chunks)):
                copy(k, True).start()
        copy(j, True).wait_send()
        if j + window < chunks:
            copy(j + window, True).start()

    def low_step(j):
        @pl.when(t == last)
        def _():
            pace(j, down)

        @pl.when(t < last)
        def _():
            down(j, False).wait_recv()
            total = from_right[low(j)].astype(F32) + x_ref[low(j)].astype(F32)

            @pl.when(t > 0)
            def _():
                to_left[low(j)] = total.astype(BF16)
                down(j, False).start()

            @pl.when(t == 0)
            def _():
                out_ref[low(j)] = total.astype(BF16)
                low_back(j).start()

    def high_step(j):
        @pl.when(t == 0)
        def _():
            pace(j, up)

        @pl.when(t > 0)
        def _():
            up(j, False).wait_recv()
            total = from_left[low(j)].astype(F32) + x_ref[high(j)].astype(F32)

            @pl.when(t < last)
            def _():
                to_right[low(j)] = total.astype(BF16)
                up(j, False).start()

            @pl.when(t == last)
            def _():
                out_ref[high(j)] = total.astype(BF16)
                high_back(j).start()

    def low_forward(j):
        @pl.when(t > 0)
        def _():
            low_back(j).wait_recv()

            @pl.when(t < last)
            def _():
                low_back(j).start()

    def high_forward(j):
        @pl.when(t < last)
        def _():
            high_back(j).wait_recv()

            @pl.when(t > 0)
            def _():
                high_back(j).start()

    for j in range(chunks + lag):

        @pl.when(t < count // 2)
        def _():
            if j < chunks:
                high_step(j)
            if 0 <= j - 1 < chunks:
                low_step(j - 1)

        @pl.when(t >= count // 2)
        def _():
            if j < chunks:
                low_step(j)
            if 0 <= j - 1 < chunks:
                high_step(j - 1)

        if j >= lag:

            @pl.when(t < count // 2)
            def _():
                low_forward(j - lag)
                high_forward(j - lag)

            @pl.when(t >= count // 2)
            def _():
                high_forward(j - lag)
                low_forward(j - lag)

    for j in range(chunks):

        @pl.when(t > 0)
        def _():
            high_back(j).wait_send()

            @pl.when(t < last)
            def _():
                down(j, False).wait_send()

        @pl.when(t < last)
        def _():
            low_back(j).wait_send()

            @pl.when(t > 0)
            def _():
                up(j, False).wait_send()


def line_sum(partial, collective_id, chunks=4, window=2, lag=4):
    count = lax.axis_size("tp")
    rows, columns = partial.shape
    while (rows // 2) % (chunks * 16):
        chunks -= 1
    half = rows // 2
    return pl.pallas_call(
        functools.partial(line_sum_kernel, count, chunks, window, lag),
        in_specs=[pl.BlockSpec(memory_space=pltpu.VMEM)],
        out_specs=pl.BlockSpec(memory_space=pltpu.VMEM),
        out_shape=jax.ShapeDtypeStruct((rows, columns), BF16),
        scratch_shapes=[pltpu.VMEM((half, columns), BF16)] * 4
        + [pltpu.SemaphoreType.DMA((chunks,))] * 8,
        compiler_params=pltpu.CompilerParams(
            collective_id=collective_id, has_side_effects=True, vmem_limit_bytes=VMEM_LIMIT
        ),
        name="line_sum",
    )(partial)


def share_stats_kernel(count, x_ref, top_ref, log_ref, picked_ref, held, send, recv):
    f, c, t = here()
    peers = [(f, c, lax.rem(t + k, count)) for k in range(1, count)]
    greet(peers)
    copies = []
    for k in range(1, count):
        copy = remote(x_ref, held.at[t], send.at[k], recv.at[k], peers[k - 1])
        copy.start()
        copies.append(copy)
    held[t] = x_ref[...]
    for copy in copies:
        copy.wait()
    highest = functools.reduce(jnp.maximum, [held[k, 0] for k in range(count)])
    total = sum(held[k, 1] * jnp.exp(held[k, 0] - highest) for k in range(count))
    top_ref[...] = highest
    log_ref[...] = highest + jnp.log(total)
    picked_ref[...] = sum(held[k, 2] for k in range(count))


def share_stats(stats, collective_id):
    count = lax.axis_size("tp")
    shape = jax.ShapeDtypeStruct(stats.shape[1:], F32)
    return pl.pallas_call(
        functools.partial(share_stats_kernel, count),
        in_specs=[pl.BlockSpec(memory_space=pltpu.VMEM)],
        out_specs=[pl.BlockSpec(memory_space=pltpu.VMEM)] * 3,
        out_shape=[shape] * 3,
        scratch_shapes=[
            pltpu.VMEM((count,) + stats.shape, F32),
            pltpu.SemaphoreType.DMA((count,)),
            pltpu.SemaphoreType.DMA((count,)),
        ],
        compiler_params=pltpu.CompilerParams(collective_id=collective_id, has_side_effects=True),
        name="share_stats",
    )(stats)


def after(value, earlier):
    return lax.optimization_barrier((value, earlier))[0]


def tp_list(value):
    count = lax.axis_size("tp")
    return [value] + [
        lax.ppermute(value, "tp", [(i, (i + k) % count) for i in range(count)])
        for k in range(1, count)
    ]


def ctx_gather(value):
    if lax.axis_size("ctx") == 2:
        return jnp.concatenate([value, swap(value, "ctx", 1)], axis=0)
    return lax.all_gather(value, "ctx", axis=0, tiled=True)


def ctx_pair(value):
    if lax.axis_size("ctx") == 2:
        return [value, swap(value, "ctx", 1)]
    return [lax.all_gather(value, "ctx", axis=0, tiled=True)]


def ctx_join(parts):
    return jnp.concatenate(parts, axis=0)


def ctx_positions(rows):
    c, count = lax.axis_index("ctx"), lax.axis_size("ctx")
    if count == 2:
        return jnp.concatenate(
            [c * rows + jnp.arange(rows), (1 - c) * rows + jnp.arange(rows)]
        ).astype(jnp.int32)
    return jnp.arange(rows * count, dtype=jnp.int32)


def ctx_scatter(value):
    if lax.axis_size("ctx") == 2:
        rows = value.shape[0] // 2
        return low_sum(value[:rows], swap(value[rows:], "ctx", 1))
    return lax.psum_scatter(value.astype(F32), "ctx", scatter_dimension=0, tiled=True).astype(BF16)


def exit_forward_kernel(
    valid, x_ref, e_ref, target_ref, logits_ref, top_ref, sum_ref, picked_ref, m_acc, l_acc, p_acc
):
    step = pl.program_id(0)
    rows, tile = logits_ref.shape

    @pl.when(step == 0)
    def _():
        m_acc[...] = jnp.full_like(m_acc, LOWEST)
        l_acc[...] = jnp.zeros_like(l_acc)
        p_acc[...] = jnp.zeros_like(p_acc)

    lanes = lax.broadcasted_iota(jnp.int32, (rows, 128), 1)
    logits_ref[...] = mat(x_ref[...], e_ref[...])
    relative = target_ref[...] - step * tile
    limit = valid - step * tile
    groups = tile // 128
    highest = m_acc[...]
    for g in range(groups):
        cols = slice(g * 128, (g + 1) * 128)
        part = jnp.where(lanes < limit - g * 128, logits_ref[:, cols], LOWEST)
        highest = jnp.maximum(highest, part)
    total = l_acc[...] * jnp.exp(m_acc[...] - highest)
    picked = p_acc[...]
    for g in range(groups):
        cols = slice(g * 128, (g + 1) * 128)
        part = jnp.where(lanes < limit - g * 128, logits_ref[:, cols], LOWEST)
        total += jnp.exp(part - highest)
        picked += jnp.where(lanes == relative - g * 128, part, 0.0)
    m_acc[...] = highest
    l_acc[...] = total
    p_acc[...] = picked

    @pl.when(step == pl.num_programs(0) - 1)
    def _():
        top = jnp.max(m_acc[...], axis=1, keepdims=True)
        top_ref[...] = top
        sum_ref[...] = jnp.sum(l_acc[...] * jnp.exp(m_acc[...] - top), axis=1, keepdims=True)
        picked_ref[...] = jnp.sum(p_acc[...], axis=1, keepdims=True)


def exit_forward(exit_in, embed_t, targets_local, valid):
    rows, features = exit_in.shape
    padded = embed_t.shape[1]
    column = pl.BlockSpec((rows, 1), lambda i: (0, 0))
    stat = jax.ShapeDtypeStruct((rows, 1), F32)
    return pl.pallas_call(
        functools.partial(exit_forward_kernel, valid),
        grid=(padded // TILE,),
        in_specs=[
            pl.BlockSpec((rows, features), lambda i: (0, 0)),
            pl.BlockSpec((features, TILE), lambda i: (0, i)),
            column,
        ],
        out_specs=[pl.BlockSpec((rows, TILE), lambda i: (0, i)), column, column, column],
        out_shape=[jax.ShapeDtypeStruct((rows, padded), F32), stat, stat, stat],
        scratch_shapes=[pltpu.VMEM((rows, 128), F32)] * 3,
        compiler_params=pltpu.CompilerParams(vmem_limit_bytes=VMEM_LIMIT),
        cost_estimate=pl.CostEstimate(
            flops=2 * rows * features * padded,
            bytes_accessed=4 * rows * padded + 2 * features * padded,
            transcendentals=rows * padded,
        ),
        name="exit_forward",
    )(exit_in, embed_t, targets_local)


def forward_kernel(heads, q_ref, kv_ref, bias_ref, out_ref, total_ref):
    width = heads * HD
    for h in range(heads):
        cols = slice(h * HD, (h + 1) * HD)
        keys = kv_ref[:, cols]
        values = kv_ref[:, width + h * HD : width + (h + 1) * HD]
        scores = mat_nt(keys, q_ref[:, cols])
        if bias_ref is not None:
            scores = scores + bias_ref[...]
        highest = jnp.max(scores, axis=0, keepdims=True)
        exponent = jnp.exp(scores - highest)
        denominator = jnp.sum(exponent, axis=0, keepdims=True)
        outcome = mat_tn(values, exponent.astype(BF16)) / denominator
        out_ref[:, cols] = outcome.T.astype(BF16)
        total_ref[h : h + 1, :] = highest + jnp.log(denominator)


def backward_kernel(
    heads, q_ref, kv_ref, bias_ref, total_ref, go_ref, dq_ref, dkv_ref, acc_ref
):
    width = heads * HD
    step = pl.program_id(0)

    @pl.when(step == 0)
    def _():
        acc_ref[...] = jnp.zeros_like(acc_ref)

    for h in range(heads):
        cols = slice(h * HD, (h + 1) * HD)
        vcols = slice(width + h * HD, width + (h + 1) * HD)
        keys, values = kv_ref[:, cols], kv_ref[:, vcols]
        queries, go = q_ref[:, cols], go_ref[:, cols]
        scores = mat_nt(keys, queries)
        if bias_ref is not None:
            scores = scores + bias_ref[...]
        probs = jnp.exp(scores - total_ref[h : h + 1, :])
        grad_probs = mat_nt(values, go)
        inner = jnp.sum(probs * grad_probs, axis=0, keepdims=True)
        grad_scores = (probs * (grad_probs - inner)).astype(BF16)
        acc_ref[:, vcols] += mat(probs.astype(BF16), go)
        acc_ref[:, cols] += mat(grad_scores, queries)
        dq_ref[:, cols] = mat_tn(keys, grad_scores).T.astype(BF16)

    @pl.when(step == pl.num_programs(0) - 1)
    def _():
        dkv_ref[...] = acc_ref[...].astype(BF16)


def attention_specs(rows, width, keys, tile, masked):
    specs = [
        pl.BlockSpec((tile, width), lambda i: (i, 0)),
        pl.BlockSpec((keys, 2 * width), lambda i: (0, 0)),
    ]
    if masked:
        specs.append(pl.BlockSpec((keys, tile), lambda i: (0, i)))
    return specs


def attend(queries, kv, bias):
    rows, width = queries.shape
    keys, heads = kv.shape[0], width // HD
    tile = min(rows, 256)
    masked = bias is not None
    body = functools.partial(forward_kernel, heads)
    if not masked:
        plain = body
        body = lambda q, k, o, t: plain(q, k, None, o, t)
    return pl.pallas_call(
        body,
        grid=(rows // tile,),
        in_specs=attention_specs(rows, width, keys, tile, masked),
        out_specs=[
            pl.BlockSpec((tile, width), lambda i: (i, 0)),
            pl.BlockSpec((heads, tile), lambda i: (0, i)),
        ],
        out_shape=[
            jax.ShapeDtypeStruct((rows, width), BF16),
            jax.ShapeDtypeStruct((heads, rows), F32),
        ],
        compiler_params=pltpu.CompilerParams(vmem_limit_bytes=VMEM_LIMIT),
        cost_estimate=pl.CostEstimate(
            flops=16 * rows * keys * width,
            bytes_accessed=4 * keys * width + 8 * rows * width,
            transcendentals=rows * keys * heads,
        ),
        name="attend_masked" if masked else "attend",
    )(*([queries, kv, bias] if masked else [queries, kv]))


def attend_back(queries, kv, bias, totals, go):
    rows, width = queries.shape
    keys, heads = kv.shape[0], width // HD
    tile = min(rows, 256)
    masked = bias is not None
    body = functools.partial(backward_kernel, heads)
    if not masked:
        plain = body
        body = lambda q, k, *rest: plain(q, k, None, *rest)
    specs = attention_specs(rows, width, keys, tile, masked) + [
        pl.BlockSpec((heads, tile), lambda i: (0, i)),
        pl.BlockSpec((tile, width), lambda i: (i, 0)),
    ]
    operands = ([queries, kv, bias] if masked else [queries, kv]) + [totals, go]
    return pl.pallas_call(
        body,
        grid=(rows // tile,),
        in_specs=specs,
        out_specs=[
            pl.BlockSpec((tile, width), lambda i: (i, 0)),
            pl.BlockSpec((keys, 2 * width), lambda i: (0, 0)),
        ],
        out_shape=[
            jax.ShapeDtypeStruct((rows, width), BF16),
            jax.ShapeDtypeStruct((keys, 2 * width), BF16),
        ],
        scratch_shapes=[pltpu.VMEM((keys, 2 * width), F32)],
        compiler_params=pltpu.CompilerParams(vmem_limit_bytes=VMEM_LIMIT),
        cost_estimate=pl.CostEstimate(
            flops=40 * rows * keys * width,
            bytes_accessed=8 * keys * width + 10 * rows * width,
            transcendentals=rows * keys * heads,
        ),
        name="attend_back_masked" if masked else "attend_back",
    )(*operands)


def rms_scale(values):
    return lax.rsqrt(jnp.mean(values * values, axis=-1, keepdims=True) + EPSILON)


def rms_back(grad_normed, normed, scale):
    return scale * (grad_normed - normed * jnp.mean(grad_normed * normed, axis=-1, keepdims=True))


def mask_bias(parent_row, row_count):
    block_count = parent_row.shape[0]
    blocks = jnp.arange(block_count, dtype=jnp.int32)
    current = blocks
    reachable = blocks[:, None] == blocks[None, :]
    for _ in range(block_count - 1):
        current = jnp.sum(
            jnp.where(current[:, None] == blocks[None, :], parent_row[None, :], 0), axis=1
        )
        reachable = reachable | (current[:, None] == blocks[None, :])
    query_pos = lax.axis_index("ctx") * row_count + jnp.arange(row_count, dtype=jnp.int32)
    key_pos = ctx_positions(row_count)
    query_onehot = (query_pos[:, None] // BLK == blocks[None, :]).astype(F32)
    key_onehot = (key_pos[:, None] // BLK == blocks[None, :]).astype(F32)
    linked = mat_nt(key_onehot, mat(query_onehot, reachable.astype(F32))) > 0.5
    causal = (query_pos[None, :] // BLK != key_pos[:, None] // BLK) | (
        key_pos[:, None] <= query_pos[None, :]
    )
    return jnp.where(linked & causal, 0.0, MASKED)


def gelu_parts(gate):
    root = math.sqrt(2.0 / math.pi)
    inner = jnp.tanh(root * (gate + 0.044715 * gate * gate * gate))
    value = 0.5 * gate * (1.0 + inner)
    slope = 0.5 * (1.0 + inner) + 0.5 * gate * (1.0 - inner * inner) * root * (
        1.0 + 3.0 * 0.044715 * gate * gate
    )
    return value, slope


FORWARD_ORDER = (
    ("GX", "h"), ("CP",), ("FL", 0), ("GY", "h"), ("OL", 0), ("GX", "e0"), ("GA", "h"),
    ("GY", "e2"), ("GF", "h"), ("GX", "e2"), ("OL", 1), ("FL", 1), ("GD", "h"), ("GY", "e0"),
    ("GE", "h"), ("GF", "e0"), ("GF", "e2"), ("OL", 2), ("PT", 1), ("CS", 1), ("FL", 2),
    ("PT", 0), ("BI",), ("OL", 3), ("CS", 0), ("GX", "e1"), ("GA", "e2"), ("PE", 1), ("FL", 3),
    ("WS", 1), ("GY", "o"), ("PE", 0), ("GX", "o"), ("S", 1, 0), ("S", 1, 1), ("S", 1, 2),
    ("WS", 0), ("GY", "e1"), ("GA", "o"), ("S", 0, 0), ("AL", 1), ("CC", 0), ("AH", 1, 1),
    ("GA", "e0"), ("S", 0, 1), ("GF", "o"), ("S", 0, 2), ("AH", 1, 2), ("AL", 0), ("GD", "o"),
    ("CC", 1), ("GY", "f0"), ("GX", "f0"), ("AH", 0, 1), ("AH", 0, 2), ("AH", 0, 3), ("GE", "o"),
    ("GX", "f1"), ("OS", 0), ("WC", 0), ("AH", 1, 3), ("GD", "e0"), ("GA", "f0"), ("X", 0, 0),
    ("X", 0, 1), ("GF", "e1"), ("X", 0, 2), ("BL", 0), ("OS", 1), ("WC", 1), ("GY", "f1"),
    ("X", 1, 0), ("BH", 0, 1), ("GF", "f0"), ("GF", "f1"), ("GE", "e0"), ("GA", "e1"),
    ("X", 1, 1), ("GD", "e2"), ("X", 1, 2), ("BL", 1), ("GD", "e1"), ("BH", 0, 2), ("BH", 0, 3),
    ("GE", "e2"), ("OC", 0), ("BH", 1, 1), ("GD", "f0"), ("BH", 1, 2), ("GA", "f1"), ("GD", "f1"),
    ("BH", 1, 3), ("GE", "e1"), ("GE", "f0"), ("OC", 1), ("GE", "f1"),
)
EMBED_PIECES = ((2816, "xy"), (2816, "xy"), (2560, "yx"))


class Line:
    def __init__(self, t, count, left, right, own, place, sems):
        self.t, self.count, self.left, self.right = t, count, left, right
        self.own, self.place = own, place
        self.to_right, self.to_left, self.recv = sems

    def copy(self, d, way):
        origin = self.t - d if way == 0 else self.t + d
        sems, peer = (self.to_right, self.right) if way == 0 else (self.to_left, self.left)
        src = self.own if d == 0 else self.place(origin)
        return remote(src, self.place(origin), sems.at[d], self.recv.at[origin], peer)

    def landed(self, origin):
        return remote(
            self.place(origin),
            self.place(origin),
            self.to_right.at[0],
            self.recv.at[origin],
            self.right,
        )

    def start(self):
        @pl.when(self.t < self.count - 1)
        def _():
            self.copy(0, 0).start()

        @pl.when(self.t > 0)
        def _():
            self.copy(0, 1).start()

    def hop(self, d):
        t, last = self.t, self.count - 1

        @pl.when(t - d >= 0)
        def _():
            self.landed(t - d).wait_recv()
            if d < last:

                @pl.when(t < last)
                def _():
                    self.copy(d, 0).start()

        @pl.when(t + d <= last)
        def _():
            self.landed(t + d).wait_recv()
            if d < last:

                @pl.when(t > 0)
                def _():
                    self.copy(d, 1).start()

    def finish(self):
        t, last = self.t, self.count - 1
        for d in range(last):

            @pl.when((t - d >= 0) & (t < last))
            def _():
                self.copy(d, 0).wait_send()

            @pl.when((t + d <= last) & (t > 0))
            def _():
                self.copy(d, 1).wait_send()


class Spread:
    def __init__(self, peers, own, blocks, send, recv):
        first_peer, second_peer, core_peer = peers
        home, across, aside, diagonal = blocks
        moves = [
            (own, home, first_peer),
            (own, home, second_peer),
            (across, across, second_peer),
            (own, home, core_peer),
            (across, across, core_peer),
            (aside, aside, core_peer),
            (diagonal, diagonal, core_peer),
        ]
        self.copies = [
            remote(src, dst, send.at[j], recv.at[j], peer)
            for j, (src, dst, peer) in enumerate(moves)
        ]

    def start_first(self):
        self.copies[0].start()

    def start_second(self):
        self.copies[1].start()
        self.copies[3].start()

    def pass_across(self):
        self.copies[0].wait_recv()
        self.copies[2].start()
        self.copies[4].start()

    def pass_aside(self):
        self.copies[1].wait_recv()
        self.copies[5].start()

    def pass_diagonal(self):
        self.copies[2].wait_recv()
        self.copies[6].start()

    def arrive(self):
        for j in (3, 4, 5, 6):
            self.copies[j].wait_recv()

    def finish(self):
        for copy in self.copies:
            copy.wait_send()


def attend_head(h, i, tile, q_ref, kv_ref, bias_ref, out_ref, total_ref):
    rows, width = q_ref.shape[0] // MB, q_ref.shape[1]
    cols = slice(h * HD, (h + 1) * HD)
    vcols = slice(width + h * HD, width + (h + 1) * HD)

    @pl.loop(0, rows // tile)
    def _(n):
        at = pl.ds(pl.multiple_of(i * rows + n * tile, tile), tile)
        here_at = pl.ds(pl.multiple_of(n * tile, tile), tile)
        scores = mat_nt(kv_ref[i, :, cols], q_ref[at, cols])
        if bias_ref is not None:
            scores = scores + bias_ref[i, :, here_at]
        highest = jnp.max(scores, axis=0, keepdims=True)
        exponent = jnp.exp(scores - highest)
        denominator = jnp.sum(exponent, axis=0, keepdims=True)
        outcome = mat_tn(kv_ref[i, :, vcols], exponent.astype(BF16)) / denominator
        out_ref[at, cols] = outcome.T.astype(BF16)
        total_ref[i, h : h + 1, here_at] = highest + jnp.log(denominator)


def build_bias(parents_ref, bias_ref, c):
    trees, keys, rows = bias_ref.shape
    mine = rows // BLK
    block_count = keys // BLK
    key_iota = lax.broadcasted_iota(jnp.int32, (BLK, BLK), 0)
    query_iota = lax.broadcasted_iota(jnp.int32, (BLK, BLK), 1)
    causal = jnp.where(key_iota <= query_iota, 0.0, MASKED)
    for i in range(trees):
        lines = [jnp.int32(1)]
        for b in range(1, block_count):
            parent = parents_ref[i, b]
            line = jnp.int32(1 << b)
            for j in range(b):
                line = line + jnp.where(parent == j, lines[j], 0)
            lines.append(line)
        for q in range(mine):
            line = jnp.int32(0)
            for b in range(block_count):
                line = line + jnp.where(c * mine + q == b, lines[b], 0)
            for k in range(block_count):
                at = (slice(k * BLK, (k + 1) * BLK), slice(q * BLK, (q + 1) * BLK))
                if k == q:
                    bias_ref[(i,) + at] = causal.astype(BF16)
                    continue
                block = c * mine + k if k < mine else (1 - c) * mine + k - mine
                seen = lax.shift_right_logical(line, block) & 1
                value = jnp.where(seen == 1, 0.0, MASKED)
                bias_ref[(i,) + at] = jnp.full((BLK, BLK), value, F32).astype(BF16)


def layer_forward_kernel(
    count, parents_ref, tok_ref, enc_ref, heads_in, op_in, ff_in, embed_in, *refs
):
    ff_all, embed_all = refs[:2]
    results, staged = refs[2:17], refs[17:32]
    (
        heads_all,
        own_out,
        query_all,
        gains_out,
        bias,
        q_out,
        kvs,
        kvc,
        att,
        tots,
        cq,
        as_out,
        crs,
        totc,
        ac_out,
    ) = staged
    (
        op_all,
        zop,
        zff,
        held_s,
        held_c,
        spread_send,
        spread_recv,
        line_right,
        line_left,
        line_recv,
        ctx_send,
        ctx_recv,
        local_sem,
    ) = refs[32:]
    f, c, t = here()
    right, left = (f, c, t + 1), (f, c, t - 1)
    x_peer, y_peer, core_peer = (f, 1 - c, t), (f ^ 2, c, t), (f ^ 1, c, t)
    rows, enc_rows = tok_ref.shape[0] // MB, enc_ref.shape[0] // MB
    width = q_out.shape[1]
    shard, ff_cols = ff_in.shape
    tile = 256

    barrier = pltpu.get_barrier_semaphore()
    for peer in (x_peer, y_peer, core_peer):
        pl.semaphore_signal(barrier, inc=1, device_id=peer, device_id_type=MESH)

    @pl.when(t > 0)
    def _():
        pl.semaphore_signal(barrier, inc=1, device_id=left, device_id_type=MESH)

    @pl.when(t < count - 1)
    def _():
        pl.semaphore_signal(barrier, inc=1, device_id=right, device_id_type=MESH)

    at_end = (t == 0) | (t == count - 1)
    pl.semaphore_wait(barrier, jnp.where(at_end, 4, 5).astype(jnp.int32))

    def block(df, dc):
        slot = (f ^ df) * 2 + (c ^ dc)
        return pl.ds(pl.multiple_of(slot * shard, shard), shard)

    def spread(j, way, own, place):
        blocks = [place(block(df, dc)) for df, dc in ((0, 0), (0, 1), (2, 0), (2, 1))]
        peers = (x_peer, y_peer, core_peer)
        if way == "yx":
            blocks = [blocks[0], blocks[2], blocks[1], blocks[3]]
            peers = (y_peer, x_peer, core_peer)
        return Spread(peers, own, blocks, spread_send.at[j], spread_recv.at[j])

    def line(j, own, place):
        sems = (line_right.at[j], line_left.at[j], line_recv.at[j])
        return Line(t, count, left, right, own, place, sems)

    def part(i):
        return pl.ds(i * rows, rows)

    def ff_place(origin):
        return zff.at[:, pl.ds(pl.multiple_of(origin * ff_cols, 128), ff_cols)]

    op_line = line(0, op_in, lambda origin: zop.at[:, origin])
    ff_line = line(1, ff_in, ff_place)
    spreads = {
        "h": spread(0, "xy", heads_in, lambda at: heads_all.at[at]),
        "o": spread(1, "xy", zop, lambda at: op_all.at[:, :, at]),
    }
    ff_half = zff.shape[1] // 2
    pieces = [("f0", "xy", zff, ff_all, 0, ff_half), ("f1", "yx", zff, ff_all, ff_half, ff_half)]
    start = 0
    for j, (size, way) in enumerate(EMBED_PIECES):
        pieces.append(("e%d" % j, way, embed_in, embed_all, start, size))
        start += size
    for name, way, own, target, first, size in pieces:
        cols = pl.ds(first, size)
        spreads[name] = spread(
            len(spreads), way, own.at[:, cols], lambda at, ref=target, cols=cols: ref.at[at, cols]
        )
    ff_own = pltpu.make_async_copy(zff, ff_all.at[block(0, 0)], local_sem.at[0])
    embed_own = pltpu.make_async_copy(embed_in, embed_all.at[block(0, 0)], local_sem.at[1])
    self_lines = [
        line(2 + i, att.at[part(i)], lambda origin, i=i: held_s.at[origin, part(i)])
        for i in range(MB)
    ]
    cross_lines = [
        line(4 + i, crs.at[part(i)], lambda origin, i=i: held_c.at[origin, part(i)])
        for i in range(MB)
    ]

    def ctx_copy(j, ref, i, size):
        return remote(
            ref.at[i, pl.ds(0, size)],
            ref.at[i, pl.ds(size, size)],
            ctx_send.at[j],
            ctx_recv.at[j],
            x_peer,
        )

    ctx_self = [ctx_copy(i, kvs, i, rows) for i in range(MB)]
    ctx_cross = [ctx_copy(2 + i, kvc, i, enc_rows) for i in range(MB)]

    def project_tokens(i):
        @pl.loop(0, rows // tile)
        def _(n):
            at = pl.ds(pl.multiple_of(i * rows + n * tile, tile), tile)
            value = tok_ref[at].astype(F32)
            hidden = (value * rms_scale(value) * gains_out[0:1]).astype(BF16)
            q_out[at] = mat(hidden, heads_all[:, 4 * width : 5 * width]).astype(BF16)
            inner = pl.ds(pl.multiple_of(n * tile, tile), tile)
            kvs[i, inner] = mat(hidden, heads_all[:, : 2 * width]).astype(BF16)

    def project_encoder(i):
        @pl.loop(0, enc_rows // tile)
        def _(n):
            at = pl.ds(pl.multiple_of(i * enc_rows + n * tile, tile), tile)
            inner = pl.ds(pl.multiple_of(n * tile, tile), tile)
            kvc[i, inner] = mat(enc_ref[at], heads_all[:, 2 * width : 4 * width]).astype(BF16)

    def self_head(i, h):
        attend_head(h, i, tile, q_out, kvs, bias, att, tots)

    def cross_head(i, h):
        attend_head(h, i, tile, cq, kvc, None, crs, totc)

    def out_self(i):
        @pl.loop(0, rows // tile)
        def _(n):
            at = pl.ds(pl.multiple_of(i * rows + n * tile, tile), tile)
            total = tok_ref[at].astype(F32)
            for origin in range(count):
                total = total + mat_nt(held_s[origin, at], op_all[0, origin])
            as_out[at] = total
            hidden = (total * rms_scale(total) * gains_out[1:2]).astype(BF16)
            cq[at] = mat(hidden, heads_all[:, Q2 : Q2 + width]).astype(BF16)

    def out_cross(i):
        @pl.loop(0, rows // tile)
        def _(n):
            at = pl.ds(pl.multiple_of(i * rows + n * tile, tile), tile)
            total = as_out[at]
            for origin in range(count):
                total = total + mat_nt(held_c[origin, at], op_all[1, origin])
            ac_out[at] = total

    def own_parts():
        heads_all[block(0, 0)] = heads_in[...]
        zop[:, t] = op_in[...]
        zff[:, pl.ds(pl.multiple_of(t * ff_cols, 128), ff_cols)] = ff_in[...]
        embed_own.start()

    def gather_done(name):
        spreads[name].arrive()
        if name == "h":
            gains_out[...] = heads_all[:, Q2 - 128 : Q2].astype(F32).T[64:72]

    def gather_first(name):
        spreads[name].start_first()
        if name == "o":
            op_all[:, :, block(0, 0)] = zop[...]
        if name == "f0":
            ff_own.start()

    def along(one, d):
        if d == 0:
            one.start()
        else:
            one.hop(d)

    def send_self(i):
        held_s[t, part(i)] = att[part(i)]
        self_lines[i].start()

    def send_cross(i):
        held_c[t, part(i)] = crs[part(i)]
        cross_lines[i].start()

    steps = {
        "GX": gather_first,
        "GY": lambda name: spreads[name].start_second(),
        "GF": lambda name: spreads[name].pass_across(),
        "GA": lambda name: spreads[name].pass_aside(),
        "GD": lambda name: spreads[name].pass_diagonal(),
        "GE": gather_done,
        "OL": lambda d: along(op_line, d),
        "FL": lambda d: along(ff_line, d),
        "CP": own_parts,
        "BI": lambda: build_bias(parents_ref, bias, c),
        "PT": project_tokens,
        "PE": project_encoder,
        "CS": lambda i: ctx_self[i].start(),
        "CC": lambda i: ctx_cross[i].start(),
        "WS": lambda i: ctx_self[i].wait_recv(),
        "WC": lambda i: ctx_cross[i].wait_recv(),
        "S": self_head,
        "X": cross_head,
        "AL": send_self,
        "AH": lambda i, d: self_lines[i].hop(d),
        "BL": send_cross,
        "BH": lambda i, d: cross_lines[i].hop(d),
        "OS": out_self,
        "OC": out_cross,
    }
    leaving = [
        pltpu.make_async_copy(src, dst, local_sem.at[2 + j])
        for j, (src, dst) in enumerate(zip(staged, results))
    ]
    ready = {("OS", 1), ("WC", 1), ("WC", 0), ("GE", "o")}
    for name, *rest in FORWARD_ORDER:
        steps[name](*rest)
        if (name, *rest) in ready:
            ready.remove((name, *rest))
            if not ready:
                own_out[...] = op_all[:2, t]
                query_all[...] = op_all[2]
                for copy in leaving[:12]:
                    copy.start()
    for copy in leaving[12:]:
        copy.start()
    for one in list(spreads.values()) + [op_line, ff_line] + self_lines + cross_lines:
        one.finish()
    for copy in ctx_self + ctx_cross:
        copy.wait_send()
    ff_own.wait()
    embed_own.wait()
    for copy in leaving:
        copy.wait()


def layer_forward(parents, tokens, encoder, heads_in, op_in, ff_in, embed_in, collective_id):
    count = lax.axis_size("tp")
    tok_rows, features = tokens.shape
    enc_rows = encoder.shape[0]
    shard, ff_cols = ff_in.shape
    width = op_in.shape[2]
    nh = width // HD
    rows = tok_rows // MB
    vmem = pl.BlockSpec(memory_space=pltpu.VMEM)
    anywhere = pl.BlockSpec(memory_space=pl.ANY)

    def low(*shape):
        return jax.ShapeDtypeStruct(shape, BF16)

    def full(*shape):
        return jax.ShapeDtypeStruct(shape, F32)

    results = [
        low(features, heads_in.shape[1]),
        low(2, features, width),
        low(count, features, width),
        full(8, features),
        low(MB, 2 * rows, rows),
        low(tok_rows, width),
        low(MB, 2 * rows, 2 * width),
        low(MB, enc_rows, 2 * width),
        low(tok_rows, width),
        full(MB, nh, rows),
        low(tok_rows, width),
        full(tok_rows, features),
        low(tok_rows, width),
        full(MB, nh, rows),
        full(tok_rows, features),
    ]
    outcome = pl.pallas_call(
        functools.partial(layer_forward_kernel, count),
        in_specs=[pl.BlockSpec(memory_space=pltpu.SMEM)] + [vmem] * 5 + [anywhere],
        out_specs=[anywhere] * 17,
        out_shape=[low(features, count * ff_cols), low(features, embed_in.shape[1])] + results,
        scratch_shapes=[pltpu.VMEM(r.shape, r.dtype) for r in results]
        + [
            pltpu.VMEM((3, count, features, width), BF16),
            pltpu.VMEM((3, count, shard, width), BF16),
            pltpu.VMEM((shard, count * ff_cols), BF16),
            pltpu.VMEM((count, tok_rows, width), BF16),
            pltpu.VMEM((count, tok_rows, width), BF16),
            pltpu.SemaphoreType.DMA((4 + len(EMBED_PIECES), 7)),
            pltpu.SemaphoreType.DMA((4 + len(EMBED_PIECES), 7)),
            pltpu.SemaphoreType.DMA((6, count)),
            pltpu.SemaphoreType.DMA((6, count)),
            pltpu.SemaphoreType.DMA((6, count)),
            pltpu.SemaphoreType.DMA((4,)),
            pltpu.SemaphoreType.DMA((4,)),
            pltpu.SemaphoreType.DMA((17,)),
        ],
        compiler_params=pltpu.CompilerParams(
            collective_id=collective_id, has_side_effects=True, vmem_limit_bytes=VMEM_MOST
        ),
        name="layer_forward",
    )(parents, tokens, encoder, heads_in, op_in, ff_in, embed_in)
    ff_all, embed_all, heads_all, own_out, query_all, gains, bias, q, kvs, kvc = outcome[:10]
    att, tots, cq, after_self, crs, totc, after_cross = outcome[10:]
    gathered = (heads_all, own_out, query_all, ff_all, embed_all, gains)
    return gathered + (bias, q, kvs, kvc, att, tots, cq, crs, totc, after_self, after_cross)


def ff_forward_kernel(
    shrink, ac_ref, gains_ref, w_ref, gate_ref, up_ref, mixed_ref, low_ref, exit_ref, exit_t_ref, h_acc
):
    step = pl.program_id(0)
    rows = ac_ref.shape[0]
    units = gate_ref.shape[1]
    tile = min(rows, FF_TILE)

    @pl.loop(0, rows // tile)
    def _(n):
        at = pl.ds(pl.multiple_of(n * tile, tile), tile)

        @pl.when(step == 0)
        def _():
            value = ac_ref[at]
            h_acc[at] = (value * rms_scale(value) * gains_ref[2:3]).astype(BF16)
            mixed_ref[at] = value

        hidden = h_acc[at]
        gate = mat(hidden, w_ref[:, :units])
        up = mat(hidden, w_ref[:, units : 2 * units])
        gate_ref[at] = gate
        up_ref[at] = up
        activated = (gelu_parts(gate)[0] * up).astype(BF16)
        mixed_ref[at] += mat_nt(activated, w_ref[:, 2 * units :])

        @pl.when(step == pl.num_programs(0) - 1)
        def _():
            value = mixed_ref[at]
            low_ref[at] = value.astype(BF16)
            exit_in = value * rms_scale(value) * gains_ref[3:4] * shrink
            exit_ref[at] = exit_in.astype(BF16)

    @pl.when(step == pl.num_programs(0) - 1)
    def _():
        exit_t_ref[...] = exit_ref[...].T


def ff_forward(after_cross, gains, ff_all, count, shrink):
    rows, features = after_cross.shape
    cols = ff_all.shape[1] // count
    units = cols // 3

    def fixed(*shape):
        return pl.BlockSpec(shape, lambda i: (0,) * len(shape))

    moving = pl.BlockSpec((rows, units), lambda i: (0, i))
    return pl.pallas_call(
        functools.partial(ff_forward_kernel, shrink),
        grid=(count,),
        in_specs=[
            fixed(rows, features),
            fixed(8, features),
            pl.BlockSpec((features, cols), lambda i: (0, i)),
        ],
        out_specs=[moving, moving] + [fixed(rows, features)] * 3 + [fixed(features, rows)],
        out_shape=[
            jax.ShapeDtypeStruct((rows, count * units), F32),
            jax.ShapeDtypeStruct((rows, count * units), F32),
            jax.ShapeDtypeStruct((rows, features), F32),
            jax.ShapeDtypeStruct((rows, features), BF16),
            jax.ShapeDtypeStruct((rows, features), BF16),
            jax.ShapeDtypeStruct((features, rows), BF16),
        ],
        scratch_shapes=[pltpu.VMEM((rows, features), BF16)],
        compiler_params=pltpu.CompilerParams(vmem_limit_bytes=VMEM_MOST),
        cost_estimate=pl.CostEstimate(
            flops=2 * rows * features * count * cols,
            bytes_accessed=2 * features * count * cols + 8 * rows * count * units,
            transcendentals=rows * count * units,
        ),
        name="ff_forward",
    )(after_cross, gains, ff_all)


def ff_backward_kernel(
    shrink,
    ge_ref,
    mixed_ref,
    cot_ref,
    ac_ref,
    gains_ref,
    co_ref,
    crs_ref,
    w_ref,
    gate_ref,
    up_ref,
    gac_ref,
    gcr_ref,
    grads_ref,
    norms_ref,
    low_ref,
    gcl_ref,
    hid_ref,
    act_ref,
    gg_ref,
    gu_ref,
    acc,
):
    step = pl.program_id(0)
    t = lax.axis_index("tp")
    last = pl.num_programs(0) - 1
    rows = ac_ref.shape[0]
    units = gate_ref.shape[1]
    tile = min(rows, FF_TILE)

    @pl.when(step == 0)
    def _():
        norms_ref[...] = jnp.zeros_like(norms_ref)

    @pl.loop(0, rows // tile)
    def _(n):
        at = pl.ds(pl.multiple_of(n * tile, tile), tile)

        @pl.when(step == 0)
        def _():
            grad_exit = ge_ref[at].astype(F32) * shrink
            mixed = mixed_ref[at]
            scale = rms_scale(mixed)
            normed = mixed * scale
            norms_ref[0:1] += jnp.sum(grad_exit * normed, axis=0, keepdims=True)
            grad_mixed = cot_ref[at].astype(F32) + rms_back(
                grad_exit * gains_ref[3:4], normed, scale
            )
            gac_ref[at] = grad_mixed
            low_ref[at] = grad_mixed.astype(BF16)
            value = ac_ref[at]
            hid_ref[at] = (value * rms_scale(value) * gains_ref[2:3]).astype(BF16)
            acc[at] = jnp.zeros_like(acc[at])

        gate = gate_ref[at]
        up = up_ref[at]
        grad_act = mat(low_ref[at], w_ref[:, 2 * units :])
        value, slope = gelu_parts(gate)
        grad_gate = (grad_act * slope * up).astype(BF16)
        grad_up = (grad_act * value).astype(BF16)
        acc[at] += mat_nt(grad_gate, w_ref[:, :units]) + mat_nt(
            grad_up, w_ref[:, units : 2 * units]
        )

        @pl.when(step == t)
        def _():
            act_ref[at] = (value * up).astype(BF16)
            gg_ref[at] = grad_gate
            gu_ref[at] = grad_up

        @pl.when(step == last)
        def _():
            value = ac_ref[at]
            scale = rms_scale(value)
            normed = value * scale
            grad = acc[at]
            norms_ref[1:2] += jnp.sum(grad * normed, axis=0, keepdims=True)
            total = gac_ref[at] + rms_back(grad * gains_ref[2:3], normed, scale)
            gac_ref[at] = total
            gcl_ref[at] = total.astype(BF16)
            gcr_ref[at] = mat(total.astype(BF16), co_ref[...]).astype(BF16)

    @pl.when(step == last)
    def _():
        pairs = [(hid_ref, gg_ref), (hid_ref, gu_ref), (low_ref, act_ref), (gcl_ref, crs_ref)]
        for k, (left, right) in enumerate(pairs):
            cols = slice(k * units, k * units + right.shape[1])

            @pl.loop(0, grads_ref.shape[0] // 256)
            def _(n):
                at = pl.ds(pl.multiple_of(n * 256, 256), 256)
                grads_ref[at, cols] = mat_tn(left[:, at], right[...]).astype(BF16)


def ff_backward(
    grad_exit,
    mixed,
    cotangent,
    after_cross,
    gains,
    c_out_own,
    crossed,
    ff_all,
    gate,
    up,
    count,
    shrink,
):
    rows, features = after_cross.shape
    cols = ff_all.shape[1] // count
    units = cols // 3
    width = c_out_own.shape[1]

    def fixed(*shape):
        return pl.BlockSpec(shape, lambda i: (0,) * len(shape))

    def low(*shape):
        return jax.ShapeDtypeStruct(shape, BF16)

    moving = pl.BlockSpec((rows, units), lambda i: (0, i))
    return pl.pallas_call(
        functools.partial(ff_backward_kernel, shrink),
        grid=(count,),
        in_specs=[fixed(rows, features)] * 4
        + [
            fixed(8, features),
            fixed(features, width),
            fixed(rows, width),
            pl.BlockSpec((features, cols), lambda i: (0, i)),
            moving,
            moving,
        ],
        out_specs=[
            fixed(rows, features),
            fixed(rows, width),
            fixed(features, cols + width),
            fixed(8, features),
        ],
        out_shape=[
            jax.ShapeDtypeStruct((rows, features), F32),
            low(rows, width),
            low(features, cols + width),
            jax.ShapeDtypeStruct((8, features), F32),
        ],
        scratch_shapes=[pltpu.VMEM((rows, features), BF16)] * 3
        + [pltpu.VMEM((rows, units), BF16)] * 3
        + [pltpu.VMEM((rows, features), F32)],
        compiler_params=pltpu.CompilerParams(vmem_limit_bytes=VMEM_MOST),
        cost_estimate=pl.CostEstimate(
            flops=2 * rows * features * count * cols,
            bytes_accessed=2 * features * count * cols + 8 * rows * count * units,
            transcendentals=rows * count * units,
        ),
        name="ff_backward",
    )(grad_exit, mixed, cotangent, after_cross, gains, c_out_own, crossed, ff_all, gate, up)


def layer_forward_plain(
    parents, tokens, encoder, heads_in, op_in, ff_in, embed_in, collective_id
):
    rows = tokens.shape[0] // MB
    enc_rows = encoder.shape[0] // MB
    width = op_in.shape[2]
    heads_all = lax.all_gather(heads_in, PLANE, axis=0, tiled=True)
    op_all = lax.all_gather(
        lax.all_gather(op_in, "tp", axis=1, tiled=False), PLANE, axis=2, tiled=True
    )
    ff_all = lax.all_gather(
        lax.all_gather(ff_in, "tp", axis=1, tiled=True), PLANE, axis=0, tiled=True
    )
    embed_all = lax.all_gather(embed_in, PLANE, axis=0, tiled=True)
    gains = heads_all[:, Q2 - 64 : Q2 - 56].astype(F32).T
    tok = tokens.astype(F32)
    hidden_one = (tok * rms_scale(tok) * gains[0:1]).astype(BF16)
    queries = mat(hidden_one, heads_all[:, 4 * width : 5 * width]).astype(BF16)
    kv = mat(hidden_one, heads_all[:, : 2 * width]).astype(BF16)
    enc_kv = mat(encoder, heads_all[:, 2 * width : 4 * width]).astype(BF16)

    def both_sides(value, i, count):
        return ctx_gather(value[i * count : (i + 1) * count])

    kv_self = jnp.stack([both_sides(kv, i, rows) for i in range(MB)])
    kv_cross = jnp.stack([both_sides(enc_kv, i, enc_rows) for i in range(MB)])
    bias = jnp.stack([mask_bias(parents[i], rows) for i in range(MB)]).astype(BF16)

    def attention(values, keys_values, masks):
        outcome = [
            attend(
                values[i * rows : (i + 1) * rows],
                keys_values[i],
                None if masks is None else masks[i],
            )
            for i in range(MB)
        ]
        return jnp.concatenate([o[0] for o in outcome]), jnp.stack([o[1] for o in outcome])

    attended, totals_self = attention(queries, kv_self, bias)
    after_self = line_project(attended, op_all[0], tok, 2)
    hidden_two = (after_self * rms_scale(after_self) * gains[1:2]).astype(BF16)
    cross_q = mat(hidden_two, heads_all[:, Q2 : Q2 + width]).astype(BF16)
    crossed, totals_cross = attention(cross_q, kv_cross, None)
    after_cross = line_project(crossed, op_all[1], after_self, 3)
    return (
        heads_all,
        lax.dynamic_index_in_dim(op_all[:2], lax.axis_index("tp"), 1, False),
        op_all[2],
        ff_all,
        embed_all,
        gains,
        bias,
        queries,
        kv_self,
        kv_cross,
        attended,
        totals_self,
        cross_q,
        crossed,
        totals_cross,
        after_self,
        after_cross,
    )


BACKWARD_ORDER = (
    ("X", 0, 0), ("X", 0, 1), ("X", 0, 2), ("XC", 0), ("SQ", 0), ("X", 1, 0), ("X", 1, 1),
    ("X", 1, 2), ("XC", 1), ("QH", 0, 1), ("SQ", 1), ("EP", 0), ("QH", 0, 2), ("ERN", 0, 0),
    ("QH", 1, 1), ("QH", 0, 3), ("AQ", 0), ("ERN", 0, 1), ("S", 0, 0), ("EP", 1), ("QH", 1, 2),
    ("ERF", 0, 0), ("QH", 1, 3), ("ERN", 0, 2), ("AQ", 1), ("ERF", 0, 1), ("ERN", 1, 0),
    ("S", 0, 1), ("S", 0, 2), ("ERN", 1, 1), ("XS", 0), ("ERF", 1, 0), ("ERN", 0, 3),
    ("ERF", 1, 1), ("ERN", 1, 2), ("S", 1, 0), ("ERF", 0, 2), ("S", 1, 1), ("EBN", 0, 0),
    ("ERF", 0, 3), ("S", 1, 2), ("EBN", 0, 1), ("TP", 0), ("ERF", 1, 2), ("EBN", 1, 0),
    ("EBF", 0, 0), ("XS", 1), ("ERN", 1, 3), ("EBN", 1, 1), ("EBF", 0, 1), ("EBF", 1, 0),
    ("EBN", 0, 2), ("TP", 1), ("EBF", 1, 1), ("ERF", 1, 3), ("ORN", 0, 0), ("ORN", 0, 1),
    ("EBN", 1, 2), ("EBF", 0, 2), ("ORF", 0, 0), ("ORF", 0, 1), ("ORN", 1, 0), ("EBF", 1, 2),
    ("ORN", 1, 1), ("EBN", 0, 3), ("ORF", 1, 0), ("ORF", 1, 1), ("OBN", 0, 0), ("OBN", 0, 1),
    ("EBF", 0, 3), ("OBF", 0, 0), ("OBF", 0, 1), ("OBN", 1, 0), ("OBN", 1, 1), ("EBN", 1, 3),
    ("FT", 0), ("OBF", 1, 0), ("OBF", 1, 1), ("FT", 1), ("EBF", 1, 3),
)


class LineSum:
    def __init__(self, t, count, left, right, x, out, buffers, sems, chunks):
        self.t, self.count, self.left, self.right = t, count, left, right
        self.x, self.out, self.chunks = x, out, chunks
        self.low_in, self.high_in = buffers.at[0], buffers.at[1]
        self.sems = sems
        self.half = x.shape[0] // 2
        self.rows = self.half // chunks

    def low(self, j):
        return pl.ds(j * self.rows, self.rows)

    def high(self, j):
        return pl.ds(self.half + j * self.rows, self.rows)

    def down(self, j, own):
        src = self.x.at[self.low(j)] if own else self.low_in.at[self.low(j)]
        dst = self.low_in.at[self.low(j)]
        return remote(src, dst, self.sems.at[0, j], self.sems.at[1, j], self.left)

    def up(self, j, own):
        src = self.x.at[self.high(j)] if own else self.high_in.at[self.low(j)]
        dst = self.high_in.at[self.low(j)]
        return remote(src, dst, self.sems.at[2, j], self.sems.at[3, j], self.right)

    def low_back(self, j):
        ref = self.out.at[self.low(j)]
        return remote(ref, ref, self.sems.at[4, j], self.sems.at[5, j], self.right)

    def high_back(self, j):
        ref = self.out.at[self.high(j)]
        return remote(ref, ref, self.sems.at[6, j], self.sems.at[7, j], self.left)

    def start(self):
        @pl.when(self.t == self.count - 1)
        def _():
            for j in range(self.chunks):
                self.down(j, True).start()

        @pl.when(self.t == 0)
        def _():
            for j in range(self.chunks):
                self.up(j, True).start()

    def low_step(self, j):
        if not 0 <= j < self.chunks:
            return

        @pl.when(self.t < self.count - 1)
        def _():
            self.down(j, False).wait_recv()
            at = self.low(j)
            total = (self.low_in[at].astype(F32) + self.x[at].astype(F32)).astype(BF16)

            @pl.when(self.t > 0)
            def _():
                self.low_in[at] = total
                self.down(j, False).start()

            @pl.when(self.t == 0)
            def _():
                self.out[at] = total
                self.low_back(j).start()

    def high_step(self, j):
        if not 0 <= j < self.chunks:
            return

        @pl.when(self.t > 0)
        def _():
            self.up(j, False).wait_recv()
            at = self.high(j)
            total = (self.high_in[self.low(j)].astype(F32) + self.x[at].astype(F32)).astype(BF16)

            @pl.when(self.t < self.count - 1)
            def _():
                self.high_in[self.low(j)] = total
                self.up(j, False).start()

            @pl.when(self.t == self.count - 1)
            def _():
                self.out[at] = total
                self.high_back(j).start()

    def low_forward(self, j):
        @pl.when(self.t > 0)
        def _():
            self.low_back(j).wait_recv()

            @pl.when(self.t < self.count - 1)
            def _():
                self.low_back(j).start()

    def high_forward(self, j):
        @pl.when(self.t < self.count - 1)
        def _():
            self.high_back(j).wait_recv()

            @pl.when(self.t > 0)
            def _():
                self.high_back(j).start()

    def by_side(self, first, second, j):
        @pl.when(self.t < self.count // 2)
        def _():
            first(j)

        @pl.when(self.t >= self.count // 2)
        def _():
            second(j)

    def reduce_near(self, j):
        self.by_side(self.high_step, self.low_step, j)

    def reduce_far(self, j):
        self.by_side(self.low_step, self.high_step, j)

    def back_near(self, j):
        self.by_side(self.low_forward, self.high_forward, j)

    def back_far(self, j):
        self.by_side(self.high_forward, self.low_forward, j)

    def finish(self):
        last = self.count - 1
        for j in range(self.chunks):

            @pl.when(self.t > 0)
            def _():
                self.down(j, False).wait_send()
                self.high_back(j).wait_send()

            @pl.when(self.t < last)
            def _():
                self.up(j, False).wait_send()
                self.low_back(j).wait_send()


def attend_back_head(
    h, i, tile, q_ref, kv_ref, bias_ref, total_ref, go_ref, dq_ref, dkv_ref, acc_ref
):
    rows, width = q_ref.shape[0] // MB, q_ref.shape[1]
    keys_count = kv_ref.shape[1]
    cols = slice(h * HD, (h + 1) * HD)
    vcols = slice(width + h * HD, width + (h + 1) * HD)
    acc_ref[:keys_count] = jnp.zeros((keys_count, 2 * HD), F32)

    @pl.loop(0, rows // tile)
    def _(n):
        at = pl.ds(pl.multiple_of(i * rows + n * tile, tile), tile)
        here_at = pl.ds(pl.multiple_of(n * tile, tile), tile)
        keys, values = kv_ref[i, :, cols], kv_ref[i, :, vcols]
        queries, go = q_ref[at, cols], go_ref[at, cols]
        scores = mat_nt(keys, queries)
        if bias_ref is not None:
            scores = scores + bias_ref[i, :, here_at]
        probs = jnp.exp(scores - total_ref[i, h : h + 1, here_at])
        grad_probs = mat_nt(values, go)
        inner = jnp.sum(probs * grad_probs, axis=0, keepdims=True)
        grad_scores = (probs * (grad_probs - inner)).astype(BF16)
        acc_ref[:keys_count, :HD] += mat(grad_scores, queries)
        acc_ref[:keys_count, HD:] += mat(probs.astype(BF16), go)
        dq_ref[at, cols] = mat_tn(keys, grad_scores).T.astype(BF16)

    dkv_ref[i, :, cols] = acc_ref[:keys_count, :HD].astype(BF16)
    dkv_ref[i, :, vcols] = acc_ref[:keys_count, HD:].astype(BF16)


def layer_backward_kernel(
    count, gcr_ref, cq_ref, kvc_ref, totc_ref, q_ref, tots_ref, wo_ref, gains_ref, *refs
):
    late, outs, scratch = refs[:7], refs[7:15], refs[15:]
    gt_out, enc_sum, gcq, gkvc, gq, gkvs, gsl, norms = outs
    dkvc, dkvc_in, dkvs, dkvs_in, acc, held, gatt, enc_part, one_part, one_sum = scratch[:10]
    enc_buffers, one_buffers = scratch[10:12]
    landed = scratch[12:19]
    line_right, line_left, line_recv, ctx_send, ctx_recv, sum_sems, load_sem = scratch[19:]
    heads_ref, query_ref, as_ref, gac_ref, kvs_ref, bias_ref, tok_ref = landed
    loads = [
        pltpu.make_async_copy(src, dst, load_sem.at[j])
        for j, (src, dst) in enumerate(zip(late, landed))
    ]
    for copy in loads:
        copy.start()
    waiting = list(range(len(loads)))

    def need(*numbers):
        for j in numbers:
            if j in waiting:
                waiting.remove(j)
                loads[j].wait()

    f, c, t = here()
    right, left = (f, c, t + 1), (f, c, t - 1)
    x_peer = (f, 1 - c, t)
    rows, enc_rows = tok_ref.shape[0] // MB, gkvc.shape[0] // MB
    width = q_ref.shape[1]
    tile = 256

    barrier = pltpu.get_barrier_semaphore()
    pl.semaphore_signal(barrier, inc=1, device_id=x_peer, device_id_type=MESH)

    @pl.when(t > 0)
    def _():
        pl.semaphore_signal(barrier, inc=1, device_id=left, device_id_type=MESH)

    @pl.when(t < count - 1)
    def _():
        pl.semaphore_signal(barrier, inc=1, device_id=right, device_id_type=MESH)

    at_end = (t == 0) | (t == count - 1)
    pl.semaphore_wait(barrier, jnp.where(at_end, 2, 3).astype(jnp.int32))

    def part(i):
        return pl.ds(i * rows, rows)

    def enc_at(i):
        return pl.ds(i * enc_rows, enc_rows)

    def line(j, own, place):
        sems = (line_right.at[j], line_left.at[j], line_recv.at[j])
        return Line(t, count, left, right, own, place, sems)

    query_lines = [
        line(i, gcq.at[part(i)], lambda origin, i=i: held.at[origin, part(i)]) for i in range(MB)
    ]

    def ctx_copy(j, ref, landing, i, size):
        return remote(
            ref.at[i, pl.ds(size, size)], landing.at[i], ctx_send.at[j], ctx_recv.at[j], x_peer
        )

    ctx_cross = [ctx_copy(i, dkvc, dkvc_in, i, enc_rows) for i in range(MB)]
    ctx_self = [ctx_copy(MB + i, dkvs, dkvs_in, i, rows) for i in range(MB)]

    def summed(j, x, out, buffers, chunks):
        return LineSum(t, count, left, right, x, out, buffers, sum_sems.at[j], chunks)

    enc_chunks = enc_rows // 256
    one_chunks = rows // 256
    enc_sums = [
        summed(i, enc_part.at[enc_at(i)], enc_sum.at[enc_at(i)], enc_buffers.at[i], enc_chunks)
        for i in range(MB)
    ]
    one_sums = [
        summed(MB + i, one_part.at[part(i)], one_sum.at[part(i)], one_buffers.at[i], one_chunks)
        for i in range(MB)
    ]

    def tiles(i, count_rows, body):
        @pl.loop(0, count_rows // tile)
        def _(n):
            at = pl.ds(pl.multiple_of(i * count_rows + n * tile, tile), tile)
            body(at, pl.ds(pl.multiple_of(n * tile, tile), tile))

    def cross_head(i, h):
        attend_back_head(h, i, tile, cq_ref, kvc_ref, None, totc_ref, gcr_ref, gcq, dkvc, acc)

    def self_head(i, h):
        attend_back_head(h, i, tile, q_ref, kvs_ref, bias_ref, tots_ref, gatt, gq, dkvs, acc)

    def send_queries(i):
        held[t, part(i)] = gcq[part(i)]
        query_lines[i].start()

    def encoder_part(i):
        ctx_cross[i].wait_recv()

        def body(at, inner):
            total = dkvc[i, inner].astype(F32) + dkvc_in[i, inner].astype(F32)
            gkvc[at] = total.astype(BF16)
            enc_part[at] = mat_nt(
                total.astype(BF16), heads_ref[:, 2 * width : 4 * width]
            ).astype(BF16)

        tiles(i, enc_rows, body)
        enc_sums[i].start()

    def after_queries(i):
        def body(at, inner):
            grad = mat_nt(held[0, at], query_ref[0])
            for origin in range(1, count):
                grad = grad + mat_nt(held[origin, at], query_ref[origin])
            value = as_ref[at]
            scale = rms_scale(value)
            normed = value * scale
            norms[1:2] += jnp.sum(grad * normed, axis=0, keepdims=True)
            total = gac_ref[at] + rms_back(grad * gains_ref[1:2], normed, scale)
            gt_out[at] = total
            gsl[at] = total.astype(BF16)
            gatt[at] = mat(total.astype(BF16), wo_ref[...]).astype(BF16)

        tiles(i, rows, body)

    def token_part(i):
        ctx_self[i].wait_recv()

        def body(at, inner):
            total = (dkvs[i, inner].astype(F32) + dkvs_in[i, inner].astype(F32)).astype(BF16)
            gkvs[at] = total
            product = mat_nt(total, heads_ref[:, : 2 * width])
            product = product + mat_nt(gq[at], heads_ref[:, 4 * width : 5 * width])
            one_part[at] = product.astype(BF16)

        tiles(i, rows, body)
        one_sums[i].start()

    def finish_tokens(i):
        def body(at, inner):
            grad = one_sum[at].astype(F32)
            value = tok_ref[at].astype(F32)
            scale = rms_scale(value)
            normed = value * scale
            norms[0:1] += jnp.sum(grad * normed, axis=0, keepdims=True)
            gt_out[at] = gt_out[at] + rms_back(grad * gains_ref[0:1], normed, scale)

        tiles(i, rows, body)

    norms[...] = jnp.zeros_like(norms)
    steps = {
        "X": cross_head,
        "SQ": send_queries,
        "XC": lambda i: ctx_cross[i].start(),
        "QH": lambda i, d: query_lines[i].hop(d),
        "AQ": after_queries,
        "S": self_head,
        "EP": encoder_part,
        "XS": lambda i: ctx_self[i].start(),
        "TP": token_part,
        "FT": finish_tokens,
        "ERN": lambda i, j: enc_sums[i].reduce_near(j),
        "ERF": lambda i, j: enc_sums[i].reduce_far(j),
        "EBN": lambda i, j: enc_sums[i].back_near(j),
        "EBF": lambda i, j: enc_sums[i].back_far(j),
        "ORN": lambda i, j: one_sums[i].reduce_near(j),
        "ORF": lambda i, j: one_sums[i].reduce_far(j),
        "OBN": lambda i, j: one_sums[i].back_near(j),
        "OBF": lambda i, j: one_sums[i].back_far(j),
    }
    needs = {"EP": (0,), "AQ": (1, 2, 3), "S": (4, 5), "TP": (0,), "FT": (6,)}
    for name, *rest in BACKWARD_ORDER:
        need(*needs.get(name, ()))
        steps[name](*rest)
    for one in query_lines + enc_sums + one_sums:
        one.finish()
    for copy in ctx_self + ctx_cross:
        copy.wait_send()


def layer_backward(operands, tokens, enc_rows, collective_id):
    count = lax.axis_size("tp")
    tok_rows, features = tokens.shape
    rows = tok_rows // MB
    enc_tree = enc_rows // MB
    width = operands[0].shape[1]
    vmem = pl.BlockSpec(memory_space=pltpu.VMEM)
    gcr, cq, kvc, totc, q, kvs, bias, tots, gac, after_self, tok, wo, query, heads, gains = operands
    late = (heads, query, after_self, gac, kvs, bias, tok)
    outs = [
        ((tok_rows, features), F32),
        ((enc_rows, features), BF16),
        ((tok_rows, width), BF16),
        ((enc_rows, 2 * width), BF16),
        ((tok_rows, width), BF16),
        ((tok_rows, 2 * width), BF16),
        ((tok_rows, features), BF16),
        ((8, features), F32),
    ]
    scratch = [
        ((MB, 2 * enc_tree, 2 * width), BF16),
        ((MB, enc_tree, 2 * width), BF16),
        ((MB, 2 * rows, 2 * width), BF16),
        ((MB, rows, 2 * width), BF16),
        ((2 * enc_tree, 2 * HD), F32),
        ((count, tok_rows, width), BF16),
        ((tok_rows, width), BF16),
        ((enc_rows, features), BF16),
        ((tok_rows, features), BF16),
        ((tok_rows, features), BF16),
        ((MB, 2, enc_tree // 2, features), BF16),
        ((MB, 2, rows // 2, features), BF16),
    ]
    return pl.pallas_call(
        functools.partial(layer_backward_kernel, count),
        in_specs=[vmem] * 8 + [pl.BlockSpec(memory_space=pl.ANY)] * len(late),
        out_specs=[vmem] * len(outs),
        out_shape=[jax.ShapeDtypeStruct(shape, kind) for shape, kind in outs],
        scratch_shapes=[pltpu.VMEM(shape, kind) for shape, kind in scratch]
        + [pltpu.VMEM(value.shape, value.dtype) for value in late]
        + [
            pltpu.SemaphoreType.DMA((MB, count)),
            pltpu.SemaphoreType.DMA((MB, count)),
            pltpu.SemaphoreType.DMA((MB, count)),
            pltpu.SemaphoreType.DMA((2 * MB,)),
            pltpu.SemaphoreType.DMA((2 * MB,)),
            pltpu.SemaphoreType.DMA((2 * MB, 8, 4)),
            pltpu.SemaphoreType.DMA((len(late),)),
        ],
        compiler_params=pltpu.CompilerParams(
            collective_id=collective_id, has_side_effects=True, vmem_limit_bytes=VMEM_MOST
        ),
        name="layer_backward",
    )(gcr, cq, kvc, totc, q, tots, wo, gains, *late)


EXIT_ORDER = (
    (8, "ST", 0), (11, "RN", 0, 0), (13, "RN", 0, 1), (14, "RN", 0, 2), (15, "ST", 1),
    (15, "RN", 0, 3), (15, "RF", 0, 0), (17, "RN", 1, 0), (17, "RF", 0, 1), (17, "RF", 0, 2),
    (17, "RN", 1, 1), (17, "RN", 1, 2), (17, "RF", 1, 0), (18, "RF", 1, 1), (18, "BN", 0, 0),
    (19, "RF", 0, 3), (19, "RN", 1, 3), (19, "BN", 0, 1), (19, "RF", 1, 2), (19, "BF", 0, 0),
    (19, "RF", 1, 3), (19, "BN", 1, 0), (20, "BN", 1, 1), (20, "BN", 0, 2), (20, "BF", 0, 1),
    (21, "BF", 1, 0), (21, "BN", 1, 2), (21, "BF", 1, 1), (22, "BN", 0, 3), (22, "BF", 0, 2),
    (23, "BN", 1, 3), (23, "BF", 1, 2), (23, "BF", 0, 3), (23, "BF", 1, 3),
)


def exit_backward_kernel(
    count,
    valid,
    logits_ref,
    e_ref,
    x_t_ref,
    target_ref,
    log_ref,
    embed_ref,
    sum_ref,
    grads,
    acc,
    partial,
    total,
    buffers,
    sems,
):
    f, c, t = here()
    right, left = (f, c, t + 1), (f, c, t - 1)
    step = pl.program_id(0)
    size, tile = logits_ref.shape
    tiles = grads.shape[1] // tile
    sums = [
        LineSum(
            t,
            count,
            left,
            right,
            partial.at[pl.ds(p * size, size)],
            total.at[pl.ds(p * size, size)],
            buffers.at[p],
            sems.at[p],
            EXIT_CHUNKS,
        )
        for p in range(EXIT_PIECES)
    ]

    @pl.when(step == 0)
    def _():
        greet_line(t, count, left, right)

    @pl.when(step < EXIT_PIECES * tiles)
    def _():
        piece, k = step // tiles, lax.rem(step, tiles)
        lanes = lax.broadcasted_iota(jnp.int32, (size, tile), 1)
        probs = jnp.exp(logits_ref[...] - log_ref[...])
        probs = jnp.where(lanes < valid - k * tile, probs, 0.0)
        hits = jnp.where(lanes == target_ref[...] - k * tile, 1.0, 0.0)
        grad = (probs - hits).astype(BF16)
        rows = pl.ds(pl.multiple_of(piece * size, size), size)
        grads[rows, pl.ds(pl.multiple_of(k * tile, tile), tile)] = grad
        product = mat_nt(grad, e_ref[...])

        @pl.when(k == 0)
        def _():
            acc[...] = product

        @pl.when(k > 0)
        def _():
            acc[...] += product

        @pl.when(k == tiles - 1)
        def _():
            partial[rows] = acc[...].astype(BF16)

    @pl.when(step >= EXIT_PIECES * tiles)
    def _():
        k = step - EXIT_PIECES * tiles
        columns = pl.ds(pl.multiple_of(k * tile, tile), tile)
        embed_ref[...] = mat(x_t_ref[...], grads[:, columns]).astype(BF16)

    steps = {
        "ST": lambda p: sums[p].start(),
        "RN": lambda p, j: sums[p].reduce_near(j),
        "RF": lambda p, j: sums[p].reduce_far(j),
        "BN": lambda p, j: sums[p].back_near(j),
        "BF": lambda p, j: sums[p].back_far(j),
    }
    for when in sorted({item[0] for item in EXIT_ORDER}):

        @pl.when(step == when)
        def _():
            for at, name, *rest in EXIT_ORDER:
                if at == when:
                    steps[name](*rest)

    @pl.when(step == pl.num_programs(0) - 1)
    def _():
        for one in sums:
            one.finish()
        sum_ref[...] = total[...]


def exit_backward(logits, embed_t, exit_in_t, targets_local, log_total, valid, collective_id):
    rows, padded = logits.shape
    features = embed_t.shape[0]
    count = lax.axis_size("tp")
    size = rows // EXIT_PIECES
    tiles = padded // TILE
    if tiles * (EXIT_PIECES + 1) != EXIT_STEPS:
        raise ValueError("steps")

    def piece_of(i):
        return jnp.minimum(i // tiles, EXIT_PIECES - 1)

    def tile_of(i):
        return jnp.where(i < EXIT_PIECES * tiles, lax.rem(i, tiles), tiles - 1)

    column = pl.BlockSpec((size, 1), lambda i: (piece_of(i), 0))
    return pl.pallas_call(
        functools.partial(exit_backward_kernel, count, valid),
        grid=(EXIT_STEPS,),
        in_specs=[
            pl.BlockSpec((size, TILE), lambda i: (piece_of(i), tile_of(i))),
            pl.BlockSpec((features, TILE), lambda i: (0, tile_of(i))),
            pl.BlockSpec((features, rows), lambda i: (0, 0)),
            column,
            column,
        ],
        out_specs=[
            pl.BlockSpec((features, TILE), lambda i: (0, jnp.maximum(i - EXIT_PIECES * tiles, 0))),
            pl.BlockSpec((rows, features), lambda i: (0, 0)),
        ],
        out_shape=[
            jax.ShapeDtypeStruct((features, padded), BF16),
            jax.ShapeDtypeStruct((rows, features), BF16),
        ],
        scratch_shapes=[
            pltpu.VMEM((rows, padded), BF16),
            pltpu.VMEM((size, features), F32),
            pltpu.VMEM((rows, features), BF16),
            pltpu.VMEM((rows, features), BF16),
            pltpu.VMEM((EXIT_PIECES, 2, size // 2, features), BF16),
            pltpu.SemaphoreType.DMA((EXIT_PIECES, 8, EXIT_CHUNKS)),
        ],
        compiler_params=pltpu.CompilerParams(
            collective_id=collective_id, has_side_effects=True, vmem_limit_bytes=VMEM_MOST
        ),
        cost_estimate=pl.CostEstimate(
            flops=4 * rows * features * padded,
            bytes_accessed=4 * rows * padded + 4 * features * padded,
            transcendentals=rows * padded,
        ),
        name="exit_backward",
    )(logits, embed_t, exit_in_t, targets_local, log_total)


def layer_backward_plain(operands, tokens, enc_rows, collective_id):
    (
        grad_crossed,
        cross_q,
        kv_cross,
        totals_cross,
        queries,
        kv_self,
        bias,
        totals_self,
        grad_after_cross,
        after_self,
        tokens,
        w_out_own,
        c_query_all,
        heads_all,
        gains,
    ) = operands
    rows, width = queries.shape[0] // MB, queries.shape[1]
    trees = range(MB)

    def tree_rows(value, i):
        return value[i * rows : (i + 1) * rows]

    outcome = [
        attend_back(
            tree_rows(cross_q, i), kv_cross[i], None, totals_cross[i], tree_rows(grad_crossed, i)
        )
        for i in trees
    ]
    grad_cq = jnp.concatenate([o[0] for o in outcome], axis=0)
    grad_kv_cross = jnp.concatenate([ctx_scatter(o[1]) for o in outcome], axis=0)
    encoder_part = mat_nt(grad_kv_cross, heads_all[:, 2 * width : 4 * width]).astype(BF16)
    grad_two = line_project(grad_cq, c_query_all, jnp.zeros_like(after_self), 6)
    scale_two = rms_scale(after_self)
    normed_two = after_self * scale_two
    norm_cross = jnp.sum(grad_two * normed_two, axis=0)
    grad_after_self = grad_after_cross + rms_back(grad_two * gains[1:2], normed_two, scale_two)
    grad_self_low = grad_after_self.astype(BF16)
    grad_attended = mat(grad_self_low, w_out_own).astype(BF16)
    outcome = [
        attend_back(
            tree_rows(queries, i), kv_self[i], bias[i], totals_self[i], tree_rows(grad_attended, i)
        )
        for i in trees
    ]
    grad_q = jnp.concatenate([o[0] for o in outcome], axis=0)
    grad_kv_self = jnp.concatenate([ctx_scatter(o[1]) for o in outcome], axis=0)
    part = mat_nt(grad_q, heads_all[:, 4 * width : 5 * width])
    part = (part + mat_nt(grad_kv_self, heads_all[:, : 2 * width])).astype(BF16)
    both = line_sum(jnp.concatenate([part, encoder_part], axis=0), 7, 12)
    grad_one = both[: MB * rows].astype(F32)
    tok = tokens.astype(F32)
    scale_one = rms_scale(tok)
    normed_one = tok * scale_one
    norm_self = jnp.sum(grad_one * normed_one, axis=0)
    grad_tokens = grad_after_self + rms_back(grad_one * gains[0:1], normed_one, scale_one)
    norms = jnp.stack([norm_self, norm_cross] + [jnp.zeros_like(norm_self)] * 6)
    return (
        grad_tokens,
        both[MB * rows :],
        grad_cq,
        grad_kv_cross,
        grad_q,
        grad_kv_self,
        grad_self_low,
        norms,
    )


def local(
    tokens,
    encoder,
    cotangent,
    parents,
    targets,
    w_query,
    w_key,
    w_value,
    w_out,
    c_query,
    c_key,
    c_value,
    c_out,
    w_gate,
    w_up,
    w_down,
    embedding,
    norm_self,
    norm_cross,
    norm_ff,
    norm_exit,
):
    t = lax.axis_index("tp")
    tp_count = lax.axis_size("tp")
    rows = tokens.shape[0] // MB
    features = tokens.shape[1]
    width = w_query.shape[1]
    hidden_units = w_gate.shape[1]
    vocab = embedding.shape[0]
    trees = range(MB)
    shrink = 1.0 / math.sqrt(features)

    def tree_rows(value, i):
        count = value.shape[0] // MB
        return value[i * count : (i + 1) * count]

    gains_in = jnp.stack([norm_self, norm_cross, norm_ff, norm_exit], axis=1)
    heads_in = jnp.concatenate(
        [w_key, w_value, c_key, c_value, w_query]
        + [jnp.pad(gains_in, ((0, 0), (0, 60))), c_query, jnp.zeros_like(c_query[:, :64])],
        axis=1,
    )
    op_in = jnp.stack([w_out.T, c_out.T, c_query])
    ff_in = jnp.concatenate([w_gate, w_up, w_down.T], axis=1)
    padded = -(-vocab // TILE) * TILE
    embed_in = jnp.pad(embedding.T, ((0, 0), (0, padded - vocab)))
    forward = layer_forward if small_plane() else layer_forward_plain
    (
        heads_all,
        own_out,
        query_all,
        ff_all,
        embed_t,
        gains,
        bias,
        queries,
        kv_self,
        kv_cross,
        attended,
        totals_self,
        cross_q,
        crossed,
        totals_cross,
        after_self,
        after_cross,
    ) = forward(parents, tokens, encoder, heads_in, op_in, ff_in, embed_in, 1)
    w_out_own, c_out_own = own_out[0], own_out[1]
    gate_pre, up_pre, mixed, mixed_low, exit_in, exit_in_t = ff_forward(
        after_cross, gains, ff_all, tp_count, shrink
    )

    targets_local = targets - t * vocab
    inside = (targets_local >= 0) & (targets_local < vocab)
    targets_local = jnp.where(inside, targets_local, -1)[:, None]
    logits, top, summed, picked = exit_forward(exit_in, embed_t, targets_local, vocab)
    stats = jnp.stack([top, summed, picked]).reshape(3, MB * rows // 128, 128)
    top, log_total, picked = share_stats(stats, 4)
    losses = (log_total - picked).reshape(-1)
    scores = (top - log_total).reshape(-1)
    grad_embed, grad_exit = exit_backward(
        logits, embed_t, exit_in_t, targets_local, log_total.reshape(-1, 1), vocab, 5
    )
    grad_embed_own = lax.optimization_barrier(
        lax.psum_scatter(grad_embed, PLANE, scatter_dimension=0, tiled=True)
    )

    grad_after_cross, grad_crossed, ff_grads, norms = ff_backward(
        grad_exit,
        mixed,
        cotangent,
        after_cross,
        gains,
        c_out_own,
        crossed,
        ff_all,
        gate_pre,
        up_pre,
        tp_count,
        shrink,
    )
    backward = layer_backward if small_plane() else layer_backward_plain
    (
        grad_tokens,
        grad_encoder,
        grad_cq,
        grad_kv_cross,
        grad_q,
        grad_kv_self,
        grad_self_low,
        norms_low,
    ) = backward(
        (
            grad_crossed,
            cross_q,
            kv_cross,
            totals_cross,
            queries,
            kv_self,
            bias,
            totals_self,
            grad_after_cross,
            after_self,
            tokens,
            w_out_own,
            query_all,
            heads_all,
            gains,
        ),
        tokens,
        encoder.shape[0],
        6,
    )
    ff_own = lax.psum_scatter(ff_grads, PLANE, scatter_dimension=0, tiled=True)
    scatter = weight_scatter if small_plane() else weight_scatter_plain
    own = scatter(
        (
            encoder,
            grad_kv_cross,
            tokens,
            grad_kv_self,
            grad_q,
            after_self,
            grad_cq,
            grad_self_low,
            attended,
            gains,
            norms_low,
            norms,
        ),
        9,
    )

    def part(value, start, size):
        return value[:, start : start + size].astype(F32)

    base = Q2 - 64
    return (
        mixed_low,
        losses,
        scores,
        grad_tokens,
        grad_encoder.astype(F32),
        part(own, 4 * width, width),
        part(own, 2 * width, width),
        part(own, 3 * width, width),
        part(own, Q2 + width, width).T,
        part(own, Q2, width),
        part(own, 0, width),
        part(own, width, width),
        part(ff_own, 3 * hidden_units, width).T,
        part(ff_own, 0, hidden_units),
        part(ff_own, hidden_units, hidden_units),
        part(ff_own, 2 * hidden_units, hidden_units).T,
        grad_embed_own[:, :vocab].astype(F32).T,
        own[:, base],
        own[:, base + 1],
        own[:, base + 2],
        own[:, base + 3],
    )


def solution(mesh):
    rows_cols = P(PLANE, "tp")
    cols_rows = P("tp", PLANE)
    data = P(PLANE, None)
    flat = P(PLANE)
    weights = (rows_cols,) * 3 + (cols_rows,) + (rows_cols,) * 3 + (cols_rows,)
    weights += (rows_cols,) * 2 + (cols_rows,) * 2 + (flat,) * 4
    return jax.shard_map(
        local,
        mesh=mesh,
        in_specs=(data, data, data, P("fsdp", None), flat) + weights,
        out_specs=(data, flat, flat, data, data) + weights,
        check_vma=False,
    )
```
